32 devices in a mesh: fsdp: 4 (over z), ctx: 2 (over x), tp: 4 (over y, core).
Axes of the slice: x: 2, y: 2, z: 4, core: 2. Of those that a mesh axis runs over, the one named last changes fastest.
Arguments:
- tokens: bfloat16 [8, 1024, 1024], P('fsdp', ('ctx', 'tp')), may hold values from -6 to 6
- key_valid: int32 [8, 1024], P('fsdp'), may hold values from 0 to 1, as said below
- first_gain: bfloat16 [2, 1024], P(None, 'fsdp'), may hold values from 0.25 to 1.75
- first_shift: bfloat16 [2, 1024], P(None, 'fsdp'), may hold values from -1.75 to 1.75
- joint_weight: bfloat16 [2, 1024, 3, 1024], P(None, 'fsdp', None, 'tp'), may hold values from -0.1875 to 0.1875
- query_bias: bfloat16 [2, 16, 64], P(None, 'tp', 'fsdp'), may hold values from -3 to 3
- value_bias: bfloat16 [2, 16, 64], P(None, 'tp', 'fsdp'), may hold values from -0.625 to 0.625
- out_weight: bfloat16 [2, 1024, 1024], P(None, 'tp', 'fsdp'), may hold values from -0.75 to 0.75
- out_bias: bfloat16 [2, 1024], P(None, 'fsdp'), may hold values from -1.75 to 1.75
- second_gain: bfloat16 [2, 1024], P(None, 'fsdp'), may hold values from 0.25 to 1.75
- second_shift: bfloat16 [2, 1024], P(None, 'fsdp'), may hold values from -1.75 to 1.75
- expand_weight: bfloat16 [2, 1024, 4096], P(None, 'fsdp', 'tp'), may hold values from -0.1875 to 0.1875
- expand_bias: bfloat16 [2, 64, 64], P(None, 'tp', 'fsdp'), may hold values from -3 to 3
- reduce_weight: bfloat16 [2, 4096, 1024], P(None, 'tp', 'fsdp'), may hold values from -0.09375 to 0.09375
- reduce_bias: bfloat16 [2, 1024], P(None, 'fsdp'), may hold values from -1.75 to 1.75
- cotangent: bfloat16 [8, 1024, 1024], P('fsdp', ('ctx', 'tp')), may hold values from -6 to 6
Outputs:
- output: bfloat16 [8, 1024, 1024], P('fsdp', ('ctx', 'tp'))
- input_grad: bfloat16 [8, 1024, 1024], P('fsdp', ('ctx', 'tp'))
- grad_first_gain: float32 [2, 1024], P(None, 'fsdp')
- grad_first_shift: float32 [2, 1024], P(None, 'fsdp')
- grad_joint_weight: float32 [2, 1024, 3, 1024], P(None, 'fsdp', None, 'tp')
- grad_query_bias: float32 [2, 16, 64], P(None, 'tp', 'fsdp')
- grad_value_bias: float32 [2, 16, 64], P(None, 'tp', 'fsdp')
- grad_out_weight: float32 [2, 1024, 1024], P(None, 'tp', 'fsdp')
- grad_out_bias: float32 [2, 1024], P(None, 'fsdp')
- grad_second_gain: float32 [2, 1024], P(None, 'fsdp')
- grad_second_shift: float32 [2, 1024], P(None, 'fsdp')
- grad_expand_weight: float32 [2, 1024, 4096], P(None, 'fsdp', 'tp')
- grad_expand_bias: float32 [2, 64, 64], P(None, 'tp', 'fsdp')
- grad_reduce_weight: float32 [2, 4096, 1024], P(None, 'tp', 'fsdp')
- grad_reduce_bias: float32 [2, 1024], P(None, 'fsdp')
The draws below stay inside these ranges and needn't reach their ends.
Inputs may be any that keep to these rules, and one draw needn't show every extreme that they name: `key_valid`: in each clip the ones form a prefix of 128 tokens or more; clip 0 has ones throughout.
All inputs are finite; a program needn't handle non-finite values.
Results may differ from the reference program's by a relative error of at most 0.02.
Values may be sent and summed in bfloat16 or wider, within the bound.
A program may use at most 256 MiB of HBM per device.

```python
import jax
import jax.numpy as jnp
from jax import lax

D = 1024
FF = 4096
HD = 64
H = 16
L = 1024
LAYERS = 2
CLIPS = 8


def draw_key_valid(key, part):
    lengths = jax.random.randint(key, (CLIPS,), L // 8, L + 1).astype(jnp.int32)
    lengths = lengths.at[0].set(L)
    places = jnp.arange(L, dtype=jnp.int32)
    return (places[None, :] < lengths[:, None]).astype(jnp.int32)


def shard_levels(key, extent, shards, smallest, high):
    level = 1.0
    for position, parts in shards:
        draws = jax.random.uniform(jax.random.fold_in(jax.random.fold_in(key, 6), position), (parts,), jnp.float32, smallest / len(shards), high / len(shards))
        level = level * jnp.repeat(jnp.exp(draws), extent[position] // parts).reshape((-1,) + (1,) * (len(extent) - 1 - position))
    return level


def scatter_about(key, extent, deviation, limit, split=(), kind=jnp.bfloat16):
    level = shard_levels(key, extent, split, -0.22, 0.18) if split else 1.0
    drawn = jax.random.normal(key, extent, jnp.float32) * deviation * level
    return jnp.minimum(jnp.maximum(drawn, -limit), limit).astype(kind)


def setup_inputs(seed: int = 0) -> dict:
    key_of = jax.random.split(jax.random.key(seed), 17)
    return {
        "tokens": scatter_about(key_of[0], (CLIPS, L, D), 1.0, 6.0, ((0, 4), (1, 8))),
        "key_valid": draw_key_valid(jax.random.fold_in(key_of[16], 71), 0),
        "first_gain": jnp.clip(1.0 + 0.15 * jax.random.normal(key_of[2], (LAYERS, D), jnp.float32), 0.25, 1.75).astype(jnp.bfloat16),
        "first_shift": scatter_about(key_of[3], (LAYERS, D), 0.3, 1.75, ((1, 4),)),
        "joint_weight": scatter_about(key_of[4], (LAYERS, D, 3, D), D ** -0.5, 0.1875, ((1, 4), (3, 4))),
        "query_bias": scatter_about(key_of[5], (LAYERS, H, HD), 0.5, 3.0, ((1, 4), (2, 4))),
        "value_bias": scatter_about(key_of[6], (LAYERS, H, HD), 0.1, 0.625, ((1, 4), (2, 4))),
        "out_weight": scatter_about(key_of[7], (LAYERS, D, D), (D // 16) ** -0.5, 0.75, ((1, 4), (2, 4))),
        "out_bias": scatter_about(key_of[8], (LAYERS, D), 0.3, 1.75, ((1, 4),)),
        "second_gain": jnp.clip(1.0 + 0.15 * jax.random.normal(key_of[9], (LAYERS, D), jnp.float32), 0.25, 1.75).astype(jnp.bfloat16),
        "second_shift": scatter_about(key_of[10], (LAYERS, D), 0.3, 1.75, ((1, 4),)),
        "expand_weight": scatter_about(key_of[11], (LAYERS, D, FF), D ** -0.5, 0.1875, ((1, 4), (2, 4))),
        "expand_bias": scatter_about(key_of[12], (LAYERS, FF // HD, HD), 0.5, 3.0, ((1, 4), (2, 4))),
        "reduce_weight": scatter_about(key_of[13], (LAYERS, FF, D), FF ** -0.5, 0.09375, ((1, 4), (2, 4))),
        "reduce_bias": scatter_about(key_of[14], (LAYERS, D), 0.3, 1.75, ((1, 4),)),
        "cotangent": scatter_about(key_of[15], (CLIPS, L, D), 1.0, 6.0, ((0, 4), (1, 8))),
    }


@jax.custom_vjp
def low(v):
    return lax.optimization_barrier(v.astype(jnp.bfloat16)).astype(jnp.float32)

@jax.custom_vjp
def low_back(v):
    return v

def low_keep(v):
    return (low(v), None)

def low_pass(kept, grad):
    return (grad,)

def back_keep(v):
    return (v, None)

def back_low(kept, grad):
    return (low(grad),)
low.defvjp(low_keep, low_pass)
low_back.defvjp(back_keep, back_low)
epsilon = 1e-06
masked_score = -10000.0
highest = lax.Precision.HIGHEST

def norm_rows(rows, gain, shift):
    middle = lax.optimization_barrier(jnp.mean(rows, axis=-1, keepdims=True))
    centred = rows - middle
    spread = lax.optimization_barrier(jnp.mean(centred * centred, axis=-1, keepdims=True))
    return centred * lax.rsqrt(spread + epsilon) * gain + shift

def product(left, right):
    return jnp.dot(left, right, precision=highest)

def encoder_layer(residual, key_bias, layer_weights):
    gain_attn, shift_attn, joint_mat, query_add, value_add, out_mat, out_add, gain_mlp, shift_mlp, expand_mat, expand_add, reduce_mat, reduce_add = layer_weights
    count = residual.shape[0]
    first_in = low(norm_rows(residual, gain_attn, shift_attn))
    queries = low_back(low(product(first_in, joint_mat[:, 0, :]) + query_add.reshape(-1)))
    keys_all = low_back(low(product(first_in, joint_mat[:, 1, :])))
    values_all = low_back(low(product(first_in, joint_mat[:, 2, :]) + value_add.reshape(-1)))
    query_heads = queries.reshape(count, -1, HD)
    key_heads = keys_all.reshape(count, -1, HD)
    value_heads = values_all.reshape(count, -1, HD)
    raw_scores = low_back(jnp.einsum('qhd,khd->hqk', query_heads, key_heads, precision=highest))
    attn_probs = jax.nn.softmax(raw_scores * HD ** (-0.5) + key_bias, axis=-1)
    mixed = jnp.einsum('hqk,khd->qhd', low(attn_probs), value_heads, precision=highest).reshape(count, -1)
    mixed = low_back(low(mixed))
    middle = residual + low_back(product(mixed, out_mat) + out_add)
    second_in = low(norm_rows(middle, gain_mlp, shift_mlp))
    before = low_back(product(second_in, expand_mat) + expand_add.reshape(-1))
    active = low(jax.nn.gelu(before, approximate=False))
    return middle + low_back(product(active, reduce_mat) + reduce_add)

def reference(tokens, key_valid, first_gain, first_shift, joint_weight, query_bias, value_bias, out_weight, out_bias, second_gain, second_shift, expand_weight, expand_bias, reduce_weight, reduce_bias, cotangent):
    weights = tuple((w.astype(jnp.float32) for w in (first_gain, first_shift, joint_weight, query_bias, value_bias, out_weight, out_bias, second_gain, second_shift, expand_weight, expand_bias, reduce_weight, reduce_bias)))

    def forward(clip_rows, key_bias, all_weights):
        hidden = clip_rows
        for layer_id in range(LAYERS):
            hidden = encoder_layer(hidden, key_bias, tuple((w[layer_id] for w in all_weights)))
        return hidden

    def one_clip(totals, item):
        clip_rows, clip_valid, clip_cot = item
        key_bias = jnp.where(clip_valid == 1, 0.0, masked_score).astype(jnp.float32)
        result, pullback = jax.vjp(lambda rows, ws: forward(rows, key_bias, ws), clip_rows.astype(jnp.float32), weights)
        row_grad, weight_grads = pullback(clip_cot.astype(jnp.float32))
        totals = tuple((old + new for old, new in zip(totals, weight_grads)))
        return (totals, (result.astype(jnp.bfloat16), row_grad.astype(jnp.bfloat16)))
    zeros = tuple((jnp.zeros_like(w) for w in weights))
    grads, (outputs, row_grads) = lax.scan(one_clip, zeros, (tokens, key_valid, cotangent))
    return (outputs, row_grads, grads[0], grads[1], grads[2], grads[3], grads[4], grads[5], grads[6], grads[7], grads[8], grads[9], grads[10], grads[11], grads[12])
```

```python
import functools
import math

import jax
import jax.numpy as jnp
from jax import lax
from jax.experimental import pallas as pl
from jax.experimental.pallas import tpu as pltpu
from jax.sharding import PartitionSpec as P

HD = 64
LAYERS = 2
LANES = 128
EPS = 1e-06
MASKED = -10000.0
SCALE = HD ** (-0.5)
VMEM_LIMIT = 60 * 1024 * 1024
F32 = jnp.float32
BF16 = jnp.bfloat16
VMEM = pltpu.VMEM
INV_SQRT2 = 1.0 / math.sqrt(2.0)
INV_SQRT_2PI = 1.0 / math.sqrt(2.0 * math.pi)


def mm(a, b):
    return lax.dot_general(a, b, (((1,), (0,)), ((), ())), preferred_element_type=F32)


def mm_nt(a, b):
    return lax.dot_general(a, b, (((1,), (1,)), ((), ())), preferred_element_type=F32)


def mm_tn(a, b):
    return lax.dot_general(a, b, (((0,), (0,)), ((), ())), preferred_element_type=F32)


def partners():
    t = lax.axis_index("tp")
    return t, t + 1 - 2 * (t % 2), (t + 2) % 4


def entry_barrier(sib, peer):
    barrier = pltpu.get_barrier_semaphore()
    for other in (sib, peer):
        pl.semaphore_signal(
            barrier, inc=1, device_id={"tp": other}, device_id_type=pl.DeviceIdType.MESH
        )
    pl.semaphore_wait(barrier, 2)


class Links:
    def __init__(self, send, recv, sib, peer):
        self.send, self.recv, self.sib, self.peer = send, recv, sib, peer

    def make(self, kind, s, src, dst, other):
        return pltpu.make_async_remote_copy(
            src_ref=src,
            dst_ref=dst,
            send_sem=self.send.at[kind, s],
            recv_sem=self.recv.at[kind, s],
            device_id={"tp": other},
            device_id_type=pl.DeviceIdType.MESH,
        )


def statistics(rows):
    mean = jnp.mean(rows, axis=-1, keepdims=True)
    centred = rows - mean
    inverse = lax.rsqrt(jnp.mean(centred * centred, axis=-1, keepdims=True) + EPS)
    return centred * inverse, inverse


def norm_back(rows, d_out, gain):
    unit, inverse = statistics(rows)
    e = d_out * gain
    back = inverse * (
        e
        - jnp.mean(e, axis=-1, keepdims=True)
        - unit * jnp.mean(e * unit, axis=-1, keepdims=True)
    )
    d_gain = jnp.sum(d_out * unit, axis=0, keepdims=True)
    d_shift = jnp.sum(d_out, axis=0, keepdims=True)
    return back, d_gain, d_shift


def rows_of(ref, b):
    block = ref[b]
    return block.reshape(block.shape[0] * block.shape[1], block.shape[2])


def gather_start(links, base, out, s):
    links.make(base, s, out.at[2 + s, 0], out.at[2 + s, 1], links.sib).start()
    links.make(base + 1, s, out.at[2 + s, 0], out.at[s, 0], links.peer).start()


def gather_end(links, base, out):
    for s in range(2):
        links.make(base + 1, s, out.at[2 + s, 0], out.at[s, 0], links.peer).wait_recv()
        links.make(base + 2, s, out.at[s, 0], out.at[s, 1], links.sib).start()
    for s in range(2):
        for kind, src, dst, other in (
            (base, out.at[2 + s, 0], out.at[2 + s, 1], links.sib),
            (base + 2, out.at[s, 0], out.at[s, 1], links.sib),
        ):
            links.make(kind, s, src, dst, other).wait()
        links.make(base + 1, s, out.at[2 + s, 0], out.at[s, 0], links.peer).wait_send()


class Scatter:
    def __init__(self, links, part, sent, got, own):
        self.links, self.part, self.sent, self.got, self.own = links, part, sent, got, own

    def copy(self, kind, s):
        other = self.links.peer if kind == 1 else self.links.sib
        return self.links.make(kind, s, self.sent.at[kind, s], self.got.at[kind, s], other)

    def block(self, b):
        s = b % 2
        half = self.part.shape[0] // 2

        @pl.when(b < 2)
        def _():
            self.sent[0, s] = self.part[half:].astype(BF16)
            first = self.copy(0, s)
            first.start()
            first.wait_recv()
            self.sent[1, s] = (self.part[:half] + self.got[0, s].astype(F32)).astype(BF16)
            self.copy(1, s).start()

        @pl.when(b >= 2)
        def _():
            self.sent[2, s] = self.part[half:].astype(BF16)
            self.copy(2, s).start()
            self.own[s] = self.part[:half]

    def total(self, s):
        self.copy(2, s).wait_recv()
        self.copy(1, s).wait_recv()
        return self.own[s] + self.got[2, s].astype(F32) + self.got[1, s].astype(F32)

    def end(self):
        for s in range(2):
            for kind in range(3):
                self.copy(kind, s).wait_send()


def scatter_scratch(half, width):
    return [
        VMEM((2 * half, width), F32),
        VMEM((3, 2, half, width), BF16),
        VMEM((3, 2, half, width), BF16),
        VMEM((2, half, width), F32),
        pltpu.SemaphoreType.DMA((6, 2)),
        pltpu.SemaphoreType.DMA((6, 2)),
    ]


def enter_kernel(tok, cot, gain, shift, first, grad, send, recv):
    t, sib, peer = partners()
    entry_barrier(sib, peer)
    links = Links(send, recv, sib, peer)
    for s in range(2):
        unit, _ = statistics(tok[s].astype(F32))
        first[2 + s, 0] = (unit * gain[...] + shift[...]).astype(BF16)
        gather_start(links, 0, first, s)
    for s in range(2):
        grad[2 + s, 0] = cot[s]
        gather_start(links, 3, grad, s)
    gather_end(links, 0, first)
    gather_end(links, 3, grad)


def pair_tile(pair, h):
    tile = pair if h % 2 == 0 else pltpu.roll(pair, HD, 1)
    return tile


def attention_kernel(
    heads,
    first, weight, q_bias, v_bias, key_extra, resid, out_bias, gain, shift,
    second, middle, q_out, k_out, v_out, mixed_out,
    part, sent, got, own, send, recv,
):
    t, sib, peer = partners()
    entry_barrier(sib, peer)
    links = Links(send, recv, sib, peer)
    scatter = Scatter(links, part, sent, got, own)
    width = heads * HD
    half = first.shape[2]
    rows = 2 * half
    lane = lax.broadcasted_iota(jnp.int32, (rows, LANES), 1)
    head_lane = lane < HD
    q_extra = jnp.where(lane < HD + 2, 1.0, 0.0).astype(BF16)
    v_extra = jnp.where(lane < HD + 3, 1.0, 0.0).astype(BF16)

    def project(b, carry):
        x = rows_of(first, b)
        y = mm(x, weight[:, : 3 * width])
        q = ((y[:, :width] + q_bias[...]).astype(BF16) * SCALE).astype(BF16)
        k = y[:, width : 2 * width].astype(BF16)
        v = (y[:, 2 * width :] + v_bias[...]).astype(BF16)
        g, s = b // 2, b % 2
        mine = jnp.where(g == 1, t, peer)
        other = mine + 1 - 2 * (mine % 2)
        extra = jnp.concatenate([key_extra[mine, s], key_extra[other, s]], axis=0)
        at = pl.ds(pl.multiple_of(b * rows, rows), rows)
        for h in range(heads):
            cut = slice(LANES * (h // 2), LANES * (h // 2 + 1))
            q_out[h, at, :] = jnp.where(head_lane, pair_tile(q[:, cut], h), q_extra)
            k_out[h, at, :] = jnp.where(head_lane, pair_tile(k[:, cut], h), extra)
            v_out[h, at, :] = jnp.where(head_lane, pair_tile(v[:, cut], h), v_extra)
        return carry

    lax.fori_loop(0, 4, project, 0)

    def attend(b, carry):
        at = pl.ds(pl.multiple_of(b * rows, rows), rows)
        outs = []
        for h in range(heads):
            q = q_out[h, at, :]
            scores = mm_nt(q, k_out[h])
            top = jnp.max(scores, axis=-1, keepdims=True)
            weights = jnp.exp(scores - top).astype(BF16)
            summed = mm(weights, v_out[h])
            total = summed[:, HD : HD + 1]
            outs.append(summed / total)
            log_total = -(top + jnp.log(total))
            high = log_total.astype(BF16).astype(F32)
            rest = log_total - high
            mid = rest.astype(BF16).astype(F32)
            low = rest - mid
            tail = jnp.where(lane == HD + 2, high, jnp.where(lane == HD + 3, mid, low))
            q_out[h, at, :] = jnp.where(
                (lane >= HD + 2) & (lane < HD + 5), tail.astype(BF16), q
            )
        tiles = [
            jnp.where(head_lane, outs[h], pltpu.roll(outs[h + 1], HD, 1))
            for h in range(0, heads, 2)
        ]
        mixed = jnp.concatenate(tiles, axis=1).astype(BF16)
        mixed_out[at, :] = mixed
        part[...] = mm_nt(mixed, weight[:, 3 * width :])
        scatter.block(b)
        return carry

    lax.fori_loop(0, 4, attend, 0)
    for s in range(2):
        mid = resid[s].astype(F32) + (scatter.total(s) + out_bias[...])
        middle[s] = mid
        unit, _ = statistics(mid)
        second[2 + s, 0] = (unit * gain[...] + shift[...]).astype(BF16)
        gather_start(links, 3, second, s)
    gather_end(links, 3, second)
    scatter.end()


def mlp_kernel(
    last,
    second, weight, bias, middle, out_bias, gain, shift,
    active_out, slope_out, resid, nxt,
    part, sent, got, own, send, recv,
):
    t, sib, peer = partners()
    entry_barrier(sib, peer)
    links = Links(send, recv, sib, peer)
    scatter = Scatter(links, part, sent, got, own)
    half = second.shape[2]
    rows = 2 * half
    hidden = bias.shape[1]
    step = 256

    def block(b, carry):
        at = pl.ds(pl.multiple_of(b * rows, rows), rows)
        x = rows_of(second, b)
        for n in range(0, hidden, step):
            before = mm(x, weight[:, n : n + step]) + bias[:, n : n + step]
            cdf = 0.5 * (1.0 + lax.erf(before * INV_SQRT2))
            active_out[at, n : n + step] = (before * cdf).astype(BF16)
            slope = cdf + before * (jnp.exp(before * before * -0.5) * INV_SQRT_2PI)
            slope_out[at, n : n + step] = slope.astype(BF16)
        part[...] = mm_nt(active_out[at, :], weight[:, hidden:])
        scatter.block(b)
        return carry

    lax.fori_loop(0, 4, block, 0)
    for s in range(2):
        res = middle[s] + (scatter.total(s) + out_bias[...])
        if last:
            nxt[s] = res.astype(BF16)
        else:
            resid[s] = res
            unit, _ = statistics(res)
            nxt[2 + s, 0] = (unit * gain[...] + shift[...]).astype(BF16)
            gather_start(links, 3, nxt, s)
    if not last:
        gather_end(links, 3, nxt)
    scatter.end()


def token_product(left, right, out, at, rows, offset):
    depth = left.shape[-1]
    total = left.shape[0] * left.shape[1] * left.shape[2]
    step = 256

    def body(j, carry):
        cut = pl.ds(pl.multiple_of(j * step, step), step)
        x = left[:, :, :, cut].reshape(total, step)
        out[cut, offset : offset + right.shape[-1]] = mm_tn(x, right[...]).astype(BF16)
        return carry

    lax.fori_loop(0, depth // step, body, 0)


def mlp_back_kernel(
    grad, weight, active, slope, second, middle, carry_in, gain,
    weight_grad, carry_out, rows_out, vectors,
    part, sent, got, own, send, recv, d_before,
):
    t, sib, peer = partners()
    entry_barrier(sib, peer)
    links = Links(send, recv, sib, peer)
    scatter = Scatter(links, part, sent, got, own)
    half = grad.shape[2]
    rows = 2 * half
    hidden = active.shape[1]
    step = 256
    vectors[...] = jnp.zeros_like(vectors)

    def block(b, carry):
        at = pl.ds(pl.multiple_of(b * rows, rows), rows)
        x = rows_of(grad, b)
        for n in range(0, hidden, step):
            d_act = mm(x, weight[:, hidden + n : hidden + n + step])
            d_bef = (d_act * slope[at, n : n + step].astype(F32)).astype(BF16)
            d_before[at, n : n + step] = d_bef
            vectors[4:5, n : n + step] += jnp.sum(d_bef.astype(F32), axis=0, keepdims=True)
        part[...] = mm_nt(d_before[at, :], weight[:, :hidden])
        scatter.block(b)
        return carry

    lax.fori_loop(0, 4, block, 0)
    token_product(grad, active, weight_grad, None, rows, hidden)

    def finish(s):
        back, d_gain, d_shift = norm_back(middle[s], scatter.total(s), gain[...])
        carry = carry_in[s].astype(F32)
        mid = carry + back
        carry_out[s] = mid
        low = mid.astype(BF16)
        rows_out[2 + s, 0] = low
        gather_start(links, 3, rows_out, s)
        vectors[0:1, :] += d_gain
        vectors[1:2, :] += d_shift
        vectors[2:3, :] += jnp.sum(low.astype(F32), axis=0, keepdims=True)
        vectors[3:4, :] += jnp.sum(carry.astype(BF16).astype(F32), axis=0, keepdims=True)

    finish(0)
    token_product(second, d_before, weight_grad, None, rows, 0)
    finish(1)
    gather_end(links, 3, rows_out)
    scatter.end()


def attention_back_kernel(
    heads, last,
    grad, weight, mixed, q_in, k_in, v_in, first, carry_in, resid, gain,
    weight_grad, carry_out, rows_out, vectors,
    part, sent, got, own, send, recv, d_out, d_joint, d_key, d_value,
):
    t, sib, peer = partners()
    entry_barrier(sib, peer)
    links = Links(send, recv, sib, peer)
    scatter = Scatter(links, part, sent, got, own)
    width = heads * HD
    half = grad.shape[2]
    rows = 2 * half
    lane = lax.broadcasted_iota(jnp.int32, (rows, LANES), 1)
    head_lane = lane < HD
    vectors[...] = jnp.zeros_like(vectors)
    d_key[...] = jnp.zeros_like(d_key)
    d_value[...] = jnp.zeros_like(d_value)

    def pairs(tiles):
        return jnp.concatenate(
            [
                jnp.where(head_lane, tiles[h], pltpu.roll(tiles[h + 1], HD, 1))
                for h in range(0, heads, 2)
            ],
            axis=1,
        )

    def attend(b, carry):
        at = pl.ds(pl.multiple_of(b * rows, rows), rows)
        d_mixed = mm(rows_of(grad, b), weight[:, 3 * width :]).astype(BF16)
        product = d_mixed.astype(F32) * mixed[at, :].astype(F32)
        d_queries = []
        for h in range(heads):
            cut = slice(LANES * (h // 2), LANES * (h // 2 + 1))
            keep = head_lane if h % 2 == 0 else lane >= HD
            delta = -jnp.sum(jnp.where(keep, product[:, cut], 0.0), axis=-1, keepdims=True)
            high = delta.astype(BF16).astype(F32)
            rest = delta - high
            mid = rest.astype(BF16).astype(F32)
            low = rest - mid
            tail = jnp.where(
                lane == HD,
                high,
                jnp.where(lane == HD + 1, mid, jnp.where(lane == HD + 2, low, 0.0)),
            ).astype(BF16)
            d_o = jnp.where(head_lane, pair_tile(d_mixed[:, cut], h), tail)
            q = q_in[h, at, :]
            probs = jnp.exp(mm_nt(k_in[h], q))
            d_value[h] += mm(probs.astype(BF16), d_o)
            d_raw = (probs * mm_nt(v_in[h], d_o)).astype(BF16)
            d_key[h] += mm(d_raw, q)
            d_queries.append(mm_tn(d_raw, k_in[h]) * SCALE)
        d_joint[at, :width] = pairs(d_queries).astype(BF16)
        return carry

    lax.fori_loop(0, 4, attend, 0)

    def project(b, carry):
        at = pl.ds(pl.multiple_of(b * rows, rows), rows)
        d_joint[at, width : 2 * width] = pairs([d_key[h, at, :] for h in range(heads)]).astype(BF16)
        d_joint[at, 2 * width :] = pairs([d_value[h, at, :] for h in range(heads)]).astype(BF16)
        d_rows = d_joint[at, :]
        sums = jnp.sum(d_rows.astype(F32), axis=0, keepdims=True)
        vectors[2:3, :width] += sums[:, :width]
        vectors[2:3, width : 2 * width] += sums[:, 2 * width :]
        part[...] = mm_nt(d_rows, weight[:, : 3 * width])
        scatter.block(b)
        return carry

    lax.fori_loop(0, 4, project, 0)
    token_product(grad, mixed, weight_grad, None, rows, 3 * width)

    def finish(s):
        back, d_gain, d_shift = norm_back(resid[s].astype(F32), scatter.total(s), gain[...])
        carry = carry_in[s] + back
        if last:
            rows_out[s] = carry.astype(BF16)
        else:
            carry_out[s] = carry
            rows_out[2 + s, 0] = carry.astype(BF16)
            gather_start(links, 3, rows_out, s)
        vectors[0:1, :] += d_gain
        vectors[1:2, :] += d_shift

    finish(0)
    token_product(first, d_joint, weight_grad, None, rows, 0)
    finish(1)
    if not last:
        gather_end(links, 3, rows_out)
    scatter.end()


def call(kernel, name, outs, scratch, collective_id, flops, args):
    size = sum(a.size * a.dtype.itemsize for a in args) + sum(
        math.prod(o.shape) * o.dtype.itemsize for o in outs
    )
    return pl.pallas_call(
        kernel,
        name=name,
        out_shape=tuple(outs),
        in_specs=[pl.BlockSpec(memory_space=VMEM)] * len(args),
        out_specs=tuple(pl.BlockSpec(memory_space=VMEM) for _ in outs),
        scratch_shapes=scratch,
        compiler_params=pltpu.CompilerParams(
            collective_id=collective_id, has_side_effects=True, vmem_limit_bytes=VMEM_LIMIT
        ),
        cost_estimate=pl.CostEstimate(flops=flops, bytes_accessed=size, transcendentals=0),
    )(*args)


def local(
    tokens, key_valid, first_gain, first_shift, joint_weight, query_bias, value_bias,
    out_weight, out_bias, second_gain, second_shift, expand_weight, expand_bias,
    reduce_weight, reduce_bias, cotangent,
):
    ctx_size = lax.axis_size("ctx")
    tp_size = lax.axis_size("tp")
    fsdp_size = lax.axis_size("fsdp")
    clips, half, dim = tokens.shape
    assert clips == ctx_size == 2 and tp_size == 4 and joint_weight.shape[0] == LAYERS
    c = lax.axis_index("ctx")
    t = lax.axis_index("tp")
    shard = joint_weight.shape[1]
    width = joint_weight.shape[3]
    heads = width // HD
    hidden = expand_weight.shape[2]
    swap = [(0, 1), (1, 0)]

    piece = shard // ctx_size

    def gathered(parts):
        packed = jnp.concatenate(parts, axis=1)
        mine = lax.dynamic_slice_in_dim(packed, c * piece, piece, 0)
        return lax.all_gather(mine, ("fsdp", "ctx"), axis=0, tiled=True)

    attn_weights, mlp_weights = [], []
    for l in range(LAYERS):
        joint = joint_weight[l]
        attn_weights.append(
            gathered([joint[:, 0], joint[:, 1], joint[:, 2], out_weight[l].T])
        )
        mlp_weights.append(gathered([expand_weight[l], reduce_weight[l].T]))

    wide = [first_gain, first_shift, out_bias, second_gain, second_shift, reduce_bias]
    narrow = [query_bias, value_bias, expand_bias]
    small = jnp.concatenate([a.reshape(-1) for a in wide + narrow])
    small = lax.all_gather(small, "fsdp", axis=0).astype(F32)
    params = []
    at = 0
    for a in wide:
        n = a.size
        got = small[:, at : at + n].reshape(fsdp_size, LAYERS, shard)
        params.append(got.transpose(1, 0, 2).reshape(LAYERS, 1, dim))
        at += n
    for a in narrow:
        n = a.size
        got = small[:, at : at + n].reshape(fsdp_size, *a.shape)
        params.append(got.transpose(1, 2, 0, 3).reshape(LAYERS, 1, a.shape[1] * HD))
        at += n
    g1, s1, ob, g2, s2, rb, qb, vb, eb = params

    def regroup(both):
        mine = lax.dynamic_index_in_dim(both, c, 0, keepdims=False)
        theirs = lax.dynamic_index_in_dim(both, 1 - c, 0, keepdims=False)
        got = lax.ppermute(theirs, "ctx", swap)
        return jnp.where(c == 0, jnp.stack([mine, got]), jnp.stack([got, mine]))

    tok = regroup(tokens)
    cot = regroup(cotangent)
    valid = lax.dynamic_index_in_dim(key_valid, c, 0, keepdims=False)
    bias = jnp.where(valid == 1, 0.0, MASKED).astype(F32)
    bias = bias.reshape(ctx_size, tp_size, half, 1).transpose(1, 0, 2, 3)
    high = bias.astype(BF16).astype(F32)
    col = lax.broadcasted_iota(jnp.int32, (1, 1, 1, LANES), 3) - HD
    key_extra = jnp.where(
        col == 0, high, jnp.where(col == 1, bias - high, jnp.where((col >= 2) & (col < 5), 1.0, 0.0))
    ).astype(BF16)

    every = jax.ShapeDtypeStruct((4, 2, half, dim), BF16)
    own = jax.ShapeDtypeStruct((2, half, dim), F32)
    own_low = jax.ShapeDtypeStruct((2, half, dim), BF16)
    count = 8 * half
    scratch = scatter_scratch(half, dim)

    first, grad = call(
        enter_kernel, "enter", [every, every],
        [pltpu.SemaphoreType.DMA((6, 2)), pltpu.SemaphoreType.DMA((6, 2))],
        0, 10**7, [tok, cot, g1[0], s1[0]],
    )
    resid = tok
    saved = []
    for l in range(LAYERS):
        heads_shape = jax.ShapeDtypeStruct((heads, count, LANES), BF16)
        second, middle, q, k, v, mixed = call(
            functools.partial(attention_kernel, heads), "attention",
            [every, own, heads_shape, heads_shape, heads_shape, jax.ShapeDtypeStruct((count, width), BF16)],
            scratch, 1 + 6 * l, 2 * count * dim * 4 * width + 16 * heads * count * count * HD,
            [first, attn_weights[l], qb[l], vb[l], key_extra, resid, ob[l], g2[l], s2[l]],
        )
        last = l == LAYERS - 1
        nxt_l = l if last else l + 1
        rows_hidden = jax.ShapeDtypeStruct((count, hidden), BF16)
        active, slope, out, nxt = call(
            functools.partial(mlp_kernel, last), "mlp_last" if last else "mlp",
            [rows_hidden, rows_hidden,
             jax.ShapeDtypeStruct((8, LANES), F32) if last else own, own_low if last else every],
            scratch, 2 + 6 * l, 4 * count * dim * hidden,
            [second, mlp_weights[l], eb[l], middle, rb[l], g1[nxt_l], s1[nxt_l]],
        )
        saved.append((resid, first, q, k, v, mixed, middle, second, active, slope))
        resid, first = out, nxt
    output = nxt

    vec = jax.ShapeDtypeStruct((8, dim), F32)
    carry = cot
    attn_grads, mlp_grads, attn_vec, mlp_vec = ([None] * LAYERS for _ in range(4))

    def reduced(full):
        part = lax.psum_scatter(full, ("fsdp", "ctx"), scatter_dimension=0, tiled=True)
        return lax.all_gather(part, "ctx", axis=0, tiled=True).astype(F32)

    for l in reversed(range(LAYERS)):
        resid, first, q, k, v, mixed, middle, second, active, slope = saved[l]
        w_grad, carry, grad, mlp_vec[l] = call(
            mlp_back_kernel, "mlp_back",
            [jax.ShapeDtypeStruct((dim, 2 * hidden), BF16), own, every, vec],
            scratch + [VMEM((count, hidden), BF16)], 3 + 6 * l, 8 * count * dim * hidden,
            [grad, mlp_weights[l], active, slope, second, middle, carry, g2[l]],
        )
        mlp_grads[l] = reduced(w_grad)
        last = l == 0
        w_grad, carry, grad, attn_vec[l] = call(
            functools.partial(attention_back_kernel, heads, last),
            "attention_back_last" if last else "attention_back",
            [jax.ShapeDtypeStruct((dim, 4 * width), BF16),
             jax.ShapeDtypeStruct((8, LANES), F32) if last else own, own_low if last else every, vec],
            scratch
            + [
                VMEM((heads, 8, LANES), BF16),
                VMEM((count, 3 * width), BF16),
                VMEM((heads, count, LANES), F32),
                VMEM((heads, count, LANES), F32),
            ],
            4 + 6 * l, 4 * count * dim * 4 * width + 40 * heads * count * count * HD,
            [grad, attn_weights[l], mixed, q, k, v, first, carry, resid, g1[l]],
        )
        attn_grads[l] = reduced(w_grad)
    row_grad = grad

    def ungroup(both):
        mine = lax.dynamic_index_in_dim(both, c, 0, keepdims=False)
        theirs = lax.dynamic_index_in_dim(both, 1 - c, 0, keepdims=False)
        got = lax.ppermute(theirs, "ctx", swap)
        return jnp.where(c == 0, jnp.stack([mine, got]), jnp.stack([got, mine]))

    pieces = []
    for l in range(LAYERS):
        pieces += [attn_vec[l][0], attn_vec[l][1], mlp_vec[l][2], mlp_vec[l][0], mlp_vec[l][1], mlp_vec[l][3]]
    flat = jnp.concatenate(pieces)
    slots = jnp.concatenate(
        [jnp.concatenate([attn_vec[l][2][: 2 * width], mlp_vec[l][4][:hidden]]) for l in range(LAYERS)]
    )
    placed = jnp.where(
        lax.broadcasted_iota(jnp.int32, (tp_size, 1), 0) == t, slots[None, :], 0.0
    )
    summed = lax.psum(jnp.concatenate([flat, placed.reshape(-1)]), ("fsdp", "ctx", "tp"))
    f = lax.axis_index("fsdp")
    rows = summed[: flat.size].reshape(LAYERS, 6, fsdp_size, shard)
    rows = lax.dynamic_index_in_dim(rows, f, 2, keepdims=False)
    mine = lax.dynamic_index_in_dim(summed[flat.size :].reshape(tp_size, -1), t, 0, keepdims=False)
    mine = mine.reshape(LAYERS, 2 * width + hidden)
    cut = HD // fsdp_size

    def spread(block, n):
        block = block.reshape(LAYERS, n // HD, fsdp_size, cut)
        return lax.dynamic_index_in_dim(block, f, 2, keepdims=False)

    joint = [g[:, : 3 * width].reshape(shard, 3, width) for g in attn_grads]
    return (
        ungroup(output),
        ungroup(row_grad),
        rows[:, 0],
        rows[:, 1],
        jnp.stack(joint),
        spread(mine[:, :width], width),
        spread(mine[:, width : 2 * width], width),
        jnp.stack([g[:, 3 * width :].T for g in attn_grads]),
        rows[:, 2],
        rows[:, 3],
        rows[:, 4],
        jnp.stack([g[:, :hidden] for g in mlp_grads]),
        spread(mine[:, 2 * width :], hidden),
        jnp.stack([g[:, hidden:].T for g in mlp_grads]),
        rows[:, 5],
    )


def solution(mesh):
    vector = P(None, "fsdp")
    by_head = P(None, "tp", "fsdp")
    rows = P("fsdp", ("ctx", "tp"), None)
    return jax.shard_map(
        local,
        mesh=mesh,
        in_specs=(
            rows, P("fsdp", None), vector, vector, P(None, "fsdp", None, "tp"), by_head, by_head,
            by_head, vector, vector, vector, P(None, "fsdp", "tp"), by_head, by_head, vector, rows,
        ),
        out_specs=(
            rows, rows, vector, vector, P(None, "fsdp", None, "tp"), by_head, by_head,
            by_head, vector, vector, vector, P(None, "fsdp", "tp"), by_head, by_head, vector,
        ),
        check_vma=False,
    )
```

```python
import functools
import math

import jax
import jax.numpy as jnp
from jax import lax
from jax.experimental import pallas as pl
from jax.experimental.pallas import tpu as pltpu
from jax.sharding import PartitionSpec as P

HD = 64
LAYERS = 2
LANES = 128
EPS = 1e-06
MASKED = -10000.0
SCALE = HD ** (-0.5)
VMEM_LIMIT = 60 * 1024 * 1024
F32 = jnp.float32
BF16 = jnp.bfloat16
VMEM = pltpu.VMEM
INV_SQRT2 = 1.0 / math.sqrt(2.0)
INV_SQRT_2PI = 1.0 / math.sqrt(2.0 * math.pi)


def mm(a, b):
    return lax.dot_general(a, b, (((1,), (0,)), ((), ())), preferred_element_type=F32)


def mm_nt(a, b):
    return lax.dot_general(a, b, (((1,), (1,)), ((), ())), preferred_element_type=F32)


def mm_tn(a, b):
    return lax.dot_general(a, b, (((0,), (0,)), ((), ())), preferred_element_type=F32)


def partners():
    t = lax.axis_index("tp")
    return t, t + 1 - 2 * (t % 2), (t + 2) % 4


def entry_barrier(jobs=()):
    t, sib, peer = partners()
    others = [{"tp": sib}, {"tp": peer}]
    if any(job.uses_ctx for job in jobs):
        others.append({"ctx": 1 - lax.axis_index("ctx")})
    if any(job.uses_fsdp for job in jobs):
        n = lax.axis_size("fsdp")
        z = lax.axis_index("fsdp")
        others += [{"fsdp": (z + k) % n} for k in range(1, n)]
    barrier = pltpu.get_barrier_semaphore()
    for other in others:
        pl.semaphore_signal(barrier, inc=1, device_id=other, device_id_type=pl.DeviceIdType.MESH)
    pl.semaphore_wait(barrier, len(others))


def remote(src, dst, send, recv, device):
    return pltpu.make_async_remote_copy(
        src_ref=src,
        dst_ref=dst,
        send_sem=send,
        recv_sem=recv,
        device_id=device,
        device_id_type=pl.DeviceIdType.MESH,
    )


DMA = pltpu.SemaphoreType.DMA
HBM_SPEC = pl.BlockSpec(memory_space=pl.ANY)
VMEM_SPEC = pl.BlockSpec(memory_space=VMEM)


class Job:
    uses_ctx = False
    uses_fsdp = False
    ins = ()
    outs = ()
    scratch = ()

    def bind(self, ins, outs, scratch):
        self.c = lax.axis_index("ctx")
        self.z = lax.axis_index("fsdp")
        self.refs(ins, outs, scratch)

    def start(self):
        pass

    def steps(self):
        return []

    def end(self):
        pass


def chunks_of(rows):
    return 2 if rows % 128 == 0 else 1


class WeightGather(Job):
    uses_ctx = uses_fsdp = True

    def __init__(self, packed, n, hooks):
        self.n, self.hooks = n, hooks
        self.ins = [(packed, HBM_SPEC)]
        self.outs = [(jax.ShapeDtypeStruct((n, *packed.shape), BF16), HBM_SPEC)]
        self.rows = packed.shape[1]
        self.ch = chunks_of(self.rows)
        self.scratch = [DMA((max(n, 5), self.ch))] + [DMA((n, self.ch))] * 3 + [DMA]

    def refs(self, ins, outs, scratch):
        (self.src,), (self.out,) = ins, outs
        self.z_send, self.z_recv, self.x_send, self.x_recv, self.near = scratch

    def cut(self, ref, ch):
        size = self.rows // self.ch
        return ref.at[pl.ds(ch * size, size)]

    def over_z(self, k, ch, to):
        return remote(
            self.cut(self.src.at[self.c], ch), self.cut(self.out.at[self.z, self.c], ch),
            self.z_send.at[k, ch], self.z_recv.at[self.z, ch], {"fsdp": to},
        )

    def arrived(self, frm, ch):
        block = self.cut(self.out.at[frm, self.c], ch)
        return remote(block, block, self.z_send.at[4, ch], self.z_recv.at[frm, ch], {"fsdp": 3 - frm})

    def over_x(self, frm, half, ch):
        block = self.cut(self.out.at[frm, half], ch)
        return remote(
            block, block, self.x_send.at[frm, ch], self.x_recv.at[frm, ch], {"ctx": 1 - self.c}
        )

    def copy_near(self):
        return pltpu.make_async_copy(self.src, self.out.at[self.z], self.near)

    def offsets(self):
        if self.n == 4:
            return [(k, off) for k, off in enumerate((1, -1, 2, -2))]
        return [(k, k) for k in range(1, self.n)]

    def inside(self, off):
        other = self.z + off
        return (other >= 0) & (other < self.n) if self.n == 4 else (other > -1)

    def start(self):
        for ch in range(self.ch):
            for k, off in self.offsets():
                @pl.when(self.inside(off))
                def _():
                    self.over_z(k, ch, (self.z + off + self.n) % self.n).start()
        self.copy_near().start()

    def take(self, off):
        frm = (self.z + off + self.n) % self.n

        @pl.when(self.inside(off))
        def _():
            for ch in range(self.ch):
                self.arrived(frm, ch).wait_recv()
                if self.n == 4 and abs(off) == 2:
                    @pl.when((self.z == 2) & (frm == 0) | (self.z == 1) & (frm == 3))
                    def _():
                        self.arrived(frm, ch).start()
                self.over_x(frm, self.c, ch).start()

    def steps(self):
        if self.n == 4:
            groups = [(1, -1), (2, -2), (3, -3)]
        else:
            groups = [tuple(range(1, self.n))]
        out = []
        for hook, group in zip(self.hooks, groups):
            for off in group:
                out.append((hook, functools.partial(self.take, off)))
        return out

    def end(self):
        for ch in range(self.ch):
            for off in (1, -1, 2, -2, 3, -3) if self.n == 4 else range(1, self.n):
                frm = (self.z + off + self.n) % self.n

                @pl.when(self.inside(off))
                def _():
                    self.over_x(frm, 1 - self.c, ch).wait_recv()
                    self.over_x(frm, self.c, ch).wait_send()
            for k, off in self.offsets():
                @pl.when(self.inside(off))
                def _():
                    self.over_z(k, ch, (self.z + off + self.n) % self.n).wait_send()
            if self.n == 4:
                @pl.when((self.z == 1) | (self.z == 2))
                def _():
                    self.arrived(jnp.where(self.z == 2, 0, 3), ch).wait_send()
        self.copy_near().wait()


class Exchange(Job):
    uses_ctx = True

    def __init__(self, both):
        self.ins = [(both, VMEM_SPEC)]
        self.outs = [(jax.ShapeDtypeStruct(both.shape, both.dtype), VMEM_SPEC)]
        self.scratch = [DMA, DMA]

    def refs(self, ins, outs, scratch):
        (self.src,), (self.out,), (self.ssem, self.rsem) = ins, outs, scratch

    def copy(self):
        c = self.c
        return remote(self.src.at[1 - c], self.out.at[c], self.ssem, self.rsem, {"ctx": 1 - c})

    def start(self):
        self.copy().start()
        self.out[self.c] = self.src[self.c]

    def end(self):
        self.copy().wait()


class RowGather(Job):
    def __init__(self, own, hook):
        self.hook = hook
        self.ins = [(own, VMEM_SPEC)]
        self.outs = [(jax.ShapeDtypeStruct((4, 2, *own.shape[1:]), own.dtype), VMEM_SPEC)]
        self.scratch = [DMA((3, 2)), DMA((3, 2))]

    def refs(self, ins, outs, scratch):
        (self.src,), (self.out,) = ins, outs
        t, sib, peer = partners()
        self.links = Links(*scratch, sib, peer)

    def start(self):
        for s in range(2):
            self.out[2 + s, 0] = self.src[s]
            gather_start(self.links, 0, self.out, s)

    def steps(self):
        return [(self.hook, lambda: gather_forward(self.links, 0, self.out))]

    def end(self):
        gather_wait(self.links, 0, self.out)


class ParamSum(Job):
    uses_fsdp = True

    def __init__(self, placed, n):
        self.n = n
        self.ins = [(placed, VMEM_SPEC)]
        self.outs = [(jax.ShapeDtypeStruct(placed.shape, F32), VMEM_SPEC)]
        self.scratch = [VMEM((n, *placed.shape), BF16), DMA((n,)), DMA((n,))]

    def refs(self, ins, outs, scratch):
        (self.src,), (self.out,), (self.got, self.ssem, self.rsem) = ins, outs, scratch

    def copy(self, k):
        return remote(
            self.src, self.got.at[k], self.ssem.at[k], self.rsem.at[k],
            {"fsdp": (self.z + k) % self.n},
        )

    def start(self):
        for k in range(1, self.n):
            self.copy(k).start()

    def finish(self):
        total = self.src[...].astype(F32)
        for k in range(1, self.n):
            self.copy(k).wait_recv()
            total += self.got[k].astype(F32)
        self.out[...] = total

    def end(self):
        for k in range(1, self.n):
            self.copy(k).wait_send()


class CtxSum(Job):
    uses_ctx = True

    def __init__(self, full, n, hooks, keep=False):
        self.n, self.hooks = n, hooks
        full = full.reshape(n, 2, full.shape[0] // (2 * n), full.shape[1])
        shape = (n, *full.shape[2:])
        self.ins = [(full, HBM_SPEC)]
        self.keep = keep
        self.outs = [] if keep else [(jax.ShapeDtypeStruct(shape, BF16), VMEM_SPEC)]
        self.scratch = [VMEM(shape, BF16), DMA((n,)), DMA((n,)), DMA((n,))]
        if keep:
            self.scratch.append(VMEM(shape, BF16))

    def refs(self, ins, outs, scratch):
        (self.full,) = ins
        self.got, self.ssem, self.rsem, self.near = scratch[:4]
        self.out = scratch[4] if self.keep else outs[0]

    def order(self):
        return (0, 3, 1, 2) if self.n == 4 else range(self.n)

    def copy(self, k):
        return remote(
            self.full.at[k, 1 - self.c], self.got.at[k], self.ssem.at[k], self.rsem.at[k],
            {"ctx": 1 - self.c},
        )

    def load(self, k):
        return pltpu.make_async_copy(self.full.at[k, self.c], self.out.at[k], self.near.at[k])

    def start(self):
        for k in self.order():
            self.copy(k).start()
        for k in self.order():
            self.load(k).start()

    def add(self, k):
        self.load(k).wait()
        self.copy(k).wait_recv()
        self.out[k] = (self.out[k].astype(F32) + self.got[k].astype(F32)).astype(BF16)

    def steps(self):
        per = -(-self.n // len(self.hooks))
        return [
            (self.hooks[i // per], functools.partial(self.add, k))
            for i, k in enumerate(self.order())
        ]

    def end(self):
        for k in range(self.n):
            self.copy(k).wait_send()


class FsdpSum(Job):
    uses_ctx = uses_fsdp = True

    def __init__(self, rows, n, hooks, source=None):
        self.n, self.hooks, self.source = n, hooks, source
        shape = rows.shape
        self.ins = [] if source else [(rows, VMEM_SPEC)]
        self.outs = [(jax.ShapeDtypeStruct((2, *shape[1:]), BF16), VMEM_SPEC)]
        self.rows = shape[1]
        self.ch = chunks_of(self.rows)
        self.scratch = [
            VMEM(shape, BF16), VMEM((2, *shape[1:]), BF16),
            DMA((n, self.ch)), DMA((n, self.ch)), DMA((2, self.ch)), DMA((2, self.ch)),
            DMA((self.ch,)), DMA((self.ch,)),
        ]

    def refs(self, ins, outs, scratch):
        self.src = self.source.out if self.source else ins[0]
        (self.out,) = outs
        (self.got, self.via, self.ssem, self.rsem, self.via_send, self.via_recv, self.x_send,
         self.x_recv) = scratch

    def cut(self, ref, ch):
        size = self.rows // self.ch
        return ref.at[pl.ds(ch * size, size)]

    def direct(self, d, ch):
        return remote(
            self.cut(self.src.at[d], ch), self.cut(self.got.at[self.z], ch),
            self.ssem.at[d, ch], self.rsem.at[self.z, ch], {"fsdp": d},
        )

    def landed(self, frm, ch):
        block = self.cut(self.got.at[frm], ch)
        return remote(block, block, self.ssem.at[frm, ch], self.rsem.at[frm, ch], {"fsdp": frm})

    def to_relay(self, d, ch):
        return remote(
            self.cut(self.src.at[d], ch), self.cut(self.via.at[0], ch),
            self.via_send.at[0, ch], self.via_recv.at[0, ch], {"fsdp": 1 if d == 0 else 2},
        )

    def relayed(self, d, ch):
        return remote(
            self.cut(self.via.at[1], ch), self.cut(self.got.at[self.z], ch),
            self.via_send.at[1, ch], self.rsem.at[self.z, ch], {"fsdp": d},
        )

    def directly(self, d):
        if self.n == 4 and d in (0, 3):
            return (self.z == 2) if d == 0 else (self.z == 1)
        return self.z != d

    def send(self, d):
        if self.n == 4 and d in (0, 3):
            @pl.when(self.z == 3 - d)
            def _():
                for ch in range(self.ch):
                    self.to_relay(d, ch).start()

        @pl.when(self.directly(d))
        def _():
            for ch in range(self.ch):
                self.direct(d, ch).start()

    def order(self):
        return (0, 3, 1, 2) if self.n == 4 else range(self.n)

    def start(self):
        if not self.source:
            for d in self.order():
                self.send(d)

    def relay(self):
        for d, me in ((0, 1), (3, 2)):
            @pl.when(self.z == me)
            def _():
                for ch in range(self.ch):
                    self.to_relay(d, ch).wait_recv()
                    mine = self.cut(self.src.at[d], ch)[...].astype(F32)
                    theirs = self.cut(self.via.at[0], ch)[...].astype(F32)
                    self.cut(self.via.at[1], ch)[...] = (mine + theirs).astype(BF16)
                    self.relayed(d, ch).start()

    def over_x(self, ch):
        block = self.cut(self.out.at[self.c], ch)
        return remote(block, block, self.x_send.at[ch], self.x_recv.at[ch], {"ctx": 1 - self.c})

    def total(self):
        n = self.n
        for ch in range(self.ch):
            mine = self.cut(self.src.at[self.z], ch)
            if n == 4:
                near = (self.z + 1) % 4
                last = jnp.where(self.z == 0, 2, jnp.where(self.z == 3, 1, (self.z + 3) % 4))
                first = jnp.where(self.z == 3, 2, near)
                inner = (self.z == 1) | (self.z == 2)
                self.landed(first, ch).wait_recv()
                self.landed(last, ch).wait_recv()
                part = (
                    mine[...].astype(F32)
                    + self.cut(self.got.at[first], ch)[...].astype(F32)
                    + self.cut(self.got.at[last], ch)[...].astype(F32)
                )
                block = self.cut(self.out.at[self.c], ch)

                @pl.when(inner)
                def _():
                    middle = (self.z + 2) % 4
                    self.landed(middle, ch).wait_recv()
                    block[...] = (part + self.cut(self.got.at[middle], ch)[...].astype(F32)).astype(BF16)

                @pl.when(jnp.logical_not(inner))
                def _():
                    block[...] = part.astype(BF16)
            else:
                part = mine[...].astype(F32)
                for k in range(1, n):
                    frm = (self.z + k) % n
                    self.landed(frm, ch).wait_recv()
                    part += self.cut(self.got.at[frm], ch)[...].astype(F32)
                self.cut(self.out.at[self.c], ch)[...] = part.astype(BF16)
            self.over_x(ch).start()

    def steps(self):
        out = [(self.hooks[0], self.relay)] if self.n == 4 else []
        return out + [(self.hooks[1], self.total)]

    def end(self):
        for ch in range(self.ch):
            other = self.cut(self.out.at[1 - self.c], ch)
            remote(other, other, self.x_send.at[ch], self.x_recv.at[ch], {"ctx": 1 - self.c}).wait_recv()
            self.over_x(ch).wait_send()
            for d in range(self.n):
                if self.n == 4 and d in (0, 3):
                    @pl.when(self.z == 3 - d)
                    def _():
                        self.to_relay(d, ch).wait_send()

                    @pl.when(self.z == (1 if d == 0 else 2))
                    def _():
                        self.relayed(d, ch).wait_send()

                @pl.when(self.directly(d))
                def _():
                    self.direct(d, ch).wait_send()


class Background:
    def __init__(self, jobs):
        self.jobs = jobs
        self.todo = [step for job in jobs for step in job.steps()]

    def start(self):
        for job in self.jobs:
            job.start()

    def at(self, hook):
        for when, function in self.todo:
            if when == hook:
                function()

    def loop(self, b, count=4, base=0):
        for k in range(count):
            if any(when == base + k for when, _ in self.todo):
                @pl.when(b == k)
                def _():
                    self.at(base + k)

    def end(self):
        for job in self.jobs:
            job.end()


class Links:
    def __init__(self, send, recv, sib, peer):
        self.send, self.recv, self.sib, self.peer = send, recv, sib, peer

    def make(self, kind, s, src, dst, other):
        return pltpu.make_async_remote_copy(
            src_ref=src,
            dst_ref=dst,
            send_sem=self.send.at[kind, s],
            recv_sem=self.recv.at[kind, s],
            device_id={"tp": other},
            device_id_type=pl.DeviceIdType.MESH,
        )


def statistics(rows):
    mean = jnp.mean(rows, axis=-1, keepdims=True)
    centred = rows - mean
    inverse = lax.rsqrt(jnp.mean(centred * centred, axis=-1, keepdims=True) + EPS)
    return centred * inverse, inverse


def norm_back(rows, d_out, gain):
    unit, inverse = statistics(rows)
    e = d_out * gain
    back = inverse * (
        e
        - jnp.mean(e, axis=-1, keepdims=True)
        - unit * jnp.mean(e * unit, axis=-1, keepdims=True)
    )
    d_gain = jnp.sum(d_out * unit, axis=0, keepdims=True)
    d_shift = jnp.sum(d_out, axis=0, keepdims=True)
    return back, d_gain, d_shift


def rows_of(ref, b):
    block = ref[b]
    return block.reshape(block.shape[0] * block.shape[1], block.shape[2])


def gather_start(links, base, out, s):
    links.make(base, s, out.at[2 + s, 0], out.at[2 + s, 1], links.sib).start()
    links.make(base + 1, s, out.at[2 + s, 0], out.at[s, 0], links.peer).start()


def gather_forward(links, base, out):
    for s in range(2):
        links.make(base + 1, s, out.at[2 + s, 0], out.at[s, 0], links.peer).wait_recv()
        links.make(base + 2, s, out.at[s, 0], out.at[s, 1], links.sib).start()


def gather_wait(links, base, out):
    for s in range(2):
        for kind, src, dst, other in (
            (base, out.at[2 + s, 0], out.at[2 + s, 1], links.sib),
            (base + 2, out.at[s, 0], out.at[s, 1], links.sib),
        ):
            links.make(kind, s, src, dst, other).wait()
        links.make(base + 1, s, out.at[2 + s, 0], out.at[s, 0], links.peer).wait_send()


def gather_end(links, base, out):
    gather_forward(links, base, out)
    gather_wait(links, base, out)


class Scatter:
    def __init__(self, links, part, sent, got, own):
        self.links, self.part, self.sent, self.got, self.own = links, part, sent, got, own

    def copy(self, kind, s):
        other = self.links.peer if kind == 1 else self.links.sib
        return self.links.make(kind, s, self.sent.at[kind, s], self.got.at[kind, s], other)

    def block(self, b):
        s = b % 2
        half = self.part.shape[0] // 2

        @pl.when(b < 2)
        def _():
            self.sent[0, s] = self.part[half:].astype(BF16)
            first = self.copy(0, s)
            first.start()
            first.wait_recv()
            self.sent[1, s] = (self.part[:half] + self.got[0, s].astype(F32)).astype(BF16)
            self.copy(1, s).start()

        @pl.when(b >= 2)
        def _():
            self.sent[2, s] = self.part[half:].astype(BF16)
            self.copy(2, s).start()
            self.own[s] = self.part[:half]

    def total(self, s):
        self.copy(2, s).wait_recv()
        self.copy(1, s).wait_recv()
        return self.own[s] + self.got[2, s].astype(F32) + self.got[1, s].astype(F32)

    def end(self):
        for s in range(2):
            for kind in range(3):
                self.copy(kind, s).wait_send()


def scatter_scratch(half, width):
    return [
        VMEM((2 * half, width), F32),
        VMEM((3, 2, half, width), BF16),
        VMEM((3, 2, half, width), BF16),
        VMEM((2, half, width), F32),
        pltpu.SemaphoreType.DMA((6, 2)),
        pltpu.SemaphoreType.DMA((6, 2)),
    ]


def enter_kernel(jobs, first, send, recv):
    t, sib, peer = partners()
    tokens, params, weights = jobs
    entry_barrier(jobs)
    links = Links(send, recv, sib, peer)
    params.start()
    tokens.start()
    weights.start()
    params.finish()
    tokens.end()
    for s in range(2):
        unit, _ = statistics(tokens.out[s].astype(F32))
        first[2 + s, 0] = (unit * params.out[0:1, :] + params.out[1:2, :]).astype(BF16)
        gather_start(links, 0, first, s)
    for hook, step in weights.steps():
        if hook == 0:
            step()
    gather_forward(links, 0, first)
    for hook, step in weights.steps():
        if hook == 1:
            step()
    gather_wait(links, 0, first)
    params.end()
    weights.end()


def pair_tile(pair, h):
    tile = pair if h % 2 == 0 else pltpu.roll(pair, HD, 1)
    return tile


def attention_kernel(
    jobs, heads, base,
    first, weight, params, key_extra, resid,
    second, middle, q_out, k_out, v_out, mixed_out,
    part, sent, got, own, send, recv,
):
    t, sib, peer = partners()
    background = Background(jobs)
    entry_barrier(jobs)
    background.start()
    links = Links(send, recv, sib, peer)
    scatter = Scatter(links, part, sent, got, own)
    width = heads * HD
    weight = whole(weight)
    out_bias, gain, shift = (params[base + k : base + k + 1, :] for k in (2, 3, 4))
    q_bias = params[base + 6 : base + 7, :width]
    v_bias = params[base + 6 : base + 7, width : 2 * width]
    half = first.shape[2]
    rows = 2 * half
    lane = lax.broadcasted_iota(jnp.int32, (rows, LANES), 1)
    head_lane = lane < HD
    q_extra = jnp.where(lane < HD + 2, 1.0, 0.0).astype(BF16)
    v_extra = jnp.where(lane < HD + 3, 1.0, 0.0).astype(BF16)

    def project(b, carry):
        x = rows_of(first, b)
        y = mm(x, weight[:, : 3 * width])
        q = ((y[:, :width] + q_bias).astype(BF16) * SCALE).astype(BF16)
        k = y[:, width : 2 * width].astype(BF16)
        v = (y[:, 2 * width :] + v_bias).astype(BF16)
        g, s = b // 2, b % 2
        mine = jnp.where(g == 1, t, peer)
        other = mine + 1 - 2 * (mine % 2)
        extra = jnp.concatenate([key_extra[mine, s], key_extra[other, s]], axis=0)
        at = pl.ds(pl.multiple_of(b * rows, rows), rows)
        for h in range(heads):
            cut = slice(LANES * (h // 2), LANES * (h // 2 + 1))
            q_out[h, at, :] = jnp.where(head_lane, pair_tile(q[:, cut], h), q_extra)
            k_out[h, at, :] = jnp.where(head_lane, pair_tile(k[:, cut], h), extra)
            v_out[h, at, :] = jnp.where(head_lane, pair_tile(v[:, cut], h), v_extra)
        return carry

    lax.fori_loop(0, 4, project, 0)

    def attend(b, carry):
        at = pl.ds(pl.multiple_of(b * rows, rows), rows)
        outs = []
        for h in range(heads):
            q = q_out[h, at, :]
            scores = mm_nt(q, k_out[h])
            top = jnp.max(scores, axis=-1, keepdims=True)
            weights = jnp.exp(scores - top).astype(BF16)
            summed = mm(weights, v_out[h])
            total = summed[:, HD : HD + 1]
            outs.append(summed / total)
            log_total = -(top + jnp.log(total))
            high = log_total.astype(BF16).astype(F32)
            rest = log_total - high
            mid = rest.astype(BF16).astype(F32)
            low = rest - mid
            tail = jnp.where(lane == HD + 2, high, jnp.where(lane == HD + 3, mid, low))
            q_out[h, at, :] = jnp.where(
                (lane >= HD + 2) & (lane < HD + 5), tail.astype(BF16), q
            )
        tiles = [
            jnp.where(head_lane, outs[h], pltpu.roll(outs[h + 1], HD, 1))
            for h in range(0, heads, 2)
        ]
        mixed = jnp.concatenate(tiles, axis=1).astype(BF16)
        mixed_out[at, :] = mixed
        part[...] = mm_nt(mixed, weight[:, 3 * width :])
        scatter.block(b)
        background.loop(b)
        return carry

    lax.fori_loop(0, 4, attend, 0)
    for s in range(2):
        mid = resid[s].astype(F32) + (scatter.total(s) + out_bias)
        middle[s] = mid
        unit, _ = statistics(mid)
        second[2 + s, 0] = (unit * gain + shift).astype(BF16)
        gather_start(links, 3, second, s)
        background.at(4 + s)
    gather_forward(links, 3, second)
    background.at(6)
    gather_wait(links, 3, second)
    scatter.end()
    background.end()


def mlp_kernel(
    jobs, last, base,
    second, weight, params, middle,
    active_out, slope_out, resid, nxt,
    part, sent, got, own, send, recv,
):
    t, sib, peer = partners()
    background = Background(jobs)
    entry_barrier(jobs)
    background.start()
    links = Links(send, recv, sib, peer)
    scatter = Scatter(links, part, sent, got, own)
    half = second.shape[2]
    rows = 2 * half
    weight = whole(weight)
    hidden = weight.shape[1] // 2
    out_bias = params[base + 5 : base + 6, :]
    following = 0 if last else base + 8
    gain, shift = (params[following + k : following + k + 1, :] for k in (0, 1))
    step = 256

    def block(b, carry):
        at = pl.ds(pl.multiple_of(b * rows, rows), rows)
        x = rows_of(second, b)
        for n in range(0, hidden, step):
            before = mm(x, weight[:, n : n + step]) + params[base + 7 : base + 8, n : n + step]
            cdf = 0.5 * (1.0 + lax.erf(before * INV_SQRT2))
            active_out[at, n : n + step] = (before * cdf).astype(BF16)
            slope = cdf + before * (jnp.exp(before * before * -0.5) * INV_SQRT_2PI)
            slope_out[at, n : n + step] = slope.astype(BF16)
        part[...] = mm_nt(active_out[at, :], weight[:, hidden:])
        scatter.block(b)
        background.loop(b)
        return carry

    lax.fori_loop(0, 4, block, 0)
    for s in range(2):
        res = middle[s] + (scatter.total(s) + out_bias)
        if last:
            nxt[s] = res.astype(BF16)
        else:
            resid[s] = res
            unit, _ = statistics(res)
            nxt[2 + s, 0] = (unit * gain + shift).astype(BF16)
            gather_start(links, 3, nxt, s)
        background.at(4 + s)
    if not last:
        gather_forward(links, 3, nxt)
    background.at(6)
    if not last:
        gather_wait(links, 3, nxt)
    scatter.end()
    background.end()


def token_product(left, right, out, offset):
    depth = left.shape[-1]
    total = left.shape[0] * left.shape[1] * left.shape[2]
    step = 256

    def body(j, carry):
        cut = pl.ds(pl.multiple_of(j * step, step), step)
        x = left[:, :, :, cut].reshape(total, step)
        out[cut, offset : offset + right.shape[-1]] = mm_tn(x, right[...]).astype(BF16)
        return carry

    lax.fori_loop(0, depth // step, body, 0)


def mlp_back_kernel(
    jobs, base,
    grad, weight, active, slope, second, middle, carry_in, params,
    weight_grad, carry_out, rows_out, vectors,
    part, sent, got, own, send, recv, d_before,
):
    t, sib, peer = partners()
    background = Background(jobs)
    entry_barrier(jobs)
    background.start()
    links = Links(send, recv, sib, peer)
    scatter = Scatter(links, part, sent, got, own)
    weight = whole(weight)
    gain = params[base + 3 : base + 4, :]
    half = grad.shape[2]
    rows = 2 * half
    hidden = active.shape[1]
    step = 256
    vectors[...] = jnp.zeros_like(vectors)

    def block(b, carry):
        at = pl.ds(pl.multiple_of(b * rows, rows), rows)
        x = rows_of(grad, b)
        for n in range(0, hidden, step):
            d_act = mm(x, weight[:, hidden + n : hidden + n + step])
            d_bef = (d_act * slope[at, n : n + step].astype(F32)).astype(BF16)
            d_before[at, n : n + step] = d_bef
            vectors[4:5, n : n + step] += jnp.sum(d_bef.astype(F32), axis=0, keepdims=True)
        part[...] = mm_nt(d_before[at, :], weight[:, :hidden])
        scatter.block(b)
        background.loop(b)
        return carry

    lax.fori_loop(0, 4, block, 0)
    token_product(grad, active, weight_grad, hidden)
    background.at(4)

    def finish(s):
        back, d_gain, d_shift = norm_back(middle[s], scatter.total(s), gain)
        carry = carry_in[s].astype(F32)
        mid = carry + back
        carry_out[s] = mid
        low = mid.astype(BF16)
        rows_out[2 + s, 0] = low
        gather_start(links, 3, rows_out, s)
        vectors[0:1, :] += d_gain
        vectors[1:2, :] += d_shift
        vectors[2:3, :] += jnp.sum(low.astype(F32), axis=0, keepdims=True)
        vectors[3:4, :] += jnp.sum(carry.astype(BF16).astype(F32), axis=0, keepdims=True)

    finish(0)
    background.at(5)
    token_product(second, d_before, weight_grad, 0)
    finish(1)
    gather_forward(links, 3, rows_out)
    background.at(6)
    gather_wait(links, 3, rows_out)
    scatter.end()
    background.end()


def attention_back_kernel(
    jobs, heads, last, base,
    grad, weight, mixed, q_in, k_in, v_in, first, carry_in, resid, params,
    weight_grad, carry_out, rows_out, vectors,
    part, sent, got, own, send, recv, d_out, d_joint, d_key, d_value,
):
    t, sib, peer = partners()
    background = Background(jobs)
    entry_barrier(jobs)
    background.start()
    links = Links(send, recv, sib, peer)
    scatter = Scatter(links, part, sent, got, own)
    width = heads * HD
    weight = whole(weight)
    gain = params[base : base + 1, :]
    half = grad.shape[2]
    rows = 2 * half
    lane = lax.broadcasted_iota(jnp.int32, (rows, LANES), 1)
    head_lane = lane < HD
    vectors[...] = jnp.zeros_like(vectors)
    d_key[...] = jnp.zeros_like(d_key)
    d_value[...] = jnp.zeros_like(d_value)

    def pairs(tiles):
        return jnp.concatenate(
            [
                jnp.where(head_lane, tiles[h], pltpu.roll(tiles[h + 1], HD, 1))
                for h in range(0, heads, 2)
            ],
            axis=1,
        )

    def attend(b, carry):
        at = pl.ds(pl.multiple_of(b * rows, rows), rows)
        d_mixed = mm(rows_of(grad, b), weight[:, 3 * width :]).astype(BF16)
        product = d_mixed.astype(F32) * mixed[at, :].astype(F32)
        d_queries = []
        for h in range(heads):
            cut = slice(LANES * (h // 2), LANES * (h // 2 + 1))
            keep = head_lane if h % 2 == 0 else lane >= HD
            delta = -jnp.sum(jnp.where(keep, product[:, cut], 0.0), axis=-1, keepdims=True)
            high = delta.astype(BF16).astype(F32)
            rest = delta - high
            mid = rest.astype(BF16).astype(F32)
            low = rest - mid
            tail = jnp.where(
                lane == HD,
                high,
                jnp.where(lane == HD + 1, mid, jnp.where(lane == HD + 2, low, 0.0)),
            ).astype(BF16)
            d_o = jnp.where(head_lane, pair_tile(d_mixed[:, cut], h), tail)
            q = q_in[h, at, :]
            probs = jnp.exp(mm_nt(k_in[h], q))
            d_value[h] += mm(probs.astype(BF16), d_o)
            d_raw = (probs * mm_nt(v_in[h], d_o)).astype(BF16)
            d_key[h] += mm(d_raw, q)
            d_queries.append(mm_tn(d_raw, k_in[h]) * SCALE)
        d_joint[at, :width] = pairs(d_queries).astype(BF16)
        background.loop(b)
        return carry

    lax.fori_loop(0, 4, attend, 0)

    def project(b, carry):
        at = pl.ds(pl.multiple_of(b * rows, rows), rows)
        d_joint[at, width : 2 * width] = pairs([d_key[h, at, :] for h in range(heads)]).astype(BF16)
        d_joint[at, 2 * width :] = pairs([d_value[h, at, :] for h in range(heads)]).astype(BF16)
        d_rows = d_joint[at, :]
        sums = jnp.sum(d_rows.astype(F32), axis=0, keepdims=True)
        vectors[2:3, :width] += sums[:, :width]
        vectors[2:3, width : 2 * width] += sums[:, 2 * width :]
        part[...] = mm_nt(d_rows, weight[:, : 3 * width])
        scatter.block(b)
        background.loop(b, 4, 4)
        return carry

    lax.fori_loop(0, 4, project, 0)
    token_product(grad, mixed, weight_grad, 3 * width)
    background.at(8)

    def finish(s):
        back, d_gain, d_shift = norm_back(resid[s].astype(F32), scatter.total(s), gain)
        carry = carry_in[s] + back
        if last:
            rows_out[s] = carry.astype(BF16)
        else:
            carry_out[s] = carry
            rows_out[2 + s, 0] = carry.astype(BF16)
            gather_start(links, 3, rows_out, s)
        vectors[0:1, :] += d_gain
        vectors[1:2, :] += d_shift

    finish(0)
    background.at(9)
    token_product(first, d_joint, weight_grad, 0)
    finish(1)
    if not last:
        gather_forward(links, 3, rows_out)
    background.at(10)
    if not last:
        gather_wait(links, 3, rows_out)
    scatter.end()
    background.end()


class VectorSum(Job):
    uses_ctx = uses_fsdp = True

    def __init__(self, vectors, n, hooks):
        self.n, self.hooks = n, hooks
        dim = vectors[0].shape[1]
        self.ins = [(v, VMEM_SPEC) for v in vectors]
        self.outs = [(jax.ShapeDtypeStruct((16, dim), F32), VMEM_SPEC)]
        self.scratch = [
            VMEM((4, 16, dim), F32), VMEM((3 + n, 16, dim), F32), DMA((3 + n,)), DMA((3 + n,))
        ]

    def refs(self, ins, outs, scratch):
        self.vectors = ins
        (self.out,) = outs
        self.held, self.got, self.ssem, self.rsem = scratch
        t, self.sib, self.peer = partners()

    def copy(self, k):
        if k < 2:
            to = {"tp": self.sib if k == 0 else self.peer}
        elif k == 2:
            to = {"ctx": 1 - self.c}
        else:
            to = {"fsdp": (self.z + k - 2) % self.n}
        return remote(
            self.held.at[min(k, 3)], self.got.at[k], self.ssem.at[k], self.rsem.at[k], to
        )

    def start(self):
        for l in range(LAYERS):
            attn, mlp = self.vectors[2 * l], self.vectors[2 * l + 1]
            for row, (ref, index) in enumerate(
                ((attn, 0), (attn, 1), (mlp, 2), (mlp, 0), (mlp, 1), (mlp, 3), (attn, 2), (mlp, 4))
            ):
                self.held[0, 8 * l + row : 8 * l + row + 1, :] = ref[index : index + 1, :]
        self.copy(0).start()

    def fold(self, k):
        self.copy(k).wait_recv()
        came = self.got[k]
        if k < 2:
            row = lax.broadcasted_iota(jnp.int32, came.shape, 0)
            came = jnp.where(row % 8 < 6, came, 0.0)
        self.held[k + 1] = self.held[k] + came
        if k < 2:
            self.copy(k + 1).start()
        else:
            for j in range(1, self.n):
                self.copy(2 + j).start()

    def finish(self):
        total = self.held[3]
        for j in range(1, self.n):
            self.copy(2 + j).wait_recv()
            total += self.got[2 + j]
        self.out[...] = total

    def steps(self):
        return [(self.hooks[k], functools.partial(self.fold, k)) for k in range(3)] + [
            (self.hooks[3], self.finish)
        ]

    def end(self):
        for k in range(2 + self.n):
            self.copy(k).wait_send()


def leave_kernel(jobs):
    attn_ctx, attn_fsdp, mlp_fsdp, vectors, rows = jobs
    entry_barrier(jobs)
    mlp_fsdp.start()
    vectors.start()
    attn_ctx.start()
    rows.start()
    vectors.fold(0)
    for i, k in enumerate(attn_ctx.order()):
        attn_ctx.add(k)
        attn_fsdp.send(k)
        if i in (1, 2):
            vectors.fold(i)
        if i == 2 and mlp_fsdp.n == 4:
            mlp_fsdp.relay()
    if attn_fsdp.n == 4:
        attn_fsdp.relay()
    vectors.finish()
    mlp_fsdp.total()
    attn_fsdp.total()
    for job in jobs:
        job.end()


def whole(ref):
    return ref.reshape(ref.shape[0] * ref.shape[1] * ref.shape[2], ref.shape[3])


def call(kernel, name, outs, scratch, collective_id, flops, args, jobs=()):
    ins = [(a, VMEM_SPEC) for a in args] + [pair for job in jobs for pair in job.ins]
    results = [(o, VMEM_SPEC) for o in outs] + [pair for job in jobs for pair in job.outs]
    scratch = list(scratch)
    n_scratch = len(scratch)
    for job in jobs:
        scratch += job.scratch

    def body(*refs):
        refs = list(refs)
        in_refs = refs[: len(ins)]
        out_refs = refs[len(ins) : len(ins) + len(results)]
        scratch_refs = refs[len(ins) + len(results) :]
        a, b, c = len(args), len(outs), n_scratch
        for job in jobs:
            ends = a + len(job.ins), b + len(job.outs), c + len(job.scratch)
            job.bind(in_refs[a : ends[0]], out_refs[b : ends[1]], scratch_refs[c : ends[2]])
            a, b, c = ends
        kernel(
            jobs, *in_refs[: len(args)], *out_refs[: len(outs)], *scratch_refs[:n_scratch]
        )

    size = sum(a.size * a.dtype.itemsize for a, _ in ins) + sum(
        math.prod(o.shape) * o.dtype.itemsize for o, _ in results
    )
    return pl.pallas_call(
        body,
        name=name,
        out_shape=tuple(o for o, _ in results),
        in_specs=[spec for _, spec in ins],
        out_specs=tuple(spec for _, spec in results),
        scratch_shapes=scratch,
        compiler_params=pltpu.CompilerParams(
            collective_id=collective_id, has_side_effects=True, vmem_limit_bytes=VMEM_LIMIT
        ),
        cost_estimate=pl.CostEstimate(flops=flops, bytes_accessed=size, transcendentals=0),
    )(*[a for a, _ in ins])


def local(
    tokens, key_valid, first_gain, first_shift, joint_weight, query_bias, value_bias,
    out_weight, out_bias, second_gain, second_shift, expand_weight, expand_bias,
    reduce_weight, reduce_bias, cotangent,
):
    ctx_size = lax.axis_size("ctx")
    tp_size = lax.axis_size("tp")
    fsdp_size = lax.axis_size("fsdp")
    clips, half, dim = tokens.shape
    assert clips == ctx_size == 2 and tp_size == 4 and joint_weight.shape[0] == LAYERS
    c = lax.axis_index("ctx")
    shard = joint_weight.shape[1]
    width = joint_weight.shape[3]
    heads = width // HD
    hidden = expand_weight.shape[2]
    z = lax.axis_index("fsdp")

    def packed(parts):
        return jnp.concatenate(parts, axis=1).reshape(ctx_size, shard // ctx_size, -1)

    def attn_parts(l):
        joint = joint_weight[l]
        return packed([joint[:, 0], joint[:, 1], joint[:, 2], out_weight[l].T])

    def mlp_parts(l):
        return packed([expand_weight[l], reduce_weight[l].T])

    slot = lax.broadcasted_iota(jnp.int32, (1, fsdp_size, 1), 1) == z

    def placed(block):
        spread = jnp.where(slot, block.reshape(-1, 1, block.shape[-1]), jnp.zeros((), BF16))
        return spread.reshape(LAYERS, -1)

    rows = [
        placed(a)
        for a in (first_gain, first_shift, out_bias, second_gain, second_shift, reduce_bias)
    ]
    both = jnp.concatenate([placed(query_bias), placed(value_bias)], axis=1)
    rows.append(jnp.pad(both, ((0, 0), (0, dim - both.shape[1]))))
    rows.append(placed(expand_bias))
    params = jnp.stack(rows, axis=1).reshape(LAYERS * 8, dim)

    def regroup(both):
        mine = lax.dynamic_index_in_dim(both, c, 0, keepdims=False)
        theirs = lax.dynamic_index_in_dim(both, 1 - c, 0, keepdims=False)
        got = lax.ppermute(theirs, "ctx", [(0, 1), (1, 0)])
        return jnp.where(c == 0, jnp.stack([mine, got]), jnp.stack([got, mine]))

    valid = lax.dynamic_index_in_dim(key_valid, c, 0, keepdims=False)
    bias = jnp.where(valid == 1, 0.0, MASKED).astype(F32)
    bias = bias.reshape(ctx_size, tp_size, half, 1).transpose(1, 0, 2, 3)
    high = bias.astype(BF16).astype(F32)
    col = lax.broadcasted_iota(jnp.int32, (1, 1, 1, LANES), 3) - HD
    key_extra = jnp.where(
        col == 0, high, jnp.where(col == 1, bias - high, jnp.where((col >= 2) & (col < 5), 1.0, 0.0))
    ).astype(BF16)

    every = jax.ShapeDtypeStruct((4, 2, half, dim), BF16)
    own = jax.ShapeDtypeStruct((2, half, dim), F32)
    own_low = jax.ShapeDtypeStruct((2, half, dim), BF16)
    count = 8 * half
    scratch = scatter_scratch(half, dim)
    n = fsdp_size

    jobs = [Exchange(tokens), ParamSum(params, n), WeightGather(attn_parts(0), n, (0, 1, 1))]
    first, tok, params, attn_weight = call(
        enter_kernel, "enter", [every], [DMA((3, 2)), DMA((3, 2))], 0, 10**7, [], jobs
    )
    resid = tok
    saved = []
    for l in range(LAYERS):
        last = l == LAYERS - 1
        heads_shape = jax.ShapeDtypeStruct((heads, count, LANES), BF16)
        jobs = [WeightGather(mlp_parts(l), n, (1, 3, 6))]
        if last:
            jobs.append(RowGather(cot, 1))
        second, middle, q, k, v, mixed, mlp_weight, *grad = call(
            lambda jobs, *refs, base=8 * l: attention_kernel(jobs, heads, base, *refs),
            f"attention_{l}",
            [every, own, heads_shape, heads_shape, heads_shape, jax.ShapeDtypeStruct((count, width), BF16)],
            scratch, 1 + 6 * l, 2 * count * dim * 4 * width + 16 * heads * count * count * HD,
            [first, attn_weight, params, key_extra, resid], jobs,
        )
        rows_hidden = jax.ShapeDtypeStruct((count, hidden), BF16)
        jobs = [] if last else [WeightGather(attn_parts(l + 1), n, (2, 4, 5)), Exchange(cotangent)]
        active, slope, out, nxt, *more = call(
            lambda jobs, *refs, base=8 * l, last=last: mlp_kernel(jobs, last, base, *refs),
            f"mlp_{l}",
            [rows_hidden, rows_hidden,
             jax.ShapeDtypeStruct((8, LANES), F32) if last else own, own_low if last else every],
            scratch, 2 + 6 * l, 4 * count * dim * hidden,
            [second, mlp_weight, params, middle], jobs,
        )
        saved.append((resid, first, q, k, v, mixed, middle, second, active, slope, attn_weight, mlp_weight))
        resid, first = out, nxt
        if not last:
            attn_weight, cot = more
    output = regroup(nxt)

    vec = jax.ShapeDtypeStruct((8, dim), F32)
    carry = cot
    (grad,) = grad
    attn_grads, mlp_grads, attn_vec, mlp_vec = ([None] * LAYERS for _ in range(4))
    attn_full = mlp_part = attn_part = None
    for l in reversed(range(LAYERS)):
        (resid, first, q, k, v, mixed, middle, second, active, slope, attn_weight, mlp_weight) = saved[l]
        last = l == 0
        jobs = []
        if attn_full is not None:
            jobs = [FsdpSum(mlp_part, n, (3, 6)), CtxSum(attn_full, n, (2, 4, 5, 6))]
        mlp_full, carry, grad, mlp_vec[l], *more = call(
            lambda jobs, *refs, base=8 * l: mlp_back_kernel(jobs, base, *refs),
            f"mlp_back_{l}",
            [jax.ShapeDtypeStruct((dim, 2 * hidden), BF16), own, every, vec],
            scratch + [VMEM((count, hidden), BF16)], 3 + 6 * l, 8 * count * dim * hidden,
            [grad, mlp_weight, active, slope, second, middle, carry, params], jobs,
        )
        if more:
            mlp_grads[l + 1], attn_part = more
        jobs = [CtxSum(mlp_full, n, (2, 5, 8, 10))]
        if attn_part is not None:
            jobs.append(FsdpSum(attn_part, n, (2, 5)))
        attn_full, carry, grad, attn_vec[l], mlp_part, *more = call(
            lambda jobs, *refs, base=8 * l, last=last: attention_back_kernel(jobs, heads, last, base, *refs),
            f"attention_back_{l}",
            [jax.ShapeDtypeStruct((dim, 4 * width), BF16),
             jax.ShapeDtypeStruct((8, LANES), F32) if last else own, own_low if last else every, vec],
            scratch
            + [
                VMEM((heads, 8, LANES), BF16),
                VMEM((count, 3 * width), BF16),
                VMEM((heads, count, LANES), F32),
                VMEM((heads, count, LANES), F32),
            ],
            4 + 6 * l, 4 * count * dim * 4 * width + 40 * heads * count * count * HD,
            [grad, attn_weight, mixed, q, k, v, first, carry, resid, params], jobs,
        )
        if more:
            (attn_grads[l + 1],) = more

    ctx_job = CtxSum(attn_full, n, (0, 1, 2, 3), keep=True)
    attn_shape = jax.ShapeDtypeStruct((n, shard // 2, attn_full.shape[1]), BF16)
    jobs = [
        ctx_job,
        FsdpSum(attn_shape, n, (0, 1), source=ctx_job),
        FsdpSum(mlp_part, n, (0, 1)),
        VectorSum([attn_vec[0], mlp_vec[0], attn_vec[1], mlp_vec[1]], n, (0, 1, 2, 3)),
        Exchange(grad),
    ]
    attn_grads[0], mlp_grads[0], vectors, row_grad = call(
        leave_kernel, "leave", [], [], 5, 10**7, [], jobs
    )
    attn_grads = [g.reshape(shard, -1).astype(F32) for g in attn_grads]
    mlp_grads = [g.reshape(shard, -1).astype(F32) for g in mlp_grads]

    vectors = vectors.reshape(LAYERS, 8, dim)
    wide = lax.dynamic_slice_in_dim(vectors[:, :6], z * shard, shard, 2)

    def spread(block):
        block = block.reshape(LAYERS, -1, fsdp_size, HD // fsdp_size)
        return lax.dynamic_index_in_dim(block, z, 2, keepdims=False)

    return (
        output,
        row_grad,
        wide[:, 0],
        wide[:, 1],
        jnp.stack([g[:, : 3 * width].reshape(shard, 3, width) for g in attn_grads]),
        spread(vectors[:, 6, :width]),
        spread(vectors[:, 6, width : 2 * width]),
        jnp.stack([g[:, 3 * width :].T for g in attn_grads]),
        wide[:, 2],
        wide[:, 3],
        wide[:, 4],
        jnp.stack([g[:, :hidden] for g in mlp_grads]),
        spread(vectors[:, 7, :hidden]),
        jnp.stack([g[:, hidden:].T for g in mlp_grads]),
        wide[:, 5],
    )


def solution(mesh):
    vector = P(None, "fsdp")
    by_head = P(None, "tp", "fsdp")
    rows = P("fsdp", ("ctx", "tp"), None)
    return jax.shard_map(
        local,
        mesh=mesh,
        in_specs=(
            rows, P("fsdp", None), vector, vector, P(None, "fsdp", None, "tp"), by_head, by_head,
            by_head, vector, vector, vector, P(None, "fsdp", "tp"), by_head, by_head, vector, rows,
        ),
        out_specs=(
            rows, rows, vector, vector, P(None, "fsdp", None, "tp"), by_head, by_head,
            by_head, vector, vector, vector, P(None, "fsdp", "tp"), by_head, by_head, vector,
        ),
        check_vma=False,
    )
```

```python
import functools
import math

import jax
import jax.numpy as jnp
from jax import lax
from jax.experimental import pallas as pl
from jax.experimental.pallas import tpu as pltpu
from jax.sharding import PartitionSpec as P

HD = 64
LAYERS = 2
LANES = 128
EPS = 1e-06
MASKED = -10000.0
SCALE = HD ** (-0.5)
VMEM_LIMIT = 60 * 1024 * 1024
F32 = jnp.float32
BF16 = jnp.bfloat16
VMEM = pltpu.VMEM
INV_SQRT2 = 1.0 / math.sqrt(2.0)
INV_SQRT_2PI = 1.0 / math.sqrt(2.0 * math.pi)


def mm(a, b):
    return lax.dot_general(a, b, (((1,), (0,)), ((), ())), preferred_element_type=F32)


def mm_nt(a, b):
    return lax.dot_general(a, b, (((1,), (1,)), ((), ())), preferred_element_type=F32)


def mm_tn(a, b):
    return lax.dot_general(a, b, (((0,), (0,)), ((), ())), preferred_element_type=F32)


def partners():
    t = lax.axis_index("tp")
    return t, t + 1 - 2 * (t % 2), (t + 2) % 4


def entry_barrier(jobs=()):
    t, sib, peer = partners()
    others = [{"tp": sib}, {"tp": peer}]
    if any(job.uses_ctx for job in jobs):
        others.append({"ctx": 1 - lax.axis_index("ctx")})
    if any(job.uses_fsdp for job in jobs):
        n = lax.axis_size("fsdp")
        z = lax.axis_index("fsdp")
        others += [{"fsdp": (z + k) % n} for k in range(1, n)]
    barrier = pltpu.get_barrier_semaphore()
    for other in others:
        pl.semaphore_signal(barrier, inc=1, device_id=other, device_id_type=pl.DeviceIdType.MESH)
    pl.semaphore_wait(barrier, len(others))


def remote(src, dst, send, recv, device):
    return pltpu.make_async_remote_copy(
        src_ref=src,
        dst_ref=dst,
        send_sem=send,
        recv_sem=recv,
        device_id=device,
        device_id_type=pl.DeviceIdType.MESH,
    )


DMA = pltpu.SemaphoreType.DMA
HBM_SPEC = pl.BlockSpec(memory_space=pl.ANY)
VMEM_SPEC = pl.BlockSpec(memory_space=VMEM)


class Job:
    uses_ctx = False
    uses_fsdp = False
    ins = ()
    outs = ()
    scratch = ()

    def bind(self, ins, outs, scratch):
        self.c = lax.axis_index("ctx")
        self.z = lax.axis_index("fsdp")
        self.refs(ins, outs, scratch)

    def start(self):
        pass

    def steps(self):
        return []

    def end(self):
        pass


def chunks_of(rows):
    return 2 if rows % 128 == 0 else 1


def cut_rows(ref, start, size):
    index = (slice(None),) * (len(ref.shape) - 2) + (pl.ds(start, size),)
    return ref.at[index]


class OverFsdp(Job):
    uses_fsdp = True

    def __init__(self, weight, layer, n, hook, chunks=1, ctx_hooks=None):
        self.n, self.layer, self.hook, self.ctx_hooks = n, layer, hook, ctx_hooks
        self.uses_ctx = ctx_hooks is not None
        shape = weight.shape[1:]
        self.rows = shape[-2] // 2
        self.ch = chunks if self.rows % (chunks * 16) == 0 else 1
        half = jax.ShapeDtypeStruct((n, *shape[:-2], self.rows, shape[-1]), BF16)
        self.ins = [(weight, HBM_SPEC)]
        self.outs = [(half, HBM_SPEC)] * (2 if self.uses_ctx else 1)
        self.scratch = [DMA((n + 1, self.ch)), DMA((n, self.ch)), DMA]
        if self.uses_ctx:
            self.scratch += [DMA((n, self.ch)), DMA((n, self.ch)), DMA]

    def refs(self, ins, outs, scratch):
        self.src = ins[0].at[self.layer]
        self.near = outs[0]
        self.send, self.recv, self.here = scratch[:3]
        if self.uses_ctx:
            self.far = outs[1]
            self.x_send, self.x_recv, self.here_far = scratch[3:]

    def mine(self, ch):
        size = self.rows // self.ch
        start = pl.multiple_of(self.c * self.rows + ch * size, size)
        return cut_rows(self.src, start, size)

    def part(self, ref, frm, ch):
        size = self.rows // self.ch
        return cut_rows(ref.at[frm], ch * size, size)

    def out_to(self, k, off, ch):
        to = (self.z + off + self.n) % self.n
        return remote(
            self.mine(ch), self.part(self.near, self.z, ch),
            self.send.at[k, ch], self.recv.at[self.z, ch], {"fsdp": to},
        )

    def arrived(self, frm, ch):
        block = self.part(self.near, frm, ch)
        return remote(
            block, block, self.send.at[self.n, ch], self.recv.at[frm, ch], {"fsdp": self.n - 1 - frm}
        )

    def over_x(self, frm, ch):
        return remote(
            self.part(self.near, frm, ch), self.part(self.far, frm, ch),
            self.x_send.at[frm, ch], self.x_recv.at[frm, ch], {"ctx": 1 - self.c},
        )

    def local(self, half, out, sem):
        start = pl.multiple_of(half * self.rows, self.rows)
        return pltpu.make_async_copy(
            cut_rows(self.src, start, self.rows), out.at[self.z], sem
        )

    def offsets(self):
        return (2, -2, 1, -1) if self.n == 4 else range(1, self.n)

    def sources(self):
        return (1, -1, 2, -2, 3, -3) if self.n == 4 else range(1, self.n)

    def inside(self, off):
        other = self.z + off
        return (other >= 0) & (other < self.n) if self.n == 4 else (other > -1)

    def relays(self):
        return (self.z == 1) | (self.z == 2)

    def start(self):
        for ch in range(self.ch):
            for k, off in enumerate(self.offsets()):
                @pl.when(self.inside(off))
                def _():
                    self.out_to(k, off, ch).start()
        self.local(self.c, self.near, self.here).start()
        if self.uses_ctx:
            self.local(1 - self.c, self.far, self.here_far).start()

    def relay(self):
        if self.n == 4:
            @pl.when(self.relays())
            def _():
                for ch in range(self.ch):
                    through = self.arrived(jnp.where(self.z == 2, 0, 3), ch)
                    through.wait_recv()
                    through.start()

    def take(self, off):
        frm = (self.z + off + self.n) % self.n

        @pl.when(self.inside(off))
        def _():
            for ch in range(self.ch):
                if self.n == 4 and abs(off) == 2:
                    @pl.when(jnp.logical_not((self.z == 2) & (frm == 0) | (self.z == 1) & (frm == 3)))
                    def _():
                        self.arrived(frm, ch).wait_recv()
                else:
                    self.arrived(frm, ch).wait_recv()
                if self.uses_ctx:
                    self.over_x(frm, ch).start()

    def steps(self):
        out = [(self.hook, self.relay)]
        if self.uses_ctx:
            for i, off in enumerate(self.sources()):
                out.append((self.ctx_hooks[min(i // 2, 2)], functools.partial(self.take, off)))
        return out

    def end(self):
        for off in self.sources():
            frm = (self.z + off + self.n) % self.n
            if not self.uses_ctx:
                self.take(off)
            else:
                @pl.when(self.inside(off))
                def _():
                    for ch in range(self.ch):
                        self.over_x(frm, ch).wait()
        for ch in range(self.ch):
            for k, off in enumerate(self.offsets()):
                @pl.when(self.inside(off))
                def _():
                    self.out_to(k, off, ch).wait_send()
            if self.n == 4:
                @pl.when(self.relays())
                def _():
                    self.arrived(jnp.where(self.z == 2, 0, 3), ch).wait_send()
        self.local(self.c, self.near, self.here).wait()
        if self.uses_ctx:
            self.local(1 - self.c, self.far, self.here_far).wait()


class OverCtx(Job):
    uses_ctx = True

    def __init__(self, weight, layer, near, n):
        self.n, self.layer = n, layer
        self.ins = [(weight, HBM_SPEC), (near, HBM_SPEC)]
        self.outs = [(jax.ShapeDtypeStruct(near.shape, BF16), HBM_SPEC)]
        self.scratch = [DMA((n,)), DMA((n,)), DMA]

    def refs(self, ins, outs, scratch):
        self.src, self.near = ins[0].at[self.layer], ins[1]
        (self.far,) = outs
        self.send, self.recv, self.here = scratch

    def copy(self, k):
        frm = (self.z + k) % self.n
        return remote(
            self.near.at[frm], self.far.at[frm], self.send.at[k], self.recv.at[k],
            {"ctx": 1 - self.c},
        )

    def local(self):
        rows = self.near.shape[-2]
        start = pl.multiple_of((1 - self.c) * rows, rows)
        return pltpu.make_async_copy(cut_rows(self.src, start, rows), self.far.at[self.z], self.here)

    def start(self):
        for k in range(1, self.n):
            self.copy(k).start()
        self.local().start()

    def end(self):
        for k in range(1, self.n):
            self.copy(k).wait()
        self.local().wait()


class Loads:
    def __init__(self, sems):
        self.sems, self.copies = sems, []

    def add(self, near, far, out):
        c = lax.axis_index("ctx")
        for half, ref in ((c, near), (1 - c, far)):
            if len(ref.shape) == 3:
                pairs = [(ref, out.at[:, half])]
            else:
                width = ref.shape[-1]
                pairs = [
                    (ref.at[:, j], out.at[:, half, :, j * width : (j + 1) * width])
                    for j in range(ref.shape[1])
                ]
            for src, dst in pairs:
                copy = pltpu.make_async_copy(src, dst, self.sems.at[len(self.copies)])
                copy.start()
                self.copies.append(copy)

    def wait(self):
        for copy in self.copies:
            copy.wait()


class ParamJob(Job):
    uses_fsdp = True

    def __init__(self, wide, narrow, n, dim):
        self.n, self.n_wide = n, len(wide)
        self.ins = [(a, VMEM_SPEC) for a in (*wide, *narrow)]
        shape = (8 * LAYERS, dim)
        self.outs = [(jax.ShapeDtypeStruct(shape, F32), VMEM_SPEC)]
        self.scratch = [
            VMEM(shape, F32), VMEM(shape, BF16), VMEM((n, *shape), BF16), DMA((n,)), DMA((n,))
        ]

    def refs(self, ins, outs, scratch):
        self.wide, self.narrow = ins[: self.n_wide], ins[self.n_wide :]
        (self.out,) = outs
        self.work, self.src, self.got, self.ssem, self.rsem = scratch

    def copy(self, k):
        return remote(
            self.src, self.got.at[k], self.ssem.at[k], self.rsem.at[k],
            {"fsdp": (self.z + k) % self.n},
        )

    def start(self):
        work = self.work
        dim = work.shape[1]
        work[...] = jnp.zeros_like(work)
        shard = self.wide[0].shape[1]
        query, value, expand = self.narrow
        cut = query.shape[2]
        heads = query.shape[1]
        for l in range(LAYERS):
            for k, ref in enumerate(self.wide):
                work[8 * l + k : 8 * l + k + 1, :shard] = ref[l : l + 1, :].astype(F32)
            for row, base, ref in ((6, 0, query), (6, heads * HD, value), (7, 0, expand)):
                block = ref[l].astype(F32)
                for h in range(ref.shape[1]):
                    at = base + h * HD
                    work[8 * l + row : 8 * l + row + 1, at : at + cut] = block[h : h + 1, :]
        all_rows = work[...]
        row = lax.broadcasted_iota(jnp.int32, all_rows.shape, 0) % 8
        by_shard = pltpu.roll(all_rows, self.z * shard, 1)
        by_cut = pltpu.roll(all_rows, self.z * cut, 1)
        placed = jnp.where(row < 6, by_shard, by_cut)
        work[...] = placed
        self.src[...] = placed.astype(BF16)
        for k in range(1, self.n):
            self.copy(k).start()

    def finish(self):
        total = self.work[...]
        for k in range(1, self.n):
            self.copy(k).wait_recv()
            total += self.got[k].astype(F32)
        self.out[...] = total

    def end(self):
        for k in range(1, self.n):
            self.copy(k).wait_send()


class Exchange(Job):
    uses_ctx = True

    def __init__(self, both):
        self.ins = [(both, VMEM_SPEC)]
        self.outs = [(jax.ShapeDtypeStruct(both.shape, both.dtype), VMEM_SPEC)]
        self.scratch = [DMA, DMA]

    def refs(self, ins, outs, scratch):
        (self.src,), (self.out,), (self.ssem, self.rsem) = ins, outs, scratch

    def copy(self):
        c = self.c
        return remote(self.src.at[1 - c], self.out.at[c], self.ssem, self.rsem, {"ctx": 1 - c})

    def start(self):
        self.copy().start()
        self.out[self.c] = self.src[self.c]

    def end(self):
        self.copy().wait()


class RowGather(Job):
    def __init__(self, own, hook):
        self.hook = hook
        self.ins = [(own, VMEM_SPEC)]
        self.outs = [(jax.ShapeDtypeStruct((4, 2, *own.shape[1:]), own.dtype), VMEM_SPEC)]
        self.scratch = [DMA((3, 2)), DMA((3, 2))]

    def refs(self, ins, outs, scratch):
        (self.src,), (self.out,) = ins, outs
        t, sib, peer = partners()
        self.links = Links(*scratch, sib, peer)

    def start(self):
        for s in range(2):
            self.out[2 + s, 0] = self.src[s]
            gather_start(self.links, 0, self.out, s)

    def steps(self):
        return [(self.hook, lambda: gather_forward(self.links, 0, self.out))]

    def end(self):
        gather_wait(self.links, 0, self.out)


class CtxSum(Job):
    uses_ctx = True

    def __init__(self, full, n, hooks, keep=False):
        self.n, self.hooks = n, hooks
        full = full.reshape(n, 2, full.shape[0] // (2 * n), full.shape[1])
        shape = (n, *full.shape[2:])
        self.ins = [(full, HBM_SPEC)]
        self.keep = keep
        self.outs = [] if keep else [(jax.ShapeDtypeStruct(shape, BF16), VMEM_SPEC)]
        self.scratch = [VMEM(shape, BF16), DMA((n,)), DMA((n,)), DMA((n,))]
        if keep:
            self.scratch.append(VMEM(shape, BF16))

    def refs(self, ins, outs, scratch):
        (self.full,) = ins
        self.got, self.ssem, self.rsem, self.near = scratch[:4]
        self.out = scratch[4] if self.keep else outs[0]

    def order(self):
        return (0, 3, 1, 2) if self.n == 4 else range(self.n)

    def copy(self, k):
        return remote(
            self.full.at[k, 1 - self.c], self.got.at[k], self.ssem.at[k], self.rsem.at[k],
            {"ctx": 1 - self.c},
        )

    def load(self, k):
        return pltpu.make_async_copy(self.full.at[k, self.c], self.out.at[k], self.near.at[k])

    def start(self):
        for k in self.order():
            self.copy(k).start()
        for k in self.order():
            self.load(k).start()

    def add(self, k):
        self.load(k).wait()
        self.copy(k).wait_recv()
        self.out[k] = (self.out[k].astype(F32) + self.got[k].astype(F32)).astype(BF16)

    def steps(self):
        per = -(-self.n // len(self.hooks))
        return [
            (self.hooks[i // per], functools.partial(self.add, k))
            for i, k in enumerate(self.order())
        ]

    def end(self):
        for k in range(self.n):
            self.copy(k).wait_send()


class FsdpSum(Job):
    uses_ctx = uses_fsdp = True

    def __init__(self, rows, n, hooks, source=None, sends=()):
        self.n, self.hooks, self.source, self.sends = n, hooks, source, sends
        shape = rows.shape
        self.ins = [] if source else [(rows, VMEM_SPEC)]
        self.outs = [(jax.ShapeDtypeStruct((2, *shape[1:]), BF16), VMEM_SPEC)]
        self.rows = shape[1]
        self.ch = chunks_of(self.rows)
        self.scratch = [
            VMEM(shape, BF16), VMEM((2, *shape[1:]), BF16),
            DMA((n, self.ch)), DMA((n, self.ch)), DMA((2, self.ch)), DMA((2, self.ch)),
            DMA((self.ch,)), DMA((self.ch,)),
        ]

    def refs(self, ins, outs, scratch):
        self.src = self.source.out if self.source else ins[0]
        (self.out,) = outs
        (self.got, self.via, self.ssem, self.rsem, self.via_send, self.via_recv, self.x_send,
         self.x_recv) = scratch

    def cut(self, ref, ch):
        size = self.rows // self.ch
        return ref.at[pl.ds(ch * size, size)]

    def direct(self, d, ch):
        return remote(
            self.cut(self.src.at[d], ch), self.cut(self.got.at[self.z], ch),
            self.ssem.at[d, ch], self.rsem.at[self.z, ch], {"fsdp": d},
        )

    def landed(self, frm, ch):
        block = self.cut(self.got.at[frm], ch)
        return remote(block, block, self.ssem.at[frm, ch], self.rsem.at[frm, ch], {"fsdp": frm})

    def to_relay(self, d, ch):
        return remote(
            self.cut(self.src.at[d], ch), self.cut(self.via.at[0], ch),
            self.via_send.at[0, ch], self.via_recv.at[0, ch], {"fsdp": 1 if d == 0 else 2},
        )

    def relayed(self, d, ch):
        return remote(
            self.cut(self.via.at[1], ch), self.cut(self.got.at[self.z], ch),
            self.via_send.at[1, ch], self.rsem.at[self.z, ch], {"fsdp": d},
        )

    def directly(self, d):
        if self.n == 4 and d in (0, 3):
            return (self.z == 2) if d == 0 else (self.z == 1)
        return self.z != d

    def send(self, d):
        if self.n == 4 and d in (0, 3):
            @pl.when(self.z == 3 - d)
            def _():
                for ch in range(self.ch):
                    self.to_relay(d, ch).start()

        @pl.when(self.directly(d))
        def _():
            for ch in range(self.ch):
                self.direct(d, ch).start()

    def order(self):
        return (0, 3, 1, 2) if self.n == 4 else range(self.n)

    def start(self):
        if not self.source:
            for d in self.order():
                self.send(d)

    def relay(self):
        for d, me in ((0, 1), (3, 2)) if self.n == 4 else ():
            @pl.when(self.z == me)
            def _():
                for ch in range(self.ch):
                    self.to_relay(d, ch).wait_recv()
                    mine = self.cut(self.src.at[d], ch)[...].astype(F32)
                    theirs = self.cut(self.via.at[0], ch)[...].astype(F32)
                    self.cut(self.via.at[1], ch)[...] = (mine + theirs).astype(BF16)
                    self.relayed(d, ch).start()

    def over_x(self, ch):
        block = self.cut(self.out.at[self.c], ch)
        return remote(block, block, self.x_send.at[ch], self.x_recv.at[ch], {"ctx": 1 - self.c})

    def total(self):
        n = self.n
        for ch in range(self.ch):
            mine = self.cut(self.src.at[self.z], ch)
            if n == 4:
                near = (self.z + 1) % 4
                last = jnp.where(self.z == 0, 2, jnp.where(self.z == 3, 1, (self.z + 3) % 4))
                first = jnp.where(self.z == 3, 2, near)
                inner = (self.z == 1) | (self.z == 2)
                self.landed(first, ch).wait_recv()
                self.landed(last, ch).wait_recv()
                part = (
                    mine[...].astype(F32)
                    + self.cut(self.got.at[first], ch)[...].astype(F32)
                    + self.cut(self.got.at[last], ch)[...].astype(F32)
                )
                block = self.cut(self.out.at[self.c], ch)

                @pl.when(inner)
                def _():
                    middle = (self.z + 2) % 4
                    self.landed(middle, ch).wait_recv()
                    block[...] = (part + self.cut(self.got.at[middle], ch)[...].astype(F32)).astype(BF16)

                @pl.when(jnp.logical_not(inner))
                def _():
                    block[...] = part.astype(BF16)
            else:
                part = mine[...].astype(F32)
                for k in range(1, n):
                    frm = (self.z + k) % n
                    self.landed(frm, ch).wait_recv()
                    part += self.cut(self.got.at[frm], ch)[...].astype(F32)
                self.cut(self.out.at[self.c], ch)[...] = part.astype(BF16)
            self.over_x(ch).start()

    def steps(self):
        out = [
            (self.sends[i * len(self.sends) // self.n], functools.partial(self.send, d))
            for i, d in enumerate(self.order())
            if self.sends
        ]
        return out + [(self.hooks[0], self.relay), (self.hooks[1], self.total)]

    def end(self):
        for ch in range(self.ch):
            other = self.cut(self.out.at[1 - self.c], ch)
            remote(other, other, self.x_send.at[ch], self.x_recv.at[ch], {"ctx": 1 - self.c}).wait_recv()
            self.over_x(ch).wait_send()
            for d in range(self.n):
                if self.n == 4 and d in (0, 3):
                    @pl.when(self.z == 3 - d)
                    def _():
                        self.to_relay(d, ch).wait_send()

                    @pl.when(self.z == (1 if d == 0 else 2))
                    def _():
                        self.relayed(d, ch).wait_send()

                @pl.when(self.directly(d))
                def _():
                    self.direct(d, ch).wait_send()


class Background:
    def __init__(self, jobs):
        self.jobs = jobs
        self.todo = [step for job in jobs for step in job.steps()]

    def start(self):
        for job in self.jobs:
            job.start()

    def at(self, hook):
        for when, function in self.todo:
            if when == hook:
                function()

    def loop(self, b, count=4, base=0):
        for k in range(count):
            if any(when == base + k for when, _ in self.todo):
                @pl.when(b == k)
                def _():
                    self.at(base + k)

    def end(self):
        for job in self.jobs:
            job.end()


class Links:
    def __init__(self, send, recv, sib, peer):
        self.send, self.recv, self.sib, self.peer = send, recv, sib, peer

    def make(self, kind, s, src, dst, other):
        return pltpu.make_async_remote_copy(
            src_ref=src,
            dst_ref=dst,
            send_sem=self.send.at[kind, s],
            recv_sem=self.recv.at[kind, s],
            device_id={"tp": other},
            device_id_type=pl.DeviceIdType.MESH,
        )


def statistics(rows):
    mean = jnp.mean(rows, axis=-1, keepdims=True)
    centred = rows - mean
    inverse = lax.rsqrt(jnp.mean(centred * centred, axis=-1, keepdims=True) + EPS)
    return centred * inverse, inverse


def norm_back(rows, d_out, gain):
    unit, inverse = statistics(rows)
    e = d_out * gain
    back = inverse * (
        e
        - jnp.mean(e, axis=-1, keepdims=True)
        - unit * jnp.mean(e * unit, axis=-1, keepdims=True)
    )
    d_gain = jnp.sum(d_out * unit, axis=0, keepdims=True)
    d_shift = jnp.sum(d_out, axis=0, keepdims=True)
    return back, d_gain, d_shift


def rows_of(ref, b):
    block = ref[b]
    return block.reshape(block.shape[0] * block.shape[1], block.shape[2])


def gather_start(links, base, out, s):
    links.make(base, s, out.at[2 + s, 0], out.at[2 + s, 1], links.sib).start()
    links.make(base + 1, s, out.at[2 + s, 0], out.at[s, 0], links.peer).start()


def gather_forward(links, base, out):
    for s in range(2):
        links.make(base + 1, s, out.at[2 + s, 0], out.at[s, 0], links.peer).wait_recv()
        links.make(base + 2, s, out.at[s, 0], out.at[s, 1], links.sib).start()


def gather_wait(links, base, out):
    for s in range(2):
        for kind, src, dst, other in (
            (base, out.at[2 + s, 0], out.at[2 + s, 1], links.sib),
            (base + 2, out.at[s, 0], out.at[s, 1], links.sib),
        ):
            links.make(kind, s, src, dst, other).wait()
        links.make(base + 1, s, out.at[2 + s, 0], out.at[s, 0], links.peer).wait_send()


def gather_end(links, base, out):
    gather_forward(links, base, out)
    gather_wait(links, base, out)


class Scatter:
    def __init__(self, links, part, sent, got, own):
        self.links, self.part, self.sent, self.got, self.own = links, part, sent, got, own

    def copy(self, kind, s):
        other = self.links.peer if kind == 1 else self.links.sib
        return self.links.make(kind, s, self.sent.at[kind, s], self.got.at[kind, s], other)

    def block(self, b):
        s = b % 2
        half = self.part.shape[0] // 2

        @pl.when(b < 2)
        def _():
            self.sent[0, s] = self.part[half:].astype(BF16)
            first = self.copy(0, s)
            first.start()
            first.wait_recv()
            self.sent[1, s] = (self.part[:half] + self.got[0, s].astype(F32)).astype(BF16)
            self.copy(1, s).start()

        @pl.when(b >= 2)
        def _():
            self.sent[2, s] = self.part[half:].astype(BF16)
            self.copy(2, s).start()
            self.own[s] = self.part[:half]

    def total(self, s):
        self.copy(2, s).wait_recv()
        self.copy(1, s).wait_recv()
        return self.own[s] + self.got[2, s].astype(F32) + self.got[1, s].astype(F32)

    def end(self):
        for s in range(2):
            for kind in range(3):
                self.copy(kind, s).wait_send()


def scatter_scratch(half, width):
    return [
        VMEM((2 * half, width), F32),
        VMEM((3, 2, half, width), BF16),
        VMEM((3, 2, half, width), BF16),
        VMEM((2, half, width), F32),
        pltpu.SemaphoreType.DMA((6, 2)),
        pltpu.SemaphoreType.DMA((6, 2)),
    ]


def enter_kernel(jobs, first, send, recv):
    t, sib, peer = partners()
    params, tokens, attn, expand = jobs
    entry_barrier(jobs)
    links = Links(send, recv, sib, peer)
    tokens.start()
    attn.start()
    params.start()
    expand.start()
    params.finish()
    tokens.end()
    for s in range(2):
        unit, _ = statistics(tokens.out[s].astype(F32))
        first[2 + s, 0] = (unit * params.out[0:1, :] + params.out[1:2, :]).astype(BF16)
        gather_start(links, 0, first, s)
    attn.relay()
    for off in attn.sources():
        attn.take(off)
    expand.relay()
    gather_forward(links, 0, first)
    gather_wait(links, 0, first)
    for job in (params, attn, expand):
        job.end()


def pair_tile(pair, h):
    tile = pair if h % 2 == 0 else pltpu.roll(pair, HD, 1)
    return tile


def attention_kernel(
    jobs, heads, base,
    first, params, key_extra, resid, near, far,
    second, middle, q_out, k_out, v_out, mixed_out,
    part, sent, got, own, send, recv, weight, load,
):
    t, sib, peer = partners()
    background = Background(jobs)
    entry_barrier(jobs)
    background.start()
    links = Links(send, recv, sib, peer)
    scatter = Scatter(links, part, sent, got, own)
    width = heads * HD
    loads = Loads(load)
    loads.add(near, far, weight)
    loads.wait()
    weight = whole(weight)
    out_bias, gain, shift = (params[base + k : base + k + 1, :] for k in (2, 3, 4))
    q_bias = params[base + 6 : base + 7, :width]
    v_bias = params[base + 6 : base + 7, width : 2 * width]
    half = first.shape[2]
    rows = 2 * half
    lane = lax.broadcasted_iota(jnp.int32, (rows, LANES), 1)
    head_lane = lane < HD
    q_extra = jnp.where(lane < HD + 2, 1.0, 0.0).astype(BF16)
    v_extra = jnp.where(lane < HD + 3, 1.0, 0.0).astype(BF16)

    def project(b, carry):
        x = rows_of(first, b)
        y = mm(x, weight[:, : 3 * width])
        q = ((y[:, :width] + q_bias).astype(BF16) * SCALE).astype(BF16)
        k = y[:, width : 2 * width].astype(BF16)
        v = (y[:, 2 * width :] + v_bias).astype(BF16)
        g, s = b // 2, b % 2
        mine = jnp.where(g == 1, t, peer)
        other = mine + 1 - 2 * (mine % 2)
        extra = jnp.concatenate([key_extra[mine, s], key_extra[other, s]], axis=0)
        at = pl.ds(pl.multiple_of(b * rows, rows), rows)
        for h in range(heads):
            cut = slice(LANES * (h // 2), LANES * (h // 2 + 1))
            q_out[h, at, :] = jnp.where(head_lane, pair_tile(q[:, cut], h), q_extra)
            k_out[h, at, :] = jnp.where(head_lane, pair_tile(k[:, cut], h), extra)
            v_out[h, at, :] = jnp.where(head_lane, pair_tile(v[:, cut], h), v_extra)
        return carry

    lax.fori_loop(0, 4, project, 0)
    background.at(0)

    def attend(b, carry):
        at = pl.ds(pl.multiple_of(b * rows, rows), rows)
        outs = []
        for h in range(heads):
            q = q_out[h, at, :]
            scores = mm_nt(q, k_out[h])
            top = jnp.max(scores, axis=-1, keepdims=True)
            weights = jnp.exp(scores - top).astype(BF16)
            summed = mm(weights, v_out[h])
            total = summed[:, HD : HD + 1]
            outs.append(summed / total)
            log_total = -(top + jnp.log(total))
            high = log_total.astype(BF16).astype(F32)
            rest = log_total - high
            mid = rest.astype(BF16).astype(F32)
            low = rest - mid
            tail = jnp.where(lane == HD + 2, high, jnp.where(lane == HD + 3, mid, low))
            q_out[h, at, :] = jnp.where(
                (lane >= HD + 2) & (lane < HD + 5), tail.astype(BF16), q
            )
        tiles = [
            jnp.where(head_lane, outs[h], pltpu.roll(outs[h + 1], HD, 1))
            for h in range(0, heads, 2)
        ]
        mixed = jnp.concatenate(tiles, axis=1).astype(BF16)
        mixed_out[at, :] = mixed
        part[...] = mm_nt(mixed, weight[:, 3 * width :])
        scatter.block(b)
        background.loop(b, 4, 1)
        return carry

    lax.fori_loop(0, 4, attend, 0)
    for s in range(2):
        mid = resid[s].astype(F32) + (scatter.total(s) + out_bias)
        middle[s] = mid
        unit, _ = statistics(mid)
        second[2 + s, 0] = (unit * gain + shift).astype(BF16)
        gather_start(links, 3, second, s)
        background.at(5 + s)
    gather_forward(links, 3, second)
    background.at(7)
    gather_wait(links, 3, second)
    scatter.end()
    background.end()


def mlp_kernel(
    jobs, last, base,
    second, params, middle, near_e, far_e, near_r, far_r,
    active_out, slope_out, resid, nxt,
    part, sent, got, own, send, recv, expand, reduce, load,
):
    t, sib, peer = partners()
    background = Background(jobs)
    entry_barrier(jobs)
    background.start()
    links = Links(send, recv, sib, peer)
    scatter = Scatter(links, part, sent, got, own)
    half = second.shape[2]
    rows = 2 * half
    loads = Loads(load)
    loads.add(near_e, far_e, expand)
    loads.add(near_r, far_r, reduce)
    loads.wait()
    expand, reduce = whole(expand), whole(reduce)
    hidden = expand.shape[1]
    out_bias = params[base + 5 : base + 6, :]
    following = 0 if last else base + 8
    gain, shift = (params[following + k : following + k + 1, :] for k in (0, 1))
    step = 256

    def block(b, carry):
        at = pl.ds(pl.multiple_of(b * rows, rows), rows)
        x = rows_of(second, b)
        for n in range(0, hidden, step):
            before = mm(x, expand[:, n : n + step]) + params[base + 7 : base + 8, n : n + step]
            cdf = 0.5 * (1.0 + lax.erf(before * INV_SQRT2))
            active_out[at, n : n + step] = (before * cdf).astype(BF16)
            slope = cdf + before * (jnp.exp(before * before * -0.5) * INV_SQRT_2PI)
            slope_out[at, n : n + step] = slope.astype(BF16)
        part[...] = mm_nt(active_out[at, :], reduce[...])
        scatter.block(b)
        background.loop(b, 4, 1)
        return carry

    lax.fori_loop(0, 4, block, 0)
    for s in range(2):
        res = middle[s] + (scatter.total(s) + out_bias)
        if last:
            nxt[s] = res.astype(BF16)
        else:
            resid[s] = res
            unit, _ = statistics(res)
            nxt[2 + s, 0] = (unit * gain + shift).astype(BF16)
            gather_start(links, 3, nxt, s)
        background.at(5 + s)
    if not last:
        gather_forward(links, 3, nxt)
    background.at(7)
    if not last:
        gather_wait(links, 3, nxt)
    scatter.end()
    background.end()


def token_product(left, right, out, offset=0):
    depth = left.shape[-1]
    total = left.shape[0] * left.shape[1] * left.shape[2]
    step = 256

    def body(j, carry):
        cut = pl.ds(pl.multiple_of(j * step, step), step)
        x = left[:, :, :, cut].reshape(total, step)
        out[cut, offset : offset + right.shape[-1]] = mm_tn(x, right[...]).astype(BF16)
        return carry

    lax.fori_loop(0, depth // step, body, 0)


def mlp_back_kernel(
    jobs, base,
    grad, active, slope, second, middle, carry_in, params, near_e, far_e, near_r, far_r,
    expand_grad, reduce_grad, carry_out, rows_out, vectors,
    part, sent, got, own, send, recv, d_before, expand, reduce, load,
):
    t, sib, peer = partners()
    background = Background(jobs)
    entry_barrier(jobs)
    background.start()
    links = Links(send, recv, sib, peer)
    scatter = Scatter(links, part, sent, got, own)
    loads = Loads(load)
    loads.add(near_e, far_e, expand)
    loads.add(near_r, far_r, reduce)
    loads.wait()
    expand, reduce = whole(expand), whole(reduce)
    gain = params[base + 3 : base + 4, :]
    half = grad.shape[2]
    rows = 2 * half
    hidden = active.shape[1]
    step = 256
    vectors[...] = jnp.zeros_like(vectors)

    def block(b, carry):
        at = pl.ds(pl.multiple_of(b * rows, rows), rows)
        x = rows_of(grad, b)
        for n in range(0, hidden, step):
            d_act = mm(x, reduce[:, n : n + step])
            d_bef = (d_act * slope[at, n : n + step].astype(F32)).astype(BF16)
            d_before[at, n : n + step] = d_bef
            vectors[4:5, n : n + step] += jnp.sum(d_bef.astype(F32), axis=0, keepdims=True)
        part[...] = mm_nt(d_before[at, :], expand[...])
        scatter.block(b)
        background.loop(b)
        return carry

    lax.fori_loop(0, 4, block, 0)
    token_product(grad, active, reduce_grad)
    background.at(4)

    def finish(s):
        back, d_gain, d_shift = norm_back(middle[s], scatter.total(s), gain)
        carry = carry_in[s].astype(F32)
        mid = carry + back
        carry_out[s] = mid
        low = mid.astype(BF16)
        rows_out[2 + s, 0] = low
        gather_start(links, 3, rows_out, s)
        vectors[0:1, :] += d_gain
        vectors[1:2, :] += d_shift
        vectors[2:3, :] += jnp.sum(low.astype(F32), axis=0, keepdims=True)
        vectors[3:4, :] += jnp.sum(carry.astype(BF16).astype(F32), axis=0, keepdims=True)

    finish(0)
    background.at(5)
    token_product(second, d_before, expand_grad)
    finish(1)
    gather_forward(links, 3, rows_out)
    background.at(6)
    gather_wait(links, 3, rows_out)
    scatter.end()
    background.end()


def attention_back_kernel(
    jobs, heads, last, base,
    grad, mixed, q_in, k_in, v_in, first, carry_in, resid, params, near, far,
    weight_grad, carry_out, rows_out, vectors,
    part, sent, got, own, send, recv, d_joint, d_key, d_value, weight, load,
):
    t, sib, peer = partners()
    background = Background(jobs)
    entry_barrier(jobs)
    background.start()
    links = Links(send, recv, sib, peer)
    scatter = Scatter(links, part, sent, got, own)
    width = heads * HD
    loads = Loads(load)
    loads.add(near, far, weight)
    loads.wait()
    weight = whole(weight)
    gain = params[base : base + 1, :]
    half = grad.shape[2]
    rows = 2 * half
    lane = lax.broadcasted_iota(jnp.int32, (rows, LANES), 1)
    head_lane = lane < HD
    vectors[...] = jnp.zeros_like(vectors)
    d_key[...] = jnp.zeros_like(d_key)
    d_value[...] = jnp.zeros_like(d_value)

    def pairs(tiles):
        return jnp.concatenate(
            [
                jnp.where(head_lane, tiles[h], pltpu.roll(tiles[h + 1], HD, 1))
                for h in range(0, heads, 2)
            ],
            axis=1,
        )

    def attend(b, carry):
        at = pl.ds(pl.multiple_of(b * rows, rows), rows)
        d_mixed = mm(rows_of(grad, b), weight[:, 3 * width :]).astype(BF16)
        product = d_mixed.astype(F32) * mixed[at, :].astype(F32)
        d_queries = []
        for h in range(heads):
            cut = slice(LANES * (h // 2), LANES * (h // 2 + 1))
            keep = head_lane if h % 2 == 0 else lane >= HD
            delta = -jnp.sum(jnp.where(keep, product[:, cut], 0.0), axis=-1, keepdims=True)
            high = delta.astype(BF16).astype(F32)
            rest = delta - high
            mid = rest.astype(BF16).astype(F32)
            low = rest - mid
            tail = jnp.where(
                lane == HD,
                high,
                jnp.where(lane == HD + 1, mid, jnp.where(lane == HD + 2, low, 0.0)),
            ).astype(BF16)
            d_o = jnp.where(head_lane, pair_tile(d_mixed[:, cut], h), tail)
            q = q_in[h, at, :]
            probs = jnp.exp(mm_nt(k_in[h], q))
            d_value[h] += mm(probs.astype(BF16), d_o)
            d_raw = (probs * mm_nt(v_in[h], d_o)).astype(BF16)
            d_key[h] += mm(d_raw, q)
            d_queries.append(mm_tn(d_raw, k_in[h]) * SCALE)
        d_joint[at, :width] = pairs(d_queries).astype(BF16)
        background.loop(b)
        return carry

    lax.fori_loop(0, 4, attend, 0)

    def project(b, carry):
        at = pl.ds(pl.multiple_of(b * rows, rows), rows)
        d_joint[at, width : 2 * width] = pairs([d_key[h, at, :] for h in range(heads)]).astype(BF16)
        d_joint[at, 2 * width :] = pairs([d_value[h, at, :] for h in range(heads)]).astype(BF16)
        d_rows = d_joint[at, :]
        sums = jnp.sum(d_rows.astype(F32), axis=0, keepdims=True)
        vectors[2:3, :width] += sums[:, :width]
        vectors[2:3, width : 2 * width] += sums[:, 2 * width :]
        part[...] = mm_nt(d_rows, weight[:, : 3 * width])
        scatter.block(b)
        background.loop(b, 4, 4)
        return carry

    lax.fori_loop(0, 4, project, 0)
    token_product(grad, mixed, weight_grad, 3 * width)
    background.at(8)

    def finish(s):
        back, d_gain, d_shift = norm_back(resid[s].astype(F32), scatter.total(s), gain)
        carry = carry_in[s] + back
        if last:
            rows_out[s] = carry.astype(BF16)
        else:
            carry_out[s] = carry
            rows_out[2 + s, 0] = carry.astype(BF16)
            gather_start(links, 3, rows_out, s)
        vectors[0:1, :] += d_gain
        vectors[1:2, :] += d_shift

    finish(0)
    background.at(9)
    token_product(first, d_joint, weight_grad, 0)
    finish(1)
    if not last:
        gather_forward(links, 3, rows_out)
    background.at(10)
    if not last:
        gather_wait(links, 3, rows_out)
    scatter.end()
    background.end()


class VectorSum(Job):
    uses_ctx = uses_fsdp = True

    def __init__(self, vectors, n, hooks):
        self.n, self.hooks = n, hooks
        dim = vectors[0].shape[1]
        self.ins = [(v, VMEM_SPEC) for v in vectors]
        self.outs = [(jax.ShapeDtypeStruct((16, dim), F32), VMEM_SPEC)]
        self.scratch = [
            VMEM((4, 16, dim), F32), VMEM((3 + n, 16, dim), F32), DMA((3 + n,)), DMA((3 + n,))
        ]

    def refs(self, ins, outs, scratch):
        self.vectors = ins
        (self.out,) = outs
        self.held, self.got, self.ssem, self.rsem = scratch
        t, self.sib, self.peer = partners()

    def copy(self, k):
        if k < 2:
            to = {"tp": self.sib if k == 0 else self.peer}
        elif k == 2:
            to = {"ctx": 1 - self.c}
        else:
            to = {"fsdp": (self.z + k - 2) % self.n}
        return remote(
            self.held.at[min(k, 3)], self.got.at[k], self.ssem.at[k], self.rsem.at[k], to
        )

    def start(self):
        for l in range(LAYERS):
            attn, mlp = self.vectors[2 * l], self.vectors[2 * l + 1]
            for row, (ref, index) in enumerate(
                ((attn, 0), (attn, 1), (mlp, 2), (mlp, 0), (mlp, 1), (mlp, 3), (attn, 2), (mlp, 4))
            ):
                self.held[0, 8 * l + row : 8 * l + row + 1, :] = ref[index : index + 1, :]
        self.copy(0).start()

    def fold(self, k):
        self.copy(k).wait_recv()
        came = self.got[k]
        if k < 2:
            row = lax.broadcasted_iota(jnp.int32, came.shape, 0)
            came = jnp.where(row % 8 < 6, came, 0.0)
        self.held[k + 1] = self.held[k] + came
        if k < 2:
            self.copy(k + 1).start()
        else:
            for j in range(1, self.n):
                self.copy(2 + j).start()

    def finish(self):
        total = self.held[3]
        for j in range(1, self.n):
            self.copy(2 + j).wait_recv()
            total += self.got[2 + j]
        self.out[...] = total

    def steps(self):
        return [(self.hooks[k], functools.partial(self.fold, k)) for k in range(3)] + [
            (self.hooks[3], self.finish)
        ]

    def end(self):
        for k in range(2 + self.n):
            self.copy(k).wait_send()


def leave_kernel(jobs):
    attn_ctx, attn_fsdp, reduce_fsdp, vectors, rows = jobs
    entry_barrier(jobs)
    attn_ctx.start()
    reduce_fsdp.start()
    vectors.start()
    rows.start()
    vectors.fold(0)
    for i, k in enumerate(attn_ctx.order()):
        attn_ctx.add(k)
        attn_fsdp.send(k)
        if i in (1, 2):
            vectors.fold(i)
        if i == 1:
            reduce_fsdp.relay()
    attn_fsdp.relay()
    reduce_fsdp.total()
    vectors.finish()
    attn_fsdp.total()
    for job in jobs:
        job.end()


def finish_kernel(
    attn_0, attn_1, expand_0, expand_1, reduce_0, reduce_1, vectors,
    joint, out, expand, reduce, wide, query, value, hidden,
):
    z = lax.axis_index("fsdp")
    half = attn_0.shape[1]
    width = joint.shape[3]
    shard = 2 * half
    for l, (a, e, r) in enumerate(((attn_0, expand_0, reduce_0), (attn_1, expand_1, reduce_1))):
        rows = a[...].reshape(shard, a.shape[2]).astype(F32)
        for k in range(3):
            joint[l, k] = rows[:, k * width : (k + 1) * width]
        out[l] = rows[:, 3 * width :].T
        expand[l] = e[...].reshape(shard, e.shape[2]).astype(F32)
        reduce[l] = r[...].reshape(shard, r.shape[2]).astype(F32).T
    cut = query.shape[2]
    heads = query.shape[1]
    dim = vectors.shape[1]
    own = pltpu.roll(vectors[...], lax.rem(dim - z * shard, dim), 1)
    by_cut = pltpu.roll(vectors[...], lax.rem(dim - z * cut, dim), 1)
    for l in range(LAYERS):
        for k in range(6):
            wide[k, l : l + 1, :] = own[8 * l + k : 8 * l + k + 1, :shard]
        for row, base, ref in ((6, 0, query), (6, heads * HD, value), (7, 0, hidden)):
            for h in range(ref.shape[1]):
                at = base + h * HD
                ref[l, h : h + 1, :] = by_cut[8 * l + row : 8 * l + row + 1, at : at + cut]


def whole(ref):
    return ref.reshape(ref.shape[0] * ref.shape[1] * ref.shape[2], ref.shape[3])


def call(kernel, name, outs, scratch, collective_id, flops, args, jobs=()):
    args = [
        (a, spec)
        for arg in args
        for a, spec in ([(arg, VMEM_SPEC)] if not isinstance(arg, tuple) else [(a, HBM_SPEC) for a in arg])
    ]
    ins = args + [pair for job in jobs for pair in job.ins]
    results = [(o, VMEM_SPEC) for o in outs] + [pair for job in jobs for pair in job.outs]
    scratch = list(scratch)
    n_scratch = len(scratch)
    for job in jobs:
        scratch += job.scratch

    def body(*refs):
        refs = list(refs)
        in_refs = refs[: len(ins)]
        out_refs = refs[len(ins) : len(ins) + len(results)]
        scratch_refs = refs[len(ins) + len(results) :]
        a, b, c = len(args), len(outs), n_scratch
        for job in jobs:
            ends = a + len(job.ins), b + len(job.outs), c + len(job.scratch)
            job.bind(in_refs[a : ends[0]], out_refs[b : ends[1]], scratch_refs[c : ends[2]])
            a, b, c = ends
        kernel(
            jobs, *in_refs[: len(args)], *out_refs[: len(outs)], *scratch_refs[:n_scratch]
        )

    size = sum(a.size * a.dtype.itemsize for a, _ in ins) + sum(
        math.prod(o.shape) * o.dtype.itemsize for o, _ in results
    )
    return pl.pallas_call(
        body,
        name=name,
        out_shape=tuple(o for o, _ in results),
        in_specs=[spec for _, spec in ins],
        out_specs=tuple(spec for _, spec in results),
        scratch_shapes=scratch,
        compiler_params=pltpu.CompilerParams(
            collective_id=collective_id, has_side_effects=True, vmem_limit_bytes=VMEM_LIMIT
        ),
        cost_estimate=pl.CostEstimate(flops=flops, bytes_accessed=size, transcendentals=0),
    )(*[a for a, _ in ins])


def local(
    tokens, key_valid, first_gain, first_shift, joint_weight, query_bias, value_bias,
    out_weight, out_bias, second_gain, second_shift, expand_weight, expand_bias,
    reduce_weight, reduce_bias, cotangent,
):
    ctx_size = lax.axis_size("ctx")
    tp_size = lax.axis_size("tp")
    fsdp_size = lax.axis_size("fsdp")
    clips, half, dim = tokens.shape
    assert clips == ctx_size == 2 and tp_size == 4 and joint_weight.shape[0] == LAYERS
    c = lax.axis_index("ctx")
    shard = joint_weight.shape[1]
    width = joint_weight.shape[3]
    heads = width // HD
    hidden = expand_weight.shape[2]
    attn_w = jnp.concatenate(
        [joint_weight.transpose(0, 2, 1, 3), out_weight.transpose(0, 2, 1)[:, None]], axis=1
    )
    reduce_w = reduce_weight.transpose(0, 2, 1)

    valid = lax.dynamic_index_in_dim(key_valid, c, 0, keepdims=False)
    bias = jnp.where(valid == 1, 0.0, MASKED).astype(F32)
    bias = bias.reshape(ctx_size, tp_size, half, 1).transpose(1, 0, 2, 3)
    high = bias.astype(BF16).astype(F32)
    col = lax.broadcasted_iota(jnp.int32, (1, 1, 1, LANES), 3) - HD
    key_extra = jnp.where(
        col == 0, high, jnp.where(col == 1, bias - high, jnp.where((col >= 2) & (col < 5), 1.0, 0.0))
    ).astype(BF16)

    every = jax.ShapeDtypeStruct((4, 2, half, dim), BF16)
    own = jax.ShapeDtypeStruct((2, half, dim), F32)
    own_low = jax.ShapeDtypeStruct((2, half, dim), BF16)
    tiny = jax.ShapeDtypeStruct((8, LANES), F32)
    vec = jax.ShapeDtypeStruct((8, dim), F32)
    square = jax.ShapeDtypeStruct((dim, hidden), BF16)
    count = 8 * half
    n = fsdp_size
    scratch = scatter_scratch(half, dim)

    def held(columns):
        return VMEM((n, 2, shard // 2, columns), BF16)

    attn_scratch = [held(4 * width), DMA((8,))]
    mlp_scratch = [held(hidden), held(hidden), DMA((4,))]

    jobs = [
        ParamJob(
            [first_gain, first_shift, out_bias, second_gain, second_shift, reduce_bias],
            [query_bias, value_bias, expand_bias], n, dim,
        ),
        Exchange(tokens),
        OverFsdp(attn_w, 0, n, None, 2, (0, 0, 0)),
        OverFsdp(expand_weight, 0, n, None),
    ]
    first, params, tok, near_a, far_a, near_e = call(
        enter_kernel, "enter", [every], [DMA((3, 2)), DMA((3, 2))], 0, 10**7, [], jobs
    )
    resid = tok
    saved = []
    for l in range(LAYERS):
        last = l == LAYERS - 1
        heads_shape = jax.ShapeDtypeStruct((heads, count, LANES), BF16)
        if last:
            jobs = [
                OverCtx(expand_weight, l, near_e, n), OverCtx(reduce_w, l, near_r, n), RowGather(cot, 1)
            ]
        else:
            jobs = [
                OverCtx(expand_weight, l, near_e, n),
                OverFsdp(reduce_w, l, n, 1, 1, (2, 3, 3)),
                OverFsdp(attn_w, l + 1, n, 4),
            ]
        second, middle, q, k, v, mixed, far_e, *more = call(
            lambda jobs, *refs, base=8 * l: attention_kernel(jobs, heads, base, *refs),
            f"attention_{l}",
            [every, own, heads_shape, heads_shape, heads_shape, jax.ShapeDtypeStruct((count, width), BF16)],
            scratch + attn_scratch, 1 + 6 * l,
            2 * count * dim * 4 * width + 16 * heads * count * count * HD,
            [first, params, key_extra, resid, (near_a, far_a)], jobs,
        )
        attn_pair = (near_a, far_a)
        if last:
            far_r, grad = more
        else:
            near_r, far_r, near_a = more
        mlp_pairs = ((near_e, far_e), (near_r, far_r))
        rows_hidden = jax.ShapeDtypeStruct((count, hidden), BF16)
        jobs = [] if last else [
            OverCtx(attn_w, l + 1, near_a, n),
            OverFsdp(expand_weight, l + 1, n, 3),
            OverFsdp(reduce_w, l + 1, n, 6),
            Exchange(cotangent),
        ]
        active, slope, out, nxt, *more = call(
            lambda jobs, *refs, base=8 * l, last=last: mlp_kernel(jobs, last, base, *refs),
            f"mlp_{l}",
            [rows_hidden, rows_hidden, tiny if last else own, own_low if last else every],
            scratch + mlp_scratch, 2 + 6 * l, 4 * count * dim * hidden,
            [second, params, middle, *mlp_pairs], jobs,
        )
        saved.append((resid, first, q, k, v, mixed, middle, second, active, slope, attn_pair, mlp_pairs))
        resid, first = out, nxt
        if not last:
            far_a, near_e, near_r, cot = more

    carry = cot
    attn_grads, expand_grads, reduce_grads, attn_vec, mlp_vec = ([None] * LAYERS for _ in range(5))
    for l in reversed(range(LAYERS)):
        (resid, first, q, k, v, mixed, middle, second, active, slope, attn_pair, mlp_pairs) = saved[l]
        last = l == 0
        if last:
            jobs = [
                FsdpSum(expand_part, n, (3, 5)), FsdpSum(reduce_part, n, (5, 6)),
                CtxSum(attn_full, n, (1, 3, 4, 5)),
            ]
        else:
            jobs = [Exchange(nxt)]
        expand_full, reduce_full, carry, grad, mlp_vec[l], *more = call(
            lambda jobs, *refs, base=8 * l: mlp_back_kernel(jobs, base, *refs),
            f"mlp_back_{l}",
            [square, square, own, every, vec],
            scratch + [VMEM((count, hidden), BF16)] + mlp_scratch, 3 + 6 * l, 8 * count * dim * hidden,
            [grad, active, slope, second, middle, carry, params, *mlp_pairs], jobs,
        )
        if last:
            expand_grads[l + 1], reduce_grads[l + 1], attn_part = more
            ctx_job = CtxSum(expand_full, n, (0, 1, 2, 3), keep=True)
            jobs = [
                ctx_job, FsdpSum(expand_shape, n, (7, 9), source=ctx_job, sends=(0, 1, 2, 3)),
                CtxSum(reduce_full, n, (5, 7, 9, 10)), FsdpSum(attn_part, n, (2, 3)),
            ]
        else:
            (output,) = more
            jobs = [CtxSum(expand_full, n, (0, 1, 2, 3)), CtxSum(reduce_full, n, (4, 7, 8, 10))]
        attn_full, carry, grad, attn_vec[l], *more = call(
            lambda jobs, *refs, base=8 * l, last=last: attention_back_kernel(jobs, heads, last, base, *refs),
            f"attention_back_{l}",
            [jax.ShapeDtypeStruct((dim, 4 * width), BF16), tiny if last else own, own_low if last else every, vec],
            scratch
            + [
                VMEM((count, 3 * width), BF16),
                VMEM((heads, count, LANES), F32),
                VMEM((heads, count, LANES), F32),
            ]
            + attn_scratch,
            4 + 6 * l, 4 * count * dim * 4 * width + 40 * heads * count * count * HD,
            [grad, mixed, q, k, v, first, carry, resid, params, attn_pair], jobs,
        )
        if last:
            expand_grads[l], reduce_part, attn_grads[l + 1] = more
        else:
            expand_part, reduce_part = more
            expand_shape = jax.ShapeDtypeStruct(expand_part.shape, BF16)

    ctx_job = CtxSum(attn_full, n, (0, 1, 2, 3), keep=True)
    jobs = [
        ctx_job,
        FsdpSum(jax.ShapeDtypeStruct((n, shard // 2, 4 * width), BF16), n, (0, 1), source=ctx_job),
        FsdpSum(reduce_part, n, (0, 1)),
        VectorSum([attn_vec[0], mlp_vec[0], attn_vec[1], mlp_vec[1]], n, (0, 1, 2, 3)),
        Exchange(grad),
    ]
    attn_grads[0], reduce_grads[0], vectors, row_grad = call(
        leave_kernel, "leave", [], [], 5, 10**7, [], jobs
    )
    results = [
        jax.ShapeDtypeStruct(shape, F32)
        for shape in (
            (LAYERS, 3, shard, width), (LAYERS, width, shard), (LAYERS, shard, hidden),
            (LAYERS, hidden, shard), (6, LAYERS, shard), query_bias.shape, value_bias.shape,
            expand_bias.shape,
        )
    ]
    joint, out, expand, reduce, wide, query, value, hidden_bias = pl.pallas_call(
        finish_kernel,
        name="finish",
        out_shape=tuple(results),
        in_specs=[VMEM_SPEC] * 7,
        out_specs=tuple([VMEM_SPEC] * 8),
        compiler_params=pltpu.CompilerParams(vmem_limit_bytes=VMEM_LIMIT),
    )(*attn_grads, *expand_grads, *reduce_grads, vectors)
    return (
        output, row_grad, wide[0], wide[1], joint.transpose(0, 2, 1, 3), query, value, out,
        wide[2], wide[3], wide[4], expand, hidden_bias, reduce, wide[5],
    )


def solution(mesh):
    vector = P(None, "fsdp")
    by_head = P(None, "tp", "fsdp")
    rows = P("fsdp", ("ctx", "tp"), None)
    return jax.shard_map(
        local,
        mesh=mesh,
        in_specs=(
            rows, P("fsdp", None), vector, vector, P(None, "fsdp", None, "tp"), by_head, by_head,
            by_head, vector, vector, vector, P(None, "fsdp", "tp"), by_head, by_head, vector, rows,
        ),
        out_specs=(
            rows, rows, vector, vector, P(None, "fsdp", None, "tp"), by_head, by_head,
            by_head, vector, vector, vector, P(None, "fsdp", "tp"), by_head, by_head, vector,
        ),
        check_vma=False,
    )
```

```python
import functools
import math

import jax
import jax.numpy as jnp
from jax import lax
from jax.experimental import pallas as pl
from jax.experimental.pallas import tpu as pltpu
from jax.sharding import PartitionSpec as P

HD = 64
LAYERS = 2
LANES = 128
EPS = 1e-06
MASKED = -10000.0
SCALE = HD ** (-0.5)
VMEM_LIMIT = 60 * 1024 * 1024
F32 = jnp.float32
BF16 = jnp.bfloat16
VMEM = pltpu.VMEM
INV_SQRT2 = 1.0 / math.sqrt(2.0)
INV_SQRT_2PI = 1.0 / math.sqrt(2.0 * math.pi)


def mm(a, b):
    return lax.dot_general(a, b, (((1,), (0,)), ((), ())), preferred_element_type=F32)


def mm_nt(a, b):
    return lax.dot_general(a, b, (((1,), (1,)), ((), ())), preferred_element_type=F32)


def mm_tn(a, b):
    return lax.dot_general(a, b, (((0,), (0,)), ((), ())), preferred_element_type=F32)


def partners():
    t = lax.axis_index("tp")
    return t, t + 1 - 2 * (t % 2), (t + 2) % 4


def entry_barrier(jobs=(), tp=True):
    t, sib, peer = partners()
    others = [{"tp": sib}, {"tp": peer}] if tp or any(job.uses_tp for job in jobs) else []
    if any(job.uses_ctx for job in jobs):
        others.append({"ctx": 1 - lax.axis_index("ctx")})
    if any(job.uses_fsdp for job in jobs):
        n = lax.axis_size("fsdp")
        z = lax.axis_index("fsdp")
        others += [{"fsdp": (z + k) % n} for k in range(1, n)]
    barrier = pltpu.get_barrier_semaphore()
    for other in others:
        pl.semaphore_signal(barrier, inc=1, device_id=other, device_id_type=pl.DeviceIdType.MESH)
    pl.semaphore_wait(barrier, len(others))


def remote(src, dst, send, recv, device):
    return pltpu.make_async_remote_copy(
        src_ref=src,
        dst_ref=dst,
        send_sem=send,
        recv_sem=recv,
        device_id=device,
        device_id_type=pl.DeviceIdType.MESH,
    )


DMA = pltpu.SemaphoreType.DMA
HBM_SPEC = pl.BlockSpec(memory_space=pl.ANY)
VMEM_SPEC = pl.BlockSpec(memory_space=VMEM)


class Job:
    uses_tp = False
    uses_ctx = False
    uses_fsdp = False
    ins = ()
    outs = ()
    scratch = ()
    start_hook = None

    def after(self, hook):
        self.start_hook = hook
        return self

    def bind(self, ins, outs, scratch):
        self.c = lax.axis_index("ctx")
        self.z = lax.axis_index("fsdp")
        self.refs(ins, outs, scratch)

    def start(self):
        pass

    def steps(self):
        return []

    def end(self):
        pass


def chunks_of(rows):
    return 2 if rows % 128 == 0 else 1


def cut_rows(ref, start, size):
    index = (slice(None),) * (len(ref.shape) - 2) + (pl.ds(start, size),)
    return ref.at[index]


class OverFsdp(Job):
    uses_fsdp = True

    def __init__(self, weight, layer, n, hook, chunks=1, ctx_hooks=None):
        self.n, self.layer, self.hook, self.ctx_hooks = n, layer, hook, ctx_hooks
        self.uses_ctx = ctx_hooks is not None
        shape = weight.shape[1:]
        self.rows = shape[-2] // 2
        self.ch = chunks if self.rows % (chunks * 16) == 0 else 1
        half = jax.ShapeDtypeStruct((n, *shape[:-2], self.rows, shape[-1]), BF16)
        self.ins = [(weight, HBM_SPEC)]
        self.outs = [(half, HBM_SPEC)] * (2 if self.uses_ctx else 1)
        self.scratch = [DMA((n + 1, self.ch)), DMA((n, self.ch)), DMA]
        if self.uses_ctx:
            self.scratch += [DMA((n, self.ch)), DMA((n, self.ch)), DMA]

    def refs(self, ins, outs, scratch):
        self.src = ins[0].at[self.layer]
        self.near = outs[0]
        self.send, self.recv, self.here = scratch[:3]
        if self.uses_ctx:
            self.far = outs[1]
            self.x_send, self.x_recv, self.here_far = scratch[3:]

    def mine(self, ch):
        size = self.rows // self.ch
        start = pl.multiple_of(self.c * self.rows + ch * size, size)
        return cut_rows(self.src, start, size)

    def part(self, ref, frm, ch):
        size = self.rows // self.ch
        return cut_rows(ref.at[frm], ch * size, size)

    def out_to(self, k, off, ch):
        to = (self.z + off + self.n) % self.n
        return remote(
            self.mine(ch), self.part(self.near, self.z, ch),
            self.send.at[k, ch], self.recv.at[self.z, ch], {"fsdp": to},
        )

    def arrived(self, frm, ch):
        block = self.part(self.near, frm, ch)
        return remote(
            block, block, self.send.at[self.n, ch], self.recv.at[frm, ch], {"fsdp": self.n - 1 - frm}
        )

    def over_x(self, frm, ch):
        return remote(
            self.part(self.near, frm, ch), self.part(self.far, frm, ch),
            self.x_send.at[frm, ch], self.x_recv.at[frm, ch], {"ctx": 1 - self.c},
        )

    def local(self, half, out, sem):
        start = pl.multiple_of(half * self.rows, self.rows)
        return pltpu.make_async_copy(
            cut_rows(self.src, start, self.rows), out.at[self.z], sem
        )

    def offsets(self):
        return (2, -2, 1, -1) if self.n == 4 else range(1, self.n)

    def sources(self):
        return (1, -1, 2, -2, 3, -3) if self.n == 4 else range(1, self.n)

    def inside(self, off):
        other = self.z + off
        return (other >= 0) & (other < self.n) if self.n == 4 else (other > -1)

    def relays(self):
        return (self.z == 1) | (self.z == 2)

    def start(self):
        for ch in range(self.ch):
            for k, off in enumerate(self.offsets()):
                @pl.when(self.inside(off))
                def _():
                    self.out_to(k, off, ch).start()
        self.local(self.c, self.near, self.here).start()
        if self.uses_ctx:
            self.local(1 - self.c, self.far, self.here_far).start()

    def relay(self):
        if self.n == 4:
            @pl.when(self.relays())
            def _():
                for ch in range(self.ch):
                    through = self.arrived(jnp.where(self.z == 2, 0, 3), ch)
                    through.wait_recv()
                    through.start()

    def take(self, off):
        frm = (self.z + off + self.n) % self.n

        @pl.when(self.inside(off))
        def _():
            for ch in range(self.ch):
                if self.n == 4 and abs(off) == 2:
                    @pl.when(jnp.logical_not((self.z == 2) & (frm == 0) | (self.z == 1) & (frm == 3)))
                    def _():
                        self.arrived(frm, ch).wait_recv()
                else:
                    self.arrived(frm, ch).wait_recv()
                if self.uses_ctx:
                    self.over_x(frm, ch).start()

    def steps(self):
        out = [(self.hook, self.relay)]
        if self.uses_ctx:
            for i, off in enumerate(self.sources()):
                out.append((self.ctx_hooks[min(i // 2, 2)], functools.partial(self.take, off)))
        return out

    def end(self):
        for off in self.sources():
            frm = (self.z + off + self.n) % self.n
            if not self.uses_ctx:
                self.take(off)
            else:
                @pl.when(self.inside(off))
                def _():
                    for ch in range(self.ch):
                        self.over_x(frm, ch).wait()
        for ch in range(self.ch):
            for k, off in enumerate(self.offsets()):
                @pl.when(self.inside(off))
                def _():
                    self.out_to(k, off, ch).wait_send()
            if self.n == 4:
                @pl.when(self.relays())
                def _():
                    self.arrived(jnp.where(self.z == 2, 0, 3), ch).wait_send()
        self.local(self.c, self.near, self.here).wait()
        if self.uses_ctx:
            self.local(1 - self.c, self.far, self.here_far).wait()


class OverCtx(Job):
    uses_ctx = True

    def __init__(self, weight, layer, near, n):
        self.n, self.layer = n, layer
        self.ins = [(weight, HBM_SPEC), (near, HBM_SPEC)]
        self.outs = [(jax.ShapeDtypeStruct(near.shape, BF16), HBM_SPEC)]
        self.scratch = [DMA((n,)), DMA((n,)), DMA]

    def refs(self, ins, outs, scratch):
        self.src, self.near = ins[0].at[self.layer], ins[1]
        (self.far,) = outs
        self.send, self.recv, self.here = scratch

    def copy(self, k):
        frm = (self.z + k) % self.n
        return remote(
            self.near.at[frm], self.far.at[frm], self.send.at[k], self.recv.at[k],
            {"ctx": 1 - self.c},
        )

    def local(self):
        rows = self.near.shape[-2]
        start = pl.multiple_of((1 - self.c) * rows, rows)
        return pltpu.make_async_copy(cut_rows(self.src, start, rows), self.far.at[self.z], self.here)

    def start(self):
        for k in range(1, self.n):
            self.copy(k).start()
        self.local().start()

    def end(self):
        for k in range(1, self.n):
            self.copy(k).wait()
        self.local().wait()


class Loads:
    def __init__(self, sems):
        self.sems, self.copies = sems, []

    def add(self, near, far, out):
        c = lax.axis_index("ctx")
        for half, ref in ((c, near), (1 - c, far)):
            if len(ref.shape) == 3:
                pairs = [(ref, out.at[:, half])]
            else:
                width = ref.shape[-1]
                pairs = [
                    (ref.at[:, j], out.at[:, half, :, j * width : (j + 1) * width])
                    for j in range(ref.shape[1])
                ]
            for src, dst in pairs:
                copy = pltpu.make_async_copy(src, dst, self.sems.at[len(self.copies)])
                copy.start()
                self.copies.append(copy)

    def wait(self):
        for copy in self.copies:
            copy.wait()


class ParamJob(Job):
    uses_fsdp = True

    def __init__(self, wide, narrow, n, dim):
        self.n, self.n_wide = n, len(wide)
        self.ins = [(a, VMEM_SPEC) for a in (*wide, *narrow)]
        shape = (8 * LAYERS, dim)
        self.outs = [(jax.ShapeDtypeStruct(shape, F32), VMEM_SPEC)]
        self.scratch = [
            VMEM(shape, F32), VMEM(shape, BF16), VMEM((n, *shape), BF16), DMA((n,)), DMA((n,))
        ]

    def refs(self, ins, outs, scratch):
        self.wide, self.narrow = ins[: self.n_wide], ins[self.n_wide :]
        (self.out,) = outs
        self.work, self.src, self.got, self.ssem, self.rsem = scratch

    def copy(self, k):
        return remote(
            self.src, self.got.at[k], self.ssem.at[k], self.rsem.at[k],
            {"fsdp": (self.z + k) % self.n},
        )

    def start(self):
        work = self.work
        dim = work.shape[1]
        work[...] = jnp.zeros_like(work)
        shard = self.wide[0].shape[1]
        query, value, expand = self.narrow
        cut = query.shape[2]
        heads = query.shape[1]
        for l in range(LAYERS):
            for k, ref in enumerate(self.wide):
                work[8 * l + k : 8 * l + k + 1, :shard] = ref[l : l + 1, :].astype(F32)
            for row, base, ref in ((6, 0, query), (6, heads * HD, value), (7, 0, expand)):
                block = ref[l].astype(F32)
                for h in range(ref.shape[1]):
                    at = base + h * HD
                    work[8 * l + row : 8 * l + row + 1, at : at + cut] = block[h : h + 1, :]
        all_rows = work[...]
        row = lax.broadcasted_iota(jnp.int32, all_rows.shape, 0) % 8
        by_shard = pltpu.roll(all_rows, self.z * shard, 1)
        by_cut = pltpu.roll(all_rows, self.z * cut, 1)
        placed = jnp.where(row < 6, by_shard, by_cut)
        work[...] = placed
        self.src[...] = placed.astype(BF16)
        for k in range(1, self.n):
            self.copy(k).start()

    def finish(self):
        total = self.work[...]
        for k in range(1, self.n):
            self.copy(k).wait_recv()
            total += self.got[k].astype(F32)
        self.out[...] = total

    def end(self):
        for k in range(1, self.n):
            self.copy(k).wait_send()


class Exchange(Job):
    uses_ctx = True

    def __init__(self, both):
        self.ins = [(both, VMEM_SPEC)]
        self.outs = [(jax.ShapeDtypeStruct(both.shape, both.dtype), VMEM_SPEC)]
        self.scratch = [DMA, DMA]

    def refs(self, ins, outs, scratch):
        (self.src,), (self.out,), (self.ssem, self.rsem) = ins, outs, scratch

    def copy(self):
        c = self.c
        return remote(self.src.at[1 - c], self.out.at[c], self.ssem, self.rsem, {"ctx": 1 - c})

    def start(self):
        self.copy().start()
        self.out[self.c] = self.src[self.c]

    def end(self):
        self.copy().wait()


class CtxSum(Job):
    uses_ctx = True

    def __init__(self, full, n, hooks, keep=False):
        self.n, self.hooks = n, hooks
        full = full.reshape(n, 2, full.shape[0] // (2 * n), full.shape[1])
        shape = (n, *full.shape[2:])
        self.ins = [(full, HBM_SPEC)]
        self.keep = keep
        self.outs = [] if keep else [(jax.ShapeDtypeStruct(shape, BF16), VMEM_SPEC)]
        self.scratch = [VMEM(shape, BF16), DMA((n,)), DMA((n,)), DMA((n,))]
        if keep:
            self.scratch.append(VMEM(shape, BF16))

    def refs(self, ins, outs, scratch):
        (self.full,) = ins
        self.got, self.ssem, self.rsem, self.near = scratch[:4]
        self.out = scratch[4] if self.keep else outs[0]

    def order(self):
        return (0, 3, 1, 2) if self.n == 4 else range(self.n)

    def copy(self, k):
        return remote(
            self.full.at[k, 1 - self.c], self.got.at[k], self.ssem.at[k], self.rsem.at[k],
            {"ctx": 1 - self.c},
        )

    def load(self, k):
        return pltpu.make_async_copy(self.full.at[k, self.c], self.out.at[k], self.near.at[k])

    def start(self):
        for k in self.order():
            self.copy(k).start()
        for k in self.order():
            self.load(k).start()

    def add(self, k):
        self.load(k).wait()
        self.copy(k).wait_recv()
        self.out[k] = (self.out[k].astype(F32) + self.got[k].astype(F32)).astype(BF16)

    def steps(self):
        per = -(-self.n // len(self.hooks))
        return [
            (self.hooks[i // per], functools.partial(self.add, k))
            for i, k in enumerate(self.order())
        ]

    def end(self):
        for k in range(self.n):
            self.copy(k).wait_send()


class FsdpSum(Job):
    uses_fsdp = True

    def __init__(self, rows, n, hooks, source=None, sends=(), spread=True, direct=False):
        self.n, self.hooks, self.source, self.sends = n, hooks, source, sends
        self.relays = n == 4 and not direct
        self.spread = self.uses_ctx = spread
        shape = rows.shape
        self.ins = [] if source else [(rows, VMEM_SPEC)]
        result = (2, *shape[1:]) if spread else shape[1:]
        self.outs = [(jax.ShapeDtypeStruct(result, BF16), VMEM_SPEC)]
        self.rows = shape[1]
        self.ch = chunks_of(self.rows)
        self.scratch = [
            VMEM(shape, BF16), VMEM((2, *shape[1:]), BF16),
            DMA((n, self.ch)), DMA((n, self.ch)), DMA((2, self.ch)), DMA((2, self.ch)),
            DMA((self.ch,)), DMA((self.ch,)),
        ]

    def refs(self, ins, outs, scratch):
        self.src = self.source.out if self.source else ins[0]
        (self.out,) = outs
        (self.got, self.via, self.ssem, self.rsem, self.via_send, self.via_recv, self.x_send,
         self.x_recv) = scratch

    def cut(self, ref, ch):
        size = self.rows // self.ch
        return ref.at[pl.ds(ch * size, size)]

    def direct(self, d, ch):
        return remote(
            self.cut(self.src.at[d], ch), self.cut(self.got.at[self.z], ch),
            self.ssem.at[d, ch], self.rsem.at[self.z, ch], {"fsdp": d},
        )

    def landed(self, frm, ch):
        block = self.cut(self.got.at[frm], ch)
        return remote(block, block, self.ssem.at[frm, ch], self.rsem.at[frm, ch], {"fsdp": frm})

    def to_relay(self, d, ch):
        return remote(
            self.cut(self.src.at[d], ch), self.cut(self.via.at[0], ch),
            self.via_send.at[0, ch], self.via_recv.at[0, ch], {"fsdp": 2 if d == 0 else 1},
        )

    def relayed(self, d, ch):
        return remote(
            self.cut(self.via.at[1], ch), self.cut(self.got.at[self.z], ch),
            self.via_send.at[1, ch], self.rsem.at[self.z, ch], {"fsdp": d},
        )

    def directly(self, d):
        if self.relays and d in (0, 3):
            return (self.z == 1) if d == 0 else (self.z == 2)
        return self.z != d

    def send(self, d):
        if self.relays and d in (0, 3):
            @pl.when(self.z == 3 - d)
            def _():
                for ch in range(self.ch):
                    self.to_relay(d, ch).start()

        @pl.when(self.directly(d))
        def _():
            for ch in range(self.ch):
                self.direct(d, ch).start()

    def order(self):
        return (0, 3, 1, 2) if self.n == 4 else range(self.n)

    def start(self):
        if not self.source:
            for d in self.order():
                self.send(d)

    def relay(self):
        for d, me in ((0, 2), (3, 1)) if self.relays else ():
            @pl.when(self.z == me)
            def _():
                for ch in range(self.ch):
                    self.to_relay(d, ch).wait_recv()
                    mine = self.cut(self.src.at[d], ch)[...].astype(F32)
                    theirs = self.cut(self.via.at[0], ch)[...].astype(F32)
                    self.cut(self.via.at[1], ch)[...] = (mine + theirs).astype(BF16)
                    self.relayed(d, ch).start()

    then = None

    def result(self, ch):
        return self.cut(self.out.at[self.c] if self.spread else self.out, ch)

    def over_x(self, ch):
        block = self.result(ch)
        return remote(block, block, self.x_send.at[ch], self.x_recv.at[ch], {"ctx": 1 - self.c})

    def total(self):
        n = self.n
        for ch in range(self.ch):
            mine = self.cut(self.src.at[self.z], ch)
            if self.relays:
                near = (self.z + 1) % 4
                last = jnp.where(self.z == 0, 2, jnp.where(self.z == 3, 1, (self.z + 3) % 4))
                first = jnp.where(self.z == 3, 2, near)
                inner = (self.z == 1) | (self.z == 2)
                self.landed(first, ch).wait_recv()
                self.landed(last, ch).wait_recv()
                part = (
                    mine[...].astype(F32)
                    + self.cut(self.got.at[first], ch)[...].astype(F32)
                    + self.cut(self.got.at[last], ch)[...].astype(F32)
                )
                block = self.result(ch)

                @pl.when(inner)
                def _():
                    middle = (self.z + 2) % 4
                    self.landed(middle, ch).wait_recv()
                    block[...] = (part + self.cut(self.got.at[middle], ch)[...].astype(F32)).astype(BF16)

                @pl.when(jnp.logical_not(inner))
                def _():
                    block[...] = part.astype(BF16)
            else:
                part = mine[...].astype(F32)
                for k in range(1, n):
                    frm = (self.z + k) % n
                    self.landed(frm, ch).wait_recv()
                    part += self.cut(self.got.at[frm], ch)[...].astype(F32)
                self.result(ch)[...] = part.astype(BF16)
            if self.spread:
                self.over_x(ch).start()
            elif self.then is not None:
                self.then(ch)

    def steps(self):
        out = [
            (self.sends[i * len(self.sends) // self.n], functools.partial(self.send, d))
            for i, d in enumerate(self.order())
            if self.sends
        ]
        return out + [(self.hooks[0], self.relay), (self.hooks[1], self.total)]

    def end(self):
        for ch in range(self.ch):
            if self.spread:
                other = self.cut(self.out.at[1 - self.c], ch)
                remote(
                    other, other, self.x_send.at[ch], self.x_recv.at[ch], {"ctx": 1 - self.c}
                ).wait_recv()
                self.over_x(ch).wait_send()
            for d in range(self.n):
                if self.relays and d in (0, 3):
                    @pl.when(self.z == 3 - d)
                    def _():
                        self.to_relay(d, ch).wait_send()

                    @pl.when(self.z == (2 if d == 0 else 1))
                    def _():
                        self.relayed(d, ch).wait_send()

                @pl.when(self.directly(d))
                def _():
                    self.direct(d, ch).wait_send()


class CtxAdd(Job):
    uses_ctx = True

    def __init__(self, rows, hook, source=None):
        self.hook, self.source = hook, source
        self.ins = [] if source else [(rows, VMEM_SPEC)]
        self.outs = [(jax.ShapeDtypeStruct(rows.shape, BF16), VMEM_SPEC)]
        self.rows = rows.shape[0]
        self.ch = chunks_of(self.rows)
        self.scratch = [VMEM(rows.shape, BF16), DMA((self.ch,)), DMA((self.ch,))]

    def refs(self, ins, outs, scratch):
        self.src = self.source.out if self.source else ins[0]
        (self.out,) = outs
        self.got, self.ssem, self.rsem = scratch
        if self.source:
            self.source.then = self.send

    def cut(self, ref, ch):
        size = self.rows // self.ch
        return ref.at[pl.ds(ch * size, size)]

    def copy(self, ch):
        return remote(
            self.cut(self.src, ch), self.cut(self.got, ch), self.ssem.at[ch], self.rsem.at[ch],
            {"ctx": 1 - self.c},
        )

    def send(self, ch):
        self.copy(ch).start()

    def start(self):
        if not self.source:
            for ch in range(self.ch):
                self.send(ch)

    def add(self):
        for ch in range(self.ch):
            self.copy(ch).wait_recv()
            mine, theirs = self.cut(self.src, ch)[...], self.cut(self.got, ch)[...]
            self.cut(self.out, ch)[...] = (mine.astype(F32) + theirs.astype(F32)).astype(BF16)

    def steps(self):
        return [(self.hook, self.add)]

    def end(self):
        for ch in range(self.ch):
            self.copy(ch).wait_send()


class Background:
    def __init__(self, jobs):
        self.jobs = jobs
        self.todo = []
        for job in jobs:
            if job.start_hook is not None:
                self.todo.append((job.start_hook, job.start))
            self.todo += job.steps()

    def start(self):
        for job in self.jobs:
            if job.start_hook is None:
                job.start()

    def at(self, hook):
        for when, function in self.todo:
            if when == hook:
                function()

    def loop(self, b, count=4, base=0):
        for k in range(count):
            if any(when == base + k for when, _ in self.todo):
                @pl.when(b == k)
                def _():
                    self.at(base + k)

    def end(self):
        for job in self.jobs:
            job.end()


class Links:
    def __init__(self, send, recv, sib, peer):
        self.send, self.recv, self.sib, self.peer = send, recv, sib, peer

    def make(self, kind, s, src, dst, other):
        return pltpu.make_async_remote_copy(
            src_ref=src,
            dst_ref=dst,
            send_sem=self.send.at[kind, s],
            recv_sem=self.recv.at[kind, s],
            device_id={"tp": other},
            device_id_type=pl.DeviceIdType.MESH,
        )


def statistics(rows):
    mean = jnp.mean(rows, axis=-1, keepdims=True)
    centred = rows - mean
    inverse = lax.rsqrt(jnp.mean(centred * centred, axis=-1, keepdims=True) + EPS)
    return centred * inverse, inverse


def norm_back(rows, d_out, gain):
    unit, inverse = statistics(rows)
    e = d_out * gain
    back = inverse * (
        e
        - jnp.mean(e, axis=-1, keepdims=True)
        - unit * jnp.mean(e * unit, axis=-1, keepdims=True)
    )
    d_gain = jnp.sum(d_out * unit, axis=0, keepdims=True)
    d_shift = jnp.sum(d_out, axis=0, keepdims=True)
    return back, d_gain, d_shift


def rows_of(ref, b):
    block = ref[b]
    return block.reshape(block.shape[0] * block.shape[1], block.shape[2])


class Gather:
    def __init__(self, links, out):
        self.links, self.out = links, out

    def near(self, s):
        return self.links.make(3, s, self.out.at[2 + s, 0], self.out.at[2 + s, 1], self.links.sib)

    def across(self, s):
        return self.links.make(4, s, self.out.at[2 + s, 0], self.out.at[s, 0], self.links.peer)

    def onward(self, s):
        return self.links.make(5, s, self.out.at[s, 0], self.out.at[s, 1], self.links.sib)

    def start(self, rows):
        for s in range(2):
            self.out[2 + s, 0] = rows(s)
            self.near(s).start()
            self.across(s).start()

    def need(self, b):
        s = b % 2

        @pl.when(b >= 2)
        def _():
            self.near(s).wait_recv()

        @pl.when(b < 2)
        def _():
            self.across(s).wait_recv()
            self.onward(s).start()
            self.onward(s).wait_recv()

    def end(self):
        for s in range(2):
            for copy in (self.near(s), self.across(s), self.onward(s)):
                copy.wait_send()


class Scatter:
    def __init__(self, links, part, sent, got, own):
        self.links, self.part, self.sent, self.got, self.own = links, part, sent, got, own

    def copy(self, kind, s):
        other = self.links.peer if kind == 1 else self.links.sib
        return self.links.make(kind, s, self.sent.at[kind, s], self.got.at[kind, s], other)

    def block(self, b):
        s = b % 2
        half = self.part.shape[0] // 2

        @pl.when(b < 2)
        def _():
            self.sent[0, s] = self.part[half:].astype(BF16)
            first = self.copy(0, s)
            first.start()
            first.wait_recv()
            self.sent[1, s] = (self.part[:half] + self.got[0, s].astype(F32)).astype(BF16)
            self.copy(1, s).start()

        @pl.when(b >= 2)
        def _():
            self.sent[2, s] = self.part[half:].astype(BF16)
            self.copy(2, s).start()
            self.own[s] = self.part[:half]

    def total(self, s):
        self.copy(2, s).wait_recv()
        self.copy(1, s).wait_recv()
        return self.own[s] + self.got[2, s].astype(F32) + self.got[1, s].astype(F32)

    def end(self):
        for s in range(2):
            for kind in range(3):
                self.copy(kind, s).wait_send()


def scatter_scratch(half, width):
    return [
        VMEM((2 * half, width), F32),
        VMEM((3, 2, half, width), BF16),
        VMEM((3, 2, half, width), BF16),
        VMEM((2, half, width), F32),
        pltpu.SemaphoreType.DMA((6, 2)),
        pltpu.SemaphoreType.DMA((6, 2)),
    ]


def enter_kernel(jobs, first):
    params, tokens, attn, expand = jobs
    entry_barrier(jobs, False)
    tokens.start()
    params.start()
    attn.start()
    params.finish()
    attn.relay()
    expand.start()
    tokens.end()
    for s in range(2):
        unit, _ = statistics(tokens.out[s].astype(F32))
        first[s] = (unit * params.out[0:1, :] + params.out[1:2, :]).astype(BF16)
    for off in attn.sources()[:4]:
        attn.take(off)
    expand.relay()
    for off in attn.sources()[4:]:
        attn.take(off)
    for job in (params, attn, expand):
        job.end()


def pair_tile(pair, h):
    tile = pair if h % 2 == 0 else pltpu.roll(pair, HD, 1)
    return tile


def attention_kernel(
    jobs, heads, base,
    own_first, params, key_extra, resid, near, far,
    first, second, middle, q_out, k_out, v_out, mixed_out,
    part, sent, got, own, send, recv, weight, load,
):
    t, sib, peer = partners()
    background = Background(jobs)
    entry_barrier(jobs)
    background.start()
    links = Links(send, recv, sib, peer)
    scatter = Scatter(links, part, sent, got, own)
    width = heads * HD
    gather = Gather(links, first)
    gather.start(lambda s: own_first[s])
    loads = Loads(load)
    loads.add(near, far, weight)
    loads.wait()
    weight = whole(weight)
    out_bias, gain, shift = (params[base + k : base + k + 1, :] for k in (2, 3, 4))
    q_bias = params[base + 6 : base + 7, :width]
    v_bias = params[base + 6 : base + 7, width : 2 * width]
    half = first.shape[2]
    rows = 2 * half
    lane = lax.broadcasted_iota(jnp.int32, (rows, LANES), 1)
    head_lane = lane < HD
    q_extra = jnp.where(lane < HD + 2, 1.0, 0.0).astype(BF16)
    v_extra = jnp.where(lane < HD + 3, 1.0, 0.0).astype(BF16)

    def project(j, carry):
        b = (j + 2) % 4
        gather.need(b)
        x = rows_of(first, b)
        y = mm(x, weight[:, : 3 * width])
        q = ((y[:, :width] + q_bias).astype(BF16) * SCALE).astype(BF16)
        k = y[:, width : 2 * width].astype(BF16)
        v = (y[:, 2 * width :] + v_bias).astype(BF16)
        g, s = b // 2, b % 2
        mine = jnp.where(g == 1, t, peer)
        other = mine + 1 - 2 * (mine % 2)
        extra = jnp.concatenate([key_extra[mine, s], key_extra[other, s]], axis=0)
        at = pl.ds(pl.multiple_of(b * rows, rows), rows)
        for h in range(heads):
            cut = slice(LANES * (h // 2), LANES * (h // 2 + 1))
            q_out[h, at, :] = jnp.where(head_lane, pair_tile(q[:, cut], h), q_extra)
            k_out[h, at, :] = jnp.where(head_lane, pair_tile(k[:, cut], h), extra)
            v_out[h, at, :] = jnp.where(head_lane, pair_tile(v[:, cut], h), v_extra)
        background.loop(j, 4, 20)
        return carry

    lax.fori_loop(0, 4, project, 0)
    background.at(0)

    def attend(b, carry):
        at = pl.ds(pl.multiple_of(b * rows, rows), rows)
        outs = []
        for h in range(heads):
            q = q_out[h, at, :]
            scores = mm_nt(q, k_out[h])
            top = jnp.max(scores, axis=-1, keepdims=True)
            weights = jnp.exp(scores - top).astype(BF16)
            summed = mm(weights, v_out[h])
            total = summed[:, HD : HD + 1]
            outs.append(summed / total)
            log_total = -(top + jnp.log(total))
            high = log_total.astype(BF16).astype(F32)
            rest = log_total - high
            mid = rest.astype(BF16).astype(F32)
            low = rest - mid
            tail = jnp.where(lane == HD + 2, high, jnp.where(lane == HD + 3, mid, low))
            q_out[h, at, :] = jnp.where(
                (lane >= HD + 2) & (lane < HD + 5), tail.astype(BF16), q
            )
        tiles = [
            jnp.where(head_lane, outs[h], pltpu.roll(outs[h + 1], HD, 1))
            for h in range(0, heads, 2)
        ]
        mixed = jnp.concatenate(tiles, axis=1).astype(BF16)
        mixed_out[at, :] = mixed
        part[...] = mm_nt(mixed, weight[:, 3 * width :])
        scatter.block(b)
        background.loop(b, 4, 1)
        return carry

    lax.fori_loop(0, 4, attend, 0)
    for s in range(2):
        mid = resid[s].astype(F32) + (scatter.total(s) + out_bias)
        middle[s] = mid
        unit, _ = statistics(mid)
        second[s] = (unit * gain + shift).astype(BF16)
        background.at(5 + s)
    gather.end()
    scatter.end()
    background.end()


def mlp_kernel(
    jobs, last, base,
    own_second, params, middle, near_e, far_e, near_r, far_r,
    second, active_out, slope_out, resid, nxt,
    part, sent, got, own, send, recv, expand, reduce, load,
):
    t, sib, peer = partners()
    background = Background(jobs)
    entry_barrier(jobs)
    background.start()
    links = Links(send, recv, sib, peer)
    scatter = Scatter(links, part, sent, got, own)
    half = second.shape[2]
    rows = 2 * half
    gather = Gather(links, second)
    gather.start(lambda s: own_second[s])
    loads = Loads(load)
    loads.add(near_e, far_e, expand)
    loads.add(near_r, far_r, reduce)
    loads.wait()
    expand, reduce = whole(expand), whole(reduce)
    hidden = expand.shape[1]
    out_bias = params[base + 5 : base + 6, :]
    following = 0 if last else base + 8
    gain, shift = (params[following + k : following + k + 1, :] for k in (0, 1))
    step = 256

    def block(j, carry):
        b = (j + 2) % 4
        gather.need(b)
        at = pl.ds(pl.multiple_of(b * rows, rows), rows)
        x = rows_of(second, b)
        for n in range(0, hidden, step):
            before = mm(x, expand[:, n : n + step]) + params[base + 7 : base + 8, n : n + step]
            cdf = 0.5 * (1.0 + lax.erf(before * INV_SQRT2))
            active_out[at, n : n + step] = (before * cdf).astype(BF16)
            slope = cdf + before * (jnp.exp(before * before * -0.5) * INV_SQRT_2PI)
            slope_out[at, n : n + step] = slope.astype(BF16)
        part[...] = mm_nt(active_out[at, :], reduce[...])
        scatter.block(b)
        background.loop(j, 4, 1)
        return carry

    lax.fori_loop(0, 4, block, 0)
    for s in range(2):
        res = middle[s] + (scatter.total(s) + out_bias)
        if last:
            nxt[s] = res.astype(BF16)
        else:
            resid[s] = res
            unit, _ = statistics(res)
            nxt[s] = (unit * gain + shift).astype(BF16)
        background.at(5 + s)
    gather.end()
    scatter.end()
    background.end()


def token_product(left, right, outs, offset=0):
    depth = left.shape[-1]
    total = left.shape[0] * left.shape[1] * left.shape[2]
    step = 256

    def body(j, carry):
        cut = pl.ds(pl.multiple_of(j * step, step), step)
        x = left[:, :, :, cut].reshape(total, step)
        product = mm_tn(x, right[...]).astype(BF16)
        width = right.shape[-1] // len(outs)
        for k, out in enumerate(outs):
            out[cut, offset : offset + width] = product[:, k * width : (k + 1) * width]
        return carry

    lax.fori_loop(0, depth // step, body, 0)


def mlp_back_kernel(
    jobs, base,
    active, slope, second, middle, carry_in, params, near_e, far_e, near_r, far_r,
    expand_grad, reduce_left, reduce_right, carry_out, vectors,
    part, sent, got, own, send, recv, grad, d_before, expand, reduce, load,
):
    t, sib, peer = partners()
    background = Background(jobs)
    entry_barrier(jobs)
    background.start()
    links = Links(send, recv, sib, peer)
    scatter = Scatter(links, part, sent, got, own)
    gather = Gather(links, grad)
    gather.start(lambda s: carry_in[s].astype(BF16))
    loads = Loads(load)
    loads.add(near_e, far_e, expand)
    loads.add(near_r, far_r, reduce)
    loads.wait()
    expand, reduce = whole(expand), whole(reduce)
    gain = params[base + 3 : base + 4, :]
    half = grad.shape[2]
    rows = 2 * half
    hidden = active.shape[1]
    step = 256
    vectors[...] = jnp.zeros_like(vectors)

    def block(j, carry):
        b = (j + 2) % 4
        gather.need(b)
        at = pl.ds(pl.multiple_of(b * rows, rows), rows)
        x = rows_of(grad, b)
        for n in range(0, hidden, step):
            d_act = mm(x, reduce[:, n : n + step])
            d_bef = (d_act * slope[at, n : n + step].astype(F32)).astype(BF16)
            d_before[at, n : n + step] = d_bef
            vectors[4:5, n : n + step] += jnp.sum(d_bef.astype(F32), axis=0, keepdims=True)
        part[...] = mm_nt(d_before[at, :], expand[...])
        scatter.block(b)
        background.loop(j)
        return carry

    lax.fori_loop(0, 4, block, 0)
    token_product(grad, active, (reduce_left, reduce_right))
    background.at(4)

    def finish(s):
        back, d_gain, d_shift = norm_back(middle[s], scatter.total(s), gain)
        carry = carry_in[s].astype(F32)
        mid = carry + back
        carry_out[s] = mid
        low = mid.astype(BF16)
        vectors[0:1, :] += d_gain
        vectors[1:2, :] += d_shift
        vectors[2:3, :] += jnp.sum(low.astype(F32), axis=0, keepdims=True)
        vectors[3:4, :] += jnp.sum(carry.astype(BF16).astype(F32), axis=0, keepdims=True)

    finish(0)
    background.at(5)
    token_product(second, d_before, (expand_grad,))
    finish(1)
    background.at(6)
    gather.end()
    scatter.end()
    background.end()


def attention_back_kernel(
    jobs, heads, base,
    mixed, q_in, k_in, v_in, first, carry_in, resid, params, near, far,
    weight_grad, carry_out, vectors,
    part, sent, got, own, send, recv, grad, d_joint, d_key, d_value, weight, load,
):
    t, sib, peer = partners()
    background = Background(jobs)
    entry_barrier(jobs)
    background.start()
    links = Links(send, recv, sib, peer)
    scatter = Scatter(links, part, sent, got, own)
    width = heads * HD
    gather = Gather(links, grad)
    gather.start(lambda s: carry_in[s].astype(BF16))
    loads = Loads(load)
    loads.add(near, far, weight)
    loads.wait()
    weight = whole(weight)
    gain = params[base : base + 1, :]
    half = grad.shape[2]
    rows = 2 * half
    lane = lax.broadcasted_iota(jnp.int32, (rows, LANES), 1)
    head_lane = lane < HD
    vectors[...] = jnp.zeros_like(vectors)
    d_key[...] = jnp.zeros_like(d_key)
    d_value[...] = jnp.zeros_like(d_value)

    def pairs(tiles):
        return jnp.concatenate(
            [
                jnp.where(head_lane, tiles[h], pltpu.roll(tiles[h + 1], HD, 1))
                for h in range(0, heads, 2)
            ],
            axis=1,
        )

    def attend(j, carry):
        b = (j + 2) % 4
        gather.need(b)
        at = pl.ds(pl.multiple_of(b * rows, rows), rows)
        d_mixed = mm(rows_of(grad, b), weight[:, 3 * width :]).astype(BF16)
        product = d_mixed.astype(F32) * mixed[at, :].astype(F32)
        d_queries = []
        for h in range(heads):
            cut = slice(LANES * (h // 2), LANES * (h // 2 + 1))
            keep = head_lane if h % 2 == 0 else lane >= HD
            delta = -jnp.sum(jnp.where(keep, product[:, cut], 0.0), axis=-1, keepdims=True)
            high = delta.astype(BF16).astype(F32)
            rest = delta - high
            mid = rest.astype(BF16).astype(F32)
            low = rest - mid
            tail = jnp.where(
                lane == HD,
                high,
                jnp.where(lane == HD + 1, mid, jnp.where(lane == HD + 2, low, 0.0)),
            ).astype(BF16)
            d_o = jnp.where(head_lane, pair_tile(d_mixed[:, cut], h), tail)
            q = q_in[h, at, :]
            probs = jnp.exp(mm_nt(k_in[h], q))
            d_value[h] += mm(probs.astype(BF16), d_o)
            d_raw = (probs * mm_nt(v_in[h], d_o)).astype(BF16)
            d_key[h] += mm(d_raw, q)
            d_queries.append(mm_tn(d_raw, k_in[h]) * SCALE)
        d_joint[at, :width] = pairs(d_queries).astype(BF16)
        background.loop(j)
        return carry

    lax.fori_loop(0, 4, attend, 0)

    def project(b, carry):
        at = pl.ds(pl.multiple_of(b * rows, rows), rows)
        d_joint[at, width : 2 * width] = pairs([d_key[h, at, :] for h in range(heads)]).astype(BF16)
        d_joint[at, 2 * width :] = pairs([d_value[h, at, :] for h in range(heads)]).astype(BF16)
        d_rows = d_joint[at, :]
        sums = jnp.sum(d_rows.astype(F32), axis=0, keepdims=True)
        vectors[2:3, :width] += sums[:, :width]
        vectors[2:3, width : 2 * width] += sums[:, 2 * width :]
        part[...] = mm_nt(d_rows, weight[:, : 3 * width])
        scatter.block(b)
        background.loop(b, 4, 4)
        return carry

    lax.fori_loop(0, 4, project, 0)
    token_product(grad, mixed, (weight_grad,), 3 * width)
    background.at(8)

    def finish(s):
        back, d_gain, d_shift = norm_back(resid[s].astype(F32), scatter.total(s), gain)
        carry = carry_in[s] + back
        carry_out[s] = carry.astype(carry_out.dtype)
        vectors[0:1, :] += d_gain
        vectors[1:2, :] += d_shift

    finish(0)
    background.at(9)
    token_product(first, d_joint, (weight_grad,))
    finish(1)
    background.at(10)
    gather.end()
    scatter.end()
    background.end()


class VectorSum(Job):
    uses_tp = uses_ctx = uses_fsdp = True

    def __init__(self, vectors, n, hooks):
        self.n, self.hooks = n, hooks
        dim = vectors[0].shape[1]
        self.ins = [(v, VMEM_SPEC) for v in vectors]
        self.outs = [(jax.ShapeDtypeStruct((16, dim), F32), VMEM_SPEC)]
        self.scratch = [
            VMEM((4, 16, dim), F32), VMEM((3 + n, 16, dim), F32), DMA((3 + n,)), DMA((3 + n,))
        ]

    def refs(self, ins, outs, scratch):
        self.vectors = ins
        (self.out,) = outs
        self.held, self.got, self.ssem, self.rsem = scratch
        t, self.sib, self.peer = partners()

    def copy(self, k):
        if k < 2:
            to = {"tp": self.sib if k == 0 else self.peer}
        elif k == 2:
            to = {"ctx": 1 - self.c}
        else:
            to = {"fsdp": (self.z + k - 2) % self.n}
        return remote(
            self.held.at[min(k, 3)], self.got.at[k], self.ssem.at[k], self.rsem.at[k], to
        )

    def start(self):
        for l in range(LAYERS):
            attn, mlp = self.vectors[2 * l], self.vectors[2 * l + 1]
            for row, (ref, index) in enumerate(
                ((attn, 0), (attn, 1), (mlp, 2), (mlp, 0), (mlp, 1), (mlp, 3), (attn, 2), (mlp, 4))
            ):
                self.held[0, 8 * l + row : 8 * l + row + 1, :] = ref[index : index + 1, :]
        self.copy(0).start()

    def fold(self, k):
        self.copy(k).wait_recv()
        came = self.got[k]
        if k < 2:
            row = lax.broadcasted_iota(jnp.int32, came.shape, 0)
            came = jnp.where(row % 8 < 6, came, 0.0)
        self.held[k + 1] = self.held[k] + came
        if k < 2:
            self.copy(k + 1).start()
        else:
            for j in range(1, self.n):
                self.copy(2 + j).start()

    def finish(self):
        total = self.held[3]
        for j in range(1, self.n):
            self.copy(2 + j).wait_recv()
            total += self.got[2 + j]
        self.out[...] = total

    def steps(self):
        return [(self.hooks[k], functools.partial(self.fold, k)) for k in range(3)] + [
            (self.hooks[3], self.finish)
        ]

    def end(self):
        for k in range(2 + self.n):
            self.copy(k).wait_send()


def leave_kernel(jobs):
    attn_ctx, attn_fsdp, left, right, right_ctx, vectors, rows, former = jobs
    entry_barrier(jobs, False)
    attn_ctx.start()
    left.start()
    right.start()
    vectors.start()
    rows.start()
    former.start()
    vectors.fold(0)
    left.relay()
    order = list(attn_ctx.order())
    for i, k in enumerate(order):
        attn_ctx.add(k)
        if i == 1:
            right.relay()
            for j in order[:2]:
                attn_fsdp.send(j)
        elif i > 1:
            attn_fsdp.send(k)
        if i in (1, 2):
            vectors.fold(i)
    left.total()
    attn_fsdp.relay()
    right.total()
    vectors.finish()
    former.add()
    attn_fsdp.total()
    right_ctx.add()
    for job in jobs:
        job.end()


def finish_kernel(
    attn_0, attn_1, expand_0, expand_1, left_0, left_1, right_0, right_1, vectors,
    joint, out, expand, reduce, wide, query, value, hidden,
):
    z = lax.axis_index("fsdp")
    half = attn_0.shape[1]
    width = joint.shape[3]
    shard = 2 * half
    layers = ((attn_0, expand_0, left_0, right_0), (attn_1, expand_1, left_1, right_1))
    for l, (a, e, left, right) in enumerate(layers):
        rows = a[...].reshape(shard, a.shape[2]).astype(F32)
        for k in range(3):
            joint[l, k] = rows[:, k * width : (k + 1) * width]
        out[l] = rows[:, 3 * width :].T
        expand[l] = e[...].reshape(shard, e.shape[2]).astype(F32)
        part = left.shape[-1]
        for k, r in enumerate((left, right)):
            reduce[l, k * part : (k + 1) * part, :] = r[...].reshape(shard, part).astype(F32).T
    cut = query.shape[2]
    heads = query.shape[1]
    dim = vectors.shape[1]
    own = pltpu.roll(vectors[...], lax.rem(dim - z * shard, dim), 1)
    by_cut = pltpu.roll(vectors[...], lax.rem(dim - z * cut, dim), 1)
    for l in range(LAYERS):
        for k in range(6):
            wide[k, l : l + 1, :] = own[8 * l + k : 8 * l + k + 1, :shard]
        for row, base, ref in ((6, 0, query), (6, heads * HD, value), (7, 0, hidden)):
            for h in range(ref.shape[1]):
                at = base + h * HD
                ref[l, h : h + 1, :] = by_cut[8 * l + row : 8 * l + row + 1, at : at + cut]


def whole(ref):
    return ref.reshape(ref.shape[0] * ref.shape[1] * ref.shape[2], ref.shape[3])


def call(kernel, name, outs, scratch, collective_id, flops, args, jobs=()):
    args = [
        (a, spec)
        for arg in args
        for a, spec in ([(arg, VMEM_SPEC)] if not isinstance(arg, tuple) else [(a, HBM_SPEC) for a in arg])
    ]
    ins = args + [pair for job in jobs for pair in job.ins]
    results = [(o, VMEM_SPEC) for o in outs] + [pair for job in jobs for pair in job.outs]
    scratch = list(scratch)
    n_scratch = len(scratch)
    for job in jobs:
        scratch += job.scratch

    def body(*refs):
        refs = list(refs)
        in_refs = refs[: len(ins)]
        out_refs = refs[len(ins) : len(ins) + len(results)]
        scratch_refs = refs[len(ins) + len(results) :]
        a, b, c = len(args), len(outs), n_scratch
        for job in jobs:
            ends = a + len(job.ins), b + len(job.outs), c + len(job.scratch)
            job.bind(in_refs[a : ends[0]], out_refs[b : ends[1]], scratch_refs[c : ends[2]])
            a, b, c = ends
        kernel(
            jobs, *in_refs[: len(args)], *out_refs[: len(outs)], *scratch_refs[:n_scratch]
        )

    size = sum(a.size * a.dtype.itemsize for a, _ in ins) + sum(
        math.prod(o.shape) * o.dtype.itemsize for o, _ in results
    )
    return pl.pallas_call(
        body,
        name=name,
        out_shape=tuple(o for o, _ in results),
        in_specs=[spec for _, spec in ins],
        out_specs=tuple(spec for _, spec in results),
        scratch_shapes=scratch,
        compiler_params=pltpu.CompilerParams(
            collective_id=collective_id, has_side_effects=True, vmem_limit_bytes=VMEM_LIMIT
        ),
        cost_estimate=pl.CostEstimate(flops=flops, bytes_accessed=size, transcendentals=0),
    )(*[a for a, _ in ins])


def local(
    tokens, key_valid, first_gain, first_shift, joint_weight, query_bias, value_bias,
    out_weight, out_bias, second_gain, second_shift, expand_weight, expand_bias,
    reduce_weight, reduce_bias, cotangent,
):
    ctx_size = lax.axis_size("ctx")
    tp_size = lax.axis_size("tp")
    fsdp_size = lax.axis_size("fsdp")
    clips, half, dim = tokens.shape
    assert clips == ctx_size == 2 and tp_size == 4 and joint_weight.shape[0] == LAYERS
    c = lax.axis_index("ctx")
    shard = joint_weight.shape[1]
    width = joint_weight.shape[3]
    heads = width // HD
    hidden = expand_weight.shape[2]
    attn_w = jnp.concatenate(
        [joint_weight.transpose(0, 2, 1, 3), out_weight.transpose(0, 2, 1)[:, None]], axis=1
    )
    reduce_w = reduce_weight.transpose(0, 2, 1)

    valid = lax.dynamic_index_in_dim(key_valid, c, 0, keepdims=False)
    bias = jnp.where(valid == 1, 0.0, MASKED).astype(F32)
    bias = bias.reshape(ctx_size, tp_size, half, 1).transpose(1, 0, 2, 3)
    high = bias.astype(BF16).astype(F32)
    col = lax.broadcasted_iota(jnp.int32, (1, 1, 1, LANES), 3) - HD
    key_extra = jnp.where(
        col == 0, high, jnp.where(col == 1, bias - high, jnp.where((col >= 2) & (col < 5), 1.0, 0.0))
    ).astype(BF16)

    every = jax.ShapeDtypeStruct((4, 2, half, dim), BF16)
    own = jax.ShapeDtypeStruct((2, half, dim), F32)
    own_low = jax.ShapeDtypeStruct((2, half, dim), BF16)
    tiny = jax.ShapeDtypeStruct((8, LANES), F32)
    vec = jax.ShapeDtypeStruct((8, dim), F32)
    square = jax.ShapeDtypeStruct((dim, hidden), BF16)
    narrow = jax.ShapeDtypeStruct((dim, hidden // 2), BF16)
    count = 8 * half
    n = fsdp_size
    scratch = scatter_scratch(half, dim)

    def held(columns):
        return VMEM((n, 2, shard // 2, columns), BF16)

    attn_scratch = [held(4 * width), DMA((8,))]
    mlp_scratch = [held(hidden), held(hidden), DMA((4,))]

    jobs = [
        ParamJob(
            [first_gain, first_shift, out_bias, second_gain, second_shift, reduce_bias],
            [query_bias, value_bias, expand_bias], n, dim,
        ),
        Exchange(tokens),
        OverFsdp(attn_w, 0, n, None, 2, (0, 0, 0)),
        OverFsdp(expand_weight, 0, n, None),
    ]
    rows, params, tok, near_a, far_a, near_e = call(
        enter_kernel, "enter", [own_low], [], 0, 10**7, [], jobs
    )
    resid = tok
    saved = []
    for l in range(LAYERS):
        last = l == LAYERS - 1
        heads_shape = jax.ShapeDtypeStruct((heads, count, LANES), BF16)
        jobs = [
            OverCtx(expand_weight, l, near_e, n),
            OverFsdp(reduce_w, l, n, 22, 1, (23, 0, 1)),
        ]
        if not last:
            jobs.append(OverFsdp(attn_w, l + 1, n, 3).after(22))
        first, rows, middle, q, k, v, mixed, *more = call(
            lambda jobs, *refs, base=8 * l: attention_kernel(jobs, heads, base, *refs),
            f"attention_{l}",
            [every, own_low, own, heads_shape, heads_shape, heads_shape,
             jax.ShapeDtypeStruct((count, width), BF16)],
            scratch + attn_scratch, 1 + 6 * l,
            2 * count * dim * 4 * width + 16 * heads * count * count * HD,
            [rows, params, key_extra, resid, (near_a, far_a)], jobs,
        )
        attn_pair = (near_a, far_a)
        far_e, near_r, far_r, *more = more
        if not last:
            (near_a,) = more
        mlp_pairs = ((near_e, far_e), (near_r, far_r))
        rows_hidden = jax.ShapeDtypeStruct((count, hidden), BF16)
        jobs = [Exchange(cotangent)] if last else [
            OverCtx(attn_w, l + 1, near_a, n), OverFsdp(expand_weight, l + 1, n, 3),
        ]
        second, active, slope, out, rows, *more = call(
            lambda jobs, *refs, base=8 * l, last=last: mlp_kernel(jobs, last, base, *refs),
            f"mlp_{l}",
            [every, rows_hidden, rows_hidden, tiny if last else own, own_low],
            scratch + mlp_scratch, 2 + 6 * l, 4 * count * dim * hidden,
            [rows, params, middle, *mlp_pairs], jobs,
        )
        saved.append((resid, first, q, k, v, mixed, middle, second, active, slope, attn_pair, mlp_pairs))
        resid = out
        if last:
            (cot,) = more
        else:
            far_a, near_e = more

    carry = cot
    attn_grads, expand_grads, left_grads, right_grads, attn_vec, mlp_vec = (
        [None] * LAYERS for _ in range(6)
    )
    for l in reversed(range(LAYERS)):
        (resid, first, q, k, v, mixed, middle, second, active, slope, attn_pair, mlp_pairs) = saved[l]
        last = l == 0
        if last:
            jobs = [
                CtxSum(attn_full, n, (6, 6, 6, 6)), FsdpSum(expand_part, n, (2, 4)),
                FsdpSum(left_part, n, (4, 5)).after(2),
            ]
        else:
            jobs = [Exchange(rows)]
        expand_full, left_full, right_full, carry, mlp_vec[l], *more = call(
            lambda jobs, *refs, base=8 * l: mlp_back_kernel(jobs, base, *refs),
            f"mlp_back_{l}",
            [square, narrow, narrow, own, vec],
            scratch + [VMEM(every.shape, BF16), VMEM((count, hidden), BF16)] + mlp_scratch, 3 + 6 * l, 8 * count * dim * hidden,
            [active, slope, second, middle, carry, params, *mlp_pairs], jobs,
        )
        if last:
            attn_part, expand_grads[l + 1], left_grads[l + 1] = more
            ctx_job = CtxSum(expand_full, n, (1, 2, 3, 4), keep=True)
            jobs = [
                FsdpSum(attn_part, n, (1, 4)), ctx_job,
                FsdpSum(expand_shape, n, (5, 9), source=ctx_job, sends=(1, 2, 3, 4)),
                CtxSum(left_full, n, (10, 10, 10, 10)),
            ]
        else:
            (output,) = more
            jobs = [
                CtxSum(expand_full, n, (5, 6, 7, 8)), CtxSum(left_full, n, (10, 10, 10, 10)),
                FsdpSum(right_full.reshape(n, shard, -1), n, (1, 10), spread=False),
            ]
        attn_full, carry, attn_vec[l], *more = call(
            lambda jobs, *refs, base=8 * l: attention_back_kernel(jobs, heads, base, *refs),
            f"attention_back_{l}",
            [jax.ShapeDtypeStruct((dim, 4 * width), BF16), own_low if last else own, vec],
            scratch
            + [
                VMEM(every.shape, BF16),
                VMEM((count, 3 * width), BF16),
                VMEM((heads, count, LANES), F32),
                VMEM((heads, count, LANES), F32),
            ]
            + attn_scratch,
            4 + 6 * l, 4 * count * dim * 4 * width + 40 * heads * count * count * HD,
            [mixed, q, k, v, first, carry, resid, params, attn_pair], jobs,
        )
        if last:
            attn_grads[l + 1], expand_grads[l], left_part = more
        else:
            expand_part, left_part, right_part = more
            expand_shape = jax.ShapeDtypeStruct(expand_part.shape, BF16)

    ctx_job = CtxSum(attn_full, n, (0, 1, 2, 3), keep=True)
    attn_shape = jax.ShapeDtypeStruct((n, shard // 2, 4 * width), BF16)
    right_job = FsdpSum(right_full.reshape(n, shard, -1), n, (0, 1), spread=False)
    jobs = [
        ctx_job,
        FsdpSum(attn_shape, n, (0, 1), source=ctx_job),
        FsdpSum(left_part, n, (0, 1)),
        right_job,
        CtxAdd(right_part, 0, source=right_job),
        VectorSum([attn_vec[0], mlp_vec[0], attn_vec[1], mlp_vec[1]], n, (0, 1, 2, 3)),
        Exchange(carry),
        CtxAdd(right_part, 0),
    ]
    attn_grads[0], left_grads[0], _, right_grads[0], vectors, row_grad, right_grads[1] = call(
        leave_kernel, "leave", [], [], 5, 10**7, [], jobs
    )
    results = [
        jax.ShapeDtypeStruct(shape, F32)
        for shape in (
            (LAYERS, 3, shard, width), (LAYERS, width, shard), (LAYERS, shard, hidden),
            (LAYERS, hidden, shard), (6, LAYERS, shard), query_bias.shape, value_bias.shape,
            expand_bias.shape,
        )
    ]
    joint, out, expand, reduce, wide, query, value, hidden_bias = pl.pallas_call(
        finish_kernel,
        name="finish",
        out_shape=tuple(results),
        in_specs=[VMEM_SPEC] * 9,
        out_specs=tuple([VMEM_SPEC] * 8),
        compiler_params=pltpu.CompilerParams(vmem_limit_bytes=VMEM_LIMIT),
    )(*attn_grads, *expand_grads, *left_grads, *right_grads, vectors)
    return (
        output, row_grad, wide[0], wide[1], joint.transpose(0, 2, 1, 3), query, value, out,
        wide[2], wide[3], wide[4], expand, hidden_bias, reduce, wide[5],
    )


def solution(mesh):
    vector = P(None, "fsdp")
    by_head = P(None, "tp", "fsdp")
    rows = P("fsdp", ("ctx", "tp"), None)
    return jax.shard_map(
        local,
        mesh=mesh,
        in_specs=(
            rows, P("fsdp", None), vector, vector, P(None, "fsdp", None, "tp"), by_head, by_head,
            by_head, vector, vector, vector, P(None, "fsdp", "tp"), by_head, by_head, vector, rows,
        ),
        out_specs=(
            rows, rows, vector, vector, P(None, "fsdp", None, "tp"), by_head, by_head,
            by_head, vector, vector, vector, P(None, "fsdp", "tp"), by_head, by_head, vector,
        ),
        check_vma=False,
    )
```

```python
import functools
import math

import jax
import jax.numpy as jnp
from jax import lax
from jax.experimental import pallas as pl
from jax.experimental.pallas import tpu as pltpu
from jax.sharding import PartitionSpec as P

HD = 64
LAYERS = 2
LANES = 128
EPS = 1e-06
MASKED = -10000.0
SCALE = HD ** (-0.5)
VMEM_LIMIT = 62 * 1024 * 1024
F32 = jnp.float32
BF16 = jnp.bfloat16
VMEM = pltpu.VMEM
INV_SQRT2 = 1.0 / math.sqrt(2.0)
INV_SQRT_2PI = 1.0 / math.sqrt(2.0 * math.pi)


def mm(a, b):
    return lax.dot_general(a, b, (((1,), (0,)), ((), ())), preferred_element_type=F32)


def mm_nt(a, b):
    return lax.dot_general(a, b, (((1,), (1,)), ((), ())), preferred_element_type=F32)


def mm_tn(a, b):
    return lax.dot_general(a, b, (((0,), (0,)), ((), ())), preferred_element_type=F32)


def partners():
    t = lax.axis_index("tp")
    return t, t + 1 - 2 * (t % 2), (t + 2) % 4


def entry_barrier(jobs=(), tp=True):
    t, sib, peer = partners()
    others = [{"tp": sib}, {"tp": peer}] if tp or any(job.uses_tp for job in jobs) else []
    if any(job.uses_ctx for job in jobs):
        others.append({"ctx": 1 - lax.axis_index("ctx")})
    if any(job.uses_fsdp for job in jobs):
        n = lax.axis_size("fsdp")
        z = lax.axis_index("fsdp")
        others += [{"fsdp": (z + k) % n} for k in range(1, n)]
    barrier = pltpu.get_barrier_semaphore()
    for other in others:
        pl.semaphore_signal(barrier, inc=1, device_id=other, device_id_type=pl.DeviceIdType.MESH)
    pl.semaphore_wait(barrier, len(others))


def remote(src, dst, send, recv, device):
    return pltpu.make_async_remote_copy(
        src_ref=src,
        dst_ref=dst,
        send_sem=send,
        recv_sem=recv,
        device_id=device,
        device_id_type=pl.DeviceIdType.MESH,
    )


DMA = pltpu.SemaphoreType.DMA
HBM_SPEC = pl.BlockSpec(memory_space=pl.ANY)
VMEM_SPEC = pl.BlockSpec(memory_space=VMEM)


class Job:
    uses_tp = False
    uses_ctx = False
    uses_fsdp = False
    ins = ()
    outs = ()
    scratch = ()
    start_hook = None
    name = None

    def after(self, hook):
        self.start_hook = hook
        return self

    def bind(self, ins, outs, scratch):
        self.c = lax.axis_index("ctx")
        self.z = lax.axis_index("fsdp")
        self.refs(ins, outs, scratch)

    def start(self):
        pass

    def steps(self):
        return []

    def end(self):
        pass


def chunks_of(rows):
    return 2 if rows % 128 == 0 else 1


def cut_rows(ref, start, size):
    index = (slice(None),) * (len(ref.shape) - 2) + (pl.ds(start, size),)
    return ref.at[index]


class OverFsdp(Job):
    uses_fsdp = True

    def __init__(self, weight, layer, n, hook, chunks=1, ctx_hooks=None):
        self.n, self.layer, self.hook, self.ctx_hooks = n, layer, hook, ctx_hooks
        self.uses_ctx = ctx_hooks is not None
        shape = weight.shape[1:]
        self.rows = shape[-2] // 2
        self.ch = chunks if self.rows % (chunks * 16) == 0 else 1
        half = jax.ShapeDtypeStruct((n, *shape[:-2], self.rows, shape[-1]), BF16)
        self.ins = [(weight, HBM_SPEC)]
        self.outs = [(half, HBM_SPEC)] * (2 if self.uses_ctx else 1)
        self.scratch = [DMA((n + 1, self.ch)), DMA((n, self.ch)), DMA]
        if self.uses_ctx:
            self.scratch += [DMA((n, self.ch)), DMA((n, self.ch)), DMA]

    def refs(self, ins, outs, scratch):
        self.src = ins[0].at[self.layer]
        self.near = outs[0]
        self.send, self.recv, self.here = scratch[:3]
        if self.uses_ctx:
            self.far = outs[1]
            self.x_send, self.x_recv, self.here_far = scratch[3:]

    def mine(self, ch):
        size = self.rows // self.ch
        start = pl.multiple_of(self.c * self.rows + ch * size, size)
        return cut_rows(self.src, start, size)

    def part(self, ref, frm, ch):
        size = self.rows // self.ch
        return cut_rows(ref.at[frm], ch * size, size)

    def out_to(self, k, off, ch):
        to = (self.z + off + self.n) % self.n
        return remote(
            self.mine(ch), self.part(self.near, self.z, ch),
            self.send.at[k, ch], self.recv.at[self.z, ch], {"fsdp": to},
        )

    def arrived(self, frm, ch):
        block = self.part(self.near, frm, ch)
        return remote(
            block, block, self.send.at[self.n, ch], self.recv.at[frm, ch], {"fsdp": self.n - 1 - frm}
        )

    def over_x(self, frm, ch):
        return remote(
            self.part(self.near, frm, ch), self.part(self.far, frm, ch),
            self.x_send.at[frm, ch], self.x_recv.at[frm, ch], {"ctx": 1 - self.c},
        )

    def local(self, half, out, sem):
        start = pl.multiple_of(half * self.rows, self.rows)
        return pltpu.make_async_copy(
            cut_rows(self.src, start, self.rows), out.at[self.z], sem
        )

    def offsets(self):
        return (2, -2, 1, -1) if self.n == 4 else range(1, self.n)

    def sources(self):
        return (1, -1, 2, -2, 3, -3) if self.n == 4 else range(1, self.n)

    def inside(self, off):
        other = self.z + off
        return (other >= 0) & (other < self.n) if self.n == 4 else (other > -1)

    def relays(self):
        return (self.z == 1) | (self.z == 2)

    def start(self):
        for ch in range(self.ch):
            for k, off in enumerate(self.offsets()):
                @pl.when(self.inside(off))
                def _():
                    self.out_to(k, off, ch).start()
        self.local(self.c, self.near, self.here).start()
        if self.uses_ctx:
            self.local(1 - self.c, self.far, self.here_far).start()

    def relay(self):
        if self.n == 4:
            @pl.when(self.relays())
            def _():
                for ch in range(self.ch):
                    through = self.arrived(jnp.where(self.z == 2, 0, 3), ch)
                    through.wait_recv()
                    through.start()

    def take(self, off):
        frm = (self.z + off + self.n) % self.n

        @pl.when(self.inside(off))
        def _():
            for ch in range(self.ch):
                if self.n == 4 and abs(off) == 2:
                    @pl.when(jnp.logical_not((self.z == 2) & (frm == 0) | (self.z == 1) & (frm == 3)))
                    def _():
                        self.arrived(frm, ch).wait_recv()
                else:
                    self.arrived(frm, ch).wait_recv()
                if self.uses_ctx:
                    self.over_x(frm, ch).start()

    def steps(self):
        out = [(self.hook, self.relay)]
        if self.uses_ctx:
            for i, off in enumerate(self.sources()):
                out.append((self.ctx_hooks[min(i // 2, 2)], functools.partial(self.take, off)))
        return out

    def end(self):
        for off in self.sources():
            frm = (self.z + off + self.n) % self.n
            if not self.uses_ctx:
                self.take(off)
            else:
                @pl.when(self.inside(off))
                def _():
                    for ch in range(self.ch):
                        self.over_x(frm, ch).wait()
        for ch in range(self.ch):
            for k, off in enumerate(self.offsets()):
                @pl.when(self.inside(off))
                def _():
                    self.out_to(k, off, ch).wait_send()
            if self.n == 4:
                @pl.when(self.relays())
                def _():
                    self.arrived(jnp.where(self.z == 2, 0, 3), ch).wait_send()
        self.local(self.c, self.near, self.here).wait()
        if self.uses_ctx:
            self.local(1 - self.c, self.far, self.here_far).wait()


class OverCtx(Job):
    uses_ctx = True

    def __init__(self, weight, layer, near, n):
        self.n, self.layer = n, layer
        self.ins = [(weight, HBM_SPEC), (near, HBM_SPEC)]
        self.outs = [(jax.ShapeDtypeStruct(near.shape, BF16), HBM_SPEC)]
        self.scratch = [DMA((n,)), DMA((n,)), DMA]

    def refs(self, ins, outs, scratch):
        self.src, self.near = ins[0].at[self.layer], ins[1]
        (self.far,) = outs
        self.send, self.recv, self.here = scratch

    def copy(self, k):
        frm = (self.z + k) % self.n
        return remote(
            self.near.at[frm], self.far.at[frm], self.send.at[k], self.recv.at[k],
            {"ctx": 1 - self.c},
        )

    def local(self):
        rows = self.near.shape[-2]
        start = pl.multiple_of((1 - self.c) * rows, rows)
        return pltpu.make_async_copy(cut_rows(self.src, start, rows), self.far.at[self.z], self.here)

    def start(self):
        for k in range(1, self.n):
            self.copy(k).start()
        self.local().start()

    def end(self):
        for k in range(1, self.n):
            self.copy(k).wait()
        self.local().wait()


class Loads:
    def __init__(self, sems):
        self.sems, self.copies = sems, []

    def add(self, near, far, out):
        c = lax.axis_index("ctx")
        for half, ref in ((c, near), (1 - c, far)):
            if len(ref.shape) == 3:
                pairs = [(ref, out.at[:, half])]
            else:
                width = ref.shape[-1]
                pairs = [
                    (ref.at[:, j], out.at[:, half, :, j * width : (j + 1) * width])
                    for j in range(ref.shape[1])
                ]
            for src, dst in pairs:
                copy = pltpu.make_async_copy(src, dst, self.sems.at[len(self.copies)])
                copy.start()
                self.copies.append(copy)

    def wait(self):
        for copy in self.copies:
            copy.wait()


class ParamJob(Job):
    uses_fsdp = True

    def __init__(self, wide, narrow, n, dim):
        self.n, self.n_wide = n, len(wide)
        self.ins = [(a, VMEM_SPEC) for a in (*wide, *narrow)]
        shape = (8 * LAYERS, dim)
        self.outs = [(jax.ShapeDtypeStruct(shape, F32), VMEM_SPEC)]
        self.scratch = [
            VMEM(shape, F32), VMEM(shape, BF16), VMEM((n, *shape), BF16), DMA((n,)), DMA((n,))
        ]

    def refs(self, ins, outs, scratch):
        self.wide, self.narrow = ins[: self.n_wide], ins[self.n_wide :]
        (self.out,) = outs
        self.work, self.src, self.got, self.ssem, self.rsem = scratch

    def copy(self, k):
        return remote(
            self.src, self.got.at[k], self.ssem.at[k], self.rsem.at[k],
            {"fsdp": (self.z + k) % self.n},
        )

    def start(self):
        work = self.work
        dim = work.shape[1]
        work[...] = jnp.zeros_like(work)
        shard = self.wide[0].shape[1]
        query, value, expand = self.narrow
        cut = query.shape[2]
        heads = query.shape[1]
        for l in range(LAYERS):
            for k, ref in enumerate(self.wide):
                work[8 * l + k : 8 * l + k + 1, :shard] = ref[l : l + 1, :].astype(F32)
            for row, base, ref in ((6, 0, query), (6, heads * HD, value), (7, 0, expand)):
                block = ref[l].astype(F32)
                for h in range(ref.shape[1]):
                    at = base + h * HD
                    work[8 * l + row : 8 * l + row + 1, at : at + cut] = block[h : h + 1, :]
        all_rows = work[...]
        row = lax.broadcasted_iota(jnp.int32, all_rows.shape, 0) % 8
        by_shard = pltpu.roll(all_rows, self.z * shard, 1)
        by_cut = pltpu.roll(all_rows, self.z * cut, 1)
        placed = jnp.where(row < 6, by_shard, by_cut)
        work[...] = placed
        self.src[...] = placed.astype(BF16)
        for k in range(1, self.n):
            self.copy(k).start()

    def finish(self):
        total = self.work[...]
        for k in range(1, self.n):
            self.copy(k).wait_recv()
            total += self.got[k].astype(F32)
        self.out[...] = total

    def end(self):
        for k in range(1, self.n):
            self.copy(k).wait_send()


class Exchange(Job):
    uses_ctx = True

    def __init__(self, both):
        self.ins = [(both, VMEM_SPEC)]
        self.outs = [(jax.ShapeDtypeStruct(both.shape, both.dtype), VMEM_SPEC)]
        self.scratch = [DMA, DMA]

    def refs(self, ins, outs, scratch):
        (self.src,), (self.out,), (self.ssem, self.rsem) = ins, outs, scratch

    def copy(self):
        c = self.c
        return remote(self.src.at[1 - c], self.out.at[c], self.ssem, self.rsem, {"ctx": 1 - c})

    def start(self):
        self.copy().start()
        self.out[self.c] = self.src[self.c]

    def end(self):
        self.copy().wait()


class CtxSum(Job):
    uses_ctx = True

    def __init__(self, full, n, hooks, keep=False, name=None):
        self.n, self.hooks, self.name = n, hooks, name
        shape = (n, full.shape[0] // (2 * n), full.shape[1])
        self.ins = [] if name else [(full.reshape(n, 2, *shape[1:]), HBM_SPEC)]
        self.keep = keep
        self.outs = [] if keep else [(jax.ShapeDtypeStruct(shape, BF16), VMEM_SPEC)]
        self.scratch = [VMEM(shape, BF16), DMA((n,)), DMA((n,)), DMA((n,))]
        if keep:
            self.scratch.append(VMEM(shape, BF16))

    def refs(self, ins, outs, scratch):
        if not self.name:
            (self.full,) = ins
        self.got, self.ssem, self.rsem, self.near = scratch[:4]
        self.out = scratch[4] if self.keep else outs[0]

    def attach(self, ref):
        self.full = ref.reshape(self.n, 2, ref.shape[0] // (2 * self.n), ref.shape[1])

    def order(self):
        return (0, 3, 1, 2) if self.n == 4 else range(self.n)

    def copy(self, k):
        return remote(
            self.full.at[k, 1 - self.c], self.got.at[k], self.ssem.at[k], self.rsem.at[k],
            {"ctx": 1 - self.c},
        )

    def load(self, k):
        return pltpu.make_async_copy(self.full.at[k, self.c], self.out.at[k], self.near.at[k])

    def start(self):
        for k in self.order():
            self.copy(k).start()
        for k in self.order():
            if not self.name:
                self.load(k).start()

    def add(self, k):
        if not self.name:
            self.load(k).wait()
        self.copy(k).wait_recv()
        mine = self.full[k, self.c] if self.name else self.out[k]
        self.out[k] = (mine.astype(F32) + self.got[k].astype(F32)).astype(BF16)

    def steps(self):
        per = -(-self.n // len(self.hooks))
        return [
            (self.hooks[i // per], functools.partial(self.add, k))
            for i, k in enumerate(self.order())
        ]

    def end(self):
        for k in range(self.n):
            self.copy(k).wait_send()


class FsdpSum(Job):
    uses_fsdp = True

    def __init__(self, rows, n, hooks, source=None, sends=(), spread=True, direct=False, name=None):
        self.name = name
        self.n, self.hooks, self.source, self.sends = n, hooks, source, sends
        self.relays = n == 4 and not direct
        self.spread = self.uses_ctx = spread
        shape = rows.shape
        self.ins = [] if source or name else [(rows, VMEM_SPEC)]
        result = (2, *shape[1:]) if spread else shape[1:]
        self.outs = [(jax.ShapeDtypeStruct(result, BF16), VMEM_SPEC)]
        self.rows = shape[1]
        self.ch = chunks_of(self.rows)
        self.scratch = [
            VMEM(shape, BF16), VMEM((2, *shape[1:]), BF16),
            DMA((n, self.ch)), DMA((n, self.ch)), DMA((2, self.ch)), DMA((2, self.ch)),
            DMA((self.ch,)), DMA((self.ch,)),
        ]

    def refs(self, ins, outs, scratch):
        if not self.name:
            self.src = self.source.out if self.source else ins[0]
        (self.out,) = outs
        (self.got, self.via, self.ssem, self.rsem, self.via_send, self.via_recv, self.x_send,
         self.x_recv) = scratch

    def attach(self, ref):
        self.src = ref.reshape(self.n, self.rows, ref.shape[1])

    def cut(self, ref, ch):
        size = self.rows // self.ch
        return ref.at[pl.ds(ch * size, size)]

    def direct(self, d, ch):
        return remote(
            self.cut(self.src.at[d], ch), self.cut(self.got.at[self.z], ch),
            self.ssem.at[d, ch], self.rsem.at[self.z, ch], {"fsdp": d},
        )

    def landed(self, frm, ch):
        block = self.cut(self.got.at[frm], ch)
        return remote(block, block, self.ssem.at[frm, ch], self.rsem.at[frm, ch], {"fsdp": frm})

    def to_relay(self, d, ch):
        return remote(
            self.cut(self.src.at[d], ch), self.cut(self.via.at[0], ch),
            self.via_send.at[0, ch], self.via_recv.at[0, ch], {"fsdp": 2 if d == 0 else 1},
        )

    def relayed(self, d, ch):
        return remote(
            self.cut(self.via.at[1], ch), self.cut(self.got.at[self.z], ch),
            self.via_send.at[1, ch], self.rsem.at[self.z, ch], {"fsdp": d},
        )

    def directly(self, d):
        if self.relays and d in (0, 3):
            return (self.z == 1) if d == 0 else (self.z == 2)
        return self.z != d

    def send(self, d):
        if self.relays and d in (0, 3):
            @pl.when(self.z == 3 - d)
            def _():
                for ch in range(self.ch):
                    self.to_relay(d, ch).start()

        @pl.when(self.directly(d))
        def _():
            for ch in range(self.ch):
                self.direct(d, ch).start()

    def order(self):
        return (0, 3, 1, 2) if self.n == 4 else range(self.n)

    def start(self):
        if not self.source:
            for d in self.order():
                self.send(d)

    def relay(self):
        for d, me in ((0, 2), (3, 1)) if self.relays else ():
            @pl.when(self.z == me)
            def _():
                for ch in range(self.ch):
                    self.to_relay(d, ch).wait_recv()
                    mine = self.cut(self.src.at[d], ch)[...].astype(F32)
                    theirs = self.cut(self.via.at[0], ch)[...].astype(F32)
                    self.cut(self.via.at[1], ch)[...] = (mine + theirs).astype(BF16)
                    self.relayed(d, ch).start()

    then = None

    def result(self, ch):
        return self.cut(self.out.at[self.c] if self.spread else self.out, ch)

    def over_x(self, ch):
        block = self.result(ch)
        return remote(block, block, self.x_send.at[ch], self.x_recv.at[ch], {"ctx": 1 - self.c})

    def total(self):
        n = self.n
        for ch in range(self.ch):
            mine = self.cut(self.src.at[self.z], ch)
            if self.relays:
                near = (self.z + 1) % 4
                last = jnp.where(self.z == 0, 2, jnp.where(self.z == 3, 1, (self.z + 3) % 4))
                first = jnp.where(self.z == 3, 2, near)
                inner = (self.z == 1) | (self.z == 2)
                self.landed(first, ch).wait_recv()
                self.landed(last, ch).wait_recv()
                part = (
                    mine[...].astype(F32)
                    + self.cut(self.got.at[first], ch)[...].astype(F32)
                    + self.cut(self.got.at[last], ch)[...].astype(F32)
                )
                block = self.result(ch)

                @pl.when(inner)
                def _():
                    middle = (self.z + 2) % 4
                    self.landed(middle, ch).wait_recv()
                    block[...] = (part + self.cut(self.got.at[middle], ch)[...].astype(F32)).astype(BF16)

                @pl.when(jnp.logical_not(inner))
                def _():
                    block[...] = part.astype(BF16)
            else:
                part = mine[...].astype(F32)
                for k in range(1, n):
                    frm = (self.z + k) % n
                    self.landed(frm, ch).wait_recv()
                    part += self.cut(self.got.at[frm], ch)[...].astype(F32)
                self.result(ch)[...] = part.astype(BF16)
            if self.spread:
                self.over_x(ch).start()
            elif self.then is not None:
                self.then(ch)

    def steps(self):
        out = [
            (self.sends[i * len(self.sends) // self.n], functools.partial(self.send, d))
            for i, d in enumerate(self.order())
            if self.sends
        ]
        return out + [(self.hooks[0], self.relay), (self.hooks[1], self.total)]

    def end(self):
        for ch in range(self.ch):
            if self.spread:
                other = self.cut(self.out.at[1 - self.c], ch)
                remote(
                    other, other, self.x_send.at[ch], self.x_recv.at[ch], {"ctx": 1 - self.c}
                ).wait_recv()
                self.over_x(ch).wait_send()
            for d in range(self.n):
                if self.relays and d in (0, 3):
                    @pl.when(self.z == 3 - d)
                    def _():
                        self.to_relay(d, ch).wait_send()

                    @pl.when(self.z == (2 if d == 0 else 1))
                    def _():
                        self.relayed(d, ch).wait_send()

                @pl.when(self.directly(d))
                def _():
                    self.direct(d, ch).wait_send()


class CtxAdd(Job):
    uses_ctx = True

    def __init__(self, rows, hook, source=None):
        self.hook, self.source = hook, source
        self.ins = [] if source else [(rows, VMEM_SPEC)]
        self.outs = [(jax.ShapeDtypeStruct(rows.shape, BF16), VMEM_SPEC)]
        self.rows = rows.shape[0]
        self.ch = chunks_of(self.rows)
        self.scratch = [VMEM(rows.shape, BF16), DMA((self.ch,)), DMA((self.ch,))]

    def refs(self, ins, outs, scratch):
        self.src = self.source.out if self.source else ins[0]
        (self.out,) = outs
        self.got, self.ssem, self.rsem = scratch
        if self.source:
            self.source.then = self.send

    def cut(self, ref, ch):
        size = self.rows // self.ch
        return ref.at[pl.ds(ch * size, size)]

    def copy(self, ch):
        return remote(
            self.cut(self.src, ch), self.cut(self.got, ch), self.ssem.at[ch], self.rsem.at[ch],
            {"ctx": 1 - self.c},
        )

    def send(self, ch):
        self.copy(ch).start()

    def start(self):
        if not self.source:
            for ch in range(self.ch):
                self.send(ch)

    def add(self):
        for ch in range(self.ch):
            self.copy(ch).wait_recv()
            mine, theirs = self.cut(self.src, ch)[...], self.cut(self.got, ch)[...]
            self.cut(self.out, ch)[...] = (mine.astype(F32) + theirs.astype(F32)).astype(BF16)

    def steps(self):
        return [(self.hook, self.add)]

    def end(self):
        for ch in range(self.ch):
            self.copy(ch).wait_send()


class Background:
    def __init__(self, jobs):
        self.jobs = jobs
        self.todo = []
        for job in jobs:
            if job.start_hook is not None:
                self.todo.append((job.start_hook, job.start))
            self.todo += job.steps()
        self.ended = []

    def start(self):
        for job in self.jobs:
            if job.start_hook is None:
                job.start()

    def at(self, hook):
        for when, function in self.todo:
            if when == hook:
                function()

    def phase(self, tag):
        return Phase(self, tag)

    def end(self, jobs=None):
        for job in self.jobs if jobs is None else jobs:
            if job not in self.ended:
                self.ended.append(job)
                job.end()


class Phase:
    def __init__(self, whole, tag):
        self.whole, self.tag = whole, tag

    def at(self, hook):
        self.whole.at((self.tag, hook))

    def loop(self, b, count=4, base=0):
        for k in range(count):
            if any(when == (self.tag, base + k) for when, _ in self.whole.todo):
                @pl.when(b == k)
                def _():
                    self.at(base + k)


class Links:
    def __init__(self, send, recv, sib, peer):
        self.send, self.recv, self.sib, self.peer = send, recv, sib, peer

    def make(self, kind, s, src, dst, other):
        return pltpu.make_async_remote_copy(
            src_ref=src,
            dst_ref=dst,
            send_sem=self.send.at[kind, s],
            recv_sem=self.recv.at[kind, s],
            device_id={"tp": other},
            device_id_type=pl.DeviceIdType.MESH,
        )


def statistics(rows):
    mean = jnp.mean(rows, axis=-1, keepdims=True)
    centred = rows - mean
    inverse = lax.rsqrt(jnp.mean(centred * centred, axis=-1, keepdims=True) + EPS)
    return centred * inverse, inverse


def norm_back(rows, d_out, gain):
    unit, inverse = statistics(rows)
    e = d_out * gain
    back = inverse * (
        e
        - jnp.mean(e, axis=-1, keepdims=True)
        - unit * jnp.mean(e * unit, axis=-1, keepdims=True)
    )
    d_gain = jnp.sum(d_out * unit, axis=0, keepdims=True)
    d_shift = jnp.sum(d_out, axis=0, keepdims=True)
    return back, d_gain, d_shift


def rows_of(ref, b):
    block = ref[b]
    return block.reshape(block.shape[0] * block.shape[1], block.shape[2])


class Gather:
    def __init__(self, links, out):
        self.links, self.out = links, out

    def near(self, s):
        return self.links.make(3, s, self.out.at[2 + s, 0], self.out.at[2 + s, 1], self.links.sib)

    def across(self, s):
        return self.links.make(4, s, self.out.at[2 + s, 0], self.out.at[s, 0], self.links.peer)

    def onward(self, s):
        return self.links.make(5, s, self.out.at[s, 0], self.out.at[s, 1], self.links.sib)

    def start(self, rows):
        for s in range(2):
            self.out[2 + s, 0] = rows(s)
            self.near(s).start()
            self.across(s).start()

    def need(self, b):
        s = b % 2

        @pl.when(b >= 2)
        def _():
            self.near(s).wait_recv()

        @pl.when(b < 2)
        def _():
            self.across(s).wait_recv()
            self.onward(s).start()
            self.onward(s).wait_recv()

    def end(self):
        for s in range(2):
            for copy in (self.near(s), self.across(s), self.onward(s)):
                copy.wait_send()


class Scatter:
    def __init__(self, links, part, sent, got, own):
        self.links, self.part, self.sent, self.got, self.own = links, part, sent, got, own

    def copy(self, kind, s):
        other = self.links.peer if kind == 1 else self.links.sib
        return self.links.make(kind, s, self.sent.at[kind, s], self.got.at[kind, s], other)

    def block(self, b):
        s = b % 2
        half = self.part.shape[0] // 2

        @pl.when(b < 2)
        def _():
            self.sent[0, s] = self.part[half:].astype(BF16)
            first = self.copy(0, s)
            first.start()
            first.wait_recv()
            self.sent[1, s] = (self.part[:half] + self.got[0, s].astype(F32)).astype(BF16)
            self.copy(1, s).start()

        @pl.when(b >= 2)
        def _():
            self.sent[2, s] = self.part[half:].astype(BF16)
            self.copy(2, s).start()
            self.own[s] = self.part[:half]

    def total(self, s):
        self.copy(2, s).wait_recv()
        self.copy(1, s).wait_recv()
        return self.own[s] + self.got[2, s].astype(F32) + self.got[1, s].astype(F32)

    def end(self):
        for s in range(2):
            for kind in range(3):
                self.copy(kind, s).wait_send()


def scatter_scratch(half, width):
    local = [VMEM((2 * half, width), F32), VMEM((2, half, width), F32)]
    linked = [
        VMEM((3, 2, half, width), BF16), VMEM((3, 2, half, width), BF16), DMA((6, 2)), DMA((6, 2))
    ]
    return local + linked + linked


def scatter_refs(scratch, phase):
    part, own = scratch[:2]
    sent, got, send, recv = scratch[2 + 4 * phase : 6 + 4 * phase]
    return part, sent, got, own, send, recv


def enter_kernel(jobs, refs):
    first = refs[1][0]
    params, tokens, attn, expand = jobs
    entry_barrier(jobs, False)
    tokens.start()
    params.start()
    attn.start()
    params.finish()
    attn.relay()
    expand.start()
    tokens.end()
    for s in range(2):
        unit, _ = statistics(tokens.out[s].astype(F32))
        first[s] = (unit * params.out[0:1, :] + params.out[1:2, :]).astype(BF16)
    for off in attn.sources()[:4]:
        attn.take(off)
    expand.relay()
    for off in attn.sources()[4:]:
        attn.take(off)
    for job in (params, attn, expand):
        job.end()


def pair_tile(pair, h):
    tile = pair if h % 2 == 0 else pltpu.roll(pair, HD, 1)
    return tile


def attention_phase(
    background, heads, base,
    own_first, params, key_extra, resid, near, far,
    first, second, middle, q_out, k_out, v_out, mixed_out,
    part, sent, got, own, send, recv, weight, load,
):
    t, sib, peer = partners()
    links = Links(send, recv, sib, peer)
    scatter = Scatter(links, part, sent, got, own)
    width = heads * HD
    gather = Gather(links, first)
    gather.start(lambda s: own_first[s])
    loads = Loads(load)
    loads.add(near, far, weight)
    loads.wait()
    weight = whole(weight)
    out_bias, gain, shift = (params[base + k : base + k + 1, :] for k in (2, 3, 4))
    q_bias = params[base + 6 : base + 7, :width]
    v_bias = params[base + 6 : base + 7, width : 2 * width]
    half = first.shape[2]
    rows = 2 * half
    lane = lax.broadcasted_iota(jnp.int32, (rows, LANES), 1)
    head_lane = lane < HD
    q_extra = jnp.where(lane < HD + 2, 1.0, 0.0).astype(BF16)
    v_extra = jnp.where(lane < HD + 3, 1.0, 0.0).astype(BF16)

    def project(j, carry):
        b = (j + 2) % 4
        gather.need(b)
        x = rows_of(first, b)
        y = mm(x, weight[:, : 3 * width])
        q = ((y[:, :width] + q_bias).astype(BF16) * SCALE).astype(BF16)
        k = y[:, width : 2 * width].astype(BF16)
        v = (y[:, 2 * width :] + v_bias).astype(BF16)
        g, s = b // 2, b % 2
        mine = jnp.where(g == 1, t, peer)
        other = mine + 1 - 2 * (mine % 2)
        extra = jnp.concatenate([key_extra[mine, s], key_extra[other, s]], axis=0)
        at = pl.ds(pl.multiple_of(b * rows, rows), rows)
        for h in range(heads):
            cut = slice(LANES * (h // 2), LANES * (h // 2 + 1))
            q_out[h, at, :] = jnp.where(head_lane, pair_tile(q[:, cut], h), q_extra)
            k_out[h, at, :] = jnp.where(head_lane, pair_tile(k[:, cut], h), extra)
            v_out[h, at, :] = jnp.where(head_lane, pair_tile(v[:, cut], h), v_extra)
        background.loop(j, 4, 20)
        return carry

    lax.fori_loop(0, 4, project, 0)
    background.at(0)

    def attend(b, carry):
        at = pl.ds(pl.multiple_of(b * rows, rows), rows)
        outs = []
        for h in range(heads):
            q = q_out[h, at, :]
            scores = mm_nt(q, k_out[h])
            top = jnp.max(scores, axis=-1, keepdims=True)
            weights = jnp.exp(scores - top).astype(BF16)
            summed = mm(weights, v_out[h])
            total = summed[:, HD : HD + 1]
            outs.append(summed / total)
            log_total = -(top + jnp.log(total))
            high = log_total.astype(BF16).astype(F32)
            rest = log_total - high
            mid = rest.astype(BF16).astype(F32)
            low = rest - mid
            tail = jnp.where(lane == HD + 2, high, jnp.where(lane == HD + 3, mid, low))
            q_out[h, at, :] = jnp.where(
                (lane >= HD + 2) & (lane < HD + 5), tail.astype(BF16), q
            )
        tiles = [
            jnp.where(head_lane, outs[h], pltpu.roll(outs[h + 1], HD, 1))
            for h in range(0, heads, 2)
        ]
        mixed = jnp.concatenate(tiles, axis=1).astype(BF16)
        mixed_out[at, :] = mixed
        part[...] = mm_nt(mixed, weight[:, 3 * width :])
        scatter.block(b)
        background.loop(b, 4, 1)
        return carry

    lax.fori_loop(0, 4, attend, 0)
    for s in range(2):
        mid = resid[s].astype(F32) + (scatter.total(s) + out_bias)
        middle[s] = mid
        unit, _ = statistics(mid)
        second[s] = (unit * gain + shift).astype(BF16)
        background.at(5 + s)
    gather.end()
    scatter.end()


def mlp_phase(
    background, last, base,
    own_second, params, middle, near_e, far_e, near_r, far_r,
    second, active_out, slope_out, resid, nxt,
    part, sent, got, own, send, recv, expand, reduce, load,
):
    t, sib, peer = partners()
    links = Links(send, recv, sib, peer)
    scatter = Scatter(links, part, sent, got, own)
    half = second.shape[2]
    rows = 2 * half
    gather = Gather(links, second)
    gather.start(lambda s: own_second[s])
    loads = Loads(load)
    loads.add(near_e, far_e, expand)
    loads.add(near_r, far_r, reduce)
    loads.wait()
    expand, reduce = whole(expand), whole(reduce)
    hidden = expand.shape[1]
    out_bias = params[base + 5 : base + 6, :]
    following = 0 if last else base + 8
    gain, shift = (params[following + k : following + k + 1, :] for k in (0, 1))
    step = 256

    def block(j, carry):
        b = (j + 2) % 4
        gather.need(b)
        at = pl.ds(pl.multiple_of(b * rows, rows), rows)
        x = rows_of(second, b)
        for n in range(0, hidden, step):
            before = mm(x, expand[:, n : n + step]) + params[base + 7 : base + 8, n : n + step]
            cdf = 0.5 * (1.0 + lax.erf(before * INV_SQRT2))
            active_out[at, n : n + step] = (before * cdf).astype(BF16)
            slope = cdf + before * (jnp.exp(before * before * -0.5) * INV_SQRT_2PI)
            slope_out[at, n : n + step] = slope.astype(BF16)
        part[...] = mm_nt(active_out[at, :], reduce[...])
        scatter.block(b)
        background.loop(j, 4, 1)
        return carry

    lax.fori_loop(0, 4, block, 0)
    for s in range(2):
        res = middle[s] + (scatter.total(s) + out_bias)
        if last:
            nxt[s] = res.astype(BF16)
        else:
            resid[s] = res
            unit, _ = statistics(res)
            nxt[s] = (unit * gain + shift).astype(BF16)
        background.at(5 + s)
    gather.end()
    scatter.end()


def token_product(left, right, outs, offset=0):
    depth = left.shape[-1]
    total = left.shape[0] * left.shape[1] * left.shape[2]
    step = 256

    def body(j, carry):
        cut = pl.ds(pl.multiple_of(j * step, step), step)
        x = left[:, :, :, cut].reshape(total, step)
        product = mm_tn(x, right[...]).astype(BF16)
        width = right.shape[-1] // len(outs)
        for k, out in enumerate(outs):
            out[cut, offset : offset + width] = product[:, k * width : (k + 1) * width]
        return carry

    lax.fori_loop(0, depth // step, body, 0)


def mlp_back_phase(
    background, base,
    active, slope, second, middle, carry_in, params, near_e, far_e, near_r, far_r,
    expand_grad, reduce_left, reduce_right, carry_out, vectors,
    part, sent, got, own, send, recv, grad, d_before, expand, reduce, load,
):
    t, sib, peer = partners()
    links = Links(send, recv, sib, peer)
    scatter = Scatter(links, part, sent, got, own)
    gather = Gather(links, grad)
    gather.start(lambda s: carry_in[s].astype(BF16))
    loads = Loads(load)
    loads.add(near_e, far_e, expand)
    loads.add(near_r, far_r, reduce)
    loads.wait()
    expand, reduce = whole(expand), whole(reduce)
    gain = params[base + 3 : base + 4, :]
    half = grad.shape[2]
    rows = 2 * half
    hidden = active.shape[1]
    step = 256
    vectors[...] = jnp.zeros_like(vectors)

    def block(j, carry):
        b = (j + 2) % 4
        gather.need(b)
        at = pl.ds(pl.multiple_of(b * rows, rows), rows)
        x = rows_of(grad, b)
        for n in range(0, hidden, step):
            d_act = mm(x, reduce[:, n : n + step])
            d_bef = (d_act * slope[at, n : n + step].astype(F32)).astype(BF16)
            d_before[at, n : n + step] = d_bef
            vectors[4:5, n : n + step] += jnp.sum(d_bef.astype(F32), axis=0, keepdims=True)
        part[...] = mm_nt(d_before[at, :], expand[...])
        scatter.block(b)
        background.loop(j)
        return carry

    lax.fori_loop(0, 4, block, 0)
    token_product(grad, active, (reduce_left, reduce_right))
    background.at(4)

    def finish(s):
        back, d_gain, d_shift = norm_back(middle[s], scatter.total(s), gain)
        carry = carry_in[s].astype(F32)
        mid = carry + back
        carry_out[s] = mid
        low = mid.astype(BF16)
        vectors[0:1, :] += d_gain
        vectors[1:2, :] += d_shift
        vectors[2:3, :] += jnp.sum(low.astype(F32), axis=0, keepdims=True)
        vectors[3:4, :] += jnp.sum(carry.astype(BF16).astype(F32), axis=0, keepdims=True)

    finish(0)
    background.at(5)
    token_product(second, d_before, (expand_grad,))
    finish(1)
    background.at(6)
    gather.end()
    scatter.end()


def attention_back_phase(
    background, heads, base,
    mixed, q_in, k_in, v_in, first, carry_in, resid, params, near, far,
    carry_out, vectors,
    part, sent, got, own, send, recv, grad, d_joint, d_key, d_value, weight, load,
):
    t, sib, peer = partners()
    links = Links(send, recv, sib, peer)
    scatter = Scatter(links, part, sent, got, own)
    width = heads * HD
    gather = Gather(links, grad)
    gather.start(lambda s: carry_in[s].astype(BF16))
    loads = Loads(load)
    loads.add(near, far, weight)
    loads.wait()
    weight = whole(weight)
    gain = params[base : base + 1, :]
    half = grad.shape[2]
    rows = 2 * half
    lane = lax.broadcasted_iota(jnp.int32, (rows, LANES), 1)
    head_lane = lane < HD
    vectors[...] = jnp.zeros_like(vectors)
    d_key[...] = jnp.zeros_like(d_key)
    d_value[...] = jnp.zeros_like(d_value)

    def pairs(tiles):
        return jnp.concatenate(
            [
                jnp.where(head_lane, tiles[h], pltpu.roll(tiles[h + 1], HD, 1))
                for h in range(0, heads, 2)
            ],
            axis=1,
        )

    def attend(j, carry):
        b = (j + 2) % 4
        gather.need(b)
        at = pl.ds(pl.multiple_of(b * rows, rows), rows)
        d_mixed = mm(rows_of(grad, b), weight[:, 3 * width :]).astype(BF16)
        product = d_mixed.astype(F32) * mixed[at, :].astype(F32)
        d_queries = []
        for h in range(heads):
            cut = slice(LANES * (h // 2), LANES * (h // 2 + 1))
            keep = head_lane if h % 2 == 0 else lane >= HD
            delta = -jnp.sum(jnp.where(keep, product[:, cut], 0.0), axis=-1, keepdims=True)
            high = delta.astype(BF16).astype(F32)
            rest = delta - high
            mid = rest.astype(BF16).astype(F32)
            low = rest - mid
            tail = jnp.where(
                lane == HD,
                high,
                jnp.where(lane == HD + 1, mid, jnp.where(lane == HD + 2, low, 0.0)),
            ).astype(BF16)
            d_o = jnp.where(head_lane, pair_tile(d_mixed[:, cut], h), tail)
            q = q_in[h, at, :]
            probs = jnp.exp(mm_nt(k_in[h], q))
            d_value[h] += mm(probs.astype(BF16), d_o)
            d_raw = (probs * mm_nt(v_in[h], d_o)).astype(BF16)
            d_key[h] += mm(d_raw, q)
            d_queries.append(mm_tn(d_raw, k_in[h]) * SCALE)
        d_joint[at, :width] = pairs(d_queries).astype(BF16)
        background.loop(j)
        return carry

    lax.fori_loop(0, 4, attend, 0)

    def project(b, carry):
        at = pl.ds(pl.multiple_of(b * rows, rows), rows)
        d_joint[at, width : 2 * width] = pairs([d_key[h, at, :] for h in range(heads)]).astype(BF16)
        d_joint[at, 2 * width :] = pairs([d_value[h, at, :] for h in range(heads)]).astype(BF16)
        d_rows = d_joint[at, :]
        sums = jnp.sum(d_rows.astype(F32), axis=0, keepdims=True)
        vectors[2:3, :width] += sums[:, :width]
        vectors[2:3, width : 2 * width] += sums[:, 2 * width :]
        part[...] = mm_nt(d_rows, weight[:, : 3 * width])
        scatter.block(b)
        background.loop(b, 4, 4)
        return carry

    lax.fori_loop(0, 4, project, 0)
    token_product(grad, mixed, (weight,), 3 * width)
    background.at(8)

    def finish(s):
        back, d_gain, d_shift = norm_back(resid[s].astype(F32), scatter.total(s), gain)
        carry = carry_in[s] + back
        carry_out[s] = carry.astype(carry_out.dtype)
        vectors[0:1, :] += d_gain
        vectors[1:2, :] += d_shift

    finish(0)
    background.at(9)
    token_product(first, d_joint, (weight,))
    finish(1)
    background.at(10)
    gather.end()
    scatter.end()


def forward_kernel(jobs, urgent, heads, last, base, refs):
    ins, outs, scratch = refs
    own_first, params, key_extra, resid, near_a, far_a, *near = ins
    first, own_rows, middle, q, k, v, mixed, second, active, slope, out, rows = outs
    attn_w, attn_load, expand, reduce, mlp_load = scratch[10:]
    background = Background(jobs)
    entry_barrier(jobs)
    background.start()
    attention_phase(
        background.phase("A"), heads, base,
        own_first, params, key_extra, resid, near_a, far_a,
        first, own_rows, middle, q, k, v, mixed, *scatter_refs(scratch, 0), attn_w, attn_load,
    )
    background.end(urgent)
    near_e = near[0]
    near_r = near[1] if len(near) > 1 else urgent[1].near
    mlp_phase(
        background.phase("M"), last, base,
        own_rows, params, middle, near_e, urgent[0].far, near_r, urgent[1].far,
        second, active, slope, out, rows, *scatter_refs(scratch, 1), expand, reduce, mlp_load,
    )
    background.end()


def backward_kernel(jobs, heads, base, refs):
    ins, outs, scratch = refs
    (active, slope, second, middle, carry_in, params, mixed, q, k, v, first, resid,
     near_e, far_e, near_r, far_r, near_a, far_a) = ins
    attn_grad, carry_out, mlp_vec, attn_vec = outs
    (left_grad, right_grad, carry_mid, grad_rows, attn_rows, d_before, expand, reduce,
     mlp_load, d_joint, d_key, d_value, attn_w, attn_load) = scratch[10:]
    expand_grad = whole(expand)
    named = dict(expand=expand_grad, left=left_grad, right=right_grad)
    for job in jobs:
        if job.name:
            job.attach(named[job.name])
    background = Background(jobs)
    entry_barrier(jobs)
    background.start()
    mlp_back_phase(
        background.phase("M"), base,
        active, slope, second, middle, carry_in, params, near_e, far_e, near_r, far_r,
        expand_grad, left_grad, right_grad, carry_mid, mlp_vec,
        *scatter_refs(scratch, 0), grad_rows, d_before, expand, reduce, mlp_load,
    )
    attention_back_phase(
        background.phase("A"), heads, base,
        mixed, q, k, v, first, carry_mid, resid, params, near_a, far_a,
        carry_out, attn_vec,
        *scatter_refs(scratch, 1), attn_rows, d_joint, d_key, d_value, attn_w, attn_load,
    )
    copy = pltpu.make_async_copy(whole(attn_w), attn_grad, attn_load.at[0])
    copy.start()
    background.end()
    copy.wait()


class VectorSum(Job):
    uses_tp = uses_ctx = uses_fsdp = True

    def __init__(self, vectors, n, hooks):
        self.n, self.hooks = n, hooks
        dim = vectors[0].shape[1]
        self.ins = [(v, VMEM_SPEC) for v in vectors]
        self.outs = [(jax.ShapeDtypeStruct((16, dim), F32), VMEM_SPEC)]
        self.scratch = [
            VMEM((4, 16, dim), F32), VMEM((3 + n, 16, dim), F32), DMA((3 + n,)), DMA((3 + n,))
        ]

    def refs(self, ins, outs, scratch):
        self.vectors = ins
        (self.out,) = outs
        self.held, self.got, self.ssem, self.rsem = scratch
        t, self.sib, self.peer = partners()

    def copy(self, k):
        if k < 2:
            to = {"tp": self.sib if k == 0 else self.peer}
        elif k == 2:
            to = {"ctx": 1 - self.c}
        else:
            to = {"fsdp": (self.z + k - 2) % self.n}
        return remote(
            self.held.at[min(k, 3)], self.got.at[k], self.ssem.at[k], self.rsem.at[k], to
        )

    def start(self):
        for l in range(LAYERS):
            attn, mlp = self.vectors[2 * l], self.vectors[2 * l + 1]
            for row, (ref, index) in enumerate(
                ((attn, 0), (attn, 1), (mlp, 2), (mlp, 0), (mlp, 1), (mlp, 3), (attn, 2), (mlp, 4))
            ):
                self.held[0, 8 * l + row : 8 * l + row + 1, :] = ref[index : index + 1, :]
        self.copy(0).start()

    def fold(self, k):
        self.copy(k).wait_recv()
        came = self.got[k]
        if k < 2:
            row = lax.broadcasted_iota(jnp.int32, came.shape, 0)
            came = jnp.where(row % 8 < 6, came, 0.0)
        self.held[k + 1] = self.held[k] + came
        if k < 2:
            self.copy(k + 1).start()
        else:
            for j in range(1, self.n):
                self.copy(2 + j).start()

    def finish(self):
        total = self.held[3]
        for j in range(1, self.n):
            self.copy(2 + j).wait_recv()
            total += self.got[2 + j]
        self.out[...] = total

    def steps(self):
        return [(self.hooks[k], functools.partial(self.fold, k)) for k in range(3)] + [
            (self.hooks[3], self.finish)
        ]

    def end(self):
        for k in range(2 + self.n):
            self.copy(k).wait_send()


def leave_kernel(jobs, refs):
    attn_ctx, attn, expand, left, vectors, rows, right = jobs
    entry_barrier(jobs, False)
    attn_ctx.start()
    expand.start()
    vectors.start()
    for job in (rows, right):
        job.start()
    order = list(attn_ctx.order())
    vectors.fold(0)
    expand.relay()
    left.start()
    attn_ctx.add(order[0])
    attn.send(order[0])
    vectors.fold(1)
    attn_ctx.add(order[1])
    attn.send(order[1])
    vectors.fold(2)
    attn_ctx.add(order[2])
    attn.send(order[2])
    left.relay()
    expand.total()
    attn_ctx.add(order[3])
    attn.send(order[3])
    attn.relay()
    left.total()
    vectors.finish()
    right.add()
    attn.total()
    for job in jobs:
        job.end()


def finish_kernel(
    attn_0, attn_1, expand_0, expand_1, left_0, left_1, right_0, right_1, vectors,
    joint, out, expand, reduce, wide, query, value, hidden,
):
    z = lax.axis_index("fsdp")
    half = attn_0.shape[1]
    width = joint.shape[3]
    shard = 2 * half
    layers = ((attn_0, expand_0, left_0, right_0), (attn_1, expand_1, left_1, right_1))
    for l, (a, e, left, right) in enumerate(layers):
        rows = a[...].reshape(shard, a.shape[2]).astype(F32)
        for k in range(3):
            joint[l, k] = rows[:, k * width : (k + 1) * width]
        out[l] = rows[:, 3 * width :].T
        expand[l] = e[...].reshape(shard, e.shape[2]).astype(F32)
        part = left.shape[-1]
        for k, r in enumerate((left, right)):
            reduce[l, k * part : (k + 1) * part, :] = r[...].reshape(shard, part).astype(F32).T
    cut = query.shape[2]
    heads = query.shape[1]
    dim = vectors.shape[1]
    own = pltpu.roll(vectors[...], lax.rem(dim - z * shard, dim), 1)
    by_cut = pltpu.roll(vectors[...], lax.rem(dim - z * cut, dim), 1)
    for l in range(LAYERS):
        for k in range(6):
            wide[k, l : l + 1, :] = own[8 * l + k : 8 * l + k + 1, :shard]
        for row, base, ref in ((6, 0, query), (6, heads * HD, value), (7, 0, hidden)):
            for h in range(ref.shape[1]):
                at = base + h * HD
                ref[l, h : h + 1, :] = by_cut[8 * l + row : 8 * l + row + 1, at : at + cut]


def whole(ref):
    return ref.reshape(ref.shape[0] * ref.shape[1] * ref.shape[2], ref.shape[3])


def call(kernel, name, outs, scratch, collective_id, flops, args, jobs=()):
    args = [
        (a, spec)
        for arg in args
        for a, spec in ([(arg, VMEM_SPEC)] if not isinstance(arg, tuple) else [(a, HBM_SPEC) for a in arg])
    ]
    ins = args + [pair for job in jobs for pair in job.ins]
    results = [o if isinstance(o, tuple) else (o, VMEM_SPEC) for o in outs] + [pair for job in jobs for pair in job.outs]
    scratch = list(scratch)
    n_scratch = len(scratch)
    for job in jobs:
        scratch += job.scratch

    def body(*refs):
        refs = list(refs)
        in_refs = refs[: len(ins)]
        out_refs = refs[len(ins) : len(ins) + len(results)]
        scratch_refs = refs[len(ins) + len(results) :]
        a, b, c = len(args), len(outs), n_scratch
        for job in jobs:
            ends = a + len(job.ins), b + len(job.outs), c + len(job.scratch)
            job.bind(in_refs[a : ends[0]], out_refs[b : ends[1]], scratch_refs[c : ends[2]])
            a, b, c = ends
        kernel(jobs, (in_refs[: len(args)], out_refs[: len(outs)], scratch_refs[:n_scratch]))

    size = sum(a.size * a.dtype.itemsize for a, _ in ins) + sum(
        math.prod(o.shape) * o.dtype.itemsize for o, _ in results
    )
    return pl.pallas_call(
        body,
        name=name,
        out_shape=tuple(o for o, _ in results),
        in_specs=[spec for _, spec in ins],
        out_specs=tuple(spec for _, spec in results),
        scratch_shapes=scratch,
        compiler_params=pltpu.CompilerParams(
            collective_id=collective_id, has_side_effects=True, vmem_limit_bytes=VMEM_LIMIT
        ),
        cost_estimate=pl.CostEstimate(flops=flops, bytes_accessed=size, transcendentals=0),
    )(*[a for a, _ in ins])


def local(
    tokens, key_valid, first_gain, first_shift, joint_weight, query_bias, value_bias,
    out_weight, out_bias, second_gain, second_shift, expand_weight, expand_bias,
    reduce_weight, reduce_bias, cotangent,
):
    ctx_size = lax.axis_size("ctx")
    tp_size = lax.axis_size("tp")
    fsdp_size = lax.axis_size("fsdp")
    clips, half, dim = tokens.shape
    assert clips == ctx_size == 2 and tp_size == 4 and joint_weight.shape[0] == LAYERS
    c = lax.axis_index("ctx")
    shard = joint_weight.shape[1]
    width = joint_weight.shape[3]
    heads = width // HD
    hidden = expand_weight.shape[2]
    attn_w = jnp.concatenate(
        [joint_weight.transpose(0, 2, 1, 3), out_weight.transpose(0, 2, 1)[:, None]], axis=1
    )
    reduce_w = reduce_weight.transpose(0, 2, 1)

    valid = lax.dynamic_index_in_dim(key_valid, c, 0, keepdims=False)
    bias = jnp.where(valid == 1, 0.0, MASKED).astype(F32)
    bias = bias.reshape(ctx_size, tp_size, half, 1).transpose(1, 0, 2, 3)
    high = bias.astype(BF16).astype(F32)
    col = lax.broadcasted_iota(jnp.int32, (1, 1, 1, LANES), 3) - HD
    key_extra = jnp.where(
        col == 0, high, jnp.where(col == 1, bias - high, jnp.where((col >= 2) & (col < 5), 1.0, 0.0))
    ).astype(BF16)

    every = jax.ShapeDtypeStruct((4, 2, half, dim), BF16)
    own = jax.ShapeDtypeStruct((2, half, dim), F32)
    own_low = jax.ShapeDtypeStruct((2, half, dim), BF16)
    tiny = jax.ShapeDtypeStruct((8, LANES), F32)
    vec = jax.ShapeDtypeStruct((8, dim), F32)
    square = jax.ShapeDtypeStruct((dim, hidden), BF16)
    narrow = jax.ShapeDtypeStruct((dim, hidden // 2), BF16)
    count = 8 * half
    n = fsdp_size
    scratch = scatter_scratch(half, dim)

    def held(columns):
        return VMEM((n, 2, shard // 2, columns), BF16)

    attn_scratch = [held(4 * width), DMA((8,))]
    mlp_scratch = [held(hidden), held(hidden), DMA((4,))]

    jobs = [
        ParamJob(
            [first_gain, first_shift, out_bias, second_gain, second_shift, reduce_bias],
            [query_bias, value_bias, expand_bias], n, dim,
        ),
        Exchange(tokens),
        OverFsdp(attn_w, 0, n, None, 2, (0, 0, 0)),
        OverFsdp(expand_weight, 0, n, None),
    ]
    rows, params, tok, near_a, far_a, near_e = call(
        enter_kernel, "enter", [own_low], [], 0, 10**7, [], jobs
    )
    resid = tok
    saved = []
    heads_shape = jax.ShapeDtypeStruct((heads, count, LANES), BF16)
    rows_width = jax.ShapeDtypeStruct((count, width), BF16)
    rows_hidden = jax.ShapeDtypeStruct((count, hidden), BF16)
    for l in range(LAYERS):
        last = l == LAYERS - 1
        urgent = [
            OverCtx(expand_weight, l, near_e, n),
            OverFsdp(reduce_w, l, n, ("A", 22), 1, (("A", 23), ("A", 0), ("A", 1))),
        ]
        jobs = list(urgent)
        if last:
            jobs.append(Exchange(cotangent).after(("M", 1)))
        else:
            jobs += [
                OverFsdp(attn_w, l + 1, n, ("A", 3), 1, (("A", 4), ("A", 5), ("M", 1))).after(("A", 22)),
                OverFsdp(expand_weight, l + 1, n, ("M", 2)).after(("A", 5)),
            ]
        (first, _, middle, q, k, v, mixed, second, active, slope, out, rows,
         far_e, near_r, far_r, *more) = call(
            lambda jobs, refs, base=8 * l, last=last, urgent=urgent: forward_kernel(
                jobs, urgent, heads, last, base, refs
            ),
            f"forward_{l}",
            [every, own_low, own, heads_shape, heads_shape, heads_shape, rows_width, every,
             rows_hidden, rows_hidden, tiny if last else own, own_low],
            scratch + attn_scratch + mlp_scratch, 1 + 2 * l,
            2 * count * dim * 4 * width + 16 * heads * count * count * HD + 4 * count * dim * hidden,
            [rows, params, key_extra, resid, (near_a, far_a, near_e)], jobs,
        )
        weights = (near_e, far_e, near_r, far_r, near_a, far_a)
        saved.append((resid, first, q, k, v, mixed, middle, second, active, slope, weights))
        resid = out
        if last:
            (cot,) = more
        else:
            near_a, far_a, near_e = more

    carry = cot
    attn_grads, expand_grads, left_grads, right_grads, attn_vec, mlp_vec = (
        [None] * LAYERS for _ in range(6)
    )
    for l in reversed(range(LAYERS)):
        resid, first, q, k, v, mixed, middle, second, active, slope, weights = saved[l]
        last = l == 0
        halves = jax.ShapeDtypeStruct((n, shard, hidden // 2), BF16)
        made = [
            CtxSum(narrow, n, (("A", 2),) * 4, name="left").after(("M", 4)),
            FsdpSum(halves, n, (("A", 1), ("A", 6)), spread=False, name="right").after(("M", 4)),
            CtxSum(square, n, (("A", 6), ("A", 7), ("A", 8), ("A", 10)), name="expand").after(("M", 6)),
        ]
        if last:
            ctx_job = CtxSum(attn_full, n, (("M", 4), ("M", 4), ("M", 5), ("M", 6)), keep=True)
            attn_shape = jax.ShapeDtypeStruct((n, shard // 2, 4 * width), BF16)
            jobs = [
                FsdpSum(expand_part, n, (("M", 2), ("M", 6))),
                FsdpSum(left_part, n, (("M", 4), ("A", 0))).after(("M", 2)),
                ctx_job,
                FsdpSum(
                    attn_shape, n, (("A", 0), ("A", 3)), source=ctx_job,
                    sends=(("M", 4), ("M", 4), ("M", 5), ("M", 6)),
                ),
                CtxAdd(right_part, ("M", 6)),
            ]
        else:
            jobs = [Exchange(rows)]
        attn_full, carry, mlp_vec[l], attn_vec[l], *more = call(
            lambda jobs, refs, base=8 * l: backward_kernel(jobs, heads, base, refs),
            f"backward_{l}",
            [(jax.ShapeDtypeStruct((dim, 4 * width), BF16), HBM_SPEC), own_low if last else own, vec, vec],
            scratch
            + [
                VMEM((dim, hidden // 2), BF16), VMEM((dim, hidden // 2), BF16),
                VMEM(own.shape, F32), VMEM(every.shape, BF16), VMEM(every.shape, BF16),
                VMEM((count, hidden), BF16),
            ]
            + mlp_scratch
            + [
                VMEM((count, 3 * width), BF16),
                VMEM((heads, count, LANES), F32),
                VMEM((heads, count, LANES), F32),
            ]
            + attn_scratch,
            2 + 2 * l,
            4 * count * dim * 4 * width + 40 * heads * count * count * HD + 8 * count * dim * hidden,
            [active, slope, second, middle, carry, params, mixed, q, k, v, first, resid, weights],
            jobs + made,
        )
        if last:
            expand_grads[1], left_grads[1], attn_grads[1], right_grads[1], *more = more
        else:
            output, *more = more
        left_part, right_part, expand_part = more

    ctx_job = CtxSum(attn_full, n, (0, 1, 2, 3), keep=True)
    attn_shape = jax.ShapeDtypeStruct((n, shard // 2, 4 * width), BF16)
    jobs = [
        ctx_job,
        FsdpSum(attn_shape, n, (0, 1), source=ctx_job),
        FsdpSum(expand_part, n, (0, 1)),
        FsdpSum(left_part, n, (0, 1)),
        VectorSum([attn_vec[0], mlp_vec[0], attn_vec[1], mlp_vec[1]], n, (0, 1, 2, 3)),
        Exchange(carry),
        CtxAdd(right_part, 0),
    ]
    (
        attn_grads[0], expand_grads[0], left_grads[0], vectors, row_grad, right_grads[0],
    ) = call(leave_kernel, "leave", [], [], 5, 10**7, [], jobs)
    results = [
        jax.ShapeDtypeStruct(shape, F32)
        for shape in (
            (LAYERS, 3, shard, width), (LAYERS, width, shard), (LAYERS, shard, hidden),
            (LAYERS, hidden, shard), (6, LAYERS, shard), query_bias.shape, value_bias.shape,
            expand_bias.shape,
        )
    ]
    joint, out, expand, reduce, wide, query, value, hidden_bias = pl.pallas_call(
        finish_kernel,
        name="finish",
        out_shape=tuple(results),
        in_specs=[VMEM_SPEC] * 9,
        out_specs=tuple([VMEM_SPEC] * 8),
        compiler_params=pltpu.CompilerParams(vmem_limit_bytes=VMEM_LIMIT),
    )(*attn_grads, *expand_grads, *left_grads, *right_grads, vectors)
    return (
        output, row_grad, wide[0], wide[1], joint.transpose(0, 2, 1, 3), query, value, out,
        wide[2], wide[3], wide[4], expand, hidden_bias, reduce, wide[5],
    )


def solution(mesh):
    vector = P(None, "fsdp")
    by_head = P(None, "tp", "fsdp")
    rows = P("fsdp", ("ctx", "tp"), None)
    return jax.shard_map(
        local,
        mesh=mesh,
        in_specs=(
            rows, P("fsdp", None), vector, vector, P(None, "fsdp", None, "tp"), by_head, by_head,
            by_head, vector, vector, vector, P(None, "fsdp", "tp"), by_head, by_head, vector, rows,
        ),
        out_specs=(
            rows, rows, vector, vector, P(None, "fsdp", None, "tp"), by_head, by_head,
            by_head, vector, vector, vector, P(None, "fsdp", "tp"), by_head, by_head, vector,
        ),
        check_vma=False,
    )
```

```python
import functools
import math

import jax
import jax.numpy as jnp
from jax import lax
from jax.experimental import pallas as pl
from jax.experimental.pallas import tpu as pltpu
from jax.sharding import PartitionSpec as P

HD = 64
LAYERS = 2
LANES = 128
EPS = 1e-06
MASKED = -10000.0
SCALE = HD ** (-0.5)
VMEM_LIMIT = 62 * 1024 * 1024
F32 = jnp.float32
BF16 = jnp.bfloat16
VMEM = pltpu.VMEM
INV_SQRT2 = 1.0 / math.sqrt(2.0)
INV_SQRT_2PI = 1.0 / math.sqrt(2.0 * math.pi)


def mm(a, b):
    return lax.dot_general(a, b, (((1,), (0,)), ((), ())), preferred_element_type=F32)


def mm_nt(a, b):
    return lax.dot_general(a, b, (((1,), (1,)), ((), ())), preferred_element_type=F32)


def mm_tn(a, b):
    return lax.dot_general(a, b, (((0,), (0,)), ((), ())), preferred_element_type=F32)


def partners():
    t = lax.axis_index("tp")
    return t, t + 1 - 2 * (t % 2), (t + 2) % 4


def entry_barrier(jobs=(), tp=True):
    t, sib, peer = partners()
    others = [{"tp": sib}, {"tp": peer}] if tp or any(job.uses_tp for job in jobs) else []
    if any(job.uses_ctx for job in jobs):
        others.append({"ctx": 1 - lax.axis_index("ctx")})
    if any(job.uses_fsdp for job in jobs):
        n = lax.axis_size("fsdp")
        z = lax.axis_index("fsdp")
        others += [{"fsdp": (z + k) % n} for k in range(1, n)]
    barrier = pltpu.get_barrier_semaphore()
    for other in others:
        pl.semaphore_signal(barrier, inc=1, device_id=other, device_id_type=pl.DeviceIdType.MESH)
    pl.semaphore_wait(barrier, len(others))


def remote(src, dst, send, recv, device):
    return pltpu.make_async_remote_copy(
        src_ref=src,
        dst_ref=dst,
        send_sem=send,
        recv_sem=recv,
        device_id=device,
        device_id_type=pl.DeviceIdType.MESH,
    )


DMA = pltpu.SemaphoreType.DMA
HBM_SPEC = pl.BlockSpec(memory_space=pl.ANY)
VMEM_SPEC = pl.BlockSpec(memory_space=VMEM)


class Job:
    uses_tp = False
    uses_ctx = False
    uses_fsdp = False
    ins = ()
    outs = ()
    scratch = ()
    start_hook = None
    name = None

    def after(self, hook):
        self.start_hook = hook
        return self

    def bind(self, ins, outs, scratch):
        self.c = lax.axis_index("ctx")
        self.z = lax.axis_index("fsdp")
        self.refs(ins, outs, scratch)

    def start(self):
        pass

    def steps(self):
        return []

    def end(self):
        pass


def chunks_of(rows):
    return 2 if rows % 128 == 0 else 1


def cut_rows(ref, start, size):
    index = (slice(None),) * (len(ref.shape) - 2) + (pl.ds(start, size),)
    return ref.at[index]


class OverFsdp(Job):
    uses_fsdp = True

    def __init__(self, weight, layer, n, hook, chunks=1, ctx_hooks=None):
        self.n, self.layer, self.hook, self.ctx_hooks = n, layer, hook, ctx_hooks
        self.uses_ctx = ctx_hooks is not None
        shape = weight.shape[1:]
        self.rows = shape[-2] // 2
        self.ch = chunks if self.rows % (chunks * 16) == 0 else 1
        half = jax.ShapeDtypeStruct((n, *shape[:-2], self.rows, shape[-1]), BF16)
        self.ins = [(weight, HBM_SPEC)]
        self.outs = [(half, HBM_SPEC)] * (2 if self.uses_ctx else 1)
        self.scratch = [DMA((n + 1, self.ch)), DMA((n, self.ch)), DMA]
        if self.uses_ctx:
            self.scratch += [DMA((n, self.ch)), DMA((n, self.ch)), DMA]

    def refs(self, ins, outs, scratch):
        self.src = ins[0].at[self.layer]
        self.near = outs[0]
        self.send, self.recv, self.here = scratch[:3]
        if self.uses_ctx:
            self.far = outs[1]
            self.x_send, self.x_recv, self.here_far = scratch[3:]

    def mine(self, ch):
        size = self.rows // self.ch
        start = pl.multiple_of(self.c * self.rows + ch * size, size)
        return cut_rows(self.src, start, size)

    def part(self, ref, frm, ch):
        size = self.rows // self.ch
        return cut_rows(ref.at[frm], ch * size, size)

    def out_to(self, k, off, ch):
        to = (self.z + off + self.n) % self.n
        return remote(
            self.mine(ch), self.part(self.near, self.z, ch),
            self.send.at[k, ch], self.recv.at[self.z, ch], {"fsdp": to},
        )

    def arrived(self, frm, ch):
        block = self.part(self.near, frm, ch)
        return remote(
            block, block, self.send.at[self.n, ch], self.recv.at[frm, ch], {"fsdp": self.n - 1 - frm}
        )

    def over_x(self, frm, ch):
        return remote(
            self.part(self.near, frm, ch), self.part(self.far, frm, ch),
            self.x_send.at[frm, ch], self.x_recv.at[frm, ch], {"ctx": 1 - self.c},
        )

    def local(self, half, out, sem):
        start = pl.multiple_of(half * self.rows, self.rows)
        return pltpu.make_async_copy(
            cut_rows(self.src, start, self.rows), out.at[self.z], sem
        )

    def offsets(self):
        return (2, -2, 1, -1) if self.n == 4 else range(1, self.n)

    def sources(self):
        return (1, -1, 2, -2, 3, -3) if self.n == 4 else range(1, self.n)

    def inside(self, off):
        other = self.z + off
        return (other >= 0) & (other < self.n) if self.n == 4 else (other > -1)

    def relays(self):
        return (self.z == 1) | (self.z == 2)

    def start(self):
        for ch in range(self.ch):
            for k, off in enumerate(self.offsets()):
                @pl.when(self.inside(off))
                def _():
                    self.out_to(k, off, ch).start()
        self.local(self.c, self.near, self.here).start()
        if self.uses_ctx:
            self.local(1 - self.c, self.far, self.here_far).start()

    def relay(self):
        if self.n == 4:
            @pl.when(self.relays())
            def _():
                for ch in range(self.ch):
                    through = self.arrived(jnp.where(self.z == 2, 0, 3), ch)
                    through.wait_recv()
                    through.start()

    def take(self, off):
        frm = (self.z + off + self.n) % self.n

        @pl.when(self.inside(off))
        def _():
            for ch in range(self.ch):
                if self.n == 4 and abs(off) == 2:
                    @pl.when(jnp.logical_not((self.z == 2) & (frm == 0) | (self.z == 1) & (frm == 3)))
                    def _():
                        self.arrived(frm, ch).wait_recv()
                else:
                    self.arrived(frm, ch).wait_recv()
                if self.uses_ctx:
                    self.over_x(frm, ch).start()

    def steps(self):
        out = [(self.hook, self.relay)]
        if self.uses_ctx:
            for i, off in enumerate(self.sources()):
                out.append((self.ctx_hooks[min(i // 2, 2)], functools.partial(self.take, off)))
        return out

    def end(self):
        for off in self.sources():
            frm = (self.z + off + self.n) % self.n
            if not self.uses_ctx:
                self.take(off)
            else:
                @pl.when(self.inside(off))
                def _():
                    for ch in range(self.ch):
                        self.over_x(frm, ch).wait()
        for ch in range(self.ch):
            for k, off in enumerate(self.offsets()):
                @pl.when(self.inside(off))
                def _():
                    self.out_to(k, off, ch).wait_send()
            if self.n == 4:
                @pl.when(self.relays())
                def _():
                    self.arrived(jnp.where(self.z == 2, 0, 3), ch).wait_send()
        self.local(self.c, self.near, self.here).wait()
        if self.uses_ctx:
            self.local(1 - self.c, self.far, self.here_far).wait()


class OverCtx(Job):
    uses_ctx = True

    def __init__(self, weight, layer, near, n):
        self.n, self.layer = n, layer
        self.ins = [(weight, HBM_SPEC), (near, HBM_SPEC)]
        self.outs = [(jax.ShapeDtypeStruct(near.shape, BF16), HBM_SPEC)]
        self.scratch = [DMA((n,)), DMA((n,)), DMA]

    def refs(self, ins, outs, scratch):
        self.src, self.near = ins[0].at[self.layer], ins[1]
        (self.far,) = outs
        self.send, self.recv, self.here = scratch

    def copy(self, k):
        frm = (self.z + k) % self.n
        return remote(
            self.near.at[frm], self.far.at[frm], self.send.at[k], self.recv.at[k],
            {"ctx": 1 - self.c},
        )

    def local(self):
        rows = self.near.shape[-2]
        start = pl.multiple_of((1 - self.c) * rows, rows)
        return pltpu.make_async_copy(cut_rows(self.src, start, rows), self.far.at[self.z], self.here)

    def start(self):
        for k in range(1, self.n):
            self.copy(k).start()
        self.local().start()

    def end(self):
        for k in range(1, self.n):
            self.copy(k).wait()
        self.local().wait()


class Loads:
    def __init__(self, sems):
        self.sems, self.copies = sems, []

    def add(self, near, far, out):
        c = lax.axis_index("ctx")
        for half, ref in ((c, near), (1 - c, far)):
            if isinstance(out, tuple):
                width = ref.shape[-1] // len(out)
                pairs = [
                    (ref.at[:, :, j * width : (j + 1) * width], part.at[:, half])
                    for j, part in enumerate(out)
                ]
            elif len(ref.shape) == 3:
                pairs = [(ref, out.at[:, half])]
            else:
                width = ref.shape[-1]
                pairs = [
                    (ref.at[:, j], out.at[:, half, :, j * width : (j + 1) * width])
                    for j in range(ref.shape[1])
                ]
            for src, dst in pairs:
                copy = pltpu.make_async_copy(src, dst, self.sems.at[len(self.copies)])
                copy.start()
                self.copies.append(copy)

    def wait(self):
        for copy in self.copies:
            copy.wait()


class ParamJob(Job):
    uses_fsdp = True

    def __init__(self, wide, narrow, n, dim):
        self.n, self.n_wide = n, len(wide)
        self.ins = [(a, VMEM_SPEC) for a in (*wide, *narrow)]
        shape = (8 * LAYERS, dim)
        self.outs = [(jax.ShapeDtypeStruct(shape, F32), VMEM_SPEC)]
        self.scratch = [
            VMEM(shape, F32), VMEM(shape, BF16), VMEM((n, *shape), BF16), DMA((n,)), DMA((n,))
        ]

    def refs(self, ins, outs, scratch):
        self.wide, self.narrow = ins[: self.n_wide], ins[self.n_wide :]
        (self.out,) = outs
        self.work, self.src, self.got, self.ssem, self.rsem = scratch

    def copy(self, k):
        return remote(
            self.src, self.got.at[k], self.ssem.at[k], self.rsem.at[k],
            {"fsdp": (self.z + k) % self.n},
        )

    def start(self):
        work = self.work
        dim = work.shape[1]
        work[...] = jnp.zeros_like(work)
        shard = self.wide[0].shape[1]
        query, value, expand = self.narrow
        cut = query.shape[2]
        heads = query.shape[1]
        for l in range(LAYERS):
            for k, ref in enumerate(self.wide):
                work[8 * l + k : 8 * l + k + 1, :shard] = ref[l : l + 1, :].astype(F32)
            for row, base, ref in ((6, 0, query), (6, heads * HD, value), (7, 0, expand)):
                block = ref[l].astype(F32)
                for h in range(ref.shape[1]):
                    at = base + h * HD
                    work[8 * l + row : 8 * l + row + 1, at : at + cut] = block[h : h + 1, :]
        all_rows = work[...]
        row = lax.broadcasted_iota(jnp.int32, all_rows.shape, 0) % 8
        by_shard = pltpu.roll(all_rows, self.z * shard, 1)
        by_cut = pltpu.roll(all_rows, self.z * cut, 1)
        placed = jnp.where(row < 6, by_shard, by_cut)
        work[...] = placed
        self.src[...] = placed.astype(BF16)
        for k in range(1, self.n):
            self.copy(k).start()

    def finish(self):
        total = self.work[...]
        for k in range(1, self.n):
            self.copy(k).wait_recv()
            total += self.got[k].astype(F32)
        self.out[...] = total

    def end(self):
        for k in range(1, self.n):
            self.copy(k).wait_send()


class Exchange(Job):
    uses_ctx = True

    def __init__(self, both, name=None):
        self.name = name
        self.ins = [] if name else [(both, VMEM_SPEC)]
        self.outs = [(jax.ShapeDtypeStruct(both.shape, both.dtype), VMEM_SPEC)]
        self.scratch = [DMA, DMA]

    def refs(self, ins, outs, scratch):
        if not self.name:
            (self.src,) = ins
        (self.out,), (self.ssem, self.rsem) = outs, scratch

    def attach(self, ref):
        self.src = ref

    def copy(self):
        c = self.c
        return remote(self.src.at[1 - c], self.out.at[c], self.ssem, self.rsem, {"ctx": 1 - c})

    def start(self):
        self.copy().start()
        self.out[self.c] = self.src[self.c]

    def end(self):
        self.copy().wait()


class CtxSum(Job):
    uses_ctx = True

    def __init__(self, full, n, hooks, keep=False, name=None):
        self.n, self.hooks, self.name = n, hooks, name
        shape = (n, full.shape[0] // (2 * n), full.shape[1])
        self.ins = [] if name else [(full.reshape(n, 2, *shape[1:]), HBM_SPEC)]
        self.keep = keep
        self.outs = [] if keep else [(jax.ShapeDtypeStruct(shape, BF16), VMEM_SPEC)]
        self.scratch = [VMEM(shape, BF16), DMA((n,)), DMA((n,)), DMA((n,))]
        if keep and not name:
            self.scratch.append(VMEM(shape, BF16))

    def refs(self, ins, outs, scratch):
        if not self.name:
            (self.full,) = ins
        self.got, self.ssem, self.rsem, self.near = scratch[:4]
        if not (self.keep and self.name):
            self.out = scratch[4] if self.keep else outs[0]

    def attach(self, ref):
        self.full = ref.reshape(self.n, 2, ref.shape[0] // (2 * self.n), ref.shape[1])
        if self.keep:
            self.out = self.full.at[:, self.c]

    def order(self):
        return (0, 3, 1, 2) if self.n == 4 else range(self.n)

    def copy(self, k):
        return remote(
            self.full.at[k, 1 - self.c], self.got.at[k], self.ssem.at[k], self.rsem.at[k],
            {"ctx": 1 - self.c},
        )

    def load(self, k):
        return pltpu.make_async_copy(self.full.at[k, self.c], self.out.at[k], self.near.at[k])

    def start(self):
        for k in self.order():
            self.copy(k).start()
        for k in self.order():
            if not self.name:
                self.load(k).start()

    def add(self, k):
        if not self.name:
            self.load(k).wait()
        self.copy(k).wait_recv()
        mine = self.full[k, self.c] if self.name else self.out[k]
        self.out[k] = (mine.astype(F32) + self.got[k].astype(F32)).astype(BF16)

    def steps(self):
        per = -(-self.n // len(self.hooks))
        return [
            (self.hooks[i // per], functools.partial(self.add, k))
            for i, k in enumerate(self.order())
        ]

    def end(self):
        for k in range(self.n):
            self.copy(k).wait_send()


class FsdpSum(Job):
    uses_fsdp = True

    def __init__(self, rows, n, hooks, source=None, sends=(), spread=True, direct=False, name=None):
        self.name = name
        self.n, self.hooks, self.source, self.sends = n, hooks, source, sends
        self.relays = n == 4 and not direct
        self.spread = self.uses_ctx = spread
        shape = rows.shape
        self.ins = [] if source or name else [(rows, VMEM_SPEC)]
        result = (2, *shape[1:]) if spread else shape[1:]
        self.outs = [(jax.ShapeDtypeStruct(result, BF16), VMEM_SPEC)]
        self.rows = shape[1]
        self.ch = chunks_of(self.rows)
        self.scratch = [
            VMEM(shape, BF16), VMEM((2, *shape[1:]), BF16),
            DMA((n, self.ch)), DMA((n, self.ch)), DMA((2, self.ch)), DMA((2, self.ch)),
            DMA((self.ch,)), DMA((self.ch,)),
        ]

    def refs(self, ins, outs, scratch):
        if not (self.name or self.source):
            self.src = ins[0]
        (self.out,) = outs
        (self.got, self.via, self.ssem, self.rsem, self.via_send, self.via_recv, self.x_send,
         self.x_recv) = scratch

    def attach(self, ref):
        self.src = ref.reshape(self.n, self.rows, ref.shape[1])

    def cut(self, ref, ch):
        size = self.rows // self.ch
        return ref.at[pl.ds(ch * size, size)]

    def direct(self, d, ch):
        return remote(
            self.cut(self.src.at[d], ch), self.cut(self.got.at[self.z], ch),
            self.ssem.at[d, ch], self.rsem.at[self.z, ch], {"fsdp": d},
        )

    def landed(self, frm, ch):
        block = self.cut(self.got.at[frm], ch)
        return remote(block, block, self.ssem.at[frm, ch], self.rsem.at[frm, ch], {"fsdp": frm})

    def to_relay(self, d, ch):
        return remote(
            self.cut(self.src.at[d], ch), self.cut(self.via.at[0], ch),
            self.via_send.at[0, ch], self.via_recv.at[0, ch], {"fsdp": 2 if d == 0 else 1},
        )

    def relayed(self, d, ch):
        return remote(
            self.cut(self.via.at[1], ch), self.cut(self.got.at[self.z], ch),
            self.via_send.at[1, ch], self.rsem.at[self.z, ch], {"fsdp": d},
        )

    def directly(self, d):
        if self.relays and d in (0, 3):
            return (self.z == 1) if d == 0 else (self.z == 2)
        return self.z != d

    def send(self, d):
        if self.relays and d in (0, 3):
            @pl.when(self.z == 3 - d)
            def _():
                for ch in range(self.ch):
                    self.to_relay(d, ch).start()

        @pl.when(self.directly(d))
        def _():
            for ch in range(self.ch):
                self.direct(d, ch).start()

    def order(self):
        return (0, 3, 1, 2) if self.n == 4 else range(self.n)

    def start(self):
        if not self.source:
            for d in self.order():
                self.send(d)

    def relay(self):
        for d, me in ((0, 2), (3, 1)) if self.relays else ():
            @pl.when(self.z == me)
            def _():
                for ch in range(self.ch):
                    self.to_relay(d, ch).wait_recv()
                    mine = self.cut(self.src.at[d], ch)[...].astype(F32)
                    theirs = self.cut(self.via.at[0], ch)[...].astype(F32)
                    self.cut(self.via.at[1], ch)[...] = (mine + theirs).astype(BF16)
                    self.relayed(d, ch).start()

    then = None

    def result(self, ch):
        return self.cut(self.out.at[self.c] if self.spread else self.out, ch)

    def over_x(self, ch):
        block = self.result(ch)
        return remote(block, block, self.x_send.at[ch], self.x_recv.at[ch], {"ctx": 1 - self.c})

    def total(self):
        n = self.n
        for ch in range(self.ch):
            mine = self.cut(self.src.at[self.z], ch)
            if self.relays:
                near = (self.z + 1) % 4
                last = jnp.where(self.z == 0, 2, jnp.where(self.z == 3, 1, (self.z + 3) % 4))
                first = jnp.where(self.z == 3, 2, near)
                inner = (self.z == 1) | (self.z == 2)
                self.landed(first, ch).wait_recv()
                self.landed(last, ch).wait_recv()
                part = (
                    mine[...].astype(F32)
                    + self.cut(self.got.at[first], ch)[...].astype(F32)
                    + self.cut(self.got.at[last], ch)[...].astype(F32)
                )
                block = self.result(ch)

                @pl.when(inner)
                def _():
                    middle = (self.z + 2) % 4
                    self.landed(middle, ch).wait_recv()
                    block[...] = (part + self.cut(self.got.at[middle], ch)[...].astype(F32)).astype(BF16)

                @pl.when(jnp.logical_not(inner))
                def _():
                    block[...] = part.astype(BF16)
            else:
                part = mine[...].astype(F32)
                for k in range(1, n):
                    frm = (self.z + k) % n
                    self.landed(frm, ch).wait_recv()
                    part += self.cut(self.got.at[frm], ch)[...].astype(F32)
                self.result(ch)[...] = part.astype(BF16)
            if self.spread:
                self.over_x(ch).start()
            elif self.then is not None:
                self.then(ch)

    def steps(self):
        out = [
            (self.sends[i * len(self.sends) // self.n], functools.partial(self.send, d))
            for i, d in enumerate(self.order())
            if self.sends
        ]
        return out + [(self.hooks[0], self.relay), (self.hooks[1], self.total)]

    def end(self):
        for ch in range(self.ch):
            if self.spread:
                other = self.cut(self.out.at[1 - self.c], ch)
                remote(
                    other, other, self.x_send.at[ch], self.x_recv.at[ch], {"ctx": 1 - self.c}
                ).wait_recv()
                self.over_x(ch).wait_send()
            for d in range(self.n):
                if self.relays and d in (0, 3):
                    @pl.when(self.z == 3 - d)
                    def _():
                        self.to_relay(d, ch).wait_send()

                    @pl.when(self.z == (2 if d == 0 else 1))
                    def _():
                        self.relayed(d, ch).wait_send()

                @pl.when(self.directly(d))
                def _():
                    self.direct(d, ch).wait_send()


class CtxAdd(Job):
    uses_ctx = True

    def __init__(self, rows, hook, source=None):
        self.hook, self.source = hook, source
        self.ins = [] if source else [(rows, VMEM_SPEC)]
        self.outs = [(jax.ShapeDtypeStruct(rows.shape, BF16), VMEM_SPEC)]
        self.rows = rows.shape[0]
        self.ch = chunks_of(self.rows)
        self.scratch = [VMEM(rows.shape, BF16), DMA((self.ch,)), DMA((self.ch,))]

    def refs(self, ins, outs, scratch):
        self.src = self.source.out if self.source else ins[0]
        (self.out,) = outs
        self.got, self.ssem, self.rsem = scratch
        if self.source:
            self.source.then = self.send

    def cut(self, ref, ch):
        size = self.rows // self.ch
        return ref.at[pl.ds(ch * size, size)]

    def copy(self, ch):
        return remote(
            self.cut(self.src, ch), self.cut(self.got, ch), self.ssem.at[ch], self.rsem.at[ch],
            {"ctx": 1 - self.c},
        )

    def send(self, ch):
        self.copy(ch).start()

    def start(self):
        if not self.source:
            for ch in range(self.ch):
                self.send(ch)

    def add(self):
        for ch in range(self.ch):
            self.copy(ch).wait_recv()
            mine, theirs = self.cut(self.src, ch)[...], self.cut(self.got, ch)[...]
            self.cut(self.out, ch)[...] = (mine.astype(F32) + theirs.astype(F32)).astype(BF16)

    def steps(self):
        return [(self.hook, self.add)]

    def end(self):
        for ch in range(self.ch):
            self.copy(ch).wait_send()


class Background:
    def __init__(self, jobs):
        self.jobs = jobs
        self.todo = []
        for job in jobs:
            if job.start_hook is not None:
                self.todo.append((job.start_hook, job.start))
            self.todo += job.steps()
        self.ended = []

    def start(self):
        for job in self.jobs:
            if job.start_hook is None:
                job.start()

    def at(self, hook):
        for when, function in self.todo:
            if when == hook:
                function()

    def phase(self, tag):
        return Phase(self, tag)

    def end(self, jobs=None):
        for job in self.jobs if jobs is None else jobs:
            if job not in self.ended:
                self.ended.append(job)
                job.end()


class Phase:
    def __init__(self, whole, tag):
        self.whole, self.tag = whole, tag

    def at(self, hook):
        self.whole.at((self.tag, hook))

    def loop(self, b, count=4, base=0):
        for k in range(count):
            if any(when == (self.tag, base + k) for when, _ in self.whole.todo):
                @pl.when(b == k)
                def _():
                    self.at(base + k)


class Links:
    def __init__(self, send, recv, sib, peer):
        self.send, self.recv, self.sib, self.peer = send, recv, sib, peer

    def make(self, kind, s, src, dst, other):
        return pltpu.make_async_remote_copy(
            src_ref=src,
            dst_ref=dst,
            send_sem=self.send.at[kind, s],
            recv_sem=self.recv.at[kind, s],
            device_id={"tp": other},
            device_id_type=pl.DeviceIdType.MESH,
        )


def statistics(rows):
    mean = jnp.mean(rows, axis=-1, keepdims=True)
    centred = rows - mean
    inverse = lax.rsqrt(jnp.mean(centred * centred, axis=-1, keepdims=True) + EPS)
    return centred * inverse, inverse


def norm_back(rows, d_out, gain):
    unit, inverse = statistics(rows)
    e = d_out * gain
    back = inverse * (
        e
        - jnp.mean(e, axis=-1, keepdims=True)
        - unit * jnp.mean(e * unit, axis=-1, keepdims=True)
    )
    d_gain = jnp.sum(d_out * unit, axis=0, keepdims=True)
    d_shift = jnp.sum(d_out, axis=0, keepdims=True)
    return back, d_gain, d_shift


def rows_of(ref, b):
    block = ref[b]
    return block.reshape(block.shape[0] * block.shape[1], block.shape[2])


class Gather:
    def __init__(self, links, out):
        self.links, self.out = links, out

    def near(self, s):
        return self.links.make(3, s, self.out.at[2 + s, 0], self.out.at[2 + s, 1], self.links.sib)

    def across(self, s):
        return self.links.make(4, s, self.out.at[2 + s, 0], self.out.at[s, 0], self.links.peer)

    def onward(self, s):
        return self.links.make(5, s, self.out.at[s, 0], self.out.at[s, 1], self.links.sib)

    def start(self, rows):
        for s in range(2):
            self.out[2 + s, 0] = rows(s)
            self.near(s).start()
            self.across(s).start()

    def need(self, b):
        s = b % 2

        @pl.when(b >= 2)
        def _():
            self.near(s).wait_recv()

        @pl.when(b < 2)
        def _():
            self.across(s).wait_recv()
            self.onward(s).start()
            self.onward(s).wait_recv()

    def end(self):
        for s in range(2):
            for copy in (self.near(s), self.across(s), self.onward(s)):
                copy.wait_send()


class Scatter:
    def __init__(self, links, part, sent, got, own):
        self.links, self.part, self.sent, self.got, self.own = links, part, sent, got, own

    def copy(self, kind, s):
        other = self.links.peer if kind == 1 else self.links.sib
        return self.links.make(kind, s, self.sent.at[kind, s], self.got.at[kind, s], other)

    def block(self, b):
        s = b % 2
        half = self.part.shape[0] // 2

        @pl.when(b < 2)
        def _():
            self.sent[0, s] = self.part[half:].astype(BF16)
            first = self.copy(0, s)
            first.start()
            first.wait_recv()
            self.sent[1, s] = (self.part[:half] + self.got[0, s].astype(F32)).astype(BF16)
            self.copy(1, s).start()

        @pl.when(b >= 2)
        def _():
            self.sent[2, s] = self.part[half:].astype(BF16)
            self.copy(2, s).start()
            self.own[s] = self.part[:half]

    def total(self, s):
        self.copy(2, s).wait_recv()
        self.copy(1, s).wait_recv()
        return self.own[s] + self.got[2, s].astype(F32) + self.got[1, s].astype(F32)

    def end(self):
        for s in range(2):
            for kind in range(3):
                self.copy(kind, s).wait_send()


def scatter_scratch(half, width):
    local = [VMEM((2 * half, width), F32), VMEM((2, half, width), F32)]
    linked = [
        VMEM((3, 2, half, width), BF16), VMEM((3, 2, half, width), BF16), DMA((6, 2)), DMA((6, 2))
    ]
    return local + linked + linked


def scatter_refs(scratch, phase):
    part, own = scratch[:2]
    sent, got, send, recv = scratch[2 + 4 * phase : 6 + 4 * phase]
    return part, sent, got, own, send, recv


def enter_kernel(jobs, refs):
    first = refs[1][0]
    params, tokens, attn, expand = jobs
    entry_barrier(jobs, False)
    tokens.start()
    params.start()
    attn.start()
    params.finish()
    attn.relay()
    expand.start()
    tokens.end()
    for s in range(2):
        unit, _ = statistics(tokens.out[s].astype(F32))
        first[s] = (unit * params.out[0:1, :] + params.out[1:2, :]).astype(BF16)
    for off in attn.sources()[:4]:
        attn.take(off)
    expand.relay()
    for off in attn.sources()[4:]:
        attn.take(off)
    for job in (params, attn, expand):
        job.end()


def pair_tile(pair, h):
    tile = pair if h % 2 == 0 else pltpu.roll(pair, HD, 1)
    return tile


def attention_phase(
    background, heads, base,
    own_first, params, key_extra, resid, near, far,
    first, second, middle, q_out, k_out, v_out, mixed_out,
    part, sent, got, own, send, recv, weight, load,
):
    t, sib, peer = partners()
    links = Links(send, recv, sib, peer)
    scatter = Scatter(links, part, sent, got, own)
    width = heads * HD
    gather = Gather(links, first)
    gather.start(lambda s: own_first[s])
    loads = Loads(load)
    loads.add(near, far, weight)
    loads.wait()
    weight = whole(weight)
    out_bias, gain, shift = (params[base + k : base + k + 1, :] for k in (2, 3, 4))
    q_bias = params[base + 6 : base + 7, :width]
    v_bias = params[base + 6 : base + 7, width : 2 * width]
    half = first.shape[2]
    rows = 2 * half
    lane = lax.broadcasted_iota(jnp.int32, (rows, LANES), 1)
    head_lane = lane < HD
    q_extra = jnp.where(lane < HD + 2, 1.0, 0.0).astype(BF16)
    v_extra = jnp.where(lane < HD + 3, 1.0, 0.0).astype(BF16)

    def project(j, carry):
        b = (j + 2) % 4
        gather.need(b)
        x = rows_of(first, b)
        y = mm(x, weight[:, : 3 * width])
        q = ((y[:, :width] + q_bias).astype(BF16) * SCALE).astype(BF16)
        k = y[:, width : 2 * width].astype(BF16)
        v = (y[:, 2 * width :] + v_bias).astype(BF16)
        g, s = b // 2, b % 2
        mine = jnp.where(g == 1, t, peer)
        other = mine + 1 - 2 * (mine % 2)
        extra = jnp.concatenate([key_extra[mine, s], key_extra[other, s]], axis=0)
        at = pl.ds(pl.multiple_of(b * rows, rows), rows)
        for h in range(heads):
            cut = slice(LANES * (h // 2), LANES * (h // 2 + 1))
            q_out[h, at, :] = jnp.where(head_lane, pair_tile(q[:, cut], h), q_extra)
            k_out[h, at, :] = jnp.where(head_lane, pair_tile(k[:, cut], h), extra)
            v_out[h, at, :] = jnp.where(head_lane, pair_tile(v[:, cut], h), v_extra)
        background.loop(j, 4, 20)
        return carry

    lax.fori_loop(0, 4, project, 0)
    background.at(0)

    def attend(b, carry):
        at = pl.ds(pl.multiple_of(b * rows, rows), rows)
        outs = []
        for h in range(heads):
            q = q_out[h, at, :]
            scores = mm_nt(q, k_out[h])
            top = jnp.max(scores, axis=-1, keepdims=True)
            weights = jnp.exp(scores - top).astype(BF16)
            summed = mm(weights, v_out[h])
            total = summed[:, HD : HD + 1]
            outs.append(summed / total)
            log_total = -(top + jnp.log(total))
            high = log_total.astype(BF16).astype(F32)
            rest = log_total - high
            mid = rest.astype(BF16).astype(F32)
            low = rest - mid
            tail = jnp.where(lane == HD + 2, high, jnp.where(lane == HD + 3, mid, low))
            q_out[h, at, :] = jnp.where(
                (lane >= HD + 2) & (lane < HD + 5), tail.astype(BF16), q
            )
        tiles = [
            jnp.where(head_lane, outs[h], pltpu.roll(outs[h + 1], HD, 1))
            for h in range(0, heads, 2)
        ]
        mixed = jnp.concatenate(tiles, axis=1).astype(BF16)
        mixed_out[at, :] = mixed
        part[...] = mm_nt(mixed, weight[:, 3 * width :])
        scatter.block(b)
        background.loop(b, 4, 1)
        return carry

    lax.fori_loop(0, 4, attend, 0)
    for s in range(2):
        mid = resid[s].astype(F32) + (scatter.total(s) + out_bias)
        middle[s] = mid
        unit, _ = statistics(mid)
        second[s] = (unit * gain + shift).astype(BF16)
        background.at(5 + s)
    gather.end()
    scatter.end()


def mlp_phase(
    background, last, base,
    own_second, params, middle, near_e, far_e, near_r, far_r,
    second, active_out, slope_out, resid, nxt,
    part, sent, got, own, send, recv, expand, reduce, load,
):
    t, sib, peer = partners()
    links = Links(send, recv, sib, peer)
    scatter = Scatter(links, part, sent, got, own)
    half = second.shape[2]
    rows = 2 * half
    gather = Gather(links, second)
    gather.start(lambda s: own_second[s])
    loads = Loads(load)
    loads.add(near_e, far_e, expand)
    loads.add(near_r, far_r, reduce)
    loads.wait()
    expand, reduce = whole(expand), whole(reduce)
    hidden = expand.shape[1]
    out_bias = params[base + 5 : base + 6, :]
    following = 0 if last else base + 8
    gain, shift = (params[following + k : following + k + 1, :] for k in (0, 1))
    step = 256

    def block(j, carry):
        b = (j + 2) % 4
        gather.need(b)
        at = pl.ds(pl.multiple_of(b * rows, rows), rows)
        x = rows_of(second, b)
        for n in range(0, hidden, step):
            before = mm(x, expand[:, n : n + step]) + params[base + 7 : base + 8, n : n + step]
            cdf = 0.5 * (1.0 + lax.erf(before * INV_SQRT2))
            active_out[at, n : n + step] = (before * cdf).astype(BF16)
            slope = cdf + before * (jnp.exp(before * before * -0.5) * INV_SQRT_2PI)
            slope_out[at, n : n + step] = slope.astype(BF16)
        part[...] = mm_nt(active_out[at, :], reduce[...])
        scatter.block(b)
        background.loop(j, 4, 1)
        return carry

    lax.fori_loop(0, 4, block, 0)
    for s in range(2):
        res = middle[s] + (scatter.total(s) + out_bias)
        if last:
            nxt[s] = res.astype(BF16)
        else:
            resid[s] = res
            unit, _ = statistics(res)
            nxt[s] = (unit * gain + shift).astype(BF16)
        background.at(5 + s)
    gather.end()
    scatter.end()


def token_product(left, right, outs, offset=0):
    depth = left.shape[-1]
    total = left.shape[0] * left.shape[1] * left.shape[2]
    step = 256

    def body(j, carry):
        cut = pl.ds(pl.multiple_of(j * step, step), step)
        x = left[:, :, :, cut].reshape(total, step)
        product = mm_tn(x, right[...]).astype(BF16)
        width = right.shape[-1] // len(outs)
        for k, out in enumerate(outs):
            out[cut, offset : offset + width] = product[:, k * width : (k + 1) * width]
        return carry

    lax.fori_loop(0, depth // step, body, 0)


def mlp_back_phase(
    background, base,
    ready, active, slope, second, middle, carry_in, params, near_e, far_e, near_r, far_r,
    expand_grad, reduce_left, reduce_right, carry_out, vectors,
    part, sent, got, own, send, recv, grad, d_before, expand, reduce, load,
):
    t, sib, peer = partners()
    links = Links(send, recv, sib, peer)
    scatter = Scatter(links, part, sent, got, own)
    gather = Gather(links, grad)
    gather.start(lambda s: carry_in[s].astype(BF16))
    loads = Loads(load)
    loads.add(near_e, far_e, expand)
    loads.add(near_r, far_r, reduce)
    loads.wait()
    expand = whole(expand)
    reduce = [whole(part) for part in reduce]
    wide = reduce[0].shape[1]
    gain = params[base + 3 : base + 4, :]
    half = grad.shape[2]
    rows = 2 * half
    hidden = active.shape[1]
    step = 256
    vectors[...] = jnp.zeros_like(vectors)

    def block(j, carry):
        b = (j + 2) % 4
        gather.need(b)
        at = pl.ds(pl.multiple_of(b * rows, rows), rows)
        x = rows_of(grad, b)
        for n in range(0, hidden, step):
            d_act = mm(x, reduce[n // wide][:, n % wide : n % wide + step])
            d_bef = (d_act * slope[at, n : n + step].astype(F32)).astype(BF16)
            d_before[at, n : n + step] = d_bef
            vectors[4:5, n : n + step] += jnp.sum(d_bef.astype(F32), axis=0, keepdims=True)
        part[...] = mm_nt(d_before[at, :], expand[...])
        scatter.block(b)
        background.loop(j)
        return carry

    lax.fori_loop(0, 4, block, 0)
    token_product(grad, active, (reduce_left, reduce_right))
    background.at(4)

    def finish(s):
        back, d_gain, d_shift = norm_back(middle[s], scatter.total(s), gain)
        carry = carry_in[s].astype(F32)
        mid = carry + back
        carry_out[s] = mid
        low = mid.astype(BF16)
        vectors[0:1, :] += d_gain
        vectors[1:2, :] += d_shift
        vectors[2:3, :] += jnp.sum(low.astype(F32), axis=0, keepdims=True)
        vectors[3:4, :] += jnp.sum(carry.astype(BF16).astype(F32), axis=0, keepdims=True)

    finish(0)
    background.at(5)
    ready.wait()
    token_product(second, d_before, (expand_grad,))
    finish(1)
    background.at(6)
    gather.end()
    scatter.end()


def attention_back_phase(
    background, heads, base,
    ready, weight_grad, mixed, q_in, k_in, v_in, first, carry_in, resid, params, near, far,
    carry_out, vectors,
    part, sent, got, own, send, recv, grad, d_joint, d_key, d_value, weight, load,
):
    t, sib, peer = partners()
    links = Links(send, recv, sib, peer)
    scatter = Scatter(links, part, sent, got, own)
    width = heads * HD
    gather = Gather(links, grad)
    gather.start(lambda s: carry_in[s].astype(BF16))
    loads = Loads(load)
    loads.add(near, far, weight)
    loads.wait()
    weight = whole(weight)
    gain = params[base : base + 1, :]
    half = grad.shape[2]
    rows = 2 * half
    lane = lax.broadcasted_iota(jnp.int32, (rows, LANES), 1)
    head_lane = lane < HD
    vectors[...] = jnp.zeros_like(vectors)
    d_joint = d_joint.at[:, : 3 * width]
    d_key[...] = jnp.zeros_like(d_key)
    d_value[...] = jnp.zeros_like(d_value)

    def pairs(tiles):
        return jnp.concatenate(
            [
                jnp.where(head_lane, tiles[h], pltpu.roll(tiles[h + 1], HD, 1))
                for h in range(0, heads, 2)
            ],
            axis=1,
        )

    def attend(j, carry):
        b = (j + 2) % 4
        gather.need(b)
        at = pl.ds(pl.multiple_of(b * rows, rows), rows)
        d_mixed = mm(rows_of(grad, b), weight[:, 3 * width :]).astype(BF16)
        product = d_mixed.astype(F32) * mixed[at, :].astype(F32)
        d_queries = []
        for h in range(heads):
            cut = slice(LANES * (h // 2), LANES * (h // 2 + 1))
            keep = head_lane if h % 2 == 0 else lane >= HD
            delta = -jnp.sum(jnp.where(keep, product[:, cut], 0.0), axis=-1, keepdims=True)
            high = delta.astype(BF16).astype(F32)
            rest = delta - high
            mid = rest.astype(BF16).astype(F32)
            low = rest - mid
            tail = jnp.where(
                lane == HD,
                high,
                jnp.where(lane == HD + 1, mid, jnp.where(lane == HD + 2, low, 0.0)),
            ).astype(BF16)
            d_o = jnp.where(head_lane, pair_tile(d_mixed[:, cut], h), tail)
            q = q_in[h, at, :]
            probs = jnp.exp(mm_nt(k_in[h], q))
            d_value[h] += mm(probs.astype(BF16), d_o)
            d_raw = (probs * mm_nt(v_in[h], d_o)).astype(BF16)
            d_key[h] += mm(d_raw, q)
            d_queries.append(mm_tn(d_raw, k_in[h]) * SCALE)
        d_joint[at, :width] = pairs(d_queries).astype(BF16)
        background.loop(j)
        return carry

    lax.fori_loop(0, 4, attend, 0)

    def gather_heads(b, carry):
        at = pl.ds(pl.multiple_of(b * rows, rows), rows)
        d_joint[at, width : 2 * width] = pairs([d_key[h, at, :] for h in range(heads)]).astype(BF16)
        d_joint[at, 2 * width : 3 * width] = pairs([d_value[h, at, :] for h in range(heads)]).astype(BF16)
        return carry

    lax.fori_loop(0, 4, gather_heads, 0)

    def project(b, carry):
        at = pl.ds(pl.multiple_of(b * rows, rows), rows)
        d_rows = d_joint[at, :]
        sums = jnp.sum(d_rows.astype(F32), axis=0, keepdims=True)
        vectors[2:3, :width] += sums[:, :width]
        vectors[2:3, width : 2 * width] += sums[:, 2 * width :]
        part[...] = mm_nt(d_rows, weight[:, : 3 * width])
        scatter.block(b)
        background.loop(b, 4, 4)
        return carry

    def out_product():
        token_product(grad, mixed, (weight if weight_grad is None else weight_grad,), 3 * width)
        background.at(8)

    def joint_product():
        for copy in ready:
            copy.wait()
        token_product(first, d_joint, (weight if weight_grad is None else weight_grad,))
        background.at(11)

    if weight_grad is not None:
        joint_product()
        out_product()
    lax.fori_loop(0, 4, project, 0)
    if weight_grad is None:
        out_product()

    def finish(s):
        back, d_gain, d_shift = norm_back(resid[s].astype(F32), scatter.total(s), gain)
        carry = carry_in[s] + back
        carry_out[s] = carry.astype(carry_out.dtype)
        vectors[0:1, :] += d_gain
        vectors[1:2, :] += d_shift

    finish(0)
    background.at(9)
    if weight_grad is None:
        joint_product()
    finish(1)
    background.at(10)
    gather.end()
    scatter.end()


def forward_kernel(jobs, urgent, heads, last, base, refs):
    ins, outs, scratch = refs
    own_first, params, key_extra, resid, near_a, far_a, *near = ins
    first, own_rows, middle, q, k, v, mixed, second, active, slope, out, rows = outs
    attn_w, attn_load, expand, reduce, mlp_load = scratch[10:]
    background = Background(jobs)
    entry_barrier(jobs)
    background.start()
    attention_phase(
        background.phase("A"), heads, base,
        own_first, params, key_extra, resid, near_a, far_a,
        first, own_rows, middle, q, k, v, mixed, *scatter_refs(scratch, 0), attn_w, attn_load,
    )
    background.end(urgent)
    near_e = near[0]
    near_r = near[1] if len(near) > 1 else urgent[1].near
    mlp_phase(
        background.phase("M"), last, base,
        own_rows, params, middle, near_e, urgent[0].far, near_r, urgent[1].far,
        second, active, slope, out, rows, *scatter_refs(scratch, 1), expand, reduce, mlp_load,
    )
    background.end()


def backward_kernel(jobs, heads, base, last, refs):
    ins, outs, scratch = refs
    carry_out = scratch[-1]
    if last:
        scratch = scratch[:-1]
    (active, slope, middle, carry_in, params, mixed, q, k, v, resid,
     near_e, far_e, near_r, far_r, near_a, far_a, second, first) = ins
    (carry_mid, grad_rows, attn_rows, d_before, held, expand, reduce_left, reduce_right, mlp_load,
     d_key, d_value, attn_w, attn_load, held_load) = scratch[10:]
    if last:
        mlp_vec, attn_vec = outs
    else:
        mlp_vec, attn_vec, carry_out, attn_grad = outs
    left_grad, right_grad = whole(reduce_left), whole(reduce_right)
    named = dict(
        expand=whole(expand), left=left_grad, right=right_grad, attn=whole(grad_rows), carry=carry_out,
        vectors=(attn_vec, mlp_vec),
    )
    for job in jobs:
        if job.name:
            job.attach(named[job.name])
    for job in jobs:
        if isinstance(job, FsdpSum) and job.source:
            job.src = job.source.out
    background = Background(jobs)
    entry_barrier(jobs)
    background.start()
    second_load = pltpu.make_async_copy(second, held, held_load.at[0])
    second_load.start()
    mlp_back_phase(
        background.phase("M"), base,
        second_load, active, slope, held, middle, carry_in, params, near_e, far_e, near_r, far_r,
        whole(expand), left_grad, right_grad, carry_mid, mlp_vec,
        *scatter_refs(scratch, 0), grad_rows, d_before, expand, (reduce_left, reduce_right), mlp_load,
    )
    first_load = pltpu.make_async_copy(first, held, held_load.at[1])
    first_load.start()
    attention_back_phase(
        background.phase("A"), heads, base,
        [first_load], whole(grad_rows) if last else None, mixed, q, k, v, held, carry_mid, resid, params, near_a, far_a,
        carry_out, attn_vec,
        *scatter_refs(scratch, 1), attn_rows, d_before, d_key, d_value, attn_w, attn_load,
    )
    copies = []
    if not last:
        copies = [pltpu.make_async_copy(whole(attn_w), attn_grad, attn_load.at[0])]
        copies[0].start()
    tail = background.phase("L")
    for hook in range(8):
        tail.at(hook)
    background.end()
    for copy in copies:
        copy.wait()


class VectorSum(Job):
    uses_tp = uses_ctx = uses_fsdp = True

    def __init__(self, vectors, n, hooks):
        self.n, self.hooks, self.name = n, hooks, "vectors"
        dim = vectors[0].shape[1]
        self.ins = [(v, VMEM_SPEC) for v in vectors]
        self.outs = [(jax.ShapeDtypeStruct((16, dim), F32), VMEM_SPEC)]
        self.scratch = [
            VMEM((4, 16, dim), F32), VMEM((3 + n, 16, dim), F32), DMA((3 + n,)), DMA((3 + n,))
        ]

    def refs(self, ins, outs, scratch):
        self.former = ins
        (self.out,) = outs
        self.held, self.got, self.ssem, self.rsem = scratch
        t, self.sib, self.peer = partners()

    def attach(self, refs):
        self.vectors = (*refs, *self.former)

    def copy(self, k):
        if k == 0:
            to = {"ctx": 1 - self.c}
        elif k < 3:
            to = {"tp": self.sib if k == 1 else self.peer}
        else:
            to = {"fsdp": (self.z + k - 2) % self.n}
        return remote(
            self.held.at[min(k, 3)], self.got.at[k], self.ssem.at[k], self.rsem.at[k], to
        )

    def start(self):
        for l in range(LAYERS):
            attn, mlp = self.vectors[2 * l], self.vectors[2 * l + 1]
            for row, (ref, index) in enumerate(
                ((attn, 0), (attn, 1), (mlp, 2), (mlp, 0), (mlp, 1), (mlp, 3), (attn, 2), (mlp, 4))
            ):
                self.held[0, 8 * l + row : 8 * l + row + 1, :] = ref[index : index + 1, :]
        self.copy(0).start()

    def fold(self, k):
        self.copy(k).wait_recv()
        came = self.got[k]
        if k > 0:
            row = lax.broadcasted_iota(jnp.int32, came.shape, 0)
            came = jnp.where(row % 8 < 6, came, 0.0)
        self.held[k + 1] = self.held[k] + came
        if k < 2:
            self.copy(k + 1).start()
        else:
            for j in range(1, self.n):
                self.copy(2 + j).start()

    def finish(self):
        total = self.held[3]
        for j in range(1, self.n):
            self.copy(2 + j).wait_recv()
            total += self.got[2 + j]
        self.out[...] = total

    def steps(self):
        return [(self.hooks[k], functools.partial(self.fold, k)) for k in range(3)] + [
            (self.hooks[3], self.finish)
        ]

    def end(self):
        for k in range(2 + self.n):
            self.copy(k).wait_send()


def finish_kernel(
    attn_0, attn_1, expand_0, expand_1, left_0, left_1, right_0, right_1, vectors,
    joint, out, expand, reduce, wide, query, value, hidden,
):
    z = lax.axis_index("fsdp")
    half = attn_0.shape[1]
    width = joint.shape[3]
    shard = 2 * half
    layers = ((attn_0, expand_0, left_0, right_0), (attn_1, expand_1, left_1, right_1))
    for l, (a, e, left, right) in enumerate(layers):
        rows = a[...].reshape(shard, a.shape[2]).astype(F32)
        for k in range(3):
            joint[l, k] = rows[:, k * width : (k + 1) * width]
        out[l] = rows[:, 3 * width :].T
        expand[l] = e[...].reshape(shard, e.shape[2]).astype(F32)
        part = left.shape[-1]
        for k, r in enumerate((left, right)):
            reduce[l, k * part : (k + 1) * part, :] = r[...].reshape(shard, part).astype(F32).T
    cut = query.shape[2]
    heads = query.shape[1]
    dim = vectors.shape[1]
    own = pltpu.roll(vectors[...], lax.rem(dim - z * shard, dim), 1)
    by_cut = pltpu.roll(vectors[...], lax.rem(dim - z * cut, dim), 1)
    for l in range(LAYERS):
        for k in range(6):
            wide[k, l : l + 1, :] = own[8 * l + k : 8 * l + k + 1, :shard]
        for row, base, ref in ((6, 0, query), (6, heads * HD, value), (7, 0, hidden)):
            for h in range(ref.shape[1]):
                at = base + h * HD
                ref[l, h : h + 1, :] = by_cut[8 * l + row : 8 * l + row + 1, at : at + cut]


def whole(ref):
    return ref.reshape(ref.shape[0] * ref.shape[1] * ref.shape[2], ref.shape[3])


def call(kernel, name, outs, scratch, collective_id, flops, args, jobs=()):
    args = [
        (a, spec)
        for arg in args
        for a, spec in ([(arg, VMEM_SPEC)] if not isinstance(arg, tuple) else [(a, HBM_SPEC) for a in arg])
    ]
    ins = args + [pair for job in jobs for pair in job.ins]
    results = [o if isinstance(o, tuple) else (o, VMEM_SPEC) for o in outs] + [pair for job in jobs for pair in job.outs]
    scratch = list(scratch)
    n_scratch = len(scratch)
    for job in jobs:
        scratch += job.scratch

    def body(*refs):
        refs = list(refs)
        in_refs = refs[: len(ins)]
        out_refs = refs[len(ins) : len(ins) + len(results)]
        scratch_refs = refs[len(ins) + len(results) :]
        a, b, c = len(args), len(outs), n_scratch
        for job in jobs:
            ends = a + len(job.ins), b + len(job.outs), c + len(job.scratch)
            job.bind(in_refs[a : ends[0]], out_refs[b : ends[1]], scratch_refs[c : ends[2]])
            a, b, c = ends
        kernel(jobs, (in_refs[: len(args)], out_refs[: len(outs)], scratch_refs[:n_scratch]))

    size = sum(a.size * a.dtype.itemsize for a, _ in ins) + sum(
        math.prod(o.shape) * o.dtype.itemsize for o, _ in results
    )
    return pl.pallas_call(
        body,
        name=name,
        out_shape=tuple(o for o, _ in results),
        in_specs=[spec for _, spec in ins],
        out_specs=tuple(spec for _, spec in results),
        scratch_shapes=scratch,
        compiler_params=pltpu.CompilerParams(
            collective_id=collective_id, has_side_effects=True, vmem_limit_bytes=VMEM_LIMIT
        ),
        cost_estimate=pl.CostEstimate(flops=flops, bytes_accessed=size, transcendentals=0),
    )(*[a for a, _ in ins])


def local(
    tokens, key_valid, first_gain, first_shift, joint_weight, query_bias, value_bias,
    out_weight, out_bias, second_gain, second_shift, expand_weight, expand_bias,
    reduce_weight, reduce_bias, cotangent,
):
    ctx_size = lax.axis_size("ctx")
    tp_size = lax.axis_size("tp")
    fsdp_size = lax.axis_size("fsdp")
    clips, half, dim = tokens.shape
    assert clips == ctx_size == 2 and tp_size == 4 and joint_weight.shape[0] == LAYERS
    c = lax.axis_index("ctx")
    shard = joint_weight.shape[1]
    width = joint_weight.shape[3]
    heads = width // HD
    hidden = expand_weight.shape[2]
    attn_w = jnp.concatenate(
        [joint_weight.transpose(0, 2, 1, 3), out_weight.transpose(0, 2, 1)[:, None]], axis=1
    )
    reduce_w = reduce_weight.transpose(0, 2, 1)

    valid = lax.dynamic_index_in_dim(key_valid, c, 0, keepdims=False)
    bias = jnp.where(valid == 1, 0.0, MASKED).astype(F32)
    bias = bias.reshape(ctx_size, tp_size, half, 1).transpose(1, 0, 2, 3)
    high = bias.astype(BF16).astype(F32)
    col = lax.broadcasted_iota(jnp.int32, (1, 1, 1, LANES), 3) - HD
    key_extra = jnp.where(
        col == 0, high, jnp.where(col == 1, bias - high, jnp.where((col >= 2) & (col < 5), 1.0, 0.0))
    ).astype(BF16)

    every = jax.ShapeDtypeStruct((4, 2, half, dim), BF16)
    own = jax.ShapeDtypeStruct((2, half, dim), F32)
    own_low = jax.ShapeDtypeStruct((2, half, dim), BF16)
    tiny = jax.ShapeDtypeStruct((8, LANES), F32)
    vec = jax.ShapeDtypeStruct((8, dim), F32)
    square = jax.ShapeDtypeStruct((dim, hidden), BF16)
    narrow = jax.ShapeDtypeStruct((dim, hidden // 2), BF16)
    count = 8 * half
    n = fsdp_size
    scratch = scatter_scratch(half, dim)

    def held(columns):
        return VMEM((n, 2, shard // 2, columns), BF16)

    attn_scratch = [held(4 * width), DMA((8,))]
    mlp_scratch = [held(hidden), held(hidden), DMA((4,))]

    jobs = [
        ParamJob(
            [first_gain, first_shift, out_bias, second_gain, second_shift, reduce_bias],
            [query_bias, value_bias, expand_bias], n, dim,
        ),
        Exchange(tokens),
        OverFsdp(attn_w, 0, n, None, 2, (0, 0, 0)),
        OverFsdp(expand_weight, 0, n, None),
    ]
    rows, params, tok, near_a, far_a, near_e = call(
        enter_kernel, "enter", [own_low], [], 0, 10**7, [], jobs
    )
    resid = tok
    saved = []
    heads_shape = jax.ShapeDtypeStruct((heads, count, LANES), BF16)
    rows_width = jax.ShapeDtypeStruct((count, width), BF16)
    rows_hidden = jax.ShapeDtypeStruct((count, hidden), BF16)
    for l in range(LAYERS):
        last = l == LAYERS - 1
        urgent = [
            OverCtx(expand_weight, l, near_e, n),
            OverFsdp(reduce_w, l, n, ("A", 22), 1, (("A", 23), ("A", 0), ("A", 1))),
        ]
        jobs = list(urgent)
        if last:
            jobs.append(Exchange(cotangent).after(("M", 1)))
        else:
            jobs += [
                OverFsdp(attn_w, l + 1, n, ("A", 3), 1, (("A", 4), ("A", 5), ("M", 1))).after(("A", 22)),
                OverFsdp(expand_weight, l + 1, n, ("M", 2)).after(("A", 5)),
            ]
        (first, _, middle, q, k, v, mixed, second, active, slope, out, rows,
         far_e, near_r, far_r, *more) = call(
            lambda jobs, refs, base=8 * l, last=last, urgent=urgent: forward_kernel(
                jobs, urgent, heads, last, base, refs
            ),
            f"forward_{l}",
            [every, own_low, own, heads_shape, heads_shape, heads_shape, rows_width, every,
             rows_hidden, rows_hidden, tiny if last else own, own_low],
            scratch + attn_scratch + mlp_scratch, 1 + 2 * l,
            2 * count * dim * 4 * width + 16 * heads * count * count * HD + 4 * count * dim * hidden,
            [rows, params, key_extra, resid, (near_a, far_a, near_e)], jobs,
        )
        weights = (near_e, far_e, near_r, far_r, near_a, far_a)
        saved.append((resid, first, q, k, v, mixed, middle, second, active, slope, weights))
        resid = out
        if last:
            (cot,) = more
        else:
            near_a, far_a, near_e = more

    carry = cot
    attn_grads, expand_grads, left_grads, right_grads, attn_vec, mlp_vec = (
        [None] * LAYERS for _ in range(6)
    )
    halves = jax.ShapeDtypeStruct((n, shard, hidden // 2), BF16)
    left_rows = jax.ShapeDtypeStruct((n, shard // 2, hidden // 2), BF16)
    square_rows = jax.ShapeDtypeStruct((n, shard // 2, hidden), BF16)
    attn_shape = jax.ShapeDtypeStruct((dim, 4 * width), BF16)
    attn_rows = jax.ShapeDtypeStruct((n, shard // 2, 4 * width), BF16)
    early = (("M", 4), ("M", 4), ("M", 5), ("M", 6))
    right_half = jax.ShapeDtypeStruct((shard, hidden // 2), BF16)
    for l in reversed(range(LAYERS)):
        resid, first, q, k, v, mixed, middle, second, active, slope, weights = saved[l]
        last = l == 0
        if last:
            attn_job = CtxSum(attn_full, n, early, keep=True)
            right_job = FsdpSum(
                halves, n, (("A", 3), ("A", 7)), spread=False, name="right"
            ).after(("M", 6))
            left_job = FsdpSum(
                halves, n, (("A", 7), ("L", 1)), spread=False, name="left"
            ).after(("A", 3))
            late = (("A", 4), ("A", 5), ("A", 6), ("A", 7))
            expand_job = CtxSum(square, n, late, keep=True, name="expand").after(("M", 6))
            final = (("L", 1), ("L", 1), ("L", 2), ("L", 2))
            final_job = CtxSum(attn_shape, n, final, keep=True, name="attn").after(("A", 8))
            jobs = [
                FsdpSum(expand_part, n, (("M", 2), ("M", 6))),
                attn_job,
                FsdpSum(attn_rows, n, (("A", 0), ("A", 3)), source=attn_job, sends=early),
                right_job,
                CtxAdd(right_half, ("L", 5), source=right_job),
                left_job,
                CtxAdd(right_half, ("L", 5), source=left_job),
                expand_job,
                FsdpSum(square_rows, n, (("L", 1), ("L", 4)), source=expand_job, sends=late),
                VectorSum(
                    [attn_vec[1], mlp_vec[1]], n, (("L", 3), ("L", 3), ("L", 3), ("L", 5))
                ).after(("A", 10)),
                final_job,
                FsdpSum(attn_rows, n, (("L", 4), ("L", 6)), source=final_job, sends=final),
                Exchange(own_low, name="carry").after(("A", 10)),
            ]
            outs = [vec, vec]
        else:
            right_job = FsdpSum(
                halves, n, (("A", 1), ("A", 6)), spread=False, name="right"
            ).after(("M", 4))
            left_job = CtxSum(narrow, n, (("A", 2),) * 4, keep=True, name="left").after(("M", 4))
            late = (("A", 6), ("A", 7), ("A", 8), ("A", 10))
            jobs = [
                Exchange(rows),
                left_job,
                FsdpSum(left_rows, n, (("A", 6), ("A", 8)), source=left_job, sends=(("A", 2),) * 4),
                right_job,
                CtxAdd(right_half, ("A", 10), source=right_job),
                CtxSum(square, n, late, name="expand").after(("M", 6)),
            ]
            outs = [vec, vec, own, (attn_shape, HBM_SPEC)]
        results = call(
            lambda jobs, refs, base=8 * l, last=last: backward_kernel(jobs, heads, base, last, refs),
            f"backward_{l}",
            outs,
            scratch
            + [
                VMEM(own.shape, F32), VMEM(every.shape, BF16), VMEM(every.shape, BF16), VMEM((count, hidden), BF16),
                VMEM(every.shape, BF16),
                held(hidden), held(hidden // 2), held(hidden // 2), DMA((6,)),
            ]
            + [VMEM((heads, count, LANES), F32), VMEM((heads, count, LANES), F32)]
            + attn_scratch
            + [DMA((2,))]
            + ([VMEM(own.shape, BF16)] if last else []),
            2 + 2 * l,
            4 * count * dim * 4 * width + 40 * heads * count * count * HD + 8 * count * dim * hidden,
            [active, slope, middle, carry, params, mixed, q, k, v, resid, (*weights, second, first)],
            jobs,
        )
        if last:
            (_, _, expand_grads[1], attn_grads[1], _, right_grads[0], _, left_grads[0],
             expand_grads[0], vectors, attn_grads[0], row_grad) = results
        else:
            (mlp_vec[l], attn_vec[l], carry, attn_full, output, left_grads[l], _, right_grads[l],
             expand_part) = results

    results = [
        jax.ShapeDtypeStruct(shape, F32)
        for shape in (
            (LAYERS, 3, shard, width), (LAYERS, width, shard), (LAYERS, shard, hidden),
            (LAYERS, hidden, shard), (6, LAYERS, shard), query_bias.shape, value_bias.shape,
            expand_bias.shape,
        )
    ]
    joint, out, expand, reduce, wide, query, value, hidden_bias = pl.pallas_call(
        finish_kernel,
        name="finish",
        out_shape=tuple(results),
        in_specs=[VMEM_SPEC] * 9,
        out_specs=tuple([VMEM_SPEC] * 8),
        compiler_params=pltpu.CompilerParams(vmem_limit_bytes=VMEM_LIMIT),
    )(*attn_grads, *expand_grads, *left_grads, *right_grads, vectors)
    return (
        output, row_grad, wide[0], wide[1], joint.transpose(0, 2, 1, 3), query, value, out,
        wide[2], wide[3], wide[4], expand, hidden_bias, reduce, wide[5],
    )


def solution(mesh):
    vector = P(None, "fsdp")
    by_head = P(None, "tp", "fsdp")
    rows = P("fsdp", ("ctx", "tp"), None)
    return jax.shard_map(
        local,
        mesh=mesh,
        in_specs=(
            rows, P("fsdp", None), vector, vector, P(None, "fsdp", None, "tp"), by_head, by_head,
            by_head, vector, vector, vector, P(None, "fsdp", "tp"), by_head, by_head, vector, rows,
        ),
        out_specs=(
            rows, rows, vector, vector, P(None, "fsdp", None, "tp"), by_head, by_head,
            by_head, vector, vector, vector, P(None, "fsdp", "tp"), by_head, by_head, vector,
        ),
        check_vma=False,
    )
```

```python
import functools
import math

import jax
import jax.numpy as jnp
from jax import lax
from jax.experimental import pallas as pl
from jax.experimental.pallas import tpu as pltpu
from jax.sharding import PartitionSpec as P

HD = 64
LAYERS = 2
LANES = 128
EPS = 1e-06
MASKED = -10000.0
SCALE = HD ** (-0.5)
VMEM_LIMIT = 62 * 1024 * 1024
F32 = jnp.float32
BF16 = jnp.bfloat16
VMEM = pltpu.VMEM
INV_SQRT2 = 1.0 / math.sqrt(2.0)
INV_SQRT_2PI = 1.0 / math.sqrt(2.0 * math.pi)


def mm(a, b):
    return lax.dot_general(a, b, (((1,), (0,)), ((), ())), preferred_element_type=F32)


def mm_nt(a, b):
    return lax.dot_general(a, b, (((1,), (1,)), ((), ())), preferred_element_type=F32)


def mm_tn(a, b):
    return lax.dot_general(a, b, (((0,), (0,)), ((), ())), preferred_element_type=F32)


def partners():
    t = lax.axis_index("tp")
    return t, t + 1 - 2 * (t % 2), (t + 2) % 4


def entry_barrier(jobs=(), tp=True):
    t, sib, peer = partners()
    others = [{"tp": sib}, {"tp": peer}] if tp or any(job.uses_tp for job in jobs) else []
    if any(job.uses_ctx for job in jobs):
        others.append({"ctx": 1 - lax.axis_index("ctx")})
    if any(job.uses_fsdp for job in jobs):
        n = lax.axis_size("fsdp")
        z = lax.axis_index("fsdp")
        others += [{"fsdp": (z + k) % n} for k in range(1, n)]
    barrier = pltpu.get_barrier_semaphore()
    for other in others:
        pl.semaphore_signal(barrier, inc=1, device_id=other, device_id_type=pl.DeviceIdType.MESH)
    pl.semaphore_wait(barrier, len(others))


def remote(src, dst, send, recv, device):
    return pltpu.make_async_remote_copy(
        src_ref=src,
        dst_ref=dst,
        send_sem=send,
        recv_sem=recv,
        device_id=device,
        device_id_type=pl.DeviceIdType.MESH,
    )


DMA = pltpu.SemaphoreType.DMA
HBM_SPEC = pl.BlockSpec(memory_space=pl.ANY)
VMEM_SPEC = pl.BlockSpec(memory_space=VMEM)


class Job:
    uses_tp = False
    uses_ctx = False
    uses_fsdp = False
    ins = ()
    outs = ()
    scratch = ()
    start_hook = None
    name = None

    def after(self, hook):
        self.start_hook = hook
        return self

    def bind(self, ins, outs, scratch):
        self.c = lax.axis_index("ctx")
        self.z = lax.axis_index("fsdp")
        self.refs(ins, outs, scratch)

    def start(self):
        pass

    def steps(self):
        return []

    def end(self):
        pass


def chunks_of(rows):
    return 2 if rows % 128 == 0 else 1


def cut_rows(ref, start, size):
    index = (slice(None),) * (len(ref.shape) - 2) + (pl.ds(start, size),)
    return ref.at[index]


class OverFsdp(Job):
    uses_fsdp = True

    def __init__(self, weight, layer, n, hook, chunks=1, ctx_hooks=None):
        self.n, self.layer, self.hook, self.ctx_hooks = n, layer, hook, ctx_hooks
        self.uses_ctx = ctx_hooks is not None
        shape = weight.shape[1:]
        self.rows = shape[-2] // 2
        self.ch = chunks if self.rows % (chunks * 16) == 0 else 1
        half = jax.ShapeDtypeStruct((n, *shape[:-2], self.rows, shape[-1]), BF16)
        self.ins = [(weight, HBM_SPEC)]
        self.outs = [(half, HBM_SPEC)] * (2 if self.uses_ctx else 1)
        self.scratch = [DMA((n + 1, self.ch)), DMA((n, self.ch)), DMA]
        if self.uses_ctx:
            self.scratch += [DMA((n, self.ch)), DMA((n, self.ch)), DMA]

    def refs(self, ins, outs, scratch):
        self.src = ins[0].at[self.layer]
        self.near = outs[0]
        self.send, self.recv, self.here = scratch[:3]
        if self.uses_ctx:
            self.far = outs[1]
            self.x_send, self.x_recv, self.here_far = scratch[3:]

    def mine(self, ch):
        size = self.rows // self.ch
        start = pl.multiple_of(self.c * self.rows + ch * size, size)
        return cut_rows(self.src, start, size)

    def part(self, ref, frm, ch):
        size = self.rows // self.ch
        return cut_rows(ref.at[frm], ch * size, size)

    def out_to(self, k, off, ch):
        to = (self.z + off + self.n) % self.n
        return remote(
            self.mine(ch), self.part(self.near, self.z, ch),
            self.send.at[k, ch], self.recv.at[self.z, ch], {"fsdp": to},
        )

    def arrived(self, frm, ch):
        block = self.part(self.near, frm, ch)
        return remote(
            block, block, self.send.at[self.n, ch], self.recv.at[frm, ch], {"fsdp": self.n - 1 - frm}
        )

    def over_x(self, frm, ch):
        return remote(
            self.part(self.near, frm, ch), self.part(self.far, frm, ch),
            self.x_send.at[frm, ch], self.x_recv.at[frm, ch], {"ctx": 1 - self.c},
        )

    def local(self, half, out, sem):
        start = pl.multiple_of(half * self.rows, self.rows)
        return pltpu.make_async_copy(
            cut_rows(self.src, start, self.rows), out.at[self.z], sem
        )

    def offsets(self):
        return (2, -2, 1, -1) if self.n == 4 else range(1, self.n)

    def sources(self):
        return (1, -1, 2, -2, 3, -3) if self.n == 4 else range(1, self.n)

    def inside(self, off):
        other = self.z + off
        return (other >= 0) & (other < self.n) if self.n == 4 else (other > -1)

    def relays(self):
        return (self.z == 1) | (self.z == 2)

    def start(self):
        for ch in range(self.ch):
            for k, off in enumerate(self.offsets()):
                @pl.when(self.inside(off))
                def _():
                    self.out_to(k, off, ch).start()
        self.local(self.c, self.near, self.here).start()
        if self.uses_ctx:
            self.local(1 - self.c, self.far, self.here_far).start()

    def relay(self):
        if self.n == 4:
            @pl.when(self.relays())
            def _():
                for ch in range(self.ch):
                    through = self.arrived(jnp.where(self.z == 2, 0, 3), ch)
                    through.wait_recv()
                    through.start()

    def take(self, off):
        frm = (self.z + off + self.n) % self.n

        @pl.when(self.inside(off))
        def _():
            for ch in range(self.ch):
                if self.n == 4 and abs(off) == 2:
                    @pl.when(jnp.logical_not((self.z == 2) & (frm == 0) | (self.z == 1) & (frm == 3)))
                    def _():
                        self.arrived(frm, ch).wait_recv()
                else:
                    self.arrived(frm, ch).wait_recv()
                if self.uses_ctx:
                    self.over_x(frm, ch).start()

    def steps(self):
        out = [(self.hook, self.relay)]
        if self.uses_ctx:
            for i, off in enumerate(self.sources()):
                out.append((self.ctx_hooks[min(i // 2, 2)], functools.partial(self.take, off)))
        return out

    def end(self):
        for off in self.sources():
            frm = (self.z + off + self.n) % self.n
            if not self.uses_ctx:
                self.take(off)
            else:
                @pl.when(self.inside(off))
                def _():
                    for ch in range(self.ch):
                        self.over_x(frm, ch).wait()
        for ch in range(self.ch):
            for k, off in enumerate(self.offsets()):
                @pl.when(self.inside(off))
                def _():
                    self.out_to(k, off, ch).wait_send()
            if self.n == 4:
                @pl.when(self.relays())
                def _():
                    self.arrived(jnp.where(self.z == 2, 0, 3), ch).wait_send()
        self.local(self.c, self.near, self.here).wait()
        if self.uses_ctx:
            self.local(1 - self.c, self.far, self.here_far).wait()


class OverCtx(Job):
    uses_ctx = True

    def __init__(self, weight, layer, near, n):
        self.n, self.layer = n, layer
        self.ins = [(weight, HBM_SPEC), (near, HBM_SPEC)]
        self.outs = [(jax.ShapeDtypeStruct(near.shape, BF16), HBM_SPEC)]
        self.scratch = [DMA((n,)), DMA((n,)), DMA]

    def refs(self, ins, outs, scratch):
        self.src, self.near = ins[0].at[self.layer], ins[1]
        (self.far,) = outs
        self.send, self.recv, self.here = scratch

    def copy(self, k):
        frm = (self.z + k) % self.n
        return remote(
            self.near.at[frm], self.far.at[frm], self.send.at[k], self.recv.at[k],
            {"ctx": 1 - self.c},
        )

    def local(self):
        rows = self.near.shape[-2]
        start = pl.multiple_of((1 - self.c) * rows, rows)
        return pltpu.make_async_copy(cut_rows(self.src, start, rows), self.far.at[self.z], self.here)

    def start(self):
        for k in range(1, self.n):
            self.copy(k).start()
        self.local().start()

    def end(self):
        for k in range(1, self.n):
            self.copy(k).wait()
        self.local().wait()


class Loads:
    def __init__(self, sems):
        self.sems, self.copies = sems, []

    def add(self, near, far, out):
        c = lax.axis_index("ctx")
        for half, ref in ((c, near), (1 - c, far)):
            if isinstance(out, tuple):
                width = ref.shape[-1] // len(out)
                pairs = [
                    (ref.at[:, :, j * width : (j + 1) * width], part.at[:, half])
                    for j, part in enumerate(out)
                ]
            elif len(ref.shape) == 3:
                pairs = [(ref, out.at[:, half])]
            else:
                width = ref.shape[-1]
                pairs = [
                    (ref.at[:, j], out.at[:, half, :, j * width : (j + 1) * width])
                    for j in range(ref.shape[1])
                ]
            for src, dst in pairs:
                copy = pltpu.make_async_copy(src, dst, self.sems.at[len(self.copies)])
                copy.start()
                self.copies.append(copy)

    def wait(self):
        for copy in self.copies:
            copy.wait()


class ParamJob(Job):
    uses_fsdp = True

    def __init__(self, wide, narrow, n, dim):
        self.n, self.n_wide = n, len(wide)
        self.ins = [(a, VMEM_SPEC) for a in (*wide, *narrow)]
        shape = (8 * LAYERS, dim)
        self.outs = [(jax.ShapeDtypeStruct(shape, F32), VMEM_SPEC)]
        self.scratch = [
            VMEM(shape, F32), VMEM(shape, BF16), VMEM((n, *shape), BF16), DMA((n,)), DMA((n,))
        ]

    def refs(self, ins, outs, scratch):
        self.wide, self.narrow = ins[: self.n_wide], ins[self.n_wide :]
        (self.out,) = outs
        self.work, self.src, self.got, self.ssem, self.rsem = scratch

    def copy(self, k):
        return remote(
            self.src, self.got.at[k], self.ssem.at[k], self.rsem.at[k],
            {"fsdp": (self.z + k) % self.n},
        )

    def start(self):
        work = self.work
        dim = work.shape[1]
        work[...] = jnp.zeros_like(work)
        shard = self.wide[0].shape[1]
        query, value, expand = self.narrow
        cut = query.shape[2]
        heads = query.shape[1]
        for l in range(LAYERS):
            for k, ref in enumerate(self.wide):
                work[8 * l + k : 8 * l + k + 1, :shard] = ref[l : l + 1, :].astype(F32)
            for row, base, ref in ((6, 0, query), (6, heads * HD, value), (7, 0, expand)):
                block = ref[l].astype(F32)
                for h in range(ref.shape[1]):
                    at = base + h * HD
                    work[8 * l + row : 8 * l + row + 1, at : at + cut] = block[h : h + 1, :]
        all_rows = work[...]
        row = lax.broadcasted_iota(jnp.int32, all_rows.shape, 0) % 8
        by_shard = pltpu.roll(all_rows, self.z * shard, 1)
        by_cut = pltpu.roll(all_rows, self.z * cut, 1)
        placed = jnp.where(row < 6, by_shard, by_cut)
        work[...] = placed
        self.src[...] = placed.astype(BF16)
        for k in range(1, self.n):
            self.copy(k).start()

    def finish(self):
        total = self.work[...]
        for k in range(1, self.n):
            self.copy(k).wait_recv()
            total += self.got[k].astype(F32)
        self.out[...] = total

    def end(self):
        for k in range(1, self.n):
            self.copy(k).wait_send()


class Exchange(Job):
    uses_ctx = True

    def __init__(self, both, name=None):
        self.name = name
        self.ins = [] if name else [(both, VMEM_SPEC)]
        self.outs = [(jax.ShapeDtypeStruct(both.shape, both.dtype), VMEM_SPEC)]
        self.scratch = [DMA, DMA]

    def refs(self, ins, outs, scratch):
        if not self.name:
            (self.src,) = ins
        (self.out,), (self.ssem, self.rsem) = outs, scratch

    def attach(self, ref):
        self.src = ref

    def copy(self):
        c = self.c
        return remote(self.src.at[1 - c], self.out.at[c], self.ssem, self.rsem, {"ctx": 1 - c})

    def start(self):
        self.copy().start()
        self.out[self.c] = self.src[self.c]

    def end(self):
        self.copy().wait()


class CtxSum(Job):
    uses_ctx = True

    def __init__(self, full, n, hooks, keep=False, name=None):
        self.n, self.hooks, self.name = n, hooks, name
        shape = (n, full.shape[0] // (2 * n), full.shape[1])
        self.ins = [] if name else [(full.reshape(n, 2, *shape[1:]), HBM_SPEC)]
        self.keep = keep
        self.outs = [] if keep else [(jax.ShapeDtypeStruct(shape, BF16), VMEM_SPEC)]
        self.scratch = [VMEM(shape, BF16), DMA((n,)), DMA((n,)), DMA((n,))]
        if keep and not name:
            self.scratch.append(VMEM(shape, BF16))

    def refs(self, ins, outs, scratch):
        if not self.name:
            (self.full,) = ins
        self.got, self.ssem, self.rsem, self.near = scratch[:4]
        if not (self.keep and self.name):
            self.out = scratch[4] if self.keep else outs[0]

    def attach(self, ref):
        self.full = ref.reshape(self.n, 2, ref.shape[0] // (2 * self.n), ref.shape[1])
        if self.keep:
            self.out = self.full.at[:, self.c]

    def order(self):
        return (0, 3, 1, 2) if self.n == 4 else range(self.n)

    def copy(self, k):
        return remote(
            self.full.at[k, 1 - self.c], self.got.at[k], self.ssem.at[k], self.rsem.at[k],
            {"ctx": 1 - self.c},
        )

    def load(self, k):
        return pltpu.make_async_copy(self.full.at[k, self.c], self.out.at[k], self.near.at[k])

    def start(self):
        for k in self.order():
            self.copy(k).start()
        for k in self.order():
            if not self.name:
                self.load(k).start()

    def add(self, k):
        if not self.name:
            self.load(k).wait()
        self.copy(k).wait_recv()
        mine = self.full[k, self.c] if self.name else self.out[k]
        self.out[k] = (mine.astype(F32) + self.got[k].astype(F32)).astype(BF16)

    def steps(self):
        per = -(-self.n // len(self.hooks))
        return [
            (self.hooks[i // per], functools.partial(self.add, k))
            for i, k in enumerate(self.order())
        ]

    def end(self):
        for k in range(self.n):
            self.copy(k).wait_send()


class FsdpSum(Job):
    uses_fsdp = True

    def __init__(self, rows, n, hooks, source=None, sends=(), spread=True, direct=False, name=None):
        self.name = name
        self.n, self.hooks, self.source, self.sends = n, hooks, source, sends
        self.relays = n == 4 and not direct
        self.spread = self.uses_ctx = spread
        shape = rows.shape
        self.ins = [] if source or name else [(rows, VMEM_SPEC)]
        result = (2, *shape[1:]) if spread else shape[1:]
        self.outs = [(jax.ShapeDtypeStruct(result, BF16), VMEM_SPEC)]
        self.rows = shape[1]
        self.ch = chunks_of(self.rows)
        self.scratch = [
            VMEM(shape, BF16), VMEM((2, *shape[1:]), BF16),
            DMA((n, self.ch)), DMA((n, self.ch)), DMA((2, self.ch)), DMA((2, self.ch)),
            DMA((self.ch,)), DMA((self.ch,)),
        ]

    def refs(self, ins, outs, scratch):
        if not (self.name or self.source):
            self.src = ins[0]
        (self.out,) = outs
        (self.got, self.via, self.ssem, self.rsem, self.via_send, self.via_recv, self.x_send,
         self.x_recv) = scratch

    def attach(self, ref):
        self.src = ref.reshape(self.n, self.rows, ref.shape[1])

    def cut(self, ref, ch):
        size = self.rows // self.ch
        return ref.at[pl.ds(ch * size, size)]

    def direct(self, d, ch):
        return remote(
            self.cut(self.src.at[d], ch), self.cut(self.got.at[self.z], ch),
            self.ssem.at[d, ch], self.rsem.at[self.z, ch], {"fsdp": d},
        )

    def landed(self, frm, ch):
        block = self.cut(self.got.at[frm], ch)
        return remote(block, block, self.ssem.at[frm, ch], self.rsem.at[frm, ch], {"fsdp": frm})

    def to_relay(self, d, ch):
        return remote(
            self.cut(self.src.at[d], ch), self.cut(self.via.at[0], ch),
            self.via_send.at[0, ch], self.via_recv.at[0, ch], {"fsdp": 2 if d == 0 else 1},
        )

    def relayed(self, d, ch):
        return remote(
            self.cut(self.via.at[1], ch), self.cut(self.got.at[self.z], ch),
            self.via_send.at[1, ch], self.rsem.at[self.z, ch], {"fsdp": d},
        )

    def directly(self, d):
        if self.relays and d in (0, 3):
            return (self.z == 1) if d == 0 else (self.z == 2)
        return self.z != d

    def send(self, d):
        if self.relays and d in (0, 3):
            @pl.when(self.z == 3 - d)
            def _():
                for ch in range(self.ch):
                    self.to_relay(d, ch).start()

        @pl.when(self.directly(d))
        def _():
            for ch in range(self.ch):
                self.direct(d, ch).start()

    def order(self):
        return (0, 3, 1, 2) if self.n == 4 else range(self.n)

    def start(self):
        if not self.source:
            for d in self.order():
                self.send(d)

    def relay(self):
        for d, me in ((0, 2), (3, 1)) if self.relays else ():
            @pl.when(self.z == me)
            def _():
                for ch in range(self.ch):
                    self.to_relay(d, ch).wait_recv()
                    mine = self.cut(self.src.at[d], ch)[...].astype(F32)
                    theirs = self.cut(self.via.at[0], ch)[...].astype(F32)
                    self.cut(self.via.at[1], ch)[...] = (mine + theirs).astype(BF16)
                    self.relayed(d, ch).start()

    then = None

    def result(self, ch):
        return self.cut(self.out.at[self.c] if self.spread else self.out, ch)

    def over_x(self, ch):
        block = self.result(ch)
        return remote(block, block, self.x_send.at[ch], self.x_recv.at[ch], {"ctx": 1 - self.c})

    def total(self):
        n = self.n
        for ch in range(self.ch):
            mine = self.cut(self.src.at[self.z], ch)
            if self.relays:
                near = (self.z + 1) % 4
                last = jnp.where(self.z == 0, 2, jnp.where(self.z == 3, 1, (self.z + 3) % 4))
                first = jnp.where(self.z == 3, 2, near)
                inner = (self.z == 1) | (self.z == 2)
                self.landed(first, ch).wait_recv()
                self.landed(last, ch).wait_recv()
                part = (
                    mine[...].astype(F32)
                    + self.cut(self.got.at[first], ch)[...].astype(F32)
                    + self.cut(self.got.at[last], ch)[...].astype(F32)
                )
                block = self.result(ch)

                @pl.when(inner)
                def _():
                    middle = (self.z + 2) % 4
                    self.landed(middle, ch).wait_recv()
                    block[...] = (part + self.cut(self.got.at[middle], ch)[...].astype(F32)).astype(BF16)

                @pl.when(jnp.logical_not(inner))
                def _():
                    block[...] = part.astype(BF16)
            else:
                part = mine[...].astype(F32)
                for k in range(1, n):
                    frm = (self.z + k) % n
                    self.landed(frm, ch).wait_recv()
                    part += self.cut(self.got.at[frm], ch)[...].astype(F32)
                self.result(ch)[...] = part.astype(BF16)
            if self.spread:
                self.over_x(ch).start()
            elif self.then is not None:
                self.then(ch)

    def steps(self):
        out = [
            (self.sends[i * len(self.sends) // self.n], functools.partial(self.send, d))
            for i, d in enumerate(self.order())
            if self.sends
        ]
        return out + [(self.hooks[0], self.relay), (self.hooks[1], self.total)]

    def end(self):
        for ch in range(self.ch):
            if self.spread:
                other = self.cut(self.out.at[1 - self.c], ch)
                remote(
                    other, other, self.x_send.at[ch], self.x_recv.at[ch], {"ctx": 1 - self.c}
                ).wait_recv()
                self.over_x(ch).wait_send()
            for d in range(self.n):
                if self.relays and d in (0, 3):
                    @pl.when(self.z == 3 - d)
                    def _():
                        self.to_relay(d, ch).wait_send()

                    @pl.when(self.z == (2 if d == 0 else 1))
                    def _():
                        self.relayed(d, ch).wait_send()

                @pl.when(self.directly(d))
                def _():
                    self.direct(d, ch).wait_send()


class CtxAdd(Job):
    uses_ctx = True

    def __init__(self, rows, hook, source=None):
        self.hook, self.source = hook, source
        self.ins = [] if source else [(rows, VMEM_SPEC)]
        self.outs = [(jax.ShapeDtypeStruct(rows.shape, BF16), VMEM_SPEC)]
        self.rows = rows.shape[0]
        self.ch = chunks_of(self.rows)
        self.scratch = [VMEM(rows.shape, BF16), DMA((self.ch,)), DMA((self.ch,))]

    def refs(self, ins, outs, scratch):
        self.src = self.source.out if self.source else ins[0]
        (self.out,) = outs
        self.got, self.ssem, self.rsem = scratch
        if self.source:
            self.source.then = self.send

    def cut(self, ref, ch):
        size = self.rows // self.ch
        return ref.at[pl.ds(ch * size, size)]

    def copy(self, ch):
        return remote(
            self.cut(self.src, ch), self.cut(self.got, ch), self.ssem.at[ch], self.rsem.at[ch],
            {"ctx": 1 - self.c},
        )

    def send(self, ch):
        self.copy(ch).start()

    def start(self):
        if not self.source:
            for ch in range(self.ch):
                self.send(ch)

    def add(self):
        for ch in range(self.ch):
            self.copy(ch).wait_recv()
            mine, theirs = self.cut(self.src, ch)[...], self.cut(self.got, ch)[...]
            self.cut(self.out, ch)[...] = (mine.astype(F32) + theirs.astype(F32)).astype(BF16)

    def steps(self):
        return [(self.hook, self.add)]

    def end(self):
        for ch in range(self.ch):
            self.copy(ch).wait_send()


class Background:
    def __init__(self, jobs):
        self.jobs = jobs
        self.todo = []
        for job in jobs:
            if job.start_hook is not None:
                self.todo.append((job.start_hook, job.start))
            self.todo += job.steps()
        self.ended = []

    def start(self):
        for job in self.jobs:
            if job.start_hook is None:
                job.start()

    def at(self, hook):
        for when, function in self.todo:
            if when == hook:
                function()

    def phase(self, tag):
        return Phase(self, tag)

    def end(self, jobs=None):
        for job in self.jobs if jobs is None else jobs:
            if job not in self.ended:
                self.ended.append(job)
                job.end()


class Phase:
    def __init__(self, whole, tag):
        self.whole, self.tag = whole, tag
        self.prepare = lambda: None

    def at(self, hook):
        self.whole.at((self.tag, hook))

    def loop(self, b, count=4, base=0):
        for k in range(count):
            if any(when == (self.tag, base + k) for when, _ in self.whole.todo):
                @pl.when(b == k)
                def _():
                    self.at(base + k)


class Links:
    def __init__(self, send, recv, sib, peer):
        self.send, self.recv, self.sib, self.peer = send, recv, sib, peer

    def make(self, kind, s, src, dst, other):
        return pltpu.make_async_remote_copy(
            src_ref=src,
            dst_ref=dst,
            send_sem=self.send.at[kind, s],
            recv_sem=self.recv.at[kind, s],
            device_id={"tp": other},
            device_id_type=pl.DeviceIdType.MESH,
        )


def statistics(rows):
    mean = jnp.mean(rows, axis=-1, keepdims=True)
    centred = rows - mean
    inverse = lax.rsqrt(jnp.mean(centred * centred, axis=-1, keepdims=True) + EPS)
    return centred * inverse, inverse


def norm_back(rows, d_out, gain):
    unit, inverse = statistics(rows)
    e = d_out * gain
    back = inverse * (
        e
        - jnp.mean(e, axis=-1, keepdims=True)
        - unit * jnp.mean(e * unit, axis=-1, keepdims=True)
    )
    d_gain = jnp.sum(d_out * unit, axis=0, keepdims=True)
    d_shift = jnp.sum(d_out, axis=0, keepdims=True)
    return back, d_gain, d_shift


def rows_of(ref, b):
    block = ref[b]
    return block.reshape(block.shape[0] * block.shape[1], block.shape[2])


class Gather:
    def __init__(self, links, out):
        self.links, self.out = links, out

    def near(self, s):
        return self.links.make(3, s, self.out.at[2 + s, 0], self.out.at[2 + s, 1], self.links.sib)

    def across(self, s):
        return self.links.make(4, s, self.out.at[2 + s, 0], self.out.at[s, 0], self.links.peer)

    def onward(self, s):
        return self.links.make(5, s, self.out.at[s, 0], self.out.at[s, 1], self.links.sib)

    def start(self, rows):
        for s in range(2):
            self.out[2 + s, 0] = rows(s)
            self.near(s).start()
            self.across(s).start()

    def need(self, b):
        s = b % 2

        @pl.when(b >= 2)
        def _():
            self.near(s).wait_recv()

        @pl.when(b < 2)
        def _():
            self.across(s).wait_recv()
            self.onward(s).start()
            self.onward(s).wait_recv()

    def end(self):
        for s in range(2):
            for copy in (self.near(s), self.across(s), self.onward(s)):
                copy.wait_send()


class Scatter:
    def __init__(self, links, part, sent, got, own):
        self.links, self.part, self.sent, self.got, self.own = links, part, sent, got, own

    def copy(self, kind, s):
        other = self.links.peer if kind == 1 else self.links.sib
        return self.links.make(kind, s, self.sent.at[kind, s], self.got.at[kind, s], other)

    def block(self, b):
        s = b % 2
        half = self.part.shape[0] // 2

        @pl.when(b < 2)
        def _():
            self.sent[0, s] = self.part[half:].astype(BF16)
            first = self.copy(0, s)
            first.start()
            first.wait_recv()
            self.sent[1, s] = (self.part[:half] + self.got[0, s].astype(F32)).astype(BF16)
            self.copy(1, s).start()

        @pl.when(b >= 2)
        def _():
            self.sent[2, s] = self.part[half:].astype(BF16)
            self.copy(2, s).start()
            self.own[s] = self.part[:half]

    def total(self, s):
        self.copy(2, s).wait_recv()
        self.copy(1, s).wait_recv()
        return self.own[s] + self.got[2, s].astype(F32) + self.got[1, s].astype(F32)

    def end(self):
        for s in range(2):
            for kind in range(3):
                self.copy(kind, s).wait_send()


def scatter_scratch(half, width):
    local = [VMEM((2 * half, width), F32), VMEM((2, half, width), F32)]
    linked = [
        VMEM((3, 2, half, width), BF16), VMEM((3, 2, half, width), BF16), DMA((6, 2)), DMA((6, 2))
    ]
    return local + linked + linked


def scatter_refs(scratch, phase):
    part, own = scratch[:2]
    sent, got, send, recv = scratch[2 + 4 * phase : 6 + 4 * phase]
    return part, sent, got, own, send, recv


def pair_tile(pair, h):
    tile = pair if h % 2 == 0 else pltpu.roll(pair, HD, 1)
    return tile


def attention_phase(
    background, heads, base,
    own_first, params, key_extra, resid, near, far,
    first, second, middle, q_out, k_out, v_out, mixed_out,
    part, sent, got, own, send, recv, weight, load,
):
    t, sib, peer = partners()
    links = Links(send, recv, sib, peer)
    scatter = Scatter(links, part, sent, got, own)
    width = heads * HD
    gather = Gather(links, first)
    gather.start(lambda s: own_first[s])
    background.prepare()
    loads = Loads(load)
    loads.add(near, far, weight)
    loads.wait()
    weight = whole(weight)
    out_bias, gain, shift = (params[base + k : base + k + 1, :] for k in (2, 3, 4))
    q_bias = params[base + 6 : base + 7, :width]
    v_bias = params[base + 6 : base + 7, width : 2 * width]
    half = first.shape[2]
    rows = 2 * half
    lane = lax.broadcasted_iota(jnp.int32, (rows, LANES), 1)
    head_lane = lane < HD
    q_extra = jnp.where(lane < HD + 2, 1.0, 0.0).astype(BF16)
    v_extra = jnp.where(lane < HD + 3, 1.0, 0.0).astype(BF16)

    def project(j, carry):
        b = (j + 2) % 4
        gather.need(b)
        x = rows_of(first, b)
        y = mm(x, weight[:, : 3 * width])
        q = ((y[:, :width] + q_bias).astype(BF16) * SCALE).astype(BF16)
        k = y[:, width : 2 * width].astype(BF16)
        v = (y[:, 2 * width :] + v_bias).astype(BF16)
        g, s = b // 2, b % 2
        mine = jnp.where(g == 1, t, peer)
        other = mine + 1 - 2 * (mine % 2)
        extra = jnp.concatenate([key_extra[mine, s], key_extra[other, s]], axis=0)
        at = pl.ds(pl.multiple_of(b * rows, rows), rows)
        for h in range(heads):
            cut = slice(LANES * (h // 2), LANES * (h // 2 + 1))
            q_out[h, at, :] = jnp.where(head_lane, pair_tile(q[:, cut], h), q_extra)
            k_out[h, at, :] = jnp.where(head_lane, pair_tile(k[:, cut], h), extra)
            v_out[h, at, :] = jnp.where(head_lane, pair_tile(v[:, cut], h), v_extra)
        background.loop(j, 4, 20)
        return carry

    lax.fori_loop(0, 4, project, 0)
    background.at(0)

    def attend(b, carry):
        at = pl.ds(pl.multiple_of(b * rows, rows), rows)
        outs = []
        for h in range(heads):
            q = q_out[h, at, :]
            scores = mm_nt(q, k_out[h])
            top = jnp.max(scores, axis=-1, keepdims=True)
            weights = jnp.exp(scores - top).astype(BF16)
            summed = mm(weights, v_out[h])
            total = summed[:, HD : HD + 1]
            outs.append(summed / total)
            log_total = -(top + jnp.log(total))
            high = log_total.astype(BF16).astype(F32)
            rest = log_total - high
            mid = rest.astype(BF16).astype(F32)
            low = rest - mid
            tail = jnp.where(lane == HD + 2, high, jnp.where(lane == HD + 3, mid, low))
            q_out[h, at, :] = jnp.where(
                (lane >= HD + 2) & (lane < HD + 5), tail.astype(BF16), q
            )
        tiles = [
            jnp.where(head_lane, outs[h], pltpu.roll(outs[h + 1], HD, 1))
            for h in range(0, heads, 2)
        ]
        mixed = jnp.concatenate(tiles, axis=1).astype(BF16)
        mixed_out[at, :] = mixed
        part[...] = mm_nt(mixed, weight[:, 3 * width :])
        scatter.block(b)
        background.loop(b, 4, 1)
        return carry

    lax.fori_loop(0, 4, attend, 0)
    for s in range(2):
        mid = resid[s].astype(F32) + (scatter.total(s) + out_bias)
        middle[s] = mid
        unit, _ = statistics(mid)
        second[s] = (unit * gain + shift).astype(BF16)
        background.at(5 + s)
    gather.end()
    scatter.end()


def mlp_phase(
    background, last, base,
    own_second, params, middle, near_e, far_e, near_r, far_r,
    second, active_out, slope_out, resid, nxt,
    part, sent, got, own, send, recv, expand, reduce, load,
):
    t, sib, peer = partners()
    links = Links(send, recv, sib, peer)
    scatter = Scatter(links, part, sent, got, own)
    half = second.shape[2]
    rows = 2 * half
    gather = Gather(links, second)
    gather.start(lambda s: own_second[s])
    loads = Loads(load)
    loads.add(near_e, far_e, expand)
    loads.add(near_r, far_r, reduce)
    loads.wait()
    expand, reduce = whole(expand), whole(reduce)
    hidden = expand.shape[1]
    out_bias = params[base + 5 : base + 6, :]
    following = 0 if last else base + 8
    gain, shift = (params[following + k : following + k + 1, :] for k in (0, 1))
    step = 256

    def block(j, carry):
        b = (j + 2) % 4
        gather.need(b)
        at = pl.ds(pl.multiple_of(b * rows, rows), rows)
        x = rows_of(second, b)
        for n in range(0, hidden, step):
            before = mm(x, expand[:, n : n + step]) + params[base + 7 : base + 8, n : n + step]
            cdf = 0.5 * (1.0 + lax.erf(before * INV_SQRT2))
            active_out[at, n : n + step] = (before * cdf).astype(BF16)
            slope = cdf + before * (jnp.exp(before * before * -0.5) * INV_SQRT_2PI)
            slope_out[at, n : n + step] = slope.astype(BF16)
        part[...] = mm_nt(active_out[at, :], reduce[...])
        scatter.block(b)
        background.loop(j, 4, 1)
        return carry

    lax.fori_loop(0, 4, block, 0)
    for s in range(2):
        res = middle[s] + (scatter.total(s) + out_bias)
        if last:
            nxt[s] = res.astype(BF16)
        else:
            resid[s] = res
            unit, _ = statistics(res)
            nxt[s] = (unit * gain + shift).astype(BF16)
        background.at(5 + s)
    gather.end()
    scatter.end()


def token_product(left, right, outs, offset=0):
    depth = left.shape[-1]
    total = left.shape[0] * left.shape[1] * left.shape[2]
    step = 256

    def body(j, carry):
        cut = pl.ds(pl.multiple_of(j * step, step), step)
        x = left[:, :, :, cut].reshape(total, step)
        product = mm_tn(x, right[...]).astype(BF16)
        width = right.shape[-1] // len(outs)
        for k, out in enumerate(outs):
            out[cut, offset : offset + width] = product[:, k * width : (k + 1) * width]
        return carry

    lax.fori_loop(0, depth // step, body, 0)


def mlp_back_phase(
    background, base,
    ready, active, slope, second, middle, carry_in, params, near_e, far_e, near_r, far_r,
    expand_grad, reduce_left, reduce_right, carry_out, vectors,
    part, sent, got, own, send, recv, grad, d_before, expand, reduce, load,
):
    t, sib, peer = partners()
    links = Links(send, recv, sib, peer)
    scatter = Scatter(links, part, sent, got, own)
    gather = Gather(links, grad)
    gather.start(lambda s: carry_in[s].astype(BF16))
    loads = Loads(load)
    loads.add(near_e, far_e, expand)
    loads.add(near_r, far_r, reduce)
    loads.wait()
    expand = whole(expand)
    reduce = [whole(part) for part in reduce]
    wide = reduce[0].shape[1]
    gain = params[base + 3 : base + 4, :]
    half = grad.shape[2]
    rows = 2 * half
    hidden = active.shape[1]
    step = 256
    vectors[...] = jnp.zeros_like(vectors)

    def block(j, carry):
        b = (j + 2) % 4
        gather.need(b)
        at = pl.ds(pl.multiple_of(b * rows, rows), rows)
        x = rows_of(grad, b)
        for n in range(0, hidden, step):
            d_act = mm(x, reduce[n // wide][:, n % wide : n % wide + step])
            d_bef = (d_act * slope[at, n : n + step].astype(F32)).astype(BF16)
            d_before[at, n : n + step] = d_bef
            vectors[4:5, n : n + step] += jnp.sum(d_bef.astype(F32), axis=0, keepdims=True)
        part[...] = mm_nt(d_before[at, :], expand[...])
        scatter.block(b)
        background.loop(j)
        return carry

    lax.fori_loop(0, 4, block, 0)
    token_product(grad, active, (reduce_left, reduce_right))
    background.at(4)

    def finish(s):
        back, d_gain, d_shift = norm_back(middle[s], scatter.total(s), gain)
        carry = carry_in[s].astype(F32)
        mid = carry + back
        carry_out[s] = mid
        low = mid.astype(BF16)
        vectors[0:1, :] += d_gain
        vectors[1:2, :] += d_shift
        vectors[2:3, :] += jnp.sum(low.astype(F32), axis=0, keepdims=True)
        vectors[3:4, :] += jnp.sum(carry.astype(BF16).astype(F32), axis=0, keepdims=True)

    finish(0)
    background.at(5)
    ready.wait()
    token_product(second, d_before, (expand_grad,))
    finish(1)
    background.at(6)
    gather.end()
    scatter.end()


def attention_back_phase(
    background, heads, base,
    ready, weight_grad, mixed, q_in, k_in, v_in, first, carry_in, resid, params, near, far,
    carry_out, vectors,
    part, sent, got, own, send, recv, grad, d_joint, d_key, d_value, weight, load,
):
    t, sib, peer = partners()
    links = Links(send, recv, sib, peer)
    scatter = Scatter(links, part, sent, got, own)
    width = heads * HD
    gather = Gather(links, grad)
    gather.start(lambda s: carry_in[s].astype(BF16))
    loads = Loads(load)
    loads.add(near, far, weight)
    loads.wait()
    weight = whole(weight)
    gain = params[base : base + 1, :]
    half = grad.shape[2]
    rows = 2 * half
    lane = lax.broadcasted_iota(jnp.int32, (rows, LANES), 1)
    head_lane = lane < HD
    vectors[...] = jnp.zeros_like(vectors)
    d_joint = d_joint.at[:, : 3 * width]
    d_key[...] = jnp.zeros_like(d_key)
    d_value[...] = jnp.zeros_like(d_value)

    def pairs(tiles):
        return jnp.concatenate(
            [
                jnp.where(head_lane, tiles[h], pltpu.roll(tiles[h + 1], HD, 1))
                for h in range(0, heads, 2)
            ],
            axis=1,
        )

    def attend(j, carry):
        b = (j + 2) % 4
        gather.need(b)
        at = pl.ds(pl.multiple_of(b * rows, rows), rows)
        d_mixed = mm(rows_of(grad, b), weight[:, 3 * width :]).astype(BF16)
        product = d_mixed.astype(F32) * mixed[at, :].astype(F32)
        d_queries = []
        for h in range(heads):
            cut = slice(LANES * (h // 2), LANES * (h // 2 + 1))
            keep = head_lane if h % 2 == 0 else lane >= HD
            delta = -jnp.sum(jnp.where(keep, product[:, cut], 0.0), axis=-1, keepdims=True)
            high = delta.astype(BF16).astype(F32)
            rest = delta - high
            mid = rest.astype(BF16).astype(F32)
            low = rest - mid
            tail = jnp.where(
                lane == HD,
                high,
                jnp.where(lane == HD + 1, mid, jnp.where(lane == HD + 2, low, 0.0)),
            ).astype(BF16)
            d_o = jnp.where(head_lane, pair_tile(d_mixed[:, cut], h), tail)
            q = q_in[h, at, :]
            probs = jnp.exp(mm_nt(k_in[h], q))
            d_value[h] += mm(probs.astype(BF16), d_o)
            d_raw = (probs * mm_nt(v_in[h], d_o)).astype(BF16)
            d_key[h] += mm(d_raw, q)
            d_queries.append(mm_tn(d_raw, k_in[h]) * SCALE)
        d_joint[at, :width] = pairs(d_queries).astype(BF16)
        background.loop(j)
        return carry

    lax.fori_loop(0, 4, attend, 0)

    def gather_heads(b, carry):
        at = pl.ds(pl.multiple_of(b * rows, rows), rows)
        d_joint[at, width : 2 * width] = pairs([d_key[h, at, :] for h in range(heads)]).astype(BF16)
        d_joint[at, 2 * width : 3 * width] = pairs([d_value[h, at, :] for h in range(heads)]).astype(BF16)
        return carry

    lax.fori_loop(0, 4, gather_heads, 0)

    def project(b, carry):
        at = pl.ds(pl.multiple_of(b * rows, rows), rows)
        d_rows = d_joint[at, :]
        sums = jnp.sum(d_rows.astype(F32), axis=0, keepdims=True)
        vectors[2:3, :width] += sums[:, :width]
        vectors[2:3, width : 2 * width] += sums[:, 2 * width :]
        part[...] = mm_nt(d_rows, weight[:, : 3 * width])
        scatter.block(b)
        background.loop(b, 4, 4)
        return carry

    def out_product():
        token_product(grad, mixed, (weight if weight_grad is None else weight_grad,), 3 * width)
        background.at(8)

    def joint_product():
        for copy in ready:
            copy.wait()
        token_product(first, d_joint, (weight if weight_grad is None else weight_grad,))
        background.at(11)

    if weight_grad is not None:
        joint_product()
        out_product()
    lax.fori_loop(0, 4, project, 0)
    if weight_grad is None:
        out_product()

    def finish(s):
        back, d_gain, d_shift = norm_back(resid[s].astype(F32), scatter.total(s), gain)
        carry = carry_in[s] + back
        carry_out[s] = carry.astype(carry_out.dtype)
        vectors[0:1, :] += d_gain
        vectors[1:2, :] += d_shift

    finish(0)
    background.at(9)
    if weight_grad is None:
        joint_product()
    finish(1)
    background.at(10)
    gather.end()
    scatter.end()


def forward_kernel(jobs, entry, urgent, heads, last, base, refs):
    ins, outs, scratch = refs
    first, own_rows, middle, q, k, v, mixed, second, active, slope, out, rows = outs
    attn_w, attn_load, expand, reduce, mlp_load = scratch[10:15]
    background = Background(jobs)
    entry_barrier(jobs)
    background.start()
    phase = background.phase("A")
    expand_job, reduce_job = urgent
    if entry:
        (key_extra,) = ins
        params_job, tokens, attn = entry
        params, resid, near_a, far_a = params_job.out, tokens.out, attn.near, attn.far
        own_first = scratch[15]
        tokens.start()
        params_job.start()
        attn.start()
        params_job.finish()
        attn.relay()
        expand_job.start()
        tokens.end()
        for s in range(2):
            unit, _ = statistics(resid[s].astype(F32))
            own_first[s] = (unit * params[0:1, :] + params[1:2, :]).astype(BF16)

        def prepare():
            for off in attn.sources()[:4]:
                attn.take(off)
            expand_job.relay()
            reduce_job.start()
            for off in attn.sources()[4:]:
                attn.take(off)
            params_job.end()
            attn.end()

        phase.prepare = prepare
        background.ended += entry
        near_e, far_e = expand_job.near, expand_job.far
    else:
        own_first, params, key_extra, resid, near_a, far_a, near_e = ins
        far_e = expand_job.far
    attention_phase(
        phase, heads, base,
        own_first, params, key_extra, resid, near_a, far_a,
        first, own_rows, middle, q, k, v, mixed, *scatter_refs(scratch, 0), attn_w, attn_load,
    )
    background.end(urgent)
    mlp_phase(
        background.phase("M"), last, base,
        own_rows, params, middle, near_e, far_e, reduce_job.near, reduce_job.far,
        second, active, slope, out, rows, *scatter_refs(scratch, 1), expand, reduce, mlp_load,
    )
    background.end()


def backward_kernel(jobs, heads, base, last, refs):
    ins, outs, scratch = refs
    carry_out = scratch[-1]
    if last:
        scratch = scratch[:-1]
    (active, slope, middle, carry_in, params, mixed, q, k, v, resid,
     near_e, far_e, near_r, far_r, near_a, far_a, second, first) = ins
    (carry_mid, grad_rows, attn_rows, d_before, held, expand, reduce_left, reduce_right, mlp_load,
     d_key, d_value, attn_w, attn_load, held_load) = scratch[10:]
    if last:
        mlp_vec, attn_vec = outs
    else:
        mlp_vec, attn_vec, carry_out, attn_grad = outs
    left_grad, right_grad = whole(reduce_left), whole(reduce_right)
    named = dict(
        expand=whole(expand), left=left_grad, right=right_grad, attn=whole(grad_rows), carry=carry_out,
        vectors=(attn_vec, mlp_vec),
    )
    for job in jobs:
        if job.name:
            job.attach(named[job.name])
    for job in jobs:
        if isinstance(job, FsdpSum) and job.source:
            job.src = job.source.out
    background = Background(jobs)
    entry_barrier(jobs)
    background.start()
    second_load = pltpu.make_async_copy(second, held, held_load.at[0])
    second_load.start()
    mlp_back_phase(
        background.phase("M"), base,
        second_load, active, slope, held, middle, carry_in, params, near_e, far_e, near_r, far_r,
        whole(expand), left_grad, right_grad, carry_mid, mlp_vec,
        *scatter_refs(scratch, 0), grad_rows, d_before, expand, (reduce_left, reduce_right), mlp_load,
    )
    first_load = pltpu.make_async_copy(first, held, held_load.at[1])
    first_load.start()
    attention_back_phase(
        background.phase("A"), heads, base,
        [first_load], whole(grad_rows) if last else None, mixed, q, k, v, held, carry_mid, resid, params, near_a, far_a,
        carry_out, attn_vec,
        *scatter_refs(scratch, 1), attn_rows, d_before, d_key, d_value, attn_w, attn_load,
    )
    copies = []
    if not last:
        copies = [pltpu.make_async_copy(whole(attn_w), attn_grad, attn_load.at[0])]
        copies[0].start()
    tail = background.phase("L")
    for hook in range(8):
        tail.at(hook)
    background.end()
    for copy in copies:
        copy.wait()


class VectorSum(Job):
    uses_tp = uses_ctx = uses_fsdp = True

    def __init__(self, vectors, n, hooks):
        self.n, self.hooks, self.name = n, hooks, "vectors"
        dim = vectors[0].shape[1]
        self.ins = [(v, VMEM_SPEC) for v in vectors]
        self.outs = [(jax.ShapeDtypeStruct((16, dim), F32), VMEM_SPEC)]
        self.scratch = [
            VMEM((4, 16, dim), F32), VMEM((3 + n, 16, dim), F32), DMA((3 + n,)), DMA((3 + n,))
        ]

    def refs(self, ins, outs, scratch):
        self.former = ins
        (self.out,) = outs
        self.held, self.got, self.ssem, self.rsem = scratch
        t, self.sib, self.peer = partners()

    def attach(self, refs):
        self.vectors = (*refs, *self.former)

    def copy(self, k):
        if k == 0:
            to = {"ctx": 1 - self.c}
        elif k < 3:
            to = {"tp": self.sib if k == 1 else self.peer}
        else:
            to = {"fsdp": (self.z + k - 2) % self.n}
        return remote(
            self.held.at[min(k, 3)], self.got.at[k], self.ssem.at[k], self.rsem.at[k], to
        )

    def start(self):
        for l in range(LAYERS):
            attn, mlp = self.vectors[2 * l], self.vectors[2 * l + 1]
            for row, (ref, index) in enumerate(
                ((attn, 0), (attn, 1), (mlp, 2), (mlp, 0), (mlp, 1), (mlp, 3), (attn, 2), (mlp, 4))
            ):
                self.held[0, 8 * l + row : 8 * l + row + 1, :] = ref[index : index + 1, :]
        self.copy(0).start()

    def fold(self, k):
        self.copy(k).wait_recv()
        came = self.got[k]
        if k > 0:
            row = lax.broadcasted_iota(jnp.int32, came.shape, 0)
            came = jnp.where(row % 8 < 6, came, 0.0)
        self.held[k + 1] = self.held[k] + came
        if k < 2:
            self.copy(k + 1).start()
        else:
            for j in range(1, self.n):
                self.copy(2 + j).start()

    def finish(self):
        total = self.held[3]
        for j in range(1, self.n):
            self.copy(2 + j).wait_recv()
            total += self.got[2 + j]
        self.out[...] = total

    def steps(self):
        return [(self.hooks[k], functools.partial(self.fold, k)) for k in range(3)] + [
            (self.hooks[3], self.finish)
        ]

    def end(self):
        for k in range(2 + self.n):
            self.copy(k).wait_send()


def finish_kernel(
    attn_0, attn_1, expand_0, expand_1, left_0, left_1, right_0, right_1, vectors,
    joint, out, expand, reduce, wide, query, value, hidden,
):
    z = lax.axis_index("fsdp")
    half = attn_0.shape[1]
    width = joint.shape[3]
    shard = 2 * half
    layers = ((attn_0, expand_0, left_0, right_0), (attn_1, expand_1, left_1, right_1))
    for l, (a, e, left, right) in enumerate(layers):
        rows = a[...].reshape(shard, a.shape[2]).astype(F32)
        for k in range(3):
            joint[l, k] = rows[:, k * width : (k + 1) * width]
        out[l] = rows[:, 3 * width :].T
        expand[l] = e[...].reshape(shard, e.shape[2]).astype(F32)
        part = left.shape[-1]
        for k, r in enumerate((left, right)):
            reduce[l, k * part : (k + 1) * part, :] = r[...].reshape(shard, part).astype(F32).T
    cut = query.shape[2]
    heads = query.shape[1]
    dim = vectors.shape[1]
    own = pltpu.roll(vectors[...], lax.rem(dim - z * shard, dim), 1)
    by_cut = pltpu.roll(vectors[...], lax.rem(dim - z * cut, dim), 1)
    for l in range(LAYERS):
        for k in range(6):
            wide[k, l : l + 1, :] = own[8 * l + k : 8 * l + k + 1, :shard]
        for row, base, ref in ((6, 0, query), (6, heads * HD, value), (7, 0, hidden)):
            for h in range(ref.shape[1]):
                at = base + h * HD
                ref[l, h : h + 1, :] = by_cut[8 * l + row : 8 * l + row + 1, at : at + cut]


def whole(ref):
    return ref.reshape(ref.shape[0] * ref.shape[1] * ref.shape[2], ref.shape[3])


def call(kernel, name, outs, scratch, collective_id, flops, args, jobs=()):
    args = [
        (a, spec)
        for arg in args
        for a, spec in ([(arg, VMEM_SPEC)] if not isinstance(arg, tuple) else [(a, HBM_SPEC) for a in arg])
    ]
    ins = args + [pair for job in jobs for pair in job.ins]
    results = [o if isinstance(o, tuple) else (o, VMEM_SPEC) for o in outs] + [pair for job in jobs for pair in job.outs]
    scratch = list(scratch)
    n_scratch = len(scratch)
    for job in jobs:
        scratch += job.scratch

    def body(*refs):
        refs = list(refs)
        in_refs = refs[: len(ins)]
        out_refs = refs[len(ins) : len(ins) + len(results)]
        scratch_refs = refs[len(ins) + len(results) :]
        a, b, c = len(args), len(outs), n_scratch
        for job in jobs:
            ends = a + len(job.ins), b + len(job.outs), c + len(job.scratch)
            job.bind(in_refs[a : ends[0]], out_refs[b : ends[1]], scratch_refs[c : ends[2]])
            a, b, c = ends
        kernel(jobs, (in_refs[: len(args)], out_refs[: len(outs)], scratch_refs[:n_scratch]))

    size = sum(a.size * a.dtype.itemsize for a, _ in ins) + sum(
        math.prod(o.shape) * o.dtype.itemsize for o, _ in results
    )
    return pl.pallas_call(
        body,
        name=name,
        out_shape=tuple(o for o, _ in results),
        in_specs=[spec for _, spec in ins],
        out_specs=tuple(spec for _, spec in results),
        scratch_shapes=scratch,
        compiler_params=pltpu.CompilerParams(
            collective_id=collective_id, has_side_effects=True, vmem_limit_bytes=VMEM_LIMIT
        ),
        cost_estimate=pl.CostEstimate(flops=flops, bytes_accessed=size, transcendentals=0),
    )(*[a for a, _ in ins])


def local(
    tokens, key_valid, first_gain, first_shift, joint_weight, query_bias, value_bias,
    out_weight, out_bias, second_gain, second_shift, expand_weight, expand_bias,
    reduce_weight, reduce_bias, cotangent,
):
    ctx_size = lax.axis_size("ctx")
    tp_size = lax.axis_size("tp")
    fsdp_size = lax.axis_size("fsdp")
    clips, half, dim = tokens.shape
    assert clips == ctx_size == 2 and tp_size == 4 and joint_weight.shape[0] == LAYERS
    c = lax.axis_index("ctx")
    shard = joint_weight.shape[1]
    width = joint_weight.shape[3]
    heads = width // HD
    hidden = expand_weight.shape[2]
    attn_w = jnp.concatenate(
        [joint_weight.transpose(0, 2, 1, 3), out_weight.transpose(0, 2, 1)[:, None]], axis=1
    )
    reduce_w = reduce_weight.transpose(0, 2, 1)

    valid = lax.dynamic_index_in_dim(key_valid, c, 0, keepdims=False)
    bias = jnp.where(valid == 1, 0.0, MASKED).astype(F32)
    bias = bias.reshape(ctx_size, tp_size, half, 1).transpose(1, 0, 2, 3)
    high = bias.astype(BF16).astype(F32)
    col = lax.broadcasted_iota(jnp.int32, (1, 1, 1, LANES), 3) - HD
    key_extra = jnp.where(
        col == 0, high, jnp.where(col == 1, bias - high, jnp.where((col >= 2) & (col < 5), 1.0, 0.0))
    ).astype(BF16)

    every = jax.ShapeDtypeStruct((4, 2, half, dim), BF16)
    own = jax.ShapeDtypeStruct((2, half, dim), F32)
    own_low = jax.ShapeDtypeStruct((2, half, dim), BF16)
    tiny = jax.ShapeDtypeStruct((8, LANES), F32)
    vec = jax.ShapeDtypeStruct((8, dim), F32)
    square = jax.ShapeDtypeStruct((dim, hidden), BF16)
    narrow = jax.ShapeDtypeStruct((dim, hidden // 2), BF16)
    count = 8 * half
    n = fsdp_size
    scratch = scatter_scratch(half, dim)

    def held(columns):
        return VMEM((n, 2, shard // 2, columns), BF16)

    attn_scratch = [held(4 * width), DMA((8,))]
    mlp_scratch = [held(hidden), held(hidden), DMA((4,))]

    entry = [
        ParamJob(
            [first_gain, first_shift, out_bias, second_gain, second_shift, reduce_bias],
            [query_bias, value_bias, expand_bias], n, dim,
        ).after("entry"),
        Exchange(tokens).after("entry"),
        OverFsdp(attn_w, 0, n, "entry", 2, ("none", "none", "none")).after("entry"),
    ]
    saved = []
    heads_shape = jax.ShapeDtypeStruct((heads, count, LANES), BF16)
    rows_width = jax.ShapeDtypeStruct((count, width), BF16)
    rows_hidden = jax.ShapeDtypeStruct((count, hidden), BF16)
    for l in range(LAYERS):
        last = l == LAYERS - 1
        if last:
            urgent = [
                OverCtx(expand_weight, l, near_e, n),
                OverFsdp(reduce_w, l, n, ("A", 22), 1, (("A", 23), ("A", 0), ("A", 1))),
            ]
            jobs = [*urgent, Exchange(cotangent).after(("M", 1))]
            begun, ins = [], [rows, params, key_extra, resid, (near_a, far_a, near_e)]
        else:
            urgent = [
                OverFsdp(expand_weight, l, n, "entry", 1, (("A", 21), ("A", 22), ("A", 0))).after("entry"),
                OverFsdp(reduce_w, l, n, ("A", 1), 1, (("A", 2), ("A", 2), ("A", 3))).after("entry"),
            ]
            jobs = [
                *entry,
                *urgent,
                OverFsdp(
                    attn_w, l + 1, n, ("A", 5), 1, (("M", 1), ("M", 1), ("M", 2))
                ).after(("A", 2)),
                OverFsdp(expand_weight, l + 1, n, ("M", 2)).after(("A", 5)),
            ]
            begun, ins = entry, [key_extra]
        (first, _, middle, q, k, v, mixed, second, active, slope, out, rows, *more) = call(
            lambda jobs, refs, base=8 * l, last=last, begun=begun, urgent=urgent: forward_kernel(
                jobs, begun, urgent, heads, last, base, refs
            ),
            f"forward_{l}",
            [every, own_low, own, heads_shape, heads_shape, heads_shape, rows_width, every,
             rows_hidden, rows_hidden, tiny if last else own, own_low],
            scratch + attn_scratch + mlp_scratch + ([] if last else [VMEM(own.shape, BF16)]), 1 + 2 * l,
            2 * count * dim * 4 * width + 16 * heads * count * count * HD + 4 * count * dim * hidden,
            ins, jobs,
        )
        if last:
            far_e, near_r, far_r, cot = more
        else:
            params, resid, near_a, far_a, near_e, far_e, near_r, far_r, *following = more
        weights = (near_e, far_e, near_r, far_r, near_a, far_a)
        saved.append((resid, first, q, k, v, mixed, middle, second, active, slope, weights))
        resid = out
        if not last:
            near_a, far_a, near_e = following

    carry = cot
    attn_grads, expand_grads, left_grads, right_grads, attn_vec, mlp_vec = (
        [None] * LAYERS for _ in range(6)
    )
    halves = jax.ShapeDtypeStruct((n, shard, hidden // 2), BF16)
    left_rows = jax.ShapeDtypeStruct((n, shard // 2, hidden // 2), BF16)
    square_rows = jax.ShapeDtypeStruct((n, shard // 2, hidden), BF16)
    attn_shape = jax.ShapeDtypeStruct((dim, 4 * width), BF16)
    attn_rows = jax.ShapeDtypeStruct((n, shard // 2, 4 * width), BF16)
    early = (("M", 4), ("M", 4), ("M", 5), ("M", 6))
    right_half = jax.ShapeDtypeStruct((shard, hidden // 2), BF16)
    for l in reversed(range(LAYERS)):
        resid, first, q, k, v, mixed, middle, second, active, slope, weights = saved[l]
        last = l == 0
        if last:
            attn_job = CtxSum(attn_full, n, early, keep=True)
            right_job = FsdpSum(
                halves, n, (("A", 3), ("A", 7)), spread=False, name="right"
            ).after(("M", 6))
            left_job = FsdpSum(
                halves, n, (("A", 7), ("L", 1)), spread=False, name="left"
            ).after(("A", 3))
            late = (("A", 4), ("A", 5), ("A", 6), ("A", 7))
            expand_job = CtxSum(square, n, late, keep=True, name="expand").after(("M", 6))
            final = (("L", 1), ("L", 1), ("L", 2), ("L", 2))
            final_job = CtxSum(attn_shape, n, final, keep=True, name="attn").after(("A", 8))
            jobs = [
                FsdpSum(expand_part, n, (("M", 2), ("M", 6))),
                attn_job,
                FsdpSum(attn_rows, n, (("A", 0), ("A", 3)), source=attn_job, sends=early),
                right_job,
                CtxAdd(right_half, ("L", 5), source=right_job),
                left_job,
                CtxAdd(right_half, ("L", 5), source=left_job),
                expand_job,
                FsdpSum(square_rows, n, (("L", 1), ("L", 4)), source=expand_job, sends=late),
                VectorSum(
                    [attn_vec[1], mlp_vec[1]], n, (("L", 3), ("L", 3), ("L", 3), ("L", 5))
                ).after(("A", 10)),
                final_job,
                FsdpSum(attn_rows, n, (("L", 4), ("L", 6)), source=final_job, sends=final),
                Exchange(own_low, name="carry").after(("A", 10)),
            ]
            outs = [vec, vec]
        else:
            right_job = FsdpSum(
                halves, n, (("A", 1), ("A", 6)), spread=False, name="right"
            ).after(("M", 4))
            left_job = CtxSum(narrow, n, (("A", 2),) * 4, keep=True, name="left").after(("M", 4))
            late = (("A", 6), ("A", 7), ("A", 8), ("A", 10))
            jobs = [
                Exchange(rows),
                left_job,
                FsdpSum(left_rows, n, (("A", 6), ("A", 8)), source=left_job, sends=(("A", 2),) * 4),
                right_job,
                CtxAdd(right_half, ("A", 10), source=right_job),
                CtxSum(square, n, late, name="expand").after(("M", 6)),
            ]
            outs = [vec, vec, own, (attn_shape, HBM_SPEC)]
        results = call(
            lambda jobs, refs, base=8 * l, last=last: backward_kernel(jobs, heads, base, last, refs),
            f"backward_{l}",
            outs,
            scratch
            + [
                VMEM(own.shape, F32), VMEM(every.shape, BF16), VMEM(every.shape, BF16), VMEM((count, hidden), BF16),
                VMEM(every.shape, BF16),
                held(hidden), held(hidden // 2), held(hidden // 2), DMA((6,)),
            ]
            + [VMEM((heads, count, LANES), F32), VMEM((heads, count, LANES), F32)]
            + attn_scratch
            + [DMA((2,))]
            + ([VMEM(own.shape, BF16)] if last else []),
            2 + 2 * l,
            4 * count * dim * 4 * width + 40 * heads * count * count * HD + 8 * count * dim * hidden,
            [active, slope, middle, carry, params, mixed, q, k, v, resid, (*weights, second, first)],
            jobs,
        )
        if last:
            (_, _, expand_grads[1], attn_grads[1], _, right_grads[0], _, left_grads[0],
             expand_grads[0], vectors, attn_grads[0], row_grad) = results
        else:
            (mlp_vec[l], attn_vec[l], carry, attn_full, output, left_grads[l], _, right_grads[l],
             expand_part) = results

    results = [
        jax.ShapeDtypeStruct(shape, F32)
        for shape in (
            (LAYERS, 3, shard, width), (LAYERS, width, shard), (LAYERS, shard, hidden),
            (LAYERS, hidden, shard), (6, LAYERS, shard), query_bias.shape, value_bias.shape,
            expand_bias.shape,
        )
    ]
    joint, out, expand, reduce, wide, query, value, hidden_bias = pl.pallas_call(
        finish_kernel,
        name="finish",
        out_shape=tuple(results),
        in_specs=[VMEM_SPEC] * 9,
        out_specs=tuple([VMEM_SPEC] * 8),
        compiler_params=pltpu.CompilerParams(vmem_limit_bytes=VMEM_LIMIT),
    )(*attn_grads, *expand_grads, *left_grads, *right_grads, vectors)
    return (
        output, row_grad, wide[0], wide[1], joint.transpose(0, 2, 1, 3), query, value, out,
        wide[2], wide[3], wide[4], expand, hidden_bias, reduce, wide[5],
    )


def solution(mesh):
    vector = P(None, "fsdp")
    by_head = P(None, "tp", "fsdp")
    rows = P("fsdp", ("ctx", "tp"), None)
    return jax.shard_map(
        local,
        mesh=mesh,
        in_specs=(
            rows, P("fsdp", None), vector, vector, P(None, "fsdp", None, "tp"), by_head, by_head,
            by_head, vector, vector, vector, P(None, "fsdp", "tp"), by_head, by_head, vector, rows,
        ),
        out_specs=(
            rows, rows, vector, vector, P(None, "fsdp", None, "tp"), by_head, by_head,
            by_head, vector, vector, vector, P(None, "fsdp", "tp"), by_head, by_head, vector,
        ),
        check_vma=False,
    )
```

```python
import functools
import math

import jax
import jax.numpy as jnp
from jax import lax
from jax.experimental import pallas as pl
from jax.experimental.pallas import tpu as pltpu
from jax.sharding import PartitionSpec as P

HD = 64
LAYERS = 2
LANES = 128
EPS = 1e-06
MASKED = -10000.0
SCALE = HD ** (-0.5)
VMEM_LIMIT = 62 * 1024 * 1024
F32 = jnp.float32
BF16 = jnp.bfloat16
VMEM = pltpu.VMEM
INV_SQRT2 = 1.0 / math.sqrt(2.0)
INV_SQRT_2PI = 1.0 / math.sqrt(2.0 * math.pi)


def mm(a, b):
    return lax.dot_general(a, b, (((1,), (0,)), ((), ())), preferred_element_type=F32)


def mm_nt(a, b):
    return lax.dot_general(a, b, (((1,), (1,)), ((), ())), preferred_element_type=F32)


def mm_tn(a, b):
    return lax.dot_general(a, b, (((0,), (0,)), ((), ())), preferred_element_type=F32)


def partners():
    t = lax.axis_index("tp")
    return t, t + 1 - 2 * (t % 2), (t + 2) % 4


def entry_barrier(jobs=(), tp=True):
    t, sib, peer = partners()
    others = [{"tp": sib}, {"tp": peer}] if tp or any(job.uses_tp for job in jobs) else []
    if any(job.uses_ctx for job in jobs):
        others.append({"ctx": 1 - lax.axis_index("ctx")})
    if any(job.uses_fsdp for job in jobs):
        n = lax.axis_size("fsdp")
        z = lax.axis_index("fsdp")
        others += [{"fsdp": (z + k) % n} for k in range(1, n)]
    barrier = pltpu.get_barrier_semaphore()
    for other in others:
        pl.semaphore_signal(barrier, inc=1, device_id=other, device_id_type=pl.DeviceIdType.MESH)
    pl.semaphore_wait(barrier, len(others))


def remote(src, dst, send, recv, device):
    return pltpu.make_async_remote_copy(
        src_ref=src,
        dst_ref=dst,
        send_sem=send,
        recv_sem=recv,
        device_id=device,
        device_id_type=pl.DeviceIdType.MESH,
    )


DMA = pltpu.SemaphoreType.DMA
HBM_SPEC = pl.BlockSpec(memory_space=pl.ANY)
VMEM_SPEC = pl.BlockSpec(memory_space=VMEM)


class Job:
    uses_tp = False
    uses_ctx = False
    uses_fsdp = False
    ins = ()
    outs = ()
    scratch = ()
    start_hook = None
    name = None

    def after(self, hook):
        self.start_hook = hook
        return self

    def bind(self, ins, outs, scratch):
        self.c = lax.axis_index("ctx")
        self.z = lax.axis_index("fsdp")
        self.refs(ins, outs, scratch)

    def start(self):
        pass

    def steps(self):
        return []

    def end(self):
        pass


def chunks_of(rows):
    return 2 if rows % 128 == 0 else 1


def cut_rows(ref, start, size):
    index = (slice(None),) * (len(ref.shape) - 2) + (pl.ds(start, size),)
    return ref.at[index]


class OverFsdp(Job):
    uses_fsdp = True

    def __init__(self, weight, layer, n, hook, chunks=1, ctx_hooks=None):
        self.n, self.layer, self.hook, self.ctx_hooks = n, layer, hook, ctx_hooks
        self.uses_ctx = ctx_hooks is not None
        shape = weight.shape[1:]
        self.rows = shape[-2] // 2
        self.ch = chunks if self.rows % (chunks * 16) == 0 else 1
        half = jax.ShapeDtypeStruct((n, *shape[:-2], self.rows, shape[-1]), BF16)
        self.ins = [(weight, HBM_SPEC)]
        self.outs = [(half, HBM_SPEC)] * (2 if self.uses_ctx else 1)
        self.scratch = [DMA((n + 1, self.ch)), DMA((n, self.ch)), DMA]
        if self.uses_ctx:
            self.scratch += [DMA((n, self.ch)), DMA((n, self.ch)), DMA]

    def refs(self, ins, outs, scratch):
        self.src = ins[0].at[self.layer]
        self.near = outs[0]
        self.send, self.recv, self.here = scratch[:3]
        if self.uses_ctx:
            self.far = outs[1]
            self.x_send, self.x_recv, self.here_far = scratch[3:]

    def mine(self, ch):
        size = self.rows // self.ch
        start = pl.multiple_of(self.c * self.rows + ch * size, size)
        return cut_rows(self.src, start, size)

    def part(self, ref, frm, ch):
        size = self.rows // self.ch
        return cut_rows(ref.at[frm], ch * size, size)

    def out_to(self, k, off, ch):
        to = (self.z + off + self.n) % self.n
        return remote(
            self.mine(ch), self.part(self.near, self.z, ch),
            self.send.at[k, ch], self.recv.at[self.z, ch], {"fsdp": to},
        )

    def arrived(self, frm, ch):
        block = self.part(self.near, frm, ch)
        return remote(
            block, block, self.send.at[self.n, ch], self.recv.at[frm, ch], {"fsdp": self.n - 1 - frm}
        )

    def over_x(self, frm, ch):
        return remote(
            self.part(self.near, frm, ch), self.part(self.far, frm, ch),
            self.x_send.at[frm, ch], self.x_recv.at[frm, ch], {"ctx": 1 - self.c},
        )

    def local(self, half, out, sem):
        start = pl.multiple_of(half * self.rows, self.rows)
        return pltpu.make_async_copy(
            cut_rows(self.src, start, self.rows), out.at[self.z], sem
        )

    def offsets(self):
        return (2, -2, 1, -1) if self.n == 4 else range(1, self.n)

    def sources(self):
        return (1, -1, 2, -2, 3, -3) if self.n == 4 else range(1, self.n)

    def inside(self, off):
        other = self.z + off
        return (other >= 0) & (other < self.n) if self.n == 4 else (other > -1)

    def relays(self):
        return (self.z == 1) | (self.z == 2)

    def start(self):
        for ch in range(self.ch):
            for k, off in enumerate(self.offsets()):
                @pl.when(self.inside(off))
                def _():
                    self.out_to(k, off, ch).start()
        self.local(self.c, self.near, self.here).start()
        if self.uses_ctx:
            self.local(1 - self.c, self.far, self.here_far).start()

    def relay(self):
        if self.n == 4:
            @pl.when(self.relays())
            def _():
                for ch in range(self.ch):
                    through = self.arrived(jnp.where(self.z == 2, 0, 3), ch)
                    through.wait_recv()
                    through.start()

    def take(self, off):
        frm = (self.z + off + self.n) % self.n

        @pl.when(self.inside(off))
        def _():
            for ch in range(self.ch):
                if self.n == 4 and abs(off) == 2:
                    @pl.when(jnp.logical_not((self.z == 2) & (frm == 0) | (self.z == 1) & (frm == 3)))
                    def _():
                        self.arrived(frm, ch).wait_recv()
                else:
                    self.arrived(frm, ch).wait_recv()
                if self.uses_ctx:
                    self.over_x(frm, ch).start()

    def steps(self):
        out = [(self.hook, self.relay)]
        if self.uses_ctx:
            for i, off in enumerate(self.sources()):
                out.append((self.ctx_hooks[min(i // 2, 2)], functools.partial(self.take, off)))
        return out

    def end(self):
        for off in self.sources():
            frm = (self.z + off + self.n) % self.n
            if not self.uses_ctx:
                self.take(off)
            else:
                @pl.when(self.inside(off))
                def _():
                    for ch in range(self.ch):
                        self.over_x(frm, ch).wait()
        for ch in range(self.ch):
            for k, off in enumerate(self.offsets()):
                @pl.when(self.inside(off))
                def _():
                    self.out_to(k, off, ch).wait_send()
            if self.n == 4:
                @pl.when(self.relays())
                def _():
                    self.arrived(jnp.where(self.z == 2, 0, 3), ch).wait_send()
        self.local(self.c, self.near, self.here).wait()
        if self.uses_ctx:
            self.local(1 - self.c, self.far, self.here_far).wait()


class OverCtx(Job):
    uses_ctx = True

    def __init__(self, weight, layer, near, n):
        self.n, self.layer = n, layer
        self.ins = [(weight, HBM_SPEC), (near, HBM_SPEC)]
        self.outs = [(jax.ShapeDtypeStruct(near.shape, BF16), HBM_SPEC)]
        self.scratch = [DMA((n,)), DMA((n,)), DMA]

    def refs(self, ins, outs, scratch):
        self.src, self.near = ins[0].at[self.layer], ins[1]
        (self.far,) = outs
        self.send, self.recv, self.here = scratch

    def copy(self, k):
        frm = (self.z + k) % self.n
        return remote(
            self.near.at[frm], self.far.at[frm], self.send.at[k], self.recv.at[k],
            {"ctx": 1 - self.c},
        )

    def local(self):
        rows = self.near.shape[-2]
        start = pl.multiple_of((1 - self.c) * rows, rows)
        return pltpu.make_async_copy(cut_rows(self.src, start, rows), self.far.at[self.z], self.here)

    def start(self):
        for k in range(1, self.n):
            self.copy(k).start()
        self.local().start()

    def end(self):
        for k in range(1, self.n):
            self.copy(k).wait()
        self.local().wait()


class Loads:
    def __init__(self, sems):
        self.sems, self.copies = sems, []

    def add(self, near, far, out):
        c = lax.axis_index("ctx")
        for half, ref in ((c, near), (1 - c, far)):
            if isinstance(out, tuple):
                width = ref.shape[-1] // len(out)
                pairs = [
                    (ref.at[:, :, j * width : (j + 1) * width], part.at[:, half])
                    for j, part in enumerate(out)
                ]
            elif len(ref.shape) == 3:
                pairs = [(ref, out.at[:, half])]
            else:
                width = ref.shape[-1]
                pairs = [
                    (ref.at[:, j], out.at[:, half, :, j * width : (j + 1) * width])
                    for j in range(ref.shape[1])
                ]
            for src, dst in pairs:
                copy = pltpu.make_async_copy(src, dst, self.sems.at[len(self.copies)])
                copy.start()
                self.copies.append(copy)

    def wait(self):
        for copy in self.copies:
            copy.wait()


class ParamJob(Job):
    uses_fsdp = True

    def __init__(self, wide, narrow, n, dim):
        self.n, self.n_wide = n, len(wide)
        self.ins = [(a, VMEM_SPEC) for a in (*wide, *narrow)]
        shape = (8 * LAYERS, dim)
        self.outs = [(jax.ShapeDtypeStruct(shape, F32), VMEM_SPEC)]
        self.scratch = [
            VMEM(shape, F32), VMEM(shape, BF16), VMEM((n, *shape), BF16), DMA((n,)), DMA((n,))
        ]

    def refs(self, ins, outs, scratch):
        self.wide, self.narrow = ins[: self.n_wide], ins[self.n_wide :]
        (self.out,) = outs
        self.work, self.src, self.got, self.ssem, self.rsem = scratch

    def copy(self, k):
        return remote(
            self.src, self.got.at[k], self.ssem.at[k], self.rsem.at[k],
            {"fsdp": (self.z + k) % self.n},
        )

    def start(self):
        work = self.work
        dim = work.shape[1]
        work[...] = jnp.zeros_like(work)
        shard = self.wide[0].shape[1]
        query, value, expand = self.narrow
        cut = query.shape[2]
        heads = query.shape[1]
        for l in range(LAYERS):
            for k, ref in enumerate(self.wide):
                work[8 * l + k : 8 * l + k + 1, :shard] = ref[l : l + 1, :].astype(F32)
            for row, base, ref in ((6, 0, query), (6, heads * HD, value), (7, 0, expand)):
                block = ref[l].astype(F32)
                for h in range(ref.shape[1]):
                    at = base + h * HD
                    work[8 * l + row : 8 * l + row + 1, at : at + cut] = block[h : h + 1, :]
        all_rows = work[...]
        row = lax.broadcasted_iota(jnp.int32, all_rows.shape, 0) % 8
        by_shard = pltpu.roll(all_rows, self.z * shard, 1)
        by_cut = pltpu.roll(all_rows, self.z * cut, 1)
        placed = jnp.where(row < 6, by_shard, by_cut)
        work[...] = placed
        self.src[...] = placed.astype(BF16)
        for k in range(1, self.n):
            self.copy(k).start()

    def finish(self):
        total = self.work[...]
        for k in range(1, self.n):
            self.copy(k).wait_recv()
            total += self.got[k].astype(F32)
        self.out[...] = total

    def end(self):
        for k in range(1, self.n):
            self.copy(k).wait_send()


class Exchange(Job):
    uses_ctx = True

    def __init__(self, both, name=None):
        self.name = name
        self.ins = [] if name else [(both, VMEM_SPEC)]
        self.outs = [(jax.ShapeDtypeStruct(both.shape, both.dtype), VMEM_SPEC)]
        self.scratch = [DMA, DMA]

    def refs(self, ins, outs, scratch):
        if not self.name:
            (self.src,) = ins
        (self.out,), (self.ssem, self.rsem) = outs, scratch

    def attach(self, ref):
        self.src = ref

    def copy(self):
        c = self.c
        return remote(self.src.at[1 - c], self.out.at[c], self.ssem, self.rsem, {"ctx": 1 - c})

    def start(self):
        self.copy().start()
        self.out[self.c] = self.src[self.c]

    def end(self):
        self.copy().wait()


class CtxSum(Job):
    uses_ctx = True

    def __init__(self, full, n, hooks, keep=False, name=None):
        self.n, self.hooks, self.name = n, hooks, name
        shape = (n, full.shape[0] // (2 * n), full.shape[1])
        self.ins = [] if name else [(full.reshape(n, 2, *shape[1:]), HBM_SPEC)]
        self.keep = keep
        self.outs = [] if keep else [(jax.ShapeDtypeStruct(shape, BF16), VMEM_SPEC)]
        self.scratch = [VMEM(shape, BF16), DMA((n,)), DMA((n,)), DMA((n,))]
        if keep and not name:
            self.scratch.append(VMEM(shape, BF16))

    def refs(self, ins, outs, scratch):
        if not self.name:
            (self.full,) = ins
        self.got, self.ssem, self.rsem, self.near = scratch[:4]
        if not (self.keep and self.name):
            self.out = scratch[4] if self.keep else outs[0]

    def attach(self, ref):
        self.full = ref.reshape(self.n, 2, ref.shape[0] // (2 * self.n), ref.shape[1])
        if self.keep:
            self.out = self.full.at[:, self.c]

    def order(self):
        return (0, 3, 1, 2) if self.n == 4 else range(self.n)

    def copy(self, k):
        return remote(
            self.full.at[k, 1 - self.c], self.got.at[k], self.ssem.at[k], self.rsem.at[k],
            {"ctx": 1 - self.c},
        )

    def load(self, k):
        return pltpu.make_async_copy(self.full.at[k, self.c], self.out.at[k], self.near.at[k])

    def start(self):
        for k in self.order():
            self.copy(k).start()
        for k in self.order():
            if not self.name:
                self.load(k).start()

    def add(self, k):
        if not self.name:
            self.load(k).wait()
        self.copy(k).wait_recv()
        mine = self.full[k, self.c] if self.name else self.out[k]
        self.out[k] = (mine.astype(F32) + self.got[k].astype(F32)).astype(BF16)

    def steps(self):
        per = -(-self.n // len(self.hooks))
        return [
            (self.hooks[i // per], functools.partial(self.add, k))
            for i, k in enumerate(self.order())
        ]

    def end(self):
        for k in range(self.n):
            self.copy(k).wait_send()


class FsdpSum(Job):
    uses_fsdp = True

    def __init__(self, rows, n, hooks, source=None, sends=(), spread=True, direct=False, name=None):
        self.name = name
        self.n, self.hooks, self.source, self.sends = n, hooks, source, sends
        self.relays = n == 4 and not direct
        self.spread = self.uses_ctx = spread
        shape = rows.shape
        self.ins = [] if source or name else [(rows, VMEM_SPEC)]
        result = (2, *shape[1:]) if spread else shape[1:]
        self.outs = [(jax.ShapeDtypeStruct(result, BF16), VMEM_SPEC)]
        self.rows = shape[1]
        self.ch = chunks_of(self.rows)
        self.scratch = [
            VMEM(shape, BF16), VMEM((2, *shape[1:]), BF16),
            DMA((n, self.ch)), DMA((n, self.ch)), DMA((2, self.ch)), DMA((2, self.ch)),
            DMA((self.ch,)), DMA((self.ch,)),
        ]

    def refs(self, ins, outs, scratch):
        if not (self.name or self.source):
            self.src = ins[0]
        (self.out,) = outs
        (self.got, self.via, self.ssem, self.rsem, self.via_send, self.via_recv, self.x_send,
         self.x_recv) = scratch

    def attach(self, ref):
        self.src = ref.reshape(self.n, self.rows, ref.shape[1])

    def cut(self, ref, ch):
        size = self.rows // self.ch
        return ref.at[pl.ds(ch * size, size)]

    def direct(self, d, ch):
        return remote(
            self.cut(self.src.at[d], ch), self.cut(self.got.at[self.z], ch),
            self.ssem.at[d, ch], self.rsem.at[self.z, ch], {"fsdp": d},
        )

    def landed(self, frm, ch):
        block = self.cut(self.got.at[frm], ch)
        return remote(block, block, self.ssem.at[frm, ch], self.rsem.at[frm, ch], {"fsdp": frm})

    def to_relay(self, d, ch):
        return remote(
            self.cut(self.src.at[d], ch), self.cut(self.via.at[0], ch),
            self.via_send.at[0, ch], self.via_recv.at[0, ch], {"fsdp": 2 if d == 0 else 1},
        )

    def relayed(self, d, ch):
        return remote(
            self.cut(self.via.at[1], ch), self.cut(self.got.at[self.z], ch),
            self.via_send.at[1, ch], self.rsem.at[self.z, ch], {"fsdp": d},
        )

    def directly(self, d):
        if self.relays and d in (0, 3):
            return (self.z == 1) if d == 0 else (self.z == 2)
        return self.z != d

    def send(self, d):
        if self.relays and d in (0, 3):
            @pl.when(self.z == 3 - d)
            def _():
                for ch in range(self.ch):
                    self.to_relay(d, ch).start()

        @pl.when(self.directly(d))
        def _():
            for ch in range(self.ch):
                self.direct(d, ch).start()

    def order(self):
        return (0, 3, 1, 2) if self.n == 4 else range(self.n)

    def start(self):
        if not self.source:
            for d in self.order():
                self.send(d)

    def relay(self):
        for d, me in ((0, 2), (3, 1)) if self.relays else ():
            @pl.when(self.z == me)
            def _():
                for ch in range(self.ch):
                    self.to_relay(d, ch).wait_recv()
                    mine = self.cut(self.src.at[d], ch)[...].astype(F32)
                    theirs = self.cut(self.via.at[0], ch)[...].astype(F32)
                    self.cut(self.via.at[1], ch)[...] = (mine + theirs).astype(BF16)
                    self.relayed(d, ch).start()

    then = None

    def result(self, ch):
        return self.cut(self.out.at[self.c] if self.spread else self.out, ch)

    def over_x(self, ch):
        block = self.result(ch)
        return remote(block, block, self.x_send.at[ch], self.x_recv.at[ch], {"ctx": 1 - self.c})

    def total(self):
        n = self.n
        for ch in range(self.ch):
            mine = self.cut(self.src.at[self.z], ch)
            if self.relays:
                near = (self.z + 1) % 4
                last = jnp.where(self.z == 0, 2, jnp.where(self.z == 3, 1, (self.z + 3) % 4))
                first = jnp.where(self.z == 3, 2, near)
                inner = (self.z == 1) | (self.z == 2)
                self.landed(first, ch).wait_recv()
                self.landed(last, ch).wait_recv()
                part = (
                    mine[...].astype(F32)
                    + self.cut(self.got.at[first], ch)[...].astype(F32)
                    + self.cut(self.got.at[last], ch)[...].astype(F32)
                )
                block = self.result(ch)

                @pl.when(inner)
                def _():
                    middle = (self.z + 2) % 4
                    self.landed(middle, ch).wait_recv()
                    block[...] = (part + self.cut(self.got.at[middle], ch)[...].astype(F32)).astype(BF16)

                @pl.when(jnp.logical_not(inner))
                def _():
                    block[...] = part.astype(BF16)
            else:
                part = mine[...].astype(F32)
                for k in range(1, n):
                    frm = (self.z + k) % n
                    self.landed(frm, ch).wait_recv()
                    part += self.cut(self.got.at[frm], ch)[...].astype(F32)
                self.result(ch)[...] = part.astype(BF16)
            if self.spread:
                self.over_x(ch).start()
            elif self.then is not None:
                self.then(ch)

    def steps(self):
        out = [
            (self.sends[i * len(self.sends) // self.n], functools.partial(self.send, d))
            for i, d in enumerate(self.order())
            if self.sends
        ]
        return out + [(self.hooks[0], self.relay), (self.hooks[1], self.total)]

    def end(self):
        for ch in range(self.ch):
            if self.spread:
                other = self.cut(self.out.at[1 - self.c], ch)
                remote(
                    other, other, self.x_send.at[ch], self.x_recv.at[ch], {"ctx": 1 - self.c}
                ).wait_recv()
                self.over_x(ch).wait_send()
            for d in range(self.n):
                if self.relays and d in (0, 3):
                    @pl.when(self.z == 3 - d)
                    def _():
                        self.to_relay(d, ch).wait_send()

                    @pl.when(self.z == (2 if d == 0 else 1))
                    def _():
                        self.relayed(d, ch).wait_send()

                @pl.when(self.directly(d))
                def _():
                    self.direct(d, ch).wait_send()


class CtxAdd(Job):
    uses_ctx = True

    def __init__(self, rows, hook, source=None):
        self.hook, self.source = hook, source
        self.ins = [] if source else [(rows, VMEM_SPEC)]
        self.outs = [(jax.ShapeDtypeStruct(rows.shape, BF16), VMEM_SPEC)]
        self.rows = rows.shape[0]
        self.ch = chunks_of(self.rows)
        self.scratch = [VMEM(rows.shape, BF16), DMA((self.ch,)), DMA((self.ch,))]

    def refs(self, ins, outs, scratch):
        self.src = self.source.out if self.source else ins[0]
        (self.out,) = outs
        self.got, self.ssem, self.rsem = scratch
        if self.source:
            self.source.then = self.send

    def cut(self, ref, ch):
        size = self.rows // self.ch
        return ref.at[pl.ds(ch * size, size)]

    def copy(self, ch):
        return remote(
            self.cut(self.src, ch), self.cut(self.got, ch), self.ssem.at[ch], self.rsem.at[ch],
            {"ctx": 1 - self.c},
        )

    def send(self, ch):
        self.copy(ch).start()

    def start(self):
        if not self.source:
            for ch in range(self.ch):
                self.send(ch)

    def add(self):
        for ch in range(self.ch):
            self.copy(ch).wait_recv()
            mine, theirs = self.cut(self.src, ch)[...], self.cut(self.got, ch)[...]
            self.cut(self.out, ch)[...] = (mine.astype(F32) + theirs.astype(F32)).astype(BF16)

    def steps(self):
        return [(self.hook, self.add)]

    def end(self):
        for ch in range(self.ch):
            self.copy(ch).wait_send()


class Background:
    def __init__(self, jobs):
        self.jobs = jobs
        self.todo = []
        for job in jobs:
            if job.start_hook is not None:
                self.todo.append((job.start_hook, job.start))
            self.todo += job.steps()
        self.ended = []

    def start(self):
        for job in self.jobs:
            if job.start_hook is None:
                job.start()

    def at(self, hook):
        for when, function in self.todo:
            if when == hook:
                function()

    def phase(self, tag):
        return Phase(self, tag)

    def end(self, jobs=None):
        for job in self.jobs if jobs is None else jobs:
            if job not in self.ended:
                self.ended.append(job)
                job.end()


class Phase:
    def __init__(self, whole, tag):
        self.whole, self.tag = whole, tag
        self.prepare = lambda: None

    def at(self, hook):
        self.whole.at((self.tag, hook))

    def loop(self, b, count=4, base=0):
        for k in range(count):
            if any(when == (self.tag, base + k) for when, _ in self.whole.todo):
                @pl.when(b == k)
                def _():
                    self.at(base + k)


class Links:
    def __init__(self, send, recv, sib, peer):
        self.send, self.recv, self.sib, self.peer = send, recv, sib, peer

    def make(self, kind, s, src, dst, other):
        return pltpu.make_async_remote_copy(
            src_ref=src,
            dst_ref=dst,
            send_sem=self.send.at[kind, s],
            recv_sem=self.recv.at[kind, s],
            device_id={"tp": other},
            device_id_type=pl.DeviceIdType.MESH,
        )


def statistics(rows):
    mean = jnp.mean(rows, axis=-1, keepdims=True)
    centred = rows - mean
    inverse = lax.rsqrt(jnp.mean(centred * centred, axis=-1, keepdims=True) + EPS)
    return centred * inverse, inverse


def norm_back(rows, d_out, gain):
    unit, inverse = statistics(rows)
    e = d_out * gain
    back = inverse * (
        e
        - jnp.mean(e, axis=-1, keepdims=True)
        - unit * jnp.mean(e * unit, axis=-1, keepdims=True)
    )
    d_gain = jnp.sum(d_out * unit, axis=0, keepdims=True)
    d_shift = jnp.sum(d_out, axis=0, keepdims=True)
    return back, d_gain, d_shift


def rows_of(ref, b):
    block = ref[b]
    return block.reshape(block.shape[0] * block.shape[1], block.shape[2])


class Gather:
    def __init__(self, links, out):
        self.links, self.out = links, out

    def near(self, s):
        return self.links.make(3, s, self.out.at[2 + s, 0], self.out.at[2 + s, 1], self.links.sib)

    def across(self, s):
        return self.links.make(4, s, self.out.at[2 + s, 0], self.out.at[s, 0], self.links.peer)

    def onward(self, s):
        return self.links.make(5, s, self.out.at[s, 0], self.out.at[s, 1], self.links.sib)

    def start(self, rows):
        for s in range(2):
            self.out[2 + s, 0] = rows(s)
            self.near(s).start()
            self.across(s).start()

    def need(self, b):
        s = b % 2

        @pl.when(b >= 2)
        def _():
            self.near(s).wait_recv()

        @pl.when(b < 2)
        def _():
            self.across(s).wait_recv()
            self.onward(s).start()
            self.onward(s).wait_recv()

    def end(self):
        for s in range(2):
            for copy in (self.near(s), self.across(s), self.onward(s)):
                copy.wait_send()


class Scatter:
    def __init__(self, links, part, sent, got, own):
        self.links, self.part, self.sent, self.got, self.own = links, part, sent, got, own

    def copy(self, kind, s):
        other = self.links.peer if kind == 1 else self.links.sib
        return self.links.make(kind, s, self.sent.at[kind, s], self.got.at[kind, s], other)

    def block(self, b):
        s = b % 2
        half = self.part.shape[0] // 2

        @pl.when(b < 2)
        def _():
            self.sent[0, s] = self.part[half:].astype(BF16)
            first = self.copy(0, s)
            first.start()
            first.wait_recv()
            self.sent[1, s] = (self.part[:half] + self.got[0, s].astype(F32)).astype(BF16)
            self.copy(1, s).start()

        @pl.when(b >= 2)
        def _():
            self.sent[2, s] = self.part[half:].astype(BF16)
            self.copy(2, s).start()
            self.own[s] = self.part[:half]

    def total(self, s):
        self.copy(2, s).wait_recv()
        self.copy(1, s).wait_recv()
        return self.own[s] + self.got[2, s].astype(F32) + self.got[1, s].astype(F32)

    def end(self):
        for s in range(2):
            for kind in range(3):
                self.copy(kind, s).wait_send()


def scatter_scratch(half, width):
    local = [VMEM((2 * half, width), F32), VMEM((2, half, width), F32)]
    linked = [
        VMEM((3, 2, half, width), BF16), VMEM((3, 2, half, width), BF16), DMA((6, 2)), DMA((6, 2))
    ]
    return local + linked + linked


def scatter_refs(scratch, phase):
    part, own = scratch[:2]
    sent, got, send, recv = scratch[2 + 4 * phase : 6 + 4 * phase]
    return part, sent, got, own, send, recv


def pair_tile(pair, h):
    tile = pair if h % 2 == 0 else pltpu.roll(pair, HD, 1)
    return tile


def attention_phase(
    background, heads, base,
    own_first, params, key_extra, resid, near, far,
    first, second, middle, q_out, k_out, v_out, mixed_out,
    part, sent, got, own, send, recv, weight, load,
):
    t, sib, peer = partners()
    links = Links(send, recv, sib, peer)
    scatter = Scatter(links, part, sent, got, own)
    width = heads * HD
    gather = Gather(links, first)
    gather.start(lambda s: own_first[s])
    background.prepare()
    loads = Loads(load)
    loads.add(near, far, weight)
    loads.wait()
    weight = whole(weight)
    out_bias, gain, shift = (params[base + k : base + k + 1, :] for k in (2, 3, 4))
    q_bias = params[base + 6 : base + 7, :width]
    v_bias = params[base + 6 : base + 7, width : 2 * width]
    half = first.shape[2]
    rows = 2 * half
    lane = lax.broadcasted_iota(jnp.int32, (rows, LANES), 1)
    head_lane = lane < HD
    q_extra = jnp.where(lane < HD + 2, 1.0, 0.0).astype(BF16)
    v_extra = jnp.where(lane < HD + 3, 1.0, 0.0).astype(BF16)

    def project(j, carry):
        b = (j + 2) % 4
        gather.need(b)
        x = rows_of(first, b)
        y = mm(x, weight[:, : 3 * width])
        q = ((y[:, :width] + q_bias).astype(BF16) * SCALE).astype(BF16)
        k = y[:, width : 2 * width].astype(BF16)
        v = (y[:, 2 * width :] + v_bias).astype(BF16)
        g, s = b // 2, b % 2
        mine = jnp.where(g == 1, t, peer)
        other = mine + 1 - 2 * (mine % 2)
        extra = jnp.concatenate([key_extra[mine, s], key_extra[other, s]], axis=0)
        at = pl.ds(pl.multiple_of(b * rows, rows), rows)
        for h in range(heads):
            cut = slice(LANES * (h // 2), LANES * (h // 2 + 1))
            q_out[h, at, :] = jnp.where(head_lane, pair_tile(q[:, cut], h), q_extra)
            k_out[h, at, :] = jnp.where(head_lane, pair_tile(k[:, cut], h), extra)
            v_out[h, at, :] = jnp.where(head_lane, pair_tile(v[:, cut], h), v_extra)
        background.loop(j, 4, 20)
        return carry

    lax.fori_loop(0, 4, project, 0)
    background.at(0)

    def attend(b, carry):
        at = pl.ds(pl.multiple_of(b * rows, rows), rows)
        outs = []
        for h in range(heads):
            q = q_out[h, at, :]
            scores = mm_nt(q, k_out[h])
            top = jnp.max(scores, axis=-1, keepdims=True)
            weights = jnp.exp(scores - top).astype(BF16)
            summed = mm(weights, v_out[h])
            total = summed[:, HD : HD + 1]
            outs.append(summed / total)
            log_total = -(top + jnp.log(total))
            high = log_total.astype(BF16).astype(F32)
            rest = log_total - high
            mid = rest.astype(BF16).astype(F32)
            low = rest - mid
            tail = jnp.where(lane == HD + 2, high, jnp.where(lane == HD + 3, mid, low))
            q_out[h, at, :] = jnp.where(
                (lane >= HD + 2) & (lane < HD + 5), tail.astype(BF16), q
            )
        tiles = [
            jnp.where(head_lane, outs[h], pltpu.roll(outs[h + 1], HD, 1))
            for h in range(0, heads, 2)
        ]
        mixed = jnp.concatenate(tiles, axis=1).astype(BF16)
        mixed_out[at, :] = mixed
        part[...] = mm_nt(mixed, weight[:, 3 * width :])
        scatter.block(b)
        background.loop(b, 4, 1)
        return carry

    lax.fori_loop(0, 4, attend, 0)
    for s in range(2):
        mid = resid[s].astype(F32) + (scatter.total(s) + out_bias)
        middle[s] = mid
        unit, _ = statistics(mid)
        second[s] = (unit * gain + shift).astype(BF16)
        background.at(5 + s)
    gather.end()
    scatter.end()


def mlp_phase(
    background, last, base,
    own_second, params, middle, near_e, far_e, near_r, far_r,
    second, active_out, slope_out, resid, nxt,
    part, sent, got, own, send, recv, expand, reduce, load,
):
    t, sib, peer = partners()
    links = Links(send, recv, sib, peer)
    scatter = Scatter(links, part, sent, got, own)
    half = second.shape[2]
    rows = 2 * half
    gather = Gather(links, second)
    gather.start(lambda s: own_second[s])
    loads = Loads(load)
    loads.add(near_e, far_e, expand)
    loads.add(near_r, far_r, reduce)
    loads.wait()
    expand, reduce = whole(expand), whole(reduce)
    hidden = expand.shape[1]
    out_bias = params[base + 5 : base + 6, :]
    following = 0 if last else base + 8
    gain, shift = (params[following + k : following + k + 1, :] for k in (0, 1))
    step = 256

    def block(j, carry):
        b = (j + 2) % 4
        gather.need(b)
        at = pl.ds(pl.multiple_of(b * rows, rows), rows)
        x = rows_of(second, b)
        for n in range(0, hidden, step):
            before = mm(x, expand[:, n : n + step]) + params[base + 7 : base + 8, n : n + step]
            cdf = 0.5 * (1.0 + lax.erf(before * INV_SQRT2))
            active_out[at, n : n + step] = (before * cdf).astype(BF16)
            slope = cdf + before * (jnp.exp(before * before * -0.5) * INV_SQRT_2PI)
            slope_out[at, n : n + step] = slope.astype(BF16)
        part[...] = mm_nt(active_out[at, :], reduce[...])
        scatter.block(b)
        background.loop(j, 4, 1)
        return carry

    lax.fori_loop(0, 4, block, 0)
    for s in range(2):
        res = middle[s] + (scatter.total(s) + out_bias)
        if last:
            nxt[s] = res.astype(BF16)
        else:
            resid[s] = res
            unit, _ = statistics(res)
            nxt[s] = (unit * gain + shift).astype(BF16)
        background.at(5 + s)
    gather.end()
    scatter.end()


def token_product(left, right, outs, offset=0):
    depth = left.shape[-1]
    total = left.shape[0] * left.shape[1] * left.shape[2]
    step = 256

    def body(j, carry):
        cut = pl.ds(pl.multiple_of(j * step, step), step)
        x = left[:, :, :, cut].reshape(total, step)
        product = mm_tn(x, right[...]).astype(BF16)
        width = right.shape[-1] // len(outs)
        for k, out in enumerate(outs):
            out[cut, offset : offset + width] = product[:, k * width : (k + 1) * width]
        return carry

    lax.fori_loop(0, depth // step, body, 0)


def mlp_back_phase(
    background, base,
    ready, active, slope, second, middle, carry_in, params, near_e, far_e, near_r, far_r,
    expand_grad, reduce_left, reduce_right, carry_out, vectors,
    part, sent, got, own, send, recv, grad, d_before, expand, reduce, load,
):
    t, sib, peer = partners()
    links = Links(send, recv, sib, peer)
    scatter = Scatter(links, part, sent, got, own)
    gather = Gather(links, grad)
    gather.start(lambda s: carry_in[s].astype(BF16))
    loads = Loads(load)
    loads.add(near_e, far_e, expand)
    loads.add(near_r, far_r, reduce)
    loads.wait()
    expand = whole(expand)
    reduce = [whole(part) for part in reduce]
    wide = reduce[0].shape[1]
    gain = params[base + 3 : base + 4, :]
    half = grad.shape[2]
    rows = 2 * half
    hidden = active.shape[1]
    step = 256
    vectors[...] = jnp.zeros_like(vectors)

    def block(j, carry):
        b = (j + 2) % 4
        gather.need(b)
        at = pl.ds(pl.multiple_of(b * rows, rows), rows)
        x = rows_of(grad, b)
        for n in range(0, hidden, step):
            d_act = mm(x, reduce[n // wide][:, n % wide : n % wide + step])
            d_bef = (d_act * slope[at, n : n + step].astype(F32)).astype(BF16)
            d_before[at, n : n + step] = d_bef
            vectors[4:5, n : n + step] += jnp.sum(d_bef.astype(F32), axis=0, keepdims=True)
        part[...] = mm_nt(d_before[at, :], expand[...])
        scatter.block(b)
        background.loop(j)
        return carry

    lax.fori_loop(0, 4, block, 0)
    token_product(grad, active, (reduce_left, reduce_right))
    background.at(4)

    def finish(s):
        back, d_gain, d_shift = norm_back(middle[s], scatter.total(s), gain)
        carry = carry_in[s].astype(F32)
        mid = carry + back
        carry_out[s] = mid
        low = mid.astype(BF16)
        vectors[0:1, :] += d_gain
        vectors[1:2, :] += d_shift
        vectors[2:3, :] += jnp.sum(low.astype(F32), axis=0, keepdims=True)
        vectors[3:4, :] += jnp.sum(carry.astype(BF16).astype(F32), axis=0, keepdims=True)

    finish(0)
    background.at(5)
    ready.wait()
    token_product(second, d_before, (expand_grad,))
    finish(1)
    background.at(6)
    gather.end()
    scatter.end()


def attention_back_phase(
    background, heads, base,
    ready, weight_grad, mixed, q_in, k_in, v_in, first, carry_in, resid, params, near, far,
    carry_out, vectors,
    part, sent, got, own, send, recv, grad, d_joint, d_key, d_value, weight, load,
):
    t, sib, peer = partners()
    links = Links(send, recv, sib, peer)
    scatter = Scatter(links, part, sent, got, own)
    width = heads * HD
    gather = Gather(links, grad)
    gather.start(lambda s: carry_in[s].astype(BF16))
    loads = Loads(load)
    loads.add(near, far, weight)
    loads.wait()
    weight = whole(weight)
    gain = params[base : base + 1, :]
    half = grad.shape[2]
    rows = 2 * half
    lane = lax.broadcasted_iota(jnp.int32, (rows, LANES), 1)
    head_lane = lane < HD
    vectors[...] = jnp.zeros_like(vectors)
    d_joint = d_joint.at[:, : 3 * width]
    d_key[...] = jnp.zeros_like(d_key)
    d_value[...] = jnp.zeros_like(d_value)

    def pairs(tiles):
        return jnp.concatenate(
            [
                jnp.where(head_lane, tiles[h], pltpu.roll(tiles[h + 1], HD, 1))
                for h in range(0, heads, 2)
            ],
            axis=1,
        )

    def attend(j, carry):
        b = (j + 2) % 4
        gather.need(b)
        at = pl.ds(pl.multiple_of(b * rows, rows), rows)
        d_mixed = mm(rows_of(grad, b), weight[:, 3 * width :]).astype(BF16)
        product = d_mixed.astype(F32) * mixed[at, :].astype(F32)
        d_queries = []
        for h in range(heads):
            cut = slice(LANES * (h // 2), LANES * (h // 2 + 1))
            keep = head_lane if h % 2 == 0 else lane >= HD
            delta = -jnp.sum(jnp.where(keep, product[:, cut], 0.0), axis=-1, keepdims=True)
            high = delta.astype(BF16).astype(F32)
            rest = delta - high
            mid = rest.astype(BF16).astype(F32)
            low = rest - mid
            tail = jnp.where(
                lane == HD,
                high,
                jnp.where(lane == HD + 1, mid, jnp.where(lane == HD + 2, low, 0.0)),
            ).astype(BF16)
            d_o = jnp.where(head_lane, pair_tile(d_mixed[:, cut], h), tail)
            q = q_in[h, at, :]
            probs = jnp.exp(mm_nt(k_in[h], q))
            d_value[h] += mm(probs.astype(BF16), d_o)
            d_raw = (probs * mm_nt(v_in[h], d_o)).astype(BF16)
            d_key[h] += mm(d_raw, q)
            d_queries.append(mm_tn(d_raw, k_in[h]) * SCALE)
        d_joint[at, :width] = pairs(d_queries).astype(BF16)
        background.loop(j)
        return carry

    lax.fori_loop(0, 4, attend, 0)

    def gather_heads(b, carry):
        at = pl.ds(pl.multiple_of(b * rows, rows), rows)
        d_joint[at, width : 2 * width] = pairs([d_key[h, at, :] for h in range(heads)]).astype(BF16)
        d_joint[at, 2 * width : 3 * width] = pairs([d_value[h, at, :] for h in range(heads)]).astype(BF16)
        return carry

    lax.fori_loop(0, 4, gather_heads, 0)

    def project(b, carry):
        at = pl.ds(pl.multiple_of(b * rows, rows), rows)
        d_rows = d_joint[at, :]
        sums = jnp.sum(d_rows.astype(F32), axis=0, keepdims=True)
        vectors[2:3, :width] += sums[:, :width]
        vectors[2:3, width : 2 * width] += sums[:, 2 * width :]
        part[...] = mm_nt(d_rows, weight[:, : 3 * width])
        scatter.block(b)
        background.loop(b, 4, 4)
        return carry

    def out_product():
        token_product(grad, mixed, (weight if weight_grad is None else weight_grad,), 3 * width)
        background.at(8)

    def joint_product():
        for copy in ready:
            copy.wait()
        token_product(first, d_joint, (weight if weight_grad is None else weight_grad,))
        background.at(11)

    if weight_grad is not None:
        joint_product()
        out_product()
    lax.fori_loop(0, 4, project, 0)
    if weight_grad is None:
        out_product()

    def finish(s):
        back, d_gain, d_shift = norm_back(resid[s].astype(F32), scatter.total(s), gain)
        carry = carry_in[s] + back
        carry_out[s] = carry.astype(carry_out.dtype)
        vectors[0:1, :] += d_gain
        vectors[1:2, :] += d_shift

    finish(0)
    background.at(9)
    if weight_grad is None:
        joint_product()
    finish(1)
    background.at(10)
    gather.end()
    scatter.end()


def forward_kernel(jobs, entry, urgent, heads, last, base, refs):
    ins, outs, scratch = refs
    first, own_rows, middle, q, k, v, mixed, second, active, slope, out, rows = outs
    attn_w, attn_load, expand, reduce, mlp_load = scratch[10:15]
    background = Background(jobs)
    entry_barrier(jobs)
    background.start()
    phase = background.phase("A")
    expand_job, reduce_job = urgent
    if entry:
        (key_extra,) = ins
        params_job, tokens, attn = entry
        params, resid, near_a, far_a = params_job.out, tokens.out, attn.near, attn.far
        own_first = scratch[15]
        tokens.start()
        params_job.start()
        attn.start()
        params_job.finish()
        attn.relay()
        expand_job.start()
        tokens.end()
        for s in range(2):
            unit, _ = statistics(resid[s].astype(F32))
            own_first[s] = (unit * params[0:1, :] + params[1:2, :]).astype(BF16)

        def prepare():
            for off in attn.sources()[:4]:
                attn.take(off)
            expand_job.relay()
            reduce_job.start()
            for off in attn.sources()[4:]:
                attn.take(off)
            params_job.end()
            attn.end()

        phase.prepare = prepare
        background.ended += entry
        near_e, far_e = expand_job.near, expand_job.far
    else:
        own_first, params, key_extra, resid, near_a, far_a, near_e = ins
        far_e = expand_job.far
    attention_phase(
        phase, heads, base,
        own_first, params, key_extra, resid, near_a, far_a,
        first, own_rows, middle, q, k, v, mixed, *scatter_refs(scratch, 0), attn_w, attn_load,
    )
    background.end(urgent)
    mlp_phase(
        background.phase("M"), last, base,
        own_rows, params, middle, near_e, far_e, reduce_job.near, reduce_job.far,
        second, active, slope, out, rows, *scatter_refs(scratch, 1), expand, reduce, mlp_load,
    )
    background.end()


def backward_kernel(jobs, heads, base, last, refs):
    ins, outs, scratch = refs
    carry_out = scratch[-1]
    if last:
        scratch = scratch[:-1]
    (active, slope, middle, carry_in, params, mixed, q, k, v, resid,
     near_e, far_e, near_r, far_r, near_a, far_a, second, first) = ins
    (carry_mid, grad_rows, attn_rows, d_before, held, expand, reduce_left, reduce_right, mlp_load,
     d_key, d_value, attn_w, attn_load, held_load) = scratch[10:]
    if last:
        mlp_vec, attn_vec = outs
    else:
        mlp_vec, attn_vec, carry_out, attn_grad = outs
    left_grad, right_grad = whole(reduce_left), whole(reduce_right)
    named = dict(
        expand=whole(expand), left=left_grad, right=right_grad, attn=whole(grad_rows), carry=carry_out,
        vectors=(attn_vec, mlp_vec),
    )
    for job in jobs:
        if job.name:
            job.attach(named[job.name])
    for job in jobs:
        if isinstance(job, FsdpSum) and job.source:
            job.src = job.source.out
    background = Background(jobs)
    entry_barrier(jobs)
    background.start()
    second_load = pltpu.make_async_copy(second, held, held_load.at[0])
    second_load.start()
    mlp_back_phase(
        background.phase("M"), base,
        second_load, active, slope, held, middle, carry_in, params, near_e, far_e, near_r, far_r,
        whole(expand), left_grad, right_grad, carry_mid, mlp_vec,
        *scatter_refs(scratch, 0), grad_rows, d_before, expand, (reduce_left, reduce_right), mlp_load,
    )
    first_load = pltpu.make_async_copy(first, held, held_load.at[1])
    first_load.start()
    attention_back_phase(
        background.phase("A"), heads, base,
        [first_load], whole(grad_rows) if last else None, mixed, q, k, v, held, carry_mid, resid, params, near_a, far_a,
        carry_out, attn_vec,
        *scatter_refs(scratch, 1), attn_rows, d_before, d_key, d_value, attn_w, attn_load,
    )
    copies = []
    if not last:
        copies = [pltpu.make_async_copy(whole(attn_w), attn_grad, attn_load.at[0])]
        copies[0].start()
    tail = background.phase("L")
    for hook in range(8):
        tail.at(hook)
    background.end()
    for copy in copies:
        copy.wait()


class VectorSum(Job):
    uses_tp = uses_ctx = uses_fsdp = True

    def __init__(self, vectors, n, hooks):
        self.n, self.hooks, self.name = n, hooks, "vectors"
        dim = vectors[0].shape[1]
        self.ins = [(v, VMEM_SPEC) for v in vectors]
        self.outs = [(jax.ShapeDtypeStruct((16, dim), F32), VMEM_SPEC)]
        self.scratch = [
            VMEM((4, 16, dim), F32), VMEM((3 + n, 16, dim), F32), DMA((3 + n,)), DMA((3 + n,))
        ]

    def refs(self, ins, outs, scratch):
        self.former = ins
        (self.out,) = outs
        self.held, self.got, self.ssem, self.rsem = scratch
        t, self.sib, self.peer = partners()

    def attach(self, refs):
        self.vectors = (*refs, *self.former)

    def copy(self, k):
        if k == 0:
            to = {"ctx": 1 - self.c}
        elif k < 3:
            to = {"tp": self.sib if k == 1 else self.peer}
        else:
            to = {"fsdp": (self.z + k - 2) % self.n}
        return remote(
            self.held.at[min(k, 3)], self.got.at[k], self.ssem.at[k], self.rsem.at[k], to
        )

    def start(self):
        for l in range(LAYERS):
            attn, mlp = self.vectors[2 * l], self.vectors[2 * l + 1]
            for row, (ref, index) in enumerate(
                ((attn, 0), (attn, 1), (mlp, 2), (mlp, 0), (mlp, 1), (mlp, 3), (attn, 2), (mlp, 4))
            ):
                self.held[0, 8 * l + row : 8 * l + row + 1, :] = ref[index : index + 1, :]
        self.copy(0).start()

    def fold(self, k):
        self.copy(k).wait_recv()
        came = self.got[k]
        if k > 0:
            row = lax.broadcasted_iota(jnp.int32, came.shape, 0)
            came = jnp.where(row % 8 < 6, came, 0.0)
        self.held[k + 1] = self.held[k] + came
        if k < 2:
            self.copy(k + 1).start()
        else:
            for j in range(1, self.n):
                self.copy(2 + j).start()

    def finish(self):
        total = self.held[3]
        for j in range(1, self.n):
            self.copy(2 + j).wait_recv()
            total += self.got[2 + j]
        self.out[...] = total

    def steps(self):
        return [(self.hooks[k], functools.partial(self.fold, k)) for k in range(3)] + [
            (self.hooks[3], self.finish)
        ]

    def end(self):
        for k in range(2 + self.n):
            self.copy(k).wait_send()


def finish_kernel(
    attn_0, attn_1, expand_0, expand_1, left_0, left_1, right_0, right_1, vectors,
    joint_out, out_out, expand_out, reduce_out, wide, query, value, hidden,
    joint, out, expand, reduce, sems,
):
    z = lax.axis_index("fsdp")
    half = attn_0.shape[1]
    width = joint.shape[3]
    shard = 2 * half
    copies = []
    layers = ((attn_0, expand_0, left_0, right_0), (attn_1, expand_1, left_1, right_1))
    for l, (a, e, left, right) in enumerate(layers):
        rows = a[...].reshape(shard, a.shape[2]).astype(F32)
        for k in range(3):
            joint[l, k] = rows[:, k * width : (k + 1) * width]
        out[l] = rows[:, 3 * width :].T
        expand[l] = e[...].reshape(shard, e.shape[2]).astype(F32)
        part = left.shape[-1]
        for k, r in enumerate((left, right)):
            reduce[l, k * part : (k + 1) * part, :] = r[...].reshape(shard, part).astype(F32).T
        for k, (held, result) in enumerate(
            ((joint, joint_out), (out, out_out), (expand, expand_out), (reduce, reduce_out))
        ):
            copies.append(pltpu.make_async_copy(held.at[l], result.at[l], sems.at[l, k]))
            copies[-1].start()
    cut = query.shape[2]
    heads = query.shape[1]
    dim = vectors.shape[1]
    own = pltpu.roll(vectors[...], lax.rem(dim - z * shard, dim), 1)
    by_cut = pltpu.roll(vectors[...], lax.rem(dim - z * cut, dim), 1)
    for l in range(LAYERS):
        for k in range(6):
            wide[k, l : l + 1, :] = own[8 * l + k : 8 * l + k + 1, :shard]
        for row, base, ref in ((6, 0, query), (6, heads * HD, value), (7, 0, hidden)):
            for h in range(ref.shape[1]):
                at = base + h * HD
                ref[l, h : h + 1, :] = by_cut[8 * l + row : 8 * l + row + 1, at : at + cut]
    for copy in copies:
        copy.wait()


def whole(ref):
    return ref.reshape(ref.shape[0] * ref.shape[1] * ref.shape[2], ref.shape[3])


def call(kernel, name, outs, scratch, collective_id, flops, args, jobs=()):
    args = [
        (a, spec)
        for arg in args
        for a, spec in ([(arg, VMEM_SPEC)] if not isinstance(arg, tuple) else [(a, HBM_SPEC) for a in arg])
    ]
    ins = args + [pair for job in jobs for pair in job.ins]
    results = [o if isinstance(o, tuple) else (o, VMEM_SPEC) for o in outs] + [pair for job in jobs for pair in job.outs]
    scratch = list(scratch)
    n_scratch = len(scratch)
    for job in jobs:
        scratch += job.scratch

    def body(*refs):
        refs = list(refs)
        in_refs = refs[: len(ins)]
        out_refs = refs[len(ins) : len(ins) + len(results)]
        scratch_refs = refs[len(ins) + len(results) :]
        a, b, c = len(args), len(outs), n_scratch
        for job in jobs:
            ends = a + len(job.ins), b + len(job.outs), c + len(job.scratch)
            job.bind(in_refs[a : ends[0]], out_refs[b : ends[1]], scratch_refs[c : ends[2]])
            a, b, c = ends
        kernel(jobs, (in_refs[: len(args)], out_refs[: len(outs)], scratch_refs[:n_scratch]))

    size = sum(a.size * a.dtype.itemsize for a, _ in ins) + sum(
        math.prod(o.shape) * o.dtype.itemsize for o, _ in results
    )
    return pl.pallas_call(
        body,
        name=name,
        out_shape=tuple(o for o, _ in results),
        in_specs=[spec for _, spec in ins],
        out_specs=tuple(spec for _, spec in results),
        scratch_shapes=scratch,
        compiler_params=pltpu.CompilerParams(
            collective_id=collective_id, has_side_effects=True, vmem_limit_bytes=VMEM_LIMIT
        ),
        cost_estimate=pl.CostEstimate(flops=flops, bytes_accessed=size, transcendentals=0),
    )(*[a for a, _ in ins])


def local(
    tokens, key_valid, first_gain, first_shift, joint_weight, query_bias, value_bias,
    out_weight, out_bias, second_gain, second_shift, expand_weight, expand_bias,
    reduce_weight, reduce_bias, cotangent,
):
    ctx_size = lax.axis_size("ctx")
    tp_size = lax.axis_size("tp")
    fsdp_size = lax.axis_size("fsdp")
    clips, half, dim = tokens.shape
    assert clips == ctx_size == 2 and tp_size == 4 and joint_weight.shape[0] == LAYERS
    c = lax.axis_index("ctx")
    shard = joint_weight.shape[1]
    width = joint_weight.shape[3]
    heads = width // HD
    hidden = expand_weight.shape[2]
    attn_w = jnp.concatenate(
        [joint_weight.transpose(0, 2, 1, 3), out_weight.transpose(0, 2, 1)[:, None]], axis=1
    )
    reduce_w = reduce_weight.transpose(0, 2, 1)

    valid = lax.dynamic_index_in_dim(key_valid, c, 0, keepdims=False)
    bias = jnp.where(valid == 1, 0.0, MASKED).astype(F32)
    bias = bias.reshape(ctx_size, tp_size, half, 1).transpose(1, 0, 2, 3)
    high = bias.astype(BF16).astype(F32)
    col = lax.broadcasted_iota(jnp.int32, (1, 1, 1, LANES), 3) - HD
    key_extra = jnp.where(
        col == 0, high, jnp.where(col == 1, bias - high, jnp.where((col >= 2) & (col < 5), 1.0, 0.0))
    ).astype(BF16)

    every = jax.ShapeDtypeStruct((4, 2, half, dim), BF16)
    own = jax.ShapeDtypeStruct((2, half, dim), F32)
    own_low = jax.ShapeDtypeStruct((2, half, dim), BF16)
    tiny = jax.ShapeDtypeStruct((8, LANES), F32)
    vec = jax.ShapeDtypeStruct((8, dim), F32)
    square = jax.ShapeDtypeStruct((dim, hidden), BF16)
    narrow = jax.ShapeDtypeStruct((dim, hidden // 2), BF16)
    count = 8 * half
    n = fsdp_size
    scratch = scatter_scratch(half, dim)

    def held(columns):
        return VMEM((n, 2, shard // 2, columns), BF16)

    attn_scratch = [held(4 * width), DMA((8,))]
    mlp_scratch = [held(hidden), held(hidden), DMA((4,))]

    entry = [
        ParamJob(
            [first_gain, first_shift, out_bias, second_gain, second_shift, reduce_bias],
            [query_bias, value_bias, expand_bias], n, dim,
        ).after("entry"),
        Exchange(tokens).after("entry"),
        OverFsdp(attn_w, 0, n, "entry", 2, ("none", "none", "none")).after("entry"),
    ]
    saved = []
    heads_shape = jax.ShapeDtypeStruct((heads, count, LANES), BF16)
    rows_width = jax.ShapeDtypeStruct((count, width), BF16)
    rows_hidden = jax.ShapeDtypeStruct((count, hidden), BF16)
    for l in range(LAYERS):
        last = l == LAYERS - 1
        if last:
            urgent = [
                OverCtx(expand_weight, l, near_e, n),
                OverFsdp(reduce_w, l, n, ("A", 22), 1, (("A", 23), ("A", 0), ("A", 1))),
            ]
            jobs = [*urgent, Exchange(cotangent).after(("M", 1))]
            begun, ins = [], [rows, params, key_extra, resid, (near_a, far_a, near_e)]
        else:
            urgent = [
                OverFsdp(expand_weight, l, n, "entry", 1, (("A", 21), ("A", 22), ("A", 0))).after("entry"),
                OverFsdp(reduce_w, l, n, ("A", 1), 1, (("A", 2), ("A", 2), ("A", 3))).after("entry"),
            ]
            jobs = [
                *entry,
                *urgent,
                OverFsdp(
                    attn_w, l + 1, n, ("A", 5), 1, (("M", 1), ("M", 1), ("M", 2))
                ).after(("A", 2)),
                OverFsdp(expand_weight, l + 1, n, ("M", 2)).after(("A", 5)),
            ]
            begun, ins = entry, [key_extra]
        (first, _, middle, q, k, v, mixed, second, active, slope, out, rows, *more) = call(
            lambda jobs, refs, base=8 * l, last=last, begun=begun, urgent=urgent: forward_kernel(
                jobs, begun, urgent, heads, last, base, refs
            ),
            f"forward_{l}",
            [every, own_low, own, heads_shape, heads_shape, heads_shape, rows_width, every,
             rows_hidden, rows_hidden, tiny if last else own, own_low],
            scratch + attn_scratch + mlp_scratch + ([] if last else [VMEM(own.shape, BF16)]), 1 + 2 * l,
            2 * count * dim * 4 * width + 16 * heads * count * count * HD + 4 * count * dim * hidden,
            ins, jobs,
        )
        if last:
            far_e, near_r, far_r, cot = more
        else:
            params, resid, near_a, far_a, near_e, far_e, near_r, far_r, *following = more
        weights = (near_e, far_e, near_r, far_r, near_a, far_a)
        saved.append((resid, first, q, k, v, mixed, middle, second, active, slope, weights))
        resid = out
        if not last:
            near_a, far_a, near_e = following

    carry = cot
    attn_grads, expand_grads, left_grads, right_grads, attn_vec, mlp_vec = (
        [None] * LAYERS for _ in range(6)
    )
    halves = jax.ShapeDtypeStruct((n, shard, hidden // 2), BF16)
    left_rows = jax.ShapeDtypeStruct((n, shard // 2, hidden // 2), BF16)
    square_rows = jax.ShapeDtypeStruct((n, shard // 2, hidden), BF16)
    attn_shape = jax.ShapeDtypeStruct((dim, 4 * width), BF16)
    attn_rows = jax.ShapeDtypeStruct((n, shard // 2, 4 * width), BF16)
    early = (("M", 4), ("M", 4), ("M", 5), ("M", 6))
    right_half = jax.ShapeDtypeStruct((shard, hidden // 2), BF16)
    for l in reversed(range(LAYERS)):
        resid, first, q, k, v, mixed, middle, second, active, slope, weights = saved[l]
        last = l == 0
        if last:
            attn_job = CtxSum(attn_full, n, early, keep=True)
            right_job = FsdpSum(
                halves, n, (("A", 3), ("A", 7)), spread=False, name="right"
            ).after(("M", 6))
            left_job = FsdpSum(
                halves, n, (("A", 7), ("L", 1)), spread=False, name="left"
            ).after(("A", 3))
            late = (("A", 4), ("A", 5), ("A", 6), ("A", 7))
            expand_job = CtxSum(square, n, late, keep=True, name="expand").after(("M", 6))
            final = (("L", 1), ("L", 1), ("L", 2), ("L", 2))
            final_job = CtxSum(attn_shape, n, final, keep=True, name="attn").after(("A", 8))
            jobs = [
                FsdpSum(expand_part, n, (("M", 2), ("M", 6))),
                attn_job,
                FsdpSum(attn_rows, n, (("A", 0), ("A", 3)), source=attn_job, sends=early),
                right_job,
                CtxAdd(right_half, ("L", 5), source=right_job),
                left_job,
                CtxAdd(right_half, ("L", 5), source=left_job),
                expand_job,
                FsdpSum(square_rows, n, (("L", 1), ("L", 4)), source=expand_job, sends=late),
                VectorSum(
                    [attn_vec[1], mlp_vec[1]], n, (("L", 3), ("L", 3), ("L", 3), ("L", 5))
                ).after(("A", 10)),
                final_job,
                FsdpSum(attn_rows, n, (("L", 4), ("L", 6)), source=final_job, sends=final),
                Exchange(own_low, name="carry").after(("A", 10)),
            ]
            outs = [vec, vec]
        else:
            right_job = FsdpSum(
                halves, n, (("A", 1), ("A", 6)), spread=False, name="right"
            ).after(("M", 4))
            left_job = CtxSum(narrow, n, (("A", 2),) * 4, keep=True, name="left").after(("M", 4))
            late = (("A", 6), ("A", 7), ("A", 8), ("A", 10))
            jobs = [
                Exchange(rows),
                left_job,
                FsdpSum(left_rows, n, (("A", 6), ("A", 8)), source=left_job, sends=(("A", 2),) * 4),
                right_job,
                CtxAdd(right_half, ("A", 10), source=right_job),
                CtxSum(square, n, late, name="expand").after(("M", 6)),
            ]
            outs = [vec, vec, own, (attn_shape, HBM_SPEC)]
        results = call(
            lambda jobs, refs, base=8 * l, last=last: backward_kernel(jobs, heads, base, last, refs),
            f"backward_{l}",
            outs,
            scratch
            + [
                VMEM(own.shape, F32), VMEM(every.shape, BF16), VMEM(every.shape, BF16), VMEM((count, hidden), BF16),
                VMEM(every.shape, BF16),
                held(hidden), held(hidden // 2), held(hidden // 2), DMA((6,)),
            ]
            + [VMEM((heads, count, LANES), F32), VMEM((heads, count, LANES), F32)]
            + attn_scratch
            + [DMA((2,))]
            + ([VMEM(own.shape, BF16)] if last else []),
            2 + 2 * l,
            4 * count * dim * 4 * width + 40 * heads * count * count * HD + 8 * count * dim * hidden,
            [active, slope, middle, carry, params, mixed, q, k, v, resid, (*weights, second, first)],
            jobs,
        )
        if last:
            (_, _, expand_grads[1], attn_grads[1], _, right_grads[0], _, left_grads[0],
             expand_grads[0], vectors, attn_grads[0], row_grad) = results
        else:
            (mlp_vec[l], attn_vec[l], carry, attn_full, output, left_grads[l], _, right_grads[l],
             expand_part) = results

    results = [
        jax.ShapeDtypeStruct(shape, F32)
        for shape in (
            (LAYERS, 3, shard, width), (LAYERS, width, shard), (LAYERS, shard, hidden),
            (LAYERS, hidden, shard), (6, LAYERS, shard), query_bias.shape, value_bias.shape,
            expand_bias.shape,
        )
    ]
    joint, out, expand, reduce, wide, query, value, hidden_bias = pl.pallas_call(
        finish_kernel,
        name="finish",
        out_shape=tuple(results),
        in_specs=[VMEM_SPEC] * 9,
        out_specs=tuple([HBM_SPEC] * 4 + [VMEM_SPEC] * 4),
        scratch_shapes=[VMEM(r.shape, F32) for r in results[:4]] + [DMA((LAYERS, 4))],
        compiler_params=pltpu.CompilerParams(vmem_limit_bytes=VMEM_LIMIT),
    )(*attn_grads, *expand_grads, *left_grads, *right_grads, vectors)
    return (
        output, row_grad, wide[0], wide[1], joint.transpose(0, 2, 1, 3), query, value, out,
        wide[2], wide[3], wide[4], expand, hidden_bias, reduce, wide[5],
    )


def solution(mesh):
    vector = P(None, "fsdp")
    by_head = P(None, "tp", "fsdp")
    rows = P("fsdp", ("ctx", "tp"), None)
    return jax.shard_map(
        local,
        mesh=mesh,
        in_specs=(
            rows, P("fsdp", None), vector, vector, P(None, "fsdp", None, "tp"), by_head, by_head,
            by_head, vector, vector, vector, P(None, "fsdp", "tp"), by_head, by_head, vector, rows,
        ),
        out_specs=(
            rows, rows, vector, vector, P(None, "fsdp", None, "tp"), by_head, by_head,
            by_head, vector, vector, vector, P(None, "fsdp", "tp"), by_head, by_head, vector,
        ),
        check_vma=False,
    )
```
